32 devices in a mesh: fsdp: 8 (over z, x), seq: 4 (over y, core).
Axes of the slice: x: 2, y: 2, z: 4, core: 2. Of those that a mesh axis runs over, the one named last changes fastest.
Arguments:
- states: bfloat16 [24576, 768], P(('fsdp', 'seq')), may hold values from -6 to 6
- query_weight: bfloat16 [768, 768], P('fsdp'), may hold values from -0.21875 to 0.21875
- key_weight: bfloat16 [768, 768], P('fsdp'), may hold values from -0.21875 to 0.21875
- value_weight: bfloat16 [768, 768], P('fsdp'), may hold values from -0.21875 to 0.21875
- out_weight: bfloat16 [768, 768], P('fsdp'), may hold values from -3 to 3
- query_bias: bfloat16 [768], P('fsdp'), may hold values from -4 to 4
- value_bias: bfloat16 [768], P('fsdp'), may hold values from -0.3125 to 0.3125
- out_bias: bfloat16 [768], P('fsdp'), may hold values from -1.5 to 1.5
- first_gain: bfloat16 [768], P('fsdp'), may hold values from 0.5 to 1.5
- first_shift: bfloat16 [768], P('fsdp'), may hold values from -4 to 4
- up_weight: bfloat16 [768, 3072], P('fsdp'), may hold values from -0.21875 to 0.21875
- up_bias: bfloat16 [3072], P('fsdp'), may hold values from -4 to 4
- down_weight: bfloat16 [3072, 768], P('fsdp'), may hold values from -0.109375 to 0.109375
- down_bias: bfloat16 [768], P('fsdp'), may hold values from -1.5 to 1.5
- second_gain: bfloat16 [768], P('fsdp'), may hold values from 0.5 to 1.5
- second_shift: bfloat16 [768], P('fsdp'), may hold values from -6 to 6
- lengths: int32 [8], P('fsdp'), may hold values from 1536 to 3072, as said below
- cotangent: bfloat16 [24576, 768], P(('fsdp', 'seq')), may hold values from -6 to 6
Outputs:
- output: bfloat16 [24576, 768], P(('fsdp', 'seq'))
- states_grad: bfloat16 [24576, 768], P(('fsdp', 'seq'))
- query_weight_grad: float32 [768, 768], P('fsdp')
- key_weight_grad: float32 [768, 768], P('fsdp')
- value_weight_grad: float32 [768, 768], P('fsdp')
- out_weight_grad: float32 [768, 768], P('fsdp')
- query_bias_grad: float32 [768], P('fsdp')
- value_bias_grad: float32 [768], P('fsdp')
- out_bias_grad: float32 [768], P('fsdp')
- first_gain_grad: float32 [768], P('fsdp')
- first_shift_grad: float32 [768], P('fsdp')
- up_weight_grad: float32 [768, 3072], P('fsdp')
- up_bias_grad: float32 [3072], P('fsdp')
- down_weight_grad: float32 [3072, 768], P('fsdp')
- down_bias_grad: float32 [768], P('fsdp')
- second_gain_grad: float32 [768], P('fsdp')
- second_shift_grad: float32 [768], P('fsdp')
The draws below stay inside these ranges and needn't reach their ends.
Inputs may be any that keep to these rules, and one draw needn't show every extreme that they name: Each group's real tokens fill its first lengths slots; the rest of its 3072 slots are padding. Some group is full in every draw.
All inputs are finite; a program needn't handle non-finite values.
Results may differ from the reference program's by a relative error of at most 0.017.
Values may be sent and summed in bfloat16 or wider, within the bound.
A program may use at most 192 MiB of HBM per device.

```python
import jax
import jax.numpy as jnp
from jax import lax

HEADS = 12
HEAD_DIM = 64
FF = 3072
D = 768
SLOT = 3072
GROUPS = 8
TOKENS = 24576


def draw_lengths(key, part):
    drawn = jax.random.randint(key, (GROUPS,), SLOT // 2, SLOT + 1)
    full_place = jax.random.randint(jax.random.fold_in(key, 7), (), 0, GROUPS)
    return jnp.where(jnp.arange(GROUPS) == full_place, SLOT, drawn).astype(jnp.int32)


def level_of(rng, shape, shards, least, largest):
    def one(dim, parts):
        draws = jax.random.uniform(jax.random.fold_in(jax.random.fold_in(rng, 6), dim), (parts,), jnp.float32, least / len(shards), largest / len(shards))
        return jnp.repeat(jnp.exp(draws), shape[dim] // parts).reshape((-1,) + (1,) * (len(shape) - dim - 1))

    level = one(*shards[0])
    for cut in shards[1:]:
        level = level * one(*cut)
    return level


def noise(rng, shape, width, limit, pieces=(), dtype=jnp.bfloat16):
    array = width * jax.random.normal(rng, shape, jnp.float32)
    if pieces:
        array = array * level_of(rng, shape, pieces, -0.22, 0.18)
    return jnp.clip(array, -limit, limit).astype(dtype)


def setup_inputs(seed: int = 0) -> dict:
    key_list = jax.random.split(jax.random.key(seed), 19)
    return {
        "states": noise(key_list[0], (TOKENS, D), 1.0, 6.0, ((0, 32),)),
        "query_weight": noise(key_list[1], (D, D), D ** -0.5, 0.21875, ((0, 8),)),
        "key_weight": noise(key_list[2], (D, D), D ** -0.5, 0.21875, ((0, 8),)),
        "value_weight": noise(key_list[3], (D, D), D ** -0.5, 0.21875, ((0, 8),)),
        "out_weight": noise(key_list[4], (D, D), (max(1, D * 16 // SLOT)) ** -0.5, 3.0, ((0, 8),)),
        "query_bias": noise(key_list[5], (D,), 0.3, 4.0, ((0, 8),)),
        "value_bias": noise(key_list[6], (D,), 0.02, 0.3125, ((0, 8),)),
        "out_bias": noise(key_list[7], (D,), 0.1, 1.5, ((0, 8),)),
        "first_gain": jnp.clip(1.0 + 0.1 * jax.random.normal(key_list[8], (D,), jnp.float32), 0.5, 1.5).astype(jnp.bfloat16),
        "first_shift": noise(key_list[9], (D,), 0.3, 4.0, ((0, 8),)),
        "up_weight": noise(key_list[10], (D, FF), D ** -0.5, 0.21875, ((0, 8),)),
        "up_bias": noise(key_list[11], (FF,), 0.3, 4.0, ((0, 8),)),
        "down_weight": noise(key_list[12], (FF, D), FF ** -0.5, 0.109375, ((0, 8),)),
        "down_bias": noise(key_list[13], (D,), 0.1, 1.5, ((0, 8),)),
        "second_gain": jnp.clip(1.0 + 0.1 * jax.random.normal(key_list[14], (D,), jnp.float32), 0.5, 1.5).astype(jnp.bfloat16),
        "second_shift": noise(key_list[15], (D,), 0.5, 6.0, ((0, 8),)),
        "lengths": draw_lengths(jax.random.fold_in(key_list[18], 71), 0),
        "cotangent": noise(key_list[17], (TOKENS, D), 1.0, 6.0, ((0, 32),)),
    }


@jax.custom_vjp
def low(v):
    return lax.optimization_barrier(v.astype(jnp.bfloat16)).astype(jnp.float32)

@jax.custom_vjp
def low_back(v):
    return v

def low_keep(v):
    return (low(v), None)

def low_pass(kept, grad):
    return (grad,)

def back_keep(v):
    return (v, None)

def back_low(kept, grad):
    return (low(grad),)
low.defvjp(low_keep, low_pass)
low_back.defvjp(back_keep, back_low)
HIGH = lax.Precision.HIGHEST
eps = 1e-12

def matmul(left, right):
    return jnp.dot(left, right, precision=HIGH)

def layer_norm(values, gain, shift):
    average = lax.optimization_barrier(jnp.mean(values, axis=-1, keepdims=True))
    centred = values - average
    spread = lax.optimization_barrier(jnp.mean(centred * centred, axis=-1, keepdims=True))
    return centred * lax.rsqrt(spread + eps) * gain + shift

def attend(packed):
    queries, keys_in, values, length = packed
    scores = low_back(jnp.dot(queries, keys_in.T, precision=HIGH) * HEAD_DIM ** (-0.5))
    keep = jnp.arange(SLOT) < length
    scores = jnp.where(keep[None, :], scores, -1000000000.0)
    probs = low(jax.nn.softmax(scores, axis=-1))
    return jnp.dot(probs, values, precision=HIGH)

def to_heads(values):
    return values.reshape(GROUPS, SLOT, HEADS, HEAD_DIM).transpose(0, 2, 1, 3).reshape(GROUPS * HEADS, SLOT, HEAD_DIM)

def from_heads(values):
    return values.reshape(GROUPS, HEADS, SLOT, HEAD_DIM).transpose(0, 2, 1, 3).reshape(TOKENS, D)

def reference(states, query_weight, key_weight, value_weight, out_weight, query_bias, value_bias, out_bias, first_gain, first_shift, up_weight, up_bias, down_weight, down_bias, second_gain, second_shift, lengths, cotangent):
    hidden = states.astype(jnp.float32)
    params = tuple((p.astype(jnp.float32) for p in (query_weight, key_weight, value_weight, out_weight, query_bias, value_bias, out_bias, first_gain, first_shift, up_weight, up_bias, down_weight, down_bias, second_gain, second_shift)))
    valid_rows = (jnp.arange(SLOT)[None, :] < lengths[:, None]).astype(jnp.float32).reshape(TOKENS, 1)
    head_lengths = jnp.repeat(lengths, HEADS)

    def forward(hidden, wquery, wkey, wvalue, wout, bquery, bvalue, bout, gfirst, sfirst, wup, bup, wdown, bdown, gsecond, ssecond):
        queries = low(low_back(matmul(hidden, wquery) + bquery))
        keys_in = low(low_back(matmul(hidden, wkey)))
        values = low(low_back(matmul(hidden, wvalue) + bvalue))
        context = lax.map(jax.checkpoint(attend), (to_heads(queries), to_heads(keys_in), to_heads(values), head_lengths))
        context = low(low_back(from_heads(context)))
        branch = low_back(matmul(context, wout) + bout)
        first_norm = layer_norm(hidden + branch, gfirst, sfirst)
        first_low = low(first_norm)
        pre_act = low_back(matmul(first_low, wup) + bup)
        activated = low(jax.nn.gelu(pre_act, approximate=False))
        feed = low_back(matmul(activated, wdown) + bdown)
        return layer_norm(first_norm + feed, gsecond, ssecond) * valid_rows
    output, pullback = jax.vjp(forward, hidden, params[0], params[1], params[2], params[3], params[4], params[5], params[6], params[7], params[8], params[9], params[10], params[11], params[12], params[13], params[14])
    grads = pullback(cotangent.astype(jnp.float32))
    return (output.astype(jnp.bfloat16), grads[0].astype(jnp.bfloat16), grads[1], grads[2], grads[3], grads[4], grads[5], grads[6], grads[7], grads[8], grads[9], grads[10], grads[11], grads[12], grads[13], grads[14], grads[15])
```

```python
import functools
import math

import jax
import jax.numpy as jnp
from jax import lax
from jax.experimental import pallas as pl
from jax.experimental.pallas import tpu as pltpu
from jax.sharding import PartitionSpec as P

HEAD_DIM = 64


eps = 1e-12


def product(left, right):
    return jnp.dot(left, right, preferred_element_type=jnp.float32)


def left_product(left, right):
    return lax.dot_general(
        left, right, (((0,), (0,)), ((), ())), preferred_element_type=jnp.float32
    )


def right_product(left, right):
    return lax.dot_general(
        left, right, (((1,), (1,)), ((), ())), preferred_element_type=jnp.float32
    )


def layer_norm(values, gain, shift):
    average = jnp.mean(values, axis=-1, keepdims=True)
    centred = values - average
    spread = jnp.mean(centred * centred, axis=-1, keepdims=True)
    return centred * lax.rsqrt(spread + eps) * gain + shift


def gelu_exact(values):
    return jax.nn.gelu(values, approximate=False)


def column_sums(values):
    return jnp.sum(values.astype(jnp.float32), axis=0)


def per_device(
    states,
    query_weight,
    key_weight,
    value_weight,
    out_weight,
    query_bias,
    value_bias,
    out_bias,
    first_gain,
    first_shift,
    up_weight,
    up_bias,
    down_weight,
    down_bias,
    second_gain,
    second_shift,
    lengths,
    cotangent,
):
    f32 = jnp.float32
    bf16 = jnp.bfloat16
    (
        query_mat,
        key_mat,
        value_mat,
        out_mat,
        query_add,
        value_add,
        out_add,
        gain_first,
        shift_first,
    ) = (
        lax.all_gather(query_weight, "fsdp", axis=0, tiled=True),
        lax.all_gather(key_weight, "fsdp", axis=0, tiled=True),
        lax.all_gather(value_weight, "fsdp", axis=0, tiled=True),
        lax.all_gather(out_weight, "fsdp", axis=0, tiled=True),
        lax.all_gather(query_bias, "fsdp", axis=0, tiled=True),
        lax.all_gather(value_bias, "fsdp", axis=0, tiled=True),
        lax.all_gather(out_bias, "fsdp", axis=0, tiled=True),
        lax.all_gather(first_gain, "fsdp", axis=0, tiled=True),
        lax.all_gather(first_shift, "fsdp", axis=0, tiled=True),
    )
    up_mat, up_add, down_mat, down_add, gain_second, shift_second = (
        lax.all_gather(up_weight, "fsdp", axis=0, tiled=True),
        lax.all_gather(up_bias, "fsdp", axis=0, tiled=True),
        lax.all_gather(down_weight, "fsdp", axis=0, tiled=True),
        lax.all_gather(down_bias, "fsdp", axis=0, tiled=True),
        lax.all_gather(second_gain, "fsdp", axis=0, tiled=True),
        lax.all_gather(second_shift, "fsdp", axis=0, tiled=True),
    )
    tokens = states.shape[0]
    slot_rows = tokens * lax.axis_size("seq")
    length = lengths[0]
    places = lax.axis_index("seq") * tokens + lax.iota(jnp.int32, tokens)
    valid_rows = (places < length).astype(f32)[:, None]
    queries = (product(states, query_mat) + query_add).astype(bf16)
    keys_in = product(states, key_mat).astype(bf16)
    values = (product(states, value_mat) + value_add).astype(bf16)
    head_queries, head_keys, head_values = (
        lax.all_to_all(queries, "seq", split_axis=1, concat_axis=0, tiled=True),
        lax.all_to_all(keys_in, "seq", split_axis=1, concat_axis=0, tiled=True),
        lax.all_to_all(values, "seq", split_axis=1, concat_axis=0, tiled=True),
    )
    local_width = head_queries.shape[1]
    head_count = local_width // HEAD_DIM
    block_rows = min(512, slot_rows)
    blocks = slot_rows // block_rows
    scaling = HEAD_DIM ** (-0.5)
    key_valid = lax.iota(jnp.int32, slot_rows) < length
    keys_heads = head_keys.reshape(slot_rows, head_count, HEAD_DIM)
    values_heads = head_values.reshape(slot_rows, head_count, HEAD_DIM)
    query_blocks = head_queries.reshape(blocks, block_rows, head_count, HEAD_DIM)

    def block_scores(query_block):
        scores = (
            jnp.einsum("qhd,khd->hqk", query_block, keys_heads, preferred_element_type=f32)
            * scaling
        )
        return jnp.where(key_valid[None, None, :], scores, -1000000000.0)

    def forward_block(query_block):
        scores = block_scores(query_block)
        highest = jnp.max(scores, axis=-1, keepdims=True)
        exponent = jnp.exp(scores - highest)
        totals = jnp.sum(exponent, axis=-1, keepdims=True)
        weights_soft = (exponent / totals).astype(bf16)
        context_part = jnp.einsum(
            "hqk,khd->qhd", weights_soft, values_heads, preferred_element_type=f32
        )
        return (context_part.astype(bf16), (highest + jnp.log(totals))[:, :, 0])

    context_blocks, log_totals = lax.map(forward_block, query_blocks)
    context = lax.all_to_all(
        context_blocks.reshape(slot_rows, local_width),
        "seq",
        split_axis=0,
        concat_axis=1,
        tiled=True,
    )
    hidden = states.astype(f32)
    first_sum = hidden + (product(context, out_mat) + out_add)
    first_norm, first_back = jax.vjp(
        layer_norm, first_sum, gain_first.astype(f32), shift_first.astype(f32)
    )
    first_low = first_norm.astype(bf16)
    pre_act = product(first_low, up_mat) + up_add
    activated = gelu_exact(pre_act).astype(bf16)
    second_sum = first_norm + (product(activated, down_mat) + down_add)
    normed, second_back = jax.vjp(
        layer_norm, second_sum, gain_second.astype(f32), shift_second.astype(f32)
    )
    output = (normed * valid_rows).astype(bf16)
    out_grad = cotangent.astype(f32) * valid_rows
    second_grad, gain_second_grad, shift_second_grad = second_back(out_grad)
    down_in = second_grad.astype(bf16)
    down_weight_grad = left_product(activated, down_in)
    down_bias_grad = column_sums(down_in)
    act_grad = right_product(down_in, down_mat)
    pre_grad = jax.vjp(gelu_exact, pre_act)[1](act_grad)[0].astype(bf16)
    up_weight_grad = left_product(first_low, pre_grad)
    up_bias_grad = column_sums(pre_grad)
    norm_grad = second_grad + right_product(pre_grad, up_mat)
    first_grad, gain_first_grad, shift_first_grad = first_back(norm_grad)
    branch_grad = first_grad.astype(bf16)
    out_weight_grad = left_product(context, branch_grad)
    out_bias_grad = column_sums(branch_grad)
    context_grad = right_product(branch_grad, out_mat).astype(bf16)
    head_grad = lax.all_to_all(context_grad, "seq", split_axis=1, concat_axis=0, tiled=True)
    grad_blocks = head_grad.reshape(blocks, block_rows, head_count, HEAD_DIM)

    def backward_step(carry, packed):
        key_acc, value_acc = carry
        query_block, grad_block, log_block = packed
        scores = block_scores(query_block)
        probs_full = jnp.exp(scores - log_block[:, :, None])
        probs_low = probs_full.astype(bf16)
        prob_grad = jnp.einsum("qhd,khd->hqk", grad_block, values_heads, preferred_element_type=f32)
        centre = jnp.sum(prob_grad * probs_full, axis=-1, keepdims=True)
        score_grad = (probs_full * (prob_grad - centre)).astype(bf16)
        query_part = (
            jnp.einsum("hqk,khd->qhd", score_grad, keys_heads, preferred_element_type=f32) * scaling
        )
        key_acc = (
            key_acc
            + jnp.einsum("hqk,qhd->khd", score_grad, query_block, preferred_element_type=f32)
            * scaling
        )
        value_acc = value_acc + jnp.einsum(
            "hqk,qhd->khd", probs_low, grad_block, preferred_element_type=f32
        )
        return ((key_acc, value_acc), query_part.astype(bf16))

    zeros_heads = jnp.zeros((slot_rows, head_count, HEAD_DIM), f32)
    (key_total, value_total), query_parts = lax.scan(
        backward_step, (zeros_heads, zeros_heads), (query_blocks, grad_blocks, log_totals)
    )
    query_back, key_back, value_back = (
        lax.all_to_all(
            query_parts.reshape(slot_rows, local_width),
            "seq",
            split_axis=0,
            concat_axis=1,
            tiled=True,
        ),
        lax.all_to_all(
            key_total.reshape(slot_rows, local_width).astype(bf16),
            "seq",
            split_axis=0,
            concat_axis=1,
            tiled=True,
        ),
        lax.all_to_all(
            value_total.reshape(slot_rows, local_width).astype(bf16),
            "seq",
            split_axis=0,
            concat_axis=1,
            tiled=True,
        ),
    )
    query_weight_grad = left_product(states, query_back)
    key_weight_grad = left_product(states, key_back)
    value_weight_grad = left_product(states, value_back)
    query_bias_grad = column_sums(query_back)
    value_bias_grad = column_sums(value_back)
    states_grad = (
        first_grad
        + right_product(query_back, query_mat)
        + right_product(key_back, key_mat)
        + right_product(value_back, value_mat)
    ).astype(bf16)
    attend_parts = (
        lax.psum_scatter(query_weight_grad, "fsdp", scatter_dimension=0, tiled=True),
        lax.psum_scatter(key_weight_grad, "fsdp", scatter_dimension=0, tiled=True),
        lax.psum_scatter(value_weight_grad, "fsdp", scatter_dimension=0, tiled=True),
        lax.psum_scatter(out_weight_grad, "fsdp", scatter_dimension=0, tiled=True),
        lax.psum_scatter(query_bias_grad, "fsdp", scatter_dimension=0, tiled=True),
        lax.psum_scatter(value_bias_grad, "fsdp", scatter_dimension=0, tiled=True),
        lax.psum_scatter(out_bias_grad, "fsdp", scatter_dimension=0, tiled=True),
        lax.psum_scatter(gain_first_grad, "fsdp", scatter_dimension=0, tiled=True),
        lax.psum_scatter(shift_first_grad, "fsdp", scatter_dimension=0, tiled=True),
    )
    feed_parts = (
        lax.psum_scatter(up_weight_grad, "fsdp", scatter_dimension=0, tiled=True),
        lax.psum_scatter(up_bias_grad, "fsdp", scatter_dimension=0, tiled=True),
        lax.psum_scatter(down_weight_grad, "fsdp", scatter_dimension=0, tiled=True),
        lax.psum_scatter(down_bias_grad, "fsdp", scatter_dimension=0, tiled=True),
        lax.psum_scatter(gain_second_grad, "fsdp", scatter_dimension=0, tiled=True),
        lax.psum_scatter(shift_second_grad, "fsdp", scatter_dimension=0, tiled=True),
    )
    summed = (
        lax.psum(attend_parts[0].astype(jnp.bfloat16), "seq").astype(jnp.float32),
        lax.psum(attend_parts[1].astype(jnp.bfloat16), "seq").astype(jnp.float32),
        lax.psum(attend_parts[2].astype(jnp.bfloat16), "seq").astype(jnp.float32),
        lax.psum(attend_parts[3].astype(jnp.bfloat16), "seq").astype(jnp.float32),
        lax.psum(attend_parts[4].astype(jnp.bfloat16), "seq").astype(jnp.float32),
        lax.psum(attend_parts[5].astype(jnp.bfloat16), "seq").astype(jnp.float32),
        lax.psum(attend_parts[6].astype(jnp.bfloat16), "seq").astype(jnp.float32),
        lax.psum(attend_parts[7].astype(jnp.bfloat16), "seq").astype(jnp.float32),
        lax.psum(attend_parts[8].astype(jnp.bfloat16), "seq").astype(jnp.float32),
        lax.psum(feed_parts[0].astype(jnp.bfloat16), "seq").astype(jnp.float32),
        lax.psum(feed_parts[1].astype(jnp.bfloat16), "seq").astype(jnp.float32),
        lax.psum(feed_parts[2].astype(jnp.bfloat16), "seq").astype(jnp.float32),
        lax.psum(feed_parts[3].astype(jnp.bfloat16), "seq").astype(jnp.float32),
        lax.psum(feed_parts[4].astype(jnp.bfloat16), "seq").astype(jnp.float32),
        lax.psum(feed_parts[5].astype(jnp.bfloat16), "seq").astype(jnp.float32),
    )
    return (
        output,
        states_grad,
        summed[0],
        summed[1],
        summed[2],
        summed[3],
        summed[4],
        summed[5],
        summed[6],
        summed[7],
        summed[8],
        summed[9],
        summed[10],
        summed[11],
        summed[12],
        summed[13],
        summed[14],
    )


LANE = 128
LOG2E = math.log2(math.e)
LN2 = math.log(2.0)
NT = (((1,), (1,)), ((), ()))
NN = (((1,), (0,)), ((), ()))
TN = (((0,), (0,)), ((), ()))
VMEM_BYTES = 66 * 1024 * 1024 - 2 * 1024 * 1024
f32 = jnp.float32
bf16 = jnp.bfloat16
ANY = pl.BlockSpec(memory_space=pl.ANY)
IN_VMEM = pl.BlockSpec(memory_space=pltpu.VMEM)
IN_SMEM = pl.BlockSpec(memory_space=pltpu.SMEM)
DMA = pltpu.SemaphoreType.DMA


def dims(left, right, numbers):
    return lax.dot_general(left, right, numbers, preferred_element_type=f32)


def remote(src, dst, send_sem, recv_sem, **where):
    return pltpu.make_async_remote_copy(
        src_ref=src,
        dst_ref=dst,
        send_sem=send_sem,
        recv_sem=recv_sem,
        device_id=where,
        device_id_type=pl.DeviceIdType.MESH,
    )


def greet(partners):
    barrier = pltpu.get_barrier_semaphore()
    for where in partners:
        pl.semaphore_signal(barrier, inc=1, device_id=where, device_id_type=pl.DeviceIdType.MESH)
    pl.semaphore_wait(barrier, len(partners))


def seq_peers():
    me = lax.axis_index("seq")
    across = (me + 2) % 4
    return me, me + 1 - 2 * (me % 2), across, across + 1 - 2 * (across % 2)


def place_of(index, count):
    half = index // 2
    return half + (index % 2) * (count - 1 - 2 * half)


def index_at(place, count):
    upper = place // (count // 2)
    return (1 - upper) * 2 * place + upper * (2 * (count - 1 - place) + 1)


def thirds(values):
    high = values.astype(bf16)
    rest = values - high.astype(f32)
    middle = rest.astype(bf16)
    low = (rest - middle.astype(f32)).astype(bf16)
    return high.astype(f32), middle.astype(f32), low.astype(f32)


def with_lanes(base, columns):
    lane = lax.broadcasted_iota(jnp.int32, base.shape, 1)
    for place, values in columns:
        base = jnp.where(lane == place, values, base)
    return base


def params(collective_id=None):
    if collective_id is None:
        return pltpu.CompilerParams(vmem_limit_bytes=VMEM_BYTES)
    return pltpu.CompilerParams(
        vmem_limit_bytes=VMEM_BYTES, collective_id=collective_id, has_side_effects=True
    )


def project_kernel(
    nf, pieces, length_ref, states, wq, wk, wv, vec, q_ref, k_ref, v_ref, x_out, vec_out,
    x_buf, w_buf, vec_buf, local_sem, out_sem, vec_send, vec_recv, w_send, w_recv,
    near_send, near_recv, far_send, far_recv, pass_send, pass_recv,
):
    f = lax.axis_index("fsdp")
    s, near, far, cross = seq_peers()
    tokens, width = states.shape
    heads = q_ref.shape[0]
    rows = wq.shape[0]
    window = w_buf.shape[3]
    own_width = heads * 64
    fine = pieces
    chunk = tokens // fine
    first_lane = pl.multiple_of((own_width * s // LANE) * LANE, LANE)
    weights = (wq, wk, wv)
    greet(
        [{"fsdp": (f + d) % nf} for d in range(1, nf)]
        + [{"seq": near}, {"seq": far}]
    )
    sends = []
    for d in range(1, nf):
        to = (f + d) % nf
        copy = remote(vec, vec_buf.at[f], vec_send.at[d - 1], vec_recv.at[d - 1], fsdp=to)
        copy.start()
        sends.append(copy)
        for m in range(3):
            copy = remote(
                weights[m].at[:, pl.ds(first_lane, window)],
                w_buf.at[m, f],
                w_send.at[d - 1, m],
                w_recv.at[d - 1, m],
                fsdp=to,
            )
            copy.start()
            sends.append(copy)
    for c in range(fine):
        part = pl.ds(c * chunk, chunk)
        copy = remote(
            states.at[part], x_buf.at[2, part], far_send.at[c], far_recv.at[c], seq=far
        )
        copy.start()
        sends.append(copy)
    near_copy = remote(states, x_buf.at[1], near_send, near_recv, seq=near)
    near_copy.start()
    sends.append(near_copy)
    locals_ = [
        pltpu.make_async_copy(states, x_buf.at[0], local_sem.at[0]),
        pltpu.make_async_copy(vec, vec_buf.at[f], local_sem.at[1]),
    ]
    for m in range(3):
        locals_.append(
            pltpu.make_async_copy(
                weights[m].at[:, pl.ds(first_lane, window)], w_buf.at[m, f], local_sem.at[2 + m]
            )
        )
    for copy in locals_:
        copy.start()
    for copy in locals_:
        copy.wait()

    def pass_on(c):
        part = pl.ds(c * chunk, chunk)
        remote(
            states.at[part], x_buf.at[2, part], far_send.at[c], far_recv.at[c], seq=far
        ).wait_recv()
        copy = remote(
            x_buf.at[2, part], x_buf.at[3, part], pass_send.at[c], pass_recv.at[c], seq=near
        )
        copy.start()
        sends.append(copy)

    outs = []

    def keep(slot, index):
        copy = pltpu.make_async_copy(x_buf.at[slot], x_out.at[index], out_sem.at[slot])
        copy.start()
        outs.append(copy)

    keep(0, s)
    early = fine // 2
    for c in range(early):
        pass_on(c)
    for d in range(1, nf):
        frm = (f + nf - d) % nf
        remote(vec, vec_buf.at[f], vec_send.at[d - 1], vec_recv.at[d - 1], fsdp=frm).wait_recv()
        for m in range(3):
            remote(
                weights[m].at[:, pl.ds(first_lane, window)],
                w_buf.at[m, f],
                w_send.at[d - 1, m],
                w_recv.at[d - 1, m],
                fsdp=frm,
            ).wait_recv()

    turn = (window - (own_width * s) % LANE) % window
    share = own_width // rows
    wide = lax.broadcasted_iota(jnp.int32, (1, window), 1)
    biases = []
    for row in (0, 1):
        line = jnp.zeros((1, window), f32)
        for i in range(share):
            piece = vec_buf[share * s + i][row : row + 1, :].astype(f32)
            piece = jnp.concatenate([piece, jnp.zeros((1, window - LANE), f32)], axis=1)
            if i:
                piece = pltpu.roll(piece, i * rows, 1)
            line = jnp.where((wide >= i * rows) & (wide < (i + 1) * rows), piece, line)
        biases.append(line)
    length = length_ref[0]
    block = min(256, tokens)
    mats = [w_buf[m].reshape(nf * rows, window) for m in range(3)]
    lane = lax.broadcasted_iota(jnp.int32, (block, LANE), 1)

    def heads_of(values, tail):
        found = []
        for h in range(heads):
            tile = values[:, (h // 2) * LANE : (h // 2 + 1) * LANE]
            if h % 2:
                tile = pltpu.roll(tile, 64, 1)
            found.append(jnp.where(lane < 64, tile, tail).astype(bf16))
        return found

    def compute(slot, index, part):
        x = x_buf[slot, pl.ds(part * block, block), :]
        start = pl.multiple_of(index * tokens + part * block, block)
        place = start + lax.broadcasted_iota(jnp.int32, (block, LANE), 0)
        queries = pltpu.roll(dims(x, mats[0], NN), turn, 1) + biases[0]
        q_tail = jnp.where(lane == 64, 1.0, 0.0)
        keys = pltpu.roll(dims(x, mats[1], NN), turn, 1)
        k_tail = jnp.where(
            lane == 64,
            jnp.where(place < length, 0.0, -1e9),
            jnp.where((lane > 64) & (lane < 68), 1.0, 0.0),
        )
        values = pltpu.roll(dims(x, mats[2], NN), turn, 1) + biases[1]
        v_tail = jnp.where((lane >= 64) & (lane < 67), 1.0, 0.0)
        at = pl.ds(start, block)
        for ref, found in (
            (q_ref, heads_of(queries * (LOG2E * 0.125), q_tail)),
            (k_ref, heads_of(keys, k_tail)),
            (v_ref, heads_of(values, v_tail)),
        ):
            for h in range(heads):
                ref[h, at, :] = found[h]

    def whole(slot, index):
        def body(part, carry):
            compute(slot, index, part)
            return carry

        lax.fori_loop(0, tokens // block, body, 0)

    whole(0, s)
    for c in range(early, fine - 1):
        pass_on(c)
    near_copy.wait_recv()
    keep(1, near)
    whole(1, near)
    pass_on(fine - 1)
    keep(2, far)
    whole(2, far)
    for c in range(fine):
        part = pl.ds(c * chunk, chunk)
        remote(
            x_buf.at[2, part], x_buf.at[3, part], pass_send.at[c], pass_recv.at[c], seq=near
        ).wait_recv()
    keep(3, cross)
    whole(3, cross)
    copy = pltpu.make_async_copy(vec_buf, vec_out, local_sem.at[0])
    copy.start()
    outs.append(copy)
    for copy in sends:
        copy.wait_send()
    for copy in outs:
        copy.wait()


def project(nf, heads, length, states, wq, wk, wv, vec):
    tokens, width = states.shape
    rows = wq.shape[0]
    pieces = 4
    window = 256
    slots = 4 * tokens
    head_shape = jax.ShapeDtypeStruct((heads, slots, LANE), bf16)
    return pl.pallas_call(
        functools.partial(project_kernel, nf, pieces),
        out_shape=[head_shape] * 3
        + [
            jax.ShapeDtypeStruct((4, tokens, width), bf16),
            jax.ShapeDtypeStruct((nf,) + vec.shape, bf16),
        ],
        in_specs=[IN_SMEM] + [ANY] * 5,
        out_specs=[IN_VMEM] * 3 + [ANY] * 2,
        scratch_shapes=[
            pltpu.VMEM((4, tokens, width), bf16),
            pltpu.VMEM((3, nf, rows, window), bf16),
            pltpu.VMEM((nf,) + vec.shape, bf16),
            DMA((5,)),
            DMA((4,)),
            DMA((nf - 1,)),
            DMA((nf - 1,)),
            DMA((nf - 1, 3)),
            DMA((nf - 1, 3)),
            DMA(()),
            DMA(()),
            DMA((pieces,)),
            DMA((pieces,)),
            DMA((pieces,)),
            DMA((pieces,)),
        ],
        compiler_params=params(1),
        name="project",
    )(length, states, wq, wk, wv, vec)


def ring_gather(nf, shards, halves, outs, ring_send, ring_recv, pair_send, pair_recv):
    f = lax.axis_index("fsdp")
    s, near, _, _ = seq_peers()
    side = s % 2
    step = 1 - 2 * side
    place = place_of(f, nf)
    ahead = index_at((place + step + nf) % nf, nf)
    behind = index_at((place - step + nf) % nf, nf)

    def half(ref, w):
        axis, size = halves[w]
        cut = pl.ds(pl.multiple_of(side * size, size), size)
        return ref.at[cut, :] if axis == 0 else ref.at[:, cut]

    def slot(hop):
        return index_at((place + nf - step * (hop + 1)) % nf, nf)

    def ring(w, hop, owner, source):
        return remote(
            half(source, w),
            half(outs[w].at[owner], w),
            ring_send.at[w, hop],
            ring_recv.at[w, hop],
            fsdp=ahead,
        )

    def pair(w, hop):
        piece = half(outs[w].at[slot(hop)], w)
        return remote(piece, piece, pair_send.at[w, hop], pair_recv.at[w, hop], seq=near)

    def start(w):
        ring(w, 0, f, shards[w]).start()

    def hop(w, h):
        owner = slot(h)
        ring(w, h, owner, outs[w].at[owner]).wait_recv()

        @pl.when(h < nf - 2)
        def _():
            ring(w, h + 1, owner, outs[w].at[owner]).start()

        pair(w, h).start()

    def finish(w, h):
        ring(w, h, f, shards[w]).wait_send()
        pair(w, h).wait()

    return (ahead, behind), start, hop, finish


def attend_kernel(nf, block, key_chunk, gap, halves, *refs):
    count = len(halves)
    q_ref, k_ref, v_ref = refs[:3]
    shards = refs[3 : 3 + count]
    refs = refs[3 + count :]
    qb_ref, o_ref, ctx_out = refs[:3]
    outs = refs[3 : 3 + count]
    (
        ctx_buf, ring_send, ring_recv, pair_send, pair_recv, ctx_send, ctx_recv, own_sem, copy_sem,
    ) = refs[3 + count :]
    heads, slots, _ = k_ref.shape
    tokens = slots // 4
    per = tokens // block
    f = lax.axis_index("fsdp")
    s, near, far, cross = seq_peers()
    neighbours, ring_start, ring_hop, ring_finish = ring_gather(
        nf, shards, halves, outs, ring_send, ring_recv, pair_send, pair_recv
    )
    greet([{"fsdp": i} for i in neighbours] + [{"seq": near}, {"seq": far}, {"seq": cross}])
    mine = []
    for w in range(count):
        ring_start(w)
        mine.append(pltpu.make_async_copy(shards[w], outs[w].at[f], copy_sem.at[w]))
        mine[-1].start()
    lane = lax.broadcasted_iota(jnp.int32, (block, LANE), 1)

    def partner(turn):
        relation = 3 - turn
        return ((s // 2 + relation // 2) % 2) * 2 + (s % 2 + relation % 2) % 2

    def ctx_copy(step):
        turn = step // per
        part = pl.ds(pl.multiple_of(step % per * block, block), block)
        return remote(
            ctx_buf.at[step],
            ctx_out.at[s, part],
            ctx_send.at[step],
            ctx_recv.at[step],
            seq=partner(turn),
        )

    def body(step, carry):
        base = partner(step // per) * tokens + step % per * block
        at = pl.ds(pl.multiple_of(base, block), block)
        parts = []
        for h in range(heads):
            q = q_ref[h, at, :]
            scores = []
            top = None
            for c in range(slots // key_chunk):
                scores.append(dims(q, k_ref[h, c * key_chunk : (c + 1) * key_chunk, :], NT))
                for j in range(key_chunk // LANE):
                    tile = scores[-1][:, j * LANE : (j + 1) * LANE]
                    top = tile if top is None else jnp.maximum(top, tile)
            top = jnp.max(top, axis=1, keepdims=True)
            total = None
            for c in range(slots // key_chunk):
                probs = jnp.exp2(scores[c] - top).astype(bf16)
                part = dims(probs, v_ref[h, c * key_chunk : (c + 1) * key_chunk, :], NN)
                total = part if total is None else total + part
            weight = total[:, 64:65]
            result = jnp.where(lane < 64, total * (1.0 / weight), 0.0)
            o_ref[h, at, :] = result.astype(bf16)
            high, middle, low = thirds(-(top + jnp.log2(weight)))
            qb_ref[h, at, :] = with_lanes(
                q.astype(f32), ((65, high), (66, middle), (67, low))
            ).astype(bf16)
            parts.append(result)
        for t in range((heads + 1) // 2):
            tile = parts[2 * t]
            if 2 * t + 1 < heads:
                tile = tile + pltpu.roll(parts[2 * t + 1], 64, 1)
            ctx_buf[step, :, t * LANE : (t + 1) * LANE] = tile.astype(bf16)

        @pl.when(step < 3 * per)
        def _():
            ctx_copy(step).start()

        @pl.when((step % gap == gap - 1) & (step // gap < nf - 1))
        def _():
            for w in range(count):
                ring_hop(w, step // gap)

        return carry

    lax.fori_loop(0, 4 * per, body, 0)
    owns = []
    for i in range(per):
        owns.append(
            pltpu.make_async_copy(
                ctx_buf.at[3 * per + i], ctx_out.at[s, pl.ds(i * block, block)], own_sem.at[i]
            )
        )
        owns[-1].start()

    def rest(h, carry):
        for w in range(count):
            ring_hop(w, h)
        return carry

    lax.fori_loop(min(4 * per // gap, nf - 1), nf - 1, rest, 0)

    def settle(step, carry):
        ctx_copy(step).wait()
        return carry

    lax.fori_loop(0, 3 * per, settle, 0)
    for copy in owns + mine:
        copy.wait()

    def close(h, carry):
        for w in range(count):
            ring_finish(w, h)
        return carry

    lax.fori_loop(0, nf - 1, close, 0)


def attend(nf, q, k, v, shards, halves, block, key_chunk, gap):
    heads, slots, _ = q.shape
    tokens = slots // 4
    count = len(shards)
    ctx_width = -(-heads // 2) * LANE
    hops = DMA((count, nf - 1))
    steps = slots // block
    return pl.pallas_call(
        functools.partial(attend_kernel, nf, block, key_chunk, gap, halves),
        out_shape=[jax.ShapeDtypeStruct(q.shape, bf16)] * 2
        + [jax.ShapeDtypeStruct((4, tokens, ctx_width), bf16)]
        + [jax.ShapeDtypeStruct((nf,) + w.shape, bf16) for w in shards],
        in_specs=[IN_VMEM] * (3 + count),
        out_specs=[IN_VMEM] * 2 + [ANY] * (1 + count),
        scratch_shapes=[
            pltpu.VMEM((steps, block, ctx_width), bf16),
            hops,
            hops,
            hops,
            hops,
            DMA((steps,)),
            DMA((steps,)),
            DMA((tokens // block,)),
            DMA((count,)),
        ],
        compiler_params=params(2),
        name="attend",
    )(q, k, v, *shards)


def feed_kernel(
    block, part, length_ref, states, cot, ctx, wout, up, down, vec, upb,
    out, first_grad_out, gctx, gup, gdn, gout, gvec,
    act_buf, pre_buf, slope_buf, low_t, down_t, branch_buf, g_buf, g_send, g_recv, own_sem,
):
    s, near, far, cross = seq_peers()
    tokens, width = states.shape
    hidden = up.shape[1]
    own = wout.shape[0] // 4
    steps = tokens // block
    wide = ctx.shape[2]
    greet([{"seq": near}, {"seq": far}, {"seq": cross}])
    length = length_ref[0]
    gvec[...] = jnp.zeros_like(gvec)
    peers = (s, near, far, cross)

    def line(row):
        return vec[row : row + 1, :]

    def add_line(row, values):
        gvec[row : row + 1, :] += jnp.sum(values, axis=0, keepdims=True)

    def norm(values):
        centred = values - jnp.mean(values, axis=1, keepdims=True)
        scale = lax.rsqrt(jnp.mean(centred * centred, axis=1, keepdims=True) + eps)
        return centred * scale, scale

    def norm_back(grad, gain, normed, scale):
        grad = grad * gain
        return scale * (
            grad
            - jnp.mean(grad, axis=1, keepdims=True)
            - normed * jnp.mean(grad * normed, axis=1, keepdims=True)
        )

    def send(relation, i):
        at = pl.ds(pl.multiple_of(i * block, block), block)
        return remote(
            g_buf.at[relation, at],
            gctx.at[s, at],
            g_send.at[relation - 1, i],
            g_recv.at[relation - 1, i],
            seq=peers[relation],
        )

    def body(i, carry):
        at = pl.ds(pl.multiple_of(i * block, block), block)
        attended = None
        for j in range(4):
            term = dims(ctx[j, at, :own], wout[own * j : own * (j + 1), :], NN)
            attended = term if attended is None else attended + term
        normed_first, scale_first = norm(states[at, :].astype(f32) + (attended + line(2)))
        first = normed_first * line(3) + line(4)
        low = first.astype(bf16)
        low_t[:, at] = jnp.transpose(low)
        fed = None
        for c in range(hidden // part):
            cut = slice(c * part, (c + 1) * part)
            pre = dims(low, up[:, cut], NN) + upb[:, cut]
            share = 0.5 + 0.5 * lax.erf(pre * (2.0**-0.5))
            slope_buf[:, cut] = share + pre * jnp.exp(-0.5 * pre * pre) * (2.0 * math.pi) ** -0.5
            act = (pre * share).astype(bf16)
            act_buf[at, cut] = act
            term = dims(act, down[cut, :], NN)
            fed = term if fed is None else fed + term
        normed, scale = norm(first + (fed + line(5)))
        place = s * tokens + i * block + lax.broadcasted_iota(jnp.int32, (block, 1), 0)
        valid = jnp.where(place < length, 1.0, 0.0)
        out[at, :] = ((normed * line(6) + line(7)) * valid).astype(bf16)
        grad = cot[at, :].astype(f32) * valid
        add_line(6, grad * normed)
        add_line(7, grad)
        second_grad = norm_back(grad, line(6), normed, scale)
        down_in = second_grad.astype(bf16)
        add_line(5, down_in.astype(f32))
        down_t[:, at] = jnp.transpose(down_in)
        back = second_grad
        for c in range(hidden // part):
            cut = slice(c * part, (c + 1) * part)
            pre_grad = (dims(down_in, down[cut, :], NT) * slope_buf[:, cut]).astype(bf16)
            pre_buf[at, cut] = pre_grad
            row = 8 + c * part // width
            col = c * part % width
            gvec[row : row + 1, col : col + part] += jnp.sum(
                pre_grad.astype(f32), axis=0, keepdims=True
            )
            back = back + dims(pre_grad, up[:, cut], NT)
        add_line(3, back * normed_first)
        add_line(4, back)
        first_grad = norm_back(back, line(3), normed_first, scale_first)
        first_grad_out[at, :] = first_grad
        branch = first_grad.astype(bf16)
        branch_buf[at, :] = branch
        add_line(2, branch.astype(f32))
        for relation in range(4):
            rows = pl.ds(pl.multiple_of(peers[relation] * own, 64), own)
            g_buf[relation, at, :own] = dims(branch, wout[rows, :], NT).astype(bf16)
            if wide > own:
                g_buf[relation, at, own:] = jnp.zeros((block, wide - own), bf16)
            if relation:
                send(relation, i).start()
        return carry

    lax.fori_loop(0, steps, body, 0)
    mine = pltpu.make_async_copy(g_buf.at[0], gctx.at[s], own_sem)
    mine.start()
    for j in range(4):
        gout[own * j : own * (j + 1), :] = dims(ctx[j, :, :own], branch_buf[...], TN).astype(bf16)
    cut_size = 512

    def grads(c, carry):
        cut = pl.ds(pl.multiple_of(c * cut_size, cut_size), cut_size)
        gup[:, cut] = dims(low_t[...], pre_buf[:, cut], NN).astype(bf16)
        gdn[:, cut] = dims(down_t[...], act_buf[:, cut], NN).astype(bf16)
        return carry

    lax.fori_loop(0, hidden // cut_size, grads, 0)
    for relation in range(1, 4):
        for i in range(steps):
            send(relation, i).wait()
    mine.wait()


def feed(length, states, cot, ctx, wout, up, down, vec, upb, block=256, part=768):
    tokens, width = states.shape
    hidden = up.shape[1]
    wide = ctx.shape[2]
    shape = jax.ShapeDtypeStruct
    return pl.pallas_call(
        functools.partial(feed_kernel, block, part),
        out_shape=[
            shape((tokens, width), bf16),
            shape((tokens, width), f32),
            shape((4, tokens, wide), bf16),
            shape((width, hidden), bf16),
            shape((width, hidden), bf16),
            shape((width, width), bf16),
            shape((16, width), f32),
        ],
        in_specs=[IN_SMEM] + [IN_VMEM] * 8,
        out_specs=[IN_VMEM] * 2 + [ANY] + [IN_VMEM] * 4,
        scratch_shapes=[
            pltpu.VMEM((tokens, hidden), bf16),
            pltpu.VMEM((tokens, hidden), bf16),
            pltpu.VMEM((block, hidden), f32),
            pltpu.VMEM((width, tokens), bf16),
            pltpu.VMEM((width, tokens), bf16),
            pltpu.VMEM((tokens, width), bf16),
            pltpu.VMEM((4, tokens, wide), bf16),
            DMA((3, tokens // block)),
            DMA((3, tokens // block)),
            DMA(()),
        ],
        compiler_params=params(3),
        name="feed",
    )(length, states, cot, ctx, wout, up, down, vec, upb)


def backward_kernel(
    nf, key_block, gap, q_ref, k_ref, v_ref, o_ref, gctx_ref, gup, gdn, gout,
    d_out, g_out, up_out, down_out, wout_out,
    k_t, k_acc, v_acc, own_up, own_dn, own_wo, far_up, far_dn, far_wo,
    ring_up, ring_dn, ring_wo, send_up, send_dn, send_wo, y_up, y_dn, y_wo, z_up, z_dn, z_wo,
    load_sem, pair_send, pair_recv, hop_send, hop_recv, y_send, y_recv, z_send, z_recv,
    d_send, d_recv, d_own,
):
    h, i = pl.program_id(0), pl.program_id(1)
    heads, blocks = pl.num_programs(0), pl.num_programs(1)
    step = h * blocks + i
    f = lax.axis_index("fsdp")
    s, near, far, cross = seq_peers()
    side = s % 2
    way = 1 - 2 * side
    place = place_of(f, nf)
    ahead = index_at((place + way + nf) % nf, nf)
    behind = index_at((place - way + nf) % nf, nf)
    block = q_ref.shape[1]
    slots = k_ref.shape[1]
    tokens = slots // 4
    own = (own_up, own_dn, own_wo)
    other = (far_up, far_dn, far_wo)
    came = (ring_up, ring_dn, ring_wo)
    goes = (send_up, send_dn, send_wo)
    y_buf = (y_up, y_dn, y_wo)
    z_buf = (z_up, z_dn, z_wo)
    full = (gup, gdn, gout)
    by_rows = (False, True, False)

    def half(w, which):
        if by_rows[w]:
            size = full[w].shape[0] // 2
            return full[w].at[pl.ds(pl.multiple_of(which * size, size), size), :]
        size = full[w].shape[1] // 2
        return full[w].at[:, pl.ds(pl.multiple_of(which * size, size), size)]

    def load(w):
        return pltpu.make_async_copy(half(w, side), own[w], load_sem.at[w])

    def pair(w):
        return remote(half(w, 1 - side), other[w], pair_send.at[w], pair_recv.at[w], seq=near)

    def summed(w, chunk):
        if by_rows[w]:
            size = goes[w].shape[2]
            at = (slice(None), pl.ds(pl.multiple_of(chunk * size, size), size))
        else:
            size = goes[w].shape[1]
            at = (pl.ds(pl.multiple_of(chunk * size, size), size), slice(None))
        return own[w][at].astype(f32) + other[w][at].astype(f32)

    def hop(w, t):
        return remote(goes[w].at[t], came[w].at[t], hop_send.at[w, t], hop_recv.at[w, t], fsdp=ahead)

    def to_far(w):
        return remote(goes[w].at[nf - 1], y_buf[w], y_send.at[w], y_recv.at[w], seq=far)

    def to_near(w):
        return remote(goes[w].at[0], z_buf[w], z_send.at[w], z_recv.at[w], seq=near)

    @pl.when(step == 0)
    def _():
        greet(
            [{"fsdp": ahead}, {"fsdp": behind}, {"seq": near}, {"seq": far}, {"seq": cross}]
        )
        for w in range(3):
            pair(w).start()
            load(w).start()

    @pl.when(i == 0)
    def _():
        k_acc[...] = jnp.zeros_like(k_acc)
        v_acc[...] = jnp.zeros_like(v_acc)
        k_t[...] = jnp.transpose(k_ref[0])[:64, :]

    lane = lax.broadcasted_iota(jnp.int32, (block, LANE), 1)
    first = gctx_ref[:, :LANE].astype(f32)
    second = gctx_ref[:, LANE:].astype(f32)
    grad = jnp.where(h == 0, first, jnp.where(h == 1, pltpu.roll(first, 64, 1), second))
    grad = jnp.where(lane < 64, grad, 0.0)
    delta = jnp.sum(grad * o_ref[0].astype(f32), axis=1, keepdims=True)
    high, middle, low = thirds(-delta)
    grad = with_lanes(grad, ((64, high), (65, middle), (66, low))).astype(bf16)
    q = q_ref[0]
    q_total = None
    for c in range(slots // key_block):
        ks = slice(c * key_block, (c + 1) * key_block)
        probs = jnp.exp2(dims(k_ref[0, ks, :], q, NT))
        score = (probs * dims(v_ref[0, ks, :], grad, NT)).astype(bf16)
        v_acc[ks, :] += dims(probs.astype(bf16), grad, NN)
        k_acc[ks, :] += dims(score, q, NN)
        term = dims(k_t[:, ks], score, NN)
        q_total = term if q_total is None else q_total + term
    at_head = pl.ds(pl.multiple_of(h * 64, 64), 64)
    d_out[0, at_head, pl.ds(pl.multiple_of(i * block, block), block)] = (q_total * 0.125).astype(bf16)

    peers = (s, near, far, cross)
    width_own = heads * 64

    def part(relation, m):
        to = peers[relation]
        source = d_out.at[m, at_head, pl.ds(pl.multiple_of(to * tokens, tokens), tokens)]
        target = g_out.at[m, pl.ds(pl.multiple_of(s * width_own + h * 64, 64), 64), :]
        return source, target

    def d_copy(relation, m):
        source, target = part(relation, m)
        return remote(
            source, target, d_send.at[relation - 1, m, h], d_recv.at[relation - 1, m, h],
            seq=peers[relation],
        )

    @pl.when(i == blocks - 1)
    def _():
        d_out[1, at_head, :] = jnp.transpose((k_acc[...] * LN2).astype(bf16))[:64, :]
        d_out[2, at_head, :] = jnp.transpose(v_acc[...].astype(bf16))[:64, :]
        for m in range(3):
            for relation in (3, 2, 1):
                d_copy(relation, m).start()
            source, target = part(0, m)
            pltpu.make_async_copy(source, target, d_own.at[m, h]).start()

    @pl.when(step == gap)
    def _():
        for w in range(3):
            load(w).wait()
            pair(w).wait_recv()
            goes[w][0] = summed(w, index_at((place + nf - way) % nf, nf)).astype(bf16)
            hop(w, 0).start()

    turn = step // gap - 1

    @pl.when((step % gap == 0) & (turn > 0) & (turn < nf - 1))
    def _():
        for w in range(3):
            hop(w, turn - 1).wait_recv()
            chunk = index_at((place + 2 * nf - way * (1 + turn)) % nf, nf)
            goes[w][turn] = (summed(w, chunk) + came[w][turn - 1].astype(f32)).astype(bf16)
            hop(w, turn).start()

    @pl.when(step == nf * gap)
    def _():
        for w in range(3):
            hop(w, nf - 2).wait_recv()
            goes[w][nf - 1] = (summed(w, f) + came[w][nf - 2].astype(f32)).astype(bf16)
            to_far(w).start()

    @pl.when(step == heads * blocks - 1)
    def _():
        for w in range(3):
            to_far(w).wait()
            hop(w, 0).wait_send()
            goes[w][0] = (goes[w][nf - 1].astype(f32) + y_buf[w][...].astype(f32)).astype(bf16)
            to_near(w).start()
        for w in range(3):
            pair(w).wait_send()
            for t in range(1, nf - 1):
                hop(w, t).wait_send()
            to_near(w).wait()
            mine = goes[w][0].astype(f32)
            theirs = z_buf[w][...].astype(f32)
            out = (up_out, down_out, wout_out)[w]
            size = out.shape[1] // 2
            if by_rows[w]:
                mine, theirs = jnp.transpose(mine), jnp.transpose(theirs)
            out[:, pl.ds(pl.multiple_of(side * size, size), size)] = mine
            out[:, pl.ds(pl.multiple_of((1 - side) * size, size), size)] = theirs

        def settle(head, carry):
            for m in range(3):
                for relation in range(1, 4):
                    source, target = part(relation, m)
                    remote(
                        source, target, d_send.at[relation - 1, m, head],
                        d_recv.at[relation - 1, m, head], seq=peers[relation],
                    ).wait()
                source, target = part(0, m)
                pltpu.make_async_copy(source, target, d_own.at[m, head]).wait()
            return carry

        lax.fori_loop(0, heads, settle, 0)


def backward(nf, qb, k, v, o, gctx, gup, gdn, gout, block, key_block, gap):
    heads, slots, _ = qb.shape
    tokens = slots // 4
    width, hidden = gup.shape
    rows, cols = width // nf, hidden // nf
    shape = jax.ShapeDtypeStruct
    per_block = pl.BlockSpec((1, block, LANE), lambda h, i: (h, i, 0))
    per_head = pl.BlockSpec((1, slots, LANE), lambda h, i: (h, 0, 0))
    fixed = lambda n: (lambda h, i: (0,) * n)
    chunk = ((rows, hidden // 2), (width // 2, cols), (rows, width // 2))
    halves = ((width, hidden // 2), (width // 2, hidden), (width, width // 2))
    vmem = lambda *dims_: pltpu.VMEM(dims_, bf16)
    pairs = DMA((3,))
    hops = DMA((3, nf - 1))
    return pl.pallas_call(
        functools.partial(backward_kernel, nf, key_block, gap),
        grid=(heads, slots // block),
        out_shape=[
            shape((3, heads * 64, slots), bf16),
            shape((3, width, tokens), bf16),
            shape((rows, hidden), f32),
            shape((cols, width), f32),
            shape((rows, width), f32),
        ],
        in_specs=[
            per_block,
            per_head,
            per_head,
            per_block,
            pl.BlockSpec((block, gctx.shape[1]), lambda h, i: (i, 0)),
        ]
        + [ANY] * 3,
        out_specs=[
            pl.BlockSpec((3, heads * 64, slots), fixed(3)),
            ANY,
            pl.BlockSpec((rows, hidden), fixed(2)),
            pl.BlockSpec((cols, width), fixed(2)),
            pl.BlockSpec((rows, width), fixed(2)),
        ],
        scratch_shapes=[
            pltpu.VMEM((64, slots), bf16),
            pltpu.VMEM((slots, LANE), f32),
            pltpu.VMEM((slots, LANE), f32),
        ]
        + [vmem(*x) for x in halves]
        + [vmem(*x) for x in halves]
        + [vmem(nf - 1, *x) for x in chunk]
        + [vmem(nf, *x) for x in chunk]
        + [vmem(*x) for x in chunk]
        + [vmem(*x) for x in chunk]
        + [pairs, pairs, pairs, hops, hops, pairs, pairs, pairs, pairs]
        + [DMA((3, 3, heads)), DMA((3, 3, heads)), DMA((3, heads))],
        compiler_params=params(4),
        name="backward",
    )(qb, k, v, o, gctx, gup, gdn, gout)


def last_kernel(
    nf, x_all, d_own, g_all, wq, wk, wv, first_grad, gvec,
    states_grad, q_out, k_out, v_out, vec_out, upb_out,
    w_buf, w_came, w_sum, w_parts, v_own, v_came, v_sum, v_parts,
    w_send, w_recv, p_send, p_recv, l_send, l_recv, m_send, m_recv,
):
    f = lax.axis_index("fsdp")
    s, near, far, cross = seq_peers()
    peers = (s, near, far, cross)
    tokens, width = first_grad.shape
    own = d_own.shape[1]
    rows = width // nf
    greet(
        [{"fsdp": (f + d) % nf} for d in range(1, nf)]
        + [{"seq": near}, {"seq": far}, {"seq": cross}]
    )
    ones = jnp.ones((8, tokens), bf16)
    v_own[...] = gvec[...]
    v_own[0:1, :] = dims(ones, g_all[0], NT)[0:1, :]
    v_own[1:2, :] = dims(ones, g_all[2], NT)[0:1, :]

    def v_copy(d, to):
        return remote(v_own, v_came.at[d], l_send.at[d - 1], l_recv.at[d - 1], fsdp=to)

    def w_copy(d, to):
        at = pl.ds(pl.multiple_of(to * rows, rows), rows)
        return remote(w_buf.at[at], w_came.at[d], w_send.at[d - 1], w_recv.at[d - 1], fsdp=to)

    for d in range(1, nf):
        v_copy(d, (f + d) % nf).start()
    for m in range(3):
        total = None
        for j in range(4):
            term = dims(d_own[m, :, j * tokens : (j + 1) * tokens], x_all[j], NN)
            total = term if total is None else total + term
        w_buf[:, m * own : (m + 1) * own] = jnp.transpose(total).astype(bf16)
    for d in range(1, nf):
        w_copy(d, (f + d) % nf).start()
    block = 256
    for c in range(width // block):
        cut = slice(c * block, (c + 1) * block)
        total = None
        for w, m in ((wq, 0), (wk, 1), (wv, 2)):
            term = dims(w[cut, :], g_all[m], NN)
            total = term if total is None else total + term
        states_grad[:, cut] = (first_grad[:, cut] + jnp.transpose(total)).astype(bf16)
    for d in range(1, nf):
        v_copy(d, (f + d) % nf).wait()
    v_came[0] = v_own[...]
    total = None
    for j in range(nf):
        term = v_came[(f + nf - j) % nf]
        total = term if total is None else total + term
    v_sum[...] = total

    def m_copy(relation):
        return remote(
            v_sum, v_parts.at[s], m_send.at[relation - 1], m_recv.at[relation - 1],
            seq=peers[relation],
        )

    for relation in range(1, 4):
        m_copy(relation).start()
    v_parts[s] = total
    for d in range(1, nf):
        w_copy(d, (f + d) % nf).wait()
    total = w_buf[pl.ds(pl.multiple_of(f * rows, rows), rows), :].astype(f32)
    for d in range(1, nf):
        total = total + w_came[d].astype(f32)
    w_sum[...] = total.astype(bf16)

    def p_copy(relation):
        return remote(
            w_sum, w_parts.at[s], p_send.at[relation - 1], p_recv.at[relation - 1],
            seq=peers[relation],
        )

    for relation in range(1, 4):
        p_copy(relation).start()
    w_parts[s] = total.astype(bf16)
    for relation in range(1, 4):
        m_copy(relation).wait()
    total = v_parts[0] + v_parts[1] + v_parts[2] + v_parts[3]
    mine = pltpu.roll(total, (width - rows * f) % width, 1)
    vec_out[...] = mine[:, :LANE]
    cols = 4 * rows
    lead = f * cols // width
    line = jnp.zeros((1, width), f32)
    for r in range(4):
        line = jnp.where(lead == r, total[8 + r : 9 + r, :], line)
    line = jnp.broadcast_to(line, (8, width))
    upb_out[...] = pltpu.roll(line, (width - f * cols % width) % width, 1)[:, :cols]
    for relation in range(1, 4):
        p_copy(relation).wait()
    for m, out in enumerate((q_out, k_out, v_out)):
        out[...] = jnp.concatenate(
            [w_parts[j][:, m * own : (m + 1) * own].astype(f32) for j in range(4)], axis=1
        )


def last(nf, x_all, d_own, g_all, wq, wk, wv, first_grad, gvec):
    tokens, width = first_grad.shape
    own = d_own.shape[1]
    rows = width // nf
    shape = jax.ShapeDtypeStruct
    peers, others = DMA((nf - 1,)), DMA((3,))
    return pl.pallas_call(
        functools.partial(last_kernel, nf),
        out_shape=[shape((tokens, width), bf16)]
        + [shape((rows, width), f32)] * 3
        + [shape((16, LANE), f32), shape((8, 4 * rows), f32)],
        in_specs=[IN_VMEM] * 8,
        out_specs=[IN_VMEM] * 6,
        scratch_shapes=[
            pltpu.VMEM((width, 3 * own), bf16),
            pltpu.VMEM((nf, rows, 3 * own), bf16),
            pltpu.VMEM((rows, 3 * own), bf16),
            pltpu.VMEM((4, rows, 3 * own), bf16),
            pltpu.VMEM((16, width), f32),
            pltpu.VMEM((nf, 16, width), f32),
            pltpu.VMEM((16, width), f32),
            pltpu.VMEM((4, 16, width), f32),
            peers, peers, others, others, peers, peers, others, others,
        ],
        compiler_params=params(5),
        name="last",
    )(x_all, d_own, g_all, wq, wk, wv, first_grad, gvec)


def fused_device(
    nf, states, query_weight, key_weight, value_weight, out_weight, query_bias, value_bias,
    out_bias, first_gain, first_shift, up_weight, up_bias, down_weight, down_bias, second_gain,
    second_shift, lengths, cotangent,
):
    tokens, width = states.shape
    rows = width // nf
    hidden = up_weight.shape[1]
    heads = width // 4 // 64
    lines = jnp.concatenate(
        [
            x.reshape(-1, rows)
            for x in (
                query_bias, value_bias, out_bias, first_gain, first_shift, down_bias, second_gain,
                second_shift, up_bias,
            )
        ],
        axis=0,
    )
    vec = jnp.pad(lines, ((0, 16 - lines.shape[0]), (0, LANE - rows)))
    q, k, v, x_all, vec_all = project(
        nf, heads, lengths, states, query_weight, key_weight, value_weight, vec
    )
    shards = (out_weight, up_weight, down_weight, query_weight, key_weight, value_weight)
    halves = ((1, width // 2), (1, hidden // 2), (1, width // 2)) + ((1, width // 2),) * 3
    qb, o, ctx, wout, up, down, wq, wk, wv = attend(
        nf, q, k, v, shards, halves, block=min(256, tokens), key_chunk=1024, gap=2
    )
    vec_all = vec_all[:, :, :rows].astype(f32)
    full = vec_all[:, :8].transpose(1, 0, 2).reshape(8, width)
    full_up = vec_all[:, 8:12].reshape(1, hidden)
    output, first_grad, gctx, gup, gdn, gout, gvec = feed(
        lengths, states, cotangent, ctx, wout.reshape(width, width), up.reshape(width, hidden),
        down.reshape(hidden, width), full, full_up,
    )
    d_own, g_all, up_grad, down_grad, out_grad = backward(
        nf, qb, k, v, o, gctx.reshape(4 * tokens, -1), gup, gdn, gout,
        block=min(512, tokens), key_block=512, gap=2,
    )
    square = lambda w: w.reshape(width, width)
    states_grad, q_grad, k_grad, v_grad, vec_grad, upb_grad = last(
        nf, x_all, d_own, g_all, square(wq), square(wk), square(wv), first_grad, gvec
    )
    line = lambda r: vec_grad[r, :rows]
    return (
        output, states_grad, q_grad, k_grad, v_grad, out_grad, line(0), line(1), line(2), line(3),
        line(4), up_grad, upb_grad[0], down_grad, line(5), line(6), line(7),
    )


def solution(mesh):
    nf, ns = mesh.shape["fsdp"], mesh.shape["seq"]

    def choose(states, query_weight, *rest):
        rows, width = query_weight.shape
        fits = ns == 4 and nf % 2 == 0 and rows % 16 == 0 and width == 768 and states.shape[0] % 768 == 0
        device = functools.partial(fused_device, nf) if fits else per_device
        return device(states, query_weight, *rest)

    return jax.shard_map(
        choose,
        mesh=mesh,
        in_specs=(
            P(("fsdp", "seq"), None),
            P("fsdp", None),
            P("fsdp", None),
            P("fsdp", None),
            P("fsdp", None),
            P("fsdp"),
            P("fsdp"),
            P("fsdp"),
            P("fsdp"),
            P("fsdp"),
            P("fsdp", None),
            P("fsdp"),
            P("fsdp", None),
            P("fsdp"),
            P("fsdp"),
            P("fsdp"),
            P("fsdp"),
            P(("fsdp", "seq"), None),
        ),
        out_specs=(
            P(("fsdp", "seq"), None),
            P(("fsdp", "seq"), None),
            P("fsdp", None),
            P("fsdp", None),
            P("fsdp", None),
            P("fsdp", None),
            P("fsdp"),
            P("fsdp"),
            P("fsdp"),
            P("fsdp"),
            P("fsdp"),
            P("fsdp", None),
            P("fsdp"),
            P("fsdp", None),
            P("fsdp"),
            P("fsdp"),
            P("fsdp"),
        ),
        check_vma=False,
    )
```

```python
import functools
import math

import jax
import jax.numpy as jnp
from jax import lax
from jax.experimental import pallas as pl
from jax.experimental.pallas import tpu as pltpu
from jax.sharding import PartitionSpec as P

HEAD_DIM = 64


eps = 1e-12


def product(left, right):
    return jnp.dot(left, right, preferred_element_type=jnp.float32)


def left_product(left, right):
    return lax.dot_general(
        left, right, (((0,), (0,)), ((), ())), preferred_element_type=jnp.float32
    )


def right_product(left, right):
    return lax.dot_general(
        left, right, (((1,), (1,)), ((), ())), preferred_element_type=jnp.float32
    )


def layer_norm(values, gain, shift):
    average = jnp.mean(values, axis=-1, keepdims=True)
    centred = values - average
    spread = jnp.mean(centred * centred, axis=-1, keepdims=True)
    return centred * lax.rsqrt(spread + eps) * gain + shift


def gelu_exact(values):
    return jax.nn.gelu(values, approximate=False)


def column_sums(values):
    return jnp.sum(values.astype(jnp.float32), axis=0)


def per_device(
    states,
    query_weight,
    key_weight,
    value_weight,
    out_weight,
    query_bias,
    value_bias,
    out_bias,
    first_gain,
    first_shift,
    up_weight,
    up_bias,
    down_weight,
    down_bias,
    second_gain,
    second_shift,
    lengths,
    cotangent,
):
    f32 = jnp.float32
    bf16 = jnp.bfloat16
    (
        query_mat,
        key_mat,
        value_mat,
        out_mat,
        query_add,
        value_add,
        out_add,
        gain_first,
        shift_first,
    ) = (
        lax.all_gather(query_weight, "fsdp", axis=0, tiled=True),
        lax.all_gather(key_weight, "fsdp", axis=0, tiled=True),
        lax.all_gather(value_weight, "fsdp", axis=0, tiled=True),
        lax.all_gather(out_weight, "fsdp", axis=0, tiled=True),
        lax.all_gather(query_bias, "fsdp", axis=0, tiled=True),
        lax.all_gather(value_bias, "fsdp", axis=0, tiled=True),
        lax.all_gather(out_bias, "fsdp", axis=0, tiled=True),
        lax.all_gather(first_gain, "fsdp", axis=0, tiled=True),
        lax.all_gather(first_shift, "fsdp", axis=0, tiled=True),
    )
    up_mat, up_add, down_mat, down_add, gain_second, shift_second = (
        lax.all_gather(up_weight, "fsdp", axis=0, tiled=True),
        lax.all_gather(up_bias, "fsdp", axis=0, tiled=True),
        lax.all_gather(down_weight, "fsdp", axis=0, tiled=True),
        lax.all_gather(down_bias, "fsdp", axis=0, tiled=True),
        lax.all_gather(second_gain, "fsdp", axis=0, tiled=True),
        lax.all_gather(second_shift, "fsdp", axis=0, tiled=True),
    )
    tokens = states.shape[0]
    slot_rows = tokens * lax.axis_size("seq")
    length = lengths[0]
    places = lax.axis_index("seq") * tokens + lax.iota(jnp.int32, tokens)
    valid_rows = (places < length).astype(f32)[:, None]
    queries = (product(states, query_mat) + query_add).astype(bf16)
    keys_in = product(states, key_mat).astype(bf16)
    values = (product(states, value_mat) + value_add).astype(bf16)
    head_queries, head_keys, head_values = (
        lax.all_to_all(queries, "seq", split_axis=1, concat_axis=0, tiled=True),
        lax.all_to_all(keys_in, "seq", split_axis=1, concat_axis=0, tiled=True),
        lax.all_to_all(values, "seq", split_axis=1, concat_axis=0, tiled=True),
    )
    local_width = head_queries.shape[1]
    head_count = local_width // HEAD_DIM
    block_rows = min(512, slot_rows)
    blocks = slot_rows // block_rows
    scaling = HEAD_DIM ** (-0.5)
    key_valid = lax.iota(jnp.int32, slot_rows) < length
    keys_heads = head_keys.reshape(slot_rows, head_count, HEAD_DIM)
    values_heads = head_values.reshape(slot_rows, head_count, HEAD_DIM)
    query_blocks = head_queries.reshape(blocks, block_rows, head_count, HEAD_DIM)

    def block_scores(query_block):
        scores = (
            jnp.einsum("qhd,khd->hqk", query_block, keys_heads, preferred_element_type=f32)
            * scaling
        )
        return jnp.where(key_valid[None, None, :], scores, -1000000000.0)

    def forward_block(query_block):
        scores = block_scores(query_block)
        highest = jnp.max(scores, axis=-1, keepdims=True)
        exponent = jnp.exp(scores - highest)
        totals = jnp.sum(exponent, axis=-1, keepdims=True)
        weights_soft = (exponent / totals).astype(bf16)
        context_part = jnp.einsum(
            "hqk,khd->qhd", weights_soft, values_heads, preferred_element_type=f32
        )
        return (context_part.astype(bf16), (highest + jnp.log(totals))[:, :, 0])

    context_blocks, log_totals = lax.map(forward_block, query_blocks)
    context = lax.all_to_all(
        context_blocks.reshape(slot_rows, local_width),
        "seq",
        split_axis=0,
        concat_axis=1,
        tiled=True,
    )
    hidden = states.astype(f32)
    first_sum = hidden + (product(context, out_mat) + out_add)
    first_norm, first_back = jax.vjp(
        layer_norm, first_sum, gain_first.astype(f32), shift_first.astype(f32)
    )
    first_low = first_norm.astype(bf16)
    pre_act = product(first_low, up_mat) + up_add
    activated = gelu_exact(pre_act).astype(bf16)
    second_sum = first_norm + (product(activated, down_mat) + down_add)
    normed, second_back = jax.vjp(
        layer_norm, second_sum, gain_second.astype(f32), shift_second.astype(f32)
    )
    output = (normed * valid_rows).astype(bf16)
    out_grad = cotangent.astype(f32) * valid_rows
    second_grad, gain_second_grad, shift_second_grad = second_back(out_grad)
    down_in = second_grad.astype(bf16)
    down_weight_grad = left_product(activated, down_in)
    down_bias_grad = column_sums(down_in)
    act_grad = right_product(down_in, down_mat)
    pre_grad = jax.vjp(gelu_exact, pre_act)[1](act_grad)[0].astype(bf16)
    up_weight_grad = left_product(first_low, pre_grad)
    up_bias_grad = column_sums(pre_grad)
    norm_grad = second_grad + right_product(pre_grad, up_mat)
    first_grad, gain_first_grad, shift_first_grad = first_back(norm_grad)
    branch_grad = first_grad.astype(bf16)
    out_weight_grad = left_product(context, branch_grad)
    out_bias_grad = column_sums(branch_grad)
    context_grad = right_product(branch_grad, out_mat).astype(bf16)
    head_grad = lax.all_to_all(context_grad, "seq", split_axis=1, concat_axis=0, tiled=True)
    grad_blocks = head_grad.reshape(blocks, block_rows, head_count, HEAD_DIM)

    def backward_step(carry, packed):
        key_acc, value_acc = carry
        query_block, grad_block, log_block = packed
        scores = block_scores(query_block)
        probs_full = jnp.exp(scores - log_block[:, :, None])
        probs_low = probs_full.astype(bf16)
        prob_grad = jnp.einsum("qhd,khd->hqk", grad_block, values_heads, preferred_element_type=f32)
        centre = jnp.sum(prob_grad * probs_full, axis=-1, keepdims=True)
        score_grad = (probs_full * (prob_grad - centre)).astype(bf16)
        query_part = (
            jnp.einsum("hqk,khd->qhd", score_grad, keys_heads, preferred_element_type=f32) * scaling
        )
        key_acc = (
            key_acc
            + jnp.einsum("hqk,qhd->khd", score_grad, query_block, preferred_element_type=f32)
            * scaling
        )
        value_acc = value_acc + jnp.einsum(
            "hqk,qhd->khd", probs_low, grad_block, preferred_element_type=f32
        )
        return ((key_acc, value_acc), query_part.astype(bf16))

    zeros_heads = jnp.zeros((slot_rows, head_count, HEAD_DIM), f32)
    (key_total, value_total), query_parts = lax.scan(
        backward_step, (zeros_heads, zeros_heads), (query_blocks, grad_blocks, log_totals)
    )
    query_back, key_back, value_back = (
        lax.all_to_all(
            query_parts.reshape(slot_rows, local_width),
            "seq",
            split_axis=0,
            concat_axis=1,
            tiled=True,
        ),
        lax.all_to_all(
            key_total.reshape(slot_rows, local_width).astype(bf16),
            "seq",
            split_axis=0,
            concat_axis=1,
            tiled=True,
        ),
        lax.all_to_all(
            value_total.reshape(slot_rows, local_width).astype(bf16),
            "seq",
            split_axis=0,
            concat_axis=1,
            tiled=True,
        ),
    )
    query_weight_grad = left_product(states, query_back)
    key_weight_grad = left_product(states, key_back)
    value_weight_grad = left_product(states, value_back)
    query_bias_grad = column_sums(query_back)
    value_bias_grad = column_sums(value_back)
    states_grad = (
        first_grad
        + right_product(query_back, query_mat)
        + right_product(key_back, key_mat)
        + right_product(value_back, value_mat)
    ).astype(bf16)
    attend_parts = (
        lax.psum_scatter(query_weight_grad, "fsdp", scatter_dimension=0, tiled=True),
        lax.psum_scatter(key_weight_grad, "fsdp", scatter_dimension=0, tiled=True),
        lax.psum_scatter(value_weight_grad, "fsdp", scatter_dimension=0, tiled=True),
        lax.psum_scatter(out_weight_grad, "fsdp", scatter_dimension=0, tiled=True),
        lax.psum_scatter(query_bias_grad, "fsdp", scatter_dimension=0, tiled=True),
        lax.psum_scatter(value_bias_grad, "fsdp", scatter_dimension=0, tiled=True),
        lax.psum_scatter(out_bias_grad, "fsdp", scatter_dimension=0, tiled=True),
        lax.psum_scatter(gain_first_grad, "fsdp", scatter_dimension=0, tiled=True),
        lax.psum_scatter(shift_first_grad, "fsdp", scatter_dimension=0, tiled=True),
    )
    feed_parts = (
        lax.psum_scatter(up_weight_grad, "fsdp", scatter_dimension=0, tiled=True),
        lax.psum_scatter(up_bias_grad, "fsdp", scatter_dimension=0, tiled=True),
        lax.psum_scatter(down_weight_grad, "fsdp", scatter_dimension=0, tiled=True),
        lax.psum_scatter(down_bias_grad, "fsdp", scatter_dimension=0, tiled=True),
        lax.psum_scatter(gain_second_grad, "fsdp", scatter_dimension=0, tiled=True),
        lax.psum_scatter(shift_second_grad, "fsdp", scatter_dimension=0, tiled=True),
    )
    summed = (
        lax.psum(attend_parts[0].astype(jnp.bfloat16), "seq").astype(jnp.float32),
        lax.psum(attend_parts[1].astype(jnp.bfloat16), "seq").astype(jnp.float32),
        lax.psum(attend_parts[2].astype(jnp.bfloat16), "seq").astype(jnp.float32),
        lax.psum(attend_parts[3].astype(jnp.bfloat16), "seq").astype(jnp.float32),
        lax.psum(attend_parts[4].astype(jnp.bfloat16), "seq").astype(jnp.float32),
        lax.psum(attend_parts[5].astype(jnp.bfloat16), "seq").astype(jnp.float32),
        lax.psum(attend_parts[6].astype(jnp.bfloat16), "seq").astype(jnp.float32),
        lax.psum(attend_parts[7].astype(jnp.bfloat16), "seq").astype(jnp.float32),
        lax.psum(attend_parts[8].astype(jnp.bfloat16), "seq").astype(jnp.float32),
        lax.psum(feed_parts[0].astype(jnp.bfloat16), "seq").astype(jnp.float32),
        lax.psum(feed_parts[1].astype(jnp.bfloat16), "seq").astype(jnp.float32),
        lax.psum(feed_parts[2].astype(jnp.bfloat16), "seq").astype(jnp.float32),
        lax.psum(feed_parts[3].astype(jnp.bfloat16), "seq").astype(jnp.float32),
        lax.psum(feed_parts[4].astype(jnp.bfloat16), "seq").astype(jnp.float32),
        lax.psum(feed_parts[5].astype(jnp.bfloat16), "seq").astype(jnp.float32),
    )
    return (
        output,
        states_grad,
        summed[0],
        summed[1],
        summed[2],
        summed[3],
        summed[4],
        summed[5],
        summed[6],
        summed[7],
        summed[8],
        summed[9],
        summed[10],
        summed[11],
        summed[12],
        summed[13],
        summed[14],
    )


LANE = 128
LOG2E = math.log2(math.e)
LN2 = math.log(2.0)
NT = (((1,), (1,)), ((), ()))
NN = (((1,), (0,)), ((), ()))
TN = (((0,), (0,)), ((), ()))
VMEM_BYTES = 66 * 1024 * 1024 - 2 * 1024 * 1024
f32 = jnp.float32
bf16 = jnp.bfloat16
ANY = pl.BlockSpec(memory_space=pl.ANY)
IN_VMEM = pl.BlockSpec(memory_space=pltpu.VMEM)
IN_SMEM = pl.BlockSpec(memory_space=pltpu.SMEM)
DMA = pltpu.SemaphoreType.DMA


def dims(left, right, numbers):
    return lax.dot_general(left, right, numbers, preferred_element_type=f32)


def remote(src, dst, send_sem, recv_sem, **where):
    return pltpu.make_async_remote_copy(
        src_ref=src,
        dst_ref=dst,
        send_sem=send_sem,
        recv_sem=recv_sem,
        device_id=where,
        device_id_type=pl.DeviceIdType.MESH,
    )


def greet(partners):
    barrier = pltpu.get_barrier_semaphore()
    for where in partners:
        pl.semaphore_signal(barrier, inc=1, device_id=where, device_id_type=pl.DeviceIdType.MESH)
    pl.semaphore_wait(barrier, len(partners))


def seq_peers():
    me = lax.axis_index("seq")
    across = (me + 2) % 4
    return me, me + 1 - 2 * (me % 2), across, across + 1 - 2 * (across % 2)


def place_of(index, count):
    half = index // 2
    return half + (index % 2) * (count - 1 - 2 * half)


def index_at(place, count):
    upper = place // (count // 2)
    return (1 - upper) * 2 * place + upper * (2 * (count - 1 - place) + 1)


def thirds(values):
    high = values.astype(bf16)
    rest = values - high.astype(f32)
    middle = rest.astype(bf16)
    low = (rest - middle.astype(f32)).astype(bf16)
    return high.astype(f32), middle.astype(f32), low.astype(f32)


def with_lanes(base, columns):
    lane = lax.broadcasted_iota(jnp.int32, base.shape, 1)
    for place, values in columns:
        base = jnp.where(lane == place, values, base)
    return base


def params(collective_id=None):
    if collective_id is None:
        return pltpu.CompilerParams(vmem_limit_bytes=VMEM_BYTES)
    return pltpu.CompilerParams(
        vmem_limit_bytes=VMEM_BYTES, collective_id=collective_id, has_side_effects=True
    )


def ring_gather(nf, shards, halves, outs, ring_send, ring_recv, pair_send, pair_recv):
    f = lax.axis_index("fsdp")
    s, near, _, _ = seq_peers()
    side = s % 2
    step = 1 - 2 * side
    place = place_of(f, nf)
    ahead = index_at((place + step + nf) % nf, nf)

    def half(ref, w):
        axis, size = halves[w]
        cut = pl.ds(pl.multiple_of(side * size, size), size)
        return ref.at[cut, :] if axis == 0 else ref.at[:, cut]

    def slot(hop):
        return index_at((place + nf - step * (hop + 1)) % nf, nf)

    def ring(w, hop, owner, source):
        return remote(
            half(source, w),
            half(outs[w].at[owner], w),
            ring_send.at[w, hop],
            ring_recv.at[w, hop],
            fsdp=ahead,
        )

    def pair(w, hop):
        piece = half(outs[w].at[slot(hop)], w)
        return remote(piece, piece, pair_send.at[w, hop], pair_recv.at[w, hop], seq=near)

    def start(w):
        ring(w, 0, f, shards[w]).start()

    def hop(w, h):
        owner = slot(h)
        ring(w, h, owner, outs[w].at[owner]).wait_recv()

        @pl.when(h < nf - 2)
        def _():
            ring(w, h + 1, owner, outs[w].at[owner]).start()

        pair(w, h).start()

    def finish(w, h):
        ring(w, h, f, shards[w]).wait_send()
        pair(w, h).wait()

    return start, hop, finish


def front_kernel(
    nf, block, key_chunk, halves, groups,
    length_ref, states, wq, wk, wv, vec, wout_s, up_s, down_s,
    qb_out, o_out, k_out, v_out, x_out, vec_out, ctx_out, wout, up, down,
    q_buf, k_buf, v_buf, qb_buf, o_buf, ctx_buf, x_buf, w_buf, vec_buf,
    local_sem, x_sem, kv_sem, keep_sem, vec_send, vec_recv, z_send, z_recv, h_send, h_recv,
    near_send, near_recv, far_send, far_recv, pass_send, pass_recv,
    ring_send, ring_recv, pair_send, pair_recv, ctx_send, ctx_recv, own_sem, copy_sem,
):
    f = lax.axis_index("fsdp")
    s, near, far, cross = seq_peers()
    tokens, width = states.shape
    heads, slots, _ = q_buf.shape
    rows = wq.shape[0]
    window = w_buf.shape[3]
    own_width = heads * 64
    parts = far_send.shape[0]
    chunk = tokens // parts
    per = tokens // block
    beside = f + 1 - 2 * (f % 2)
    stages = nf // 2
    first_lane = pl.multiple_of((own_width * s // LANE) * LANE, LANE)
    weights = (wq, wk, wv)
    shards, outs = (wout_s, up_s, down_s), (wout, up, down)
    ring_start, ring_hop, ring_finish = ring_gather(
        nf, shards, halves, outs, ring_send, ring_recv, pair_send, pair_recv
    )
    greet(
        [{"fsdp": (f + d) % nf} for d in range(1, nf)]
        + [{"seq": near}, {"seq": far}, {"seq": cross}]
    )

    def windowed(m):
        return weights[m].at[:, pl.ds(first_lane, window)]

    def along(d, m):
        to = (f + 2 * d) % nf
        return remote(windowed(m), w_buf.at[m, f], z_send.at[d - 1, m], z_recv.at[d - 1, m], fsdp=to)

    def aside(d, m):
        owner = (f + nf - 2 * d) % nf
        source = w_buf.at[m, owner] if d else windowed(m)
        return remote(source, w_buf.at[m, owner], h_send.at[d, m], h_recv.at[d, m], fsdp=beside)

    def vec_copy(d):
        return remote(vec, vec_buf.at[f], vec_send.at[d - 1], vec_recv.at[d - 1], fsdp=(f + d) % nf)

    def far_copy(c):
        at = pl.ds(c * chunk, chunk)
        return remote(states.at[at], x_buf.at[2, at], far_send.at[c], far_recv.at[c], seq=far)

    def pass_copy(c):
        at = pl.ds(c * chunk, chunk)
        return remote(
            x_buf.at[2, at], x_buf.at[3, at], pass_send.at[c], pass_recv.at[c], seq=near
        )

    near_copy = remote(states, x_buf.at[1], near_send, near_recv, seq=near)
    for d in range(1, stages):
        for m in range(3):
            along(d, m).start()
    for m in range(3):
        aside(0, m).start()
    for c in range(parts):
        far_copy(c).start()
    near_copy.start()
    for d in range(1, nf):
        vec_copy(d).start()
    local = [
        pltpu.make_async_copy(states, x_buf.at[0], local_sem.at[0]),
        pltpu.make_async_copy(vec, vec_buf.at[f], local_sem.at[1]),
    ]
    for m in range(3):
        local.append(pltpu.make_async_copy(windowed(m), w_buf.at[m, f], local_sem.at[2 + m]))
    mine = [
        pltpu.make_async_copy(shards[w], outs[w].at[f], copy_sem.at[w]) for w in range(len(shards))
    ]
    for copy in local + mine:
        copy.start()
    for copy in local:
        copy.wait()
    kept = []

    def keep(slot, index):
        copy = pltpu.make_async_copy(x_buf.at[slot], x_out.at[index], x_sem.at[slot])
        copy.start()
        kept.append(copy)

    def pass_on(c):
        far_copy(c).wait_recv()
        pass_copy(c).start()

    def turn_aside(d):
        for m in range(3):
            along(d, m).wait_recv()
            aside(d, m).start()

    keep(0, s)
    passed = 0
    for d in range(1, stages):
        turn_aside(d)
        if d != 2 and passed < parts - 2:
            pass_on(passed)
            passed += 1
    for w in range(len(shards)):
        ring_start(w)
    for d in range(1, nf):
        vec_copy(d).wait_recv()
    for d in range(stages):
        for m in range(3):
            aside(d, m).wait_recv()

    turn = (window - (own_width * s) % LANE) % window
    share = own_width // rows
    wide = lax.broadcasted_iota(jnp.int32, (1, window), 1)
    biases = []
    for row in (0, 1):
        line = jnp.zeros((1, window), f32)
        for i in range(share):
            piece = vec_buf[share * s + i][row : row + 1, :].astype(f32)
            piece = jnp.concatenate([piece, jnp.zeros((1, window - LANE), f32)], axis=1)
            if i:
                piece = pltpu.roll(piece, i * rows, 1)
            line = jnp.where((wide >= i * rows) & (wide < (i + 1) * rows), piece, line)
        biases.append(line)
    length = length_ref[0]
    mats = [w_buf[m].reshape(nf * rows, window) for m in range(3)]
    small = lax.broadcasted_iota(jnp.int32, (chunk, LANE), 1)
    q_tail = jnp.where(small == 64, 1.0, 0.0)
    v_tail = jnp.where((small >= 64) & (small < 67), 1.0, 0.0)

    def heads_of(values, tail):
        found = []
        for h in range(heads):
            tile = values[:, (h // 2) * LANE : (h // 2 + 1) * LANE]
            if h % 2:
                tile = pltpu.roll(tile, 64, 1)
            found.append(jnp.where(small < 64, tile, tail).astype(bf16))
        return found

    def compute(slot, index, part):
        x = x_buf[slot, pl.ds(pl.multiple_of(part * chunk, chunk), chunk), :]
        start = pl.multiple_of(index * tokens + part * chunk, chunk)
        where = start + lax.broadcasted_iota(jnp.int32, (chunk, LANE), 0)
        queries = pltpu.roll(dims(x, mats[0], NN), turn, 1) + biases[0]
        keys = pltpu.roll(dims(x, mats[1], NN), turn, 1)
        k_tail = jnp.where(
            small == 64,
            jnp.where(where < length, 0.0, -1e9),
            jnp.where((small > 64) & (small < 68), 1.0, 0.0),
        )
        values = pltpu.roll(dims(x, mats[2], NN), turn, 1) + biases[1]
        at = pl.ds(start, chunk)
        for ref, found in (
            (q_buf, heads_of(queries * (LOG2E * 0.125), q_tail)),
            (k_buf, heads_of(keys, k_tail)),
            (v_buf, heads_of(values, v_tail)),
        ):
            for h in range(heads):
                ref[h, at, :] = found[h]

    def whole(slot, index, low, high):
        def body(part, carry):
            compute(slot, index, part)
            return carry

        lax.fori_loop(low, high, body, 0)

    whole(0, s, 0, parts)
    for c in range(passed, parts - 1):
        pass_on(c)
    near_copy.wait_recv()
    keep(1, near)
    whole(1, near, 0, parts)
    for w in range(len(shards)):
        ring_hop(w, 0)
    whole(2, far, 0, parts - 1)
    pass_on(parts - 1)
    whole(2, far, parts - 1, parts)
    keep(2, far)
    for c in range(parts):
        pass_copy(c).wait_recv()
    keep(3, cross)
    whole(3, cross, 0, parts)
    saved = [
        pltpu.make_async_copy(k_buf, k_out, kv_sem.at[0]),
        pltpu.make_async_copy(v_buf, v_out, kv_sem.at[1]),
        pltpu.make_async_copy(vec_buf, vec_out, kv_sem.at[2]),
    ]
    for copy in saved:
        copy.start()

    lane = lax.broadcasted_iota(jnp.int32, (block, LANE), 1)

    def partner(round_):
        relation = 3 - round_
        return ((s // 2 + relation // 2) % 2) * 2 + (s % 2 + relation % 2) % 2

    def ctx_copy(step):
        at = pl.ds(pl.multiple_of(step % per * block, block), block)
        return remote(
            ctx_buf.at[step],
            ctx_out.at[s, at],
            ctx_send.at[step],
            ctx_recv.at[step],
            seq=partner(step // per),
        )

    def rows_of(step):
        base = partner(step // per) * tokens + step % per * block
        return pl.ds(pl.multiple_of(base, block), block)

    def keep_copies(step):
        at = rows_of(step)
        return (
            pltpu.make_async_copy(qb_buf.at[:, at], qb_out.at[:, at], keep_sem.at[0, step]),
            pltpu.make_async_copy(o_buf.at[:, at], o_out.at[:, at], keep_sem.at[1, step]),
        )

    def attend(step, carry):
        at = rows_of(step)
        results = []
        for h in range(heads):
            q = q_buf[h, at, :]
            scores = []
            top = None
            for c in range(slots // key_chunk):
                scores.append(dims(q, k_buf[h, c * key_chunk : (c + 1) * key_chunk, :], NT))
                for j in range(key_chunk // LANE):
                    tile = scores[-1][:, j * LANE : (j + 1) * LANE]
                    top = tile if top is None else jnp.maximum(top, tile)
            top = jnp.max(top, axis=1, keepdims=True)
            total = None
            for c in range(slots // key_chunk):
                probs = jnp.exp2(scores[c] - top).astype(bf16)
                term = dims(probs, v_buf[h, c * key_chunk : (c + 1) * key_chunk, :], NN)
                total = term if total is None else total + term
            weight = total[:, 64:65]
            result = jnp.where(lane < 64, total * (1.0 / weight), 0.0)
            o_buf[h, at, :] = result.astype(bf16)
            high, middle, low = thirds(-(top + jnp.log2(weight)))
            qb_buf[h, at, :] = with_lanes(
                q.astype(f32), ((65, high), (66, middle), (67, low))
            ).astype(bf16)
            results.append(result)
        for t in range((heads + 1) // 2):
            tile = results[2 * t]
            if 2 * t + 1 < heads:
                tile = tile + pltpu.roll(results[2 * t + 1], 64, 1)
            ctx_buf[step, :, t * LANE : (t + 1) * LANE] = tile.astype(bf16)

        @pl.when(step < 3 * per)
        def _():
            ctx_copy(step).start()

        for copy in keep_copies(step):
            copy.start()
        for g in range(2):
            @pl.when((step % 2 == g) & (step // 2 + 1 < nf - 1))
            def _():
                for w in groups[g]:
                    ring_hop(w, step // 2 + 1)

        return carry

    lax.fori_loop(0, 4 * per, attend, 0)
    owns = []
    for i in range(per):
        owns.append(
            pltpu.make_async_copy(
                ctx_buf.at[3 * per + i], ctx_out.at[s, pl.ds(i * block, block)], own_sem.at[i]
            )
        )
        owns[-1].start()

    def rest(h, carry):
        for w in range(len(shards)):
            ring_hop(w, h)
        return carry

    lax.fori_loop(min(2 * per + 1, nf - 1), nf - 1, rest, 0)

    def settle(step, carry):
        @pl.when(step < 3 * per)
        def _():
            ctx_copy(step).wait()

        for copy in keep_copies(step):
            copy.wait()
        return carry

    lax.fori_loop(0, 4 * per, settle, 0)
    for d in range(1, stages):
        for m in range(3):
            along(d, m).wait_send()
    for d in range(stages):
        for m in range(3):
            aside(d, m).wait_send()
    for d in range(1, nf):
        vec_copy(d).wait_send()
    for c in range(parts):
        far_copy(c).wait_send()
        pass_copy(c).wait_send()
    near_copy.wait_send()
    for copy in owns + mine + kept + saved:
        copy.wait()

    def close(h, carry):
        for w in range(len(shards)):
            ring_finish(w, h)
        return carry

    lax.fori_loop(0, nf - 1, close, 0)


def front(nf, heads, length, states, wq, wk, wv, vec, wout, up, down, block, key_chunk):
    tokens, width = states.shape
    rows = wq.shape[0]
    slots = 4 * tokens
    parts = 4
    window = 256
    shards = (wout, up, down)
    halves = tuple((1, w.shape[1] // 2) for w in shards)
    wide = -(-heads // 2) * LANE
    steps = slots // block
    shape = jax.ShapeDtypeStruct
    head_shape = shape((heads, slots, LANE), bf16)
    head_buf = pltpu.VMEM((heads, slots, LANE), bf16)
    hops = DMA((3, nf - 1))
    stage = DMA((nf // 2 - 1, 3))
    stage_aside = DMA((nf // 2, 3))
    peers = DMA((nf - 1,))
    fine = DMA((parts,))
    return pl.pallas_call(
        functools.partial(front_kernel, nf, block, key_chunk, halves, ((1,), (0, 2))),
        out_shape=[head_shape] * 4
        + [
            shape((4, tokens, width), bf16),
            shape((nf,) + vec.shape, bf16),
            shape((4, tokens, wide), bf16),
        ]
        + [shape((nf,) + w.shape, bf16) for w in shards],
        in_specs=[IN_SMEM] + [ANY] * 8,
        out_specs=[ANY] * 10,
        scratch_shapes=[head_buf] * 5
        + [
            pltpu.VMEM((steps, block, wide), bf16),
            pltpu.VMEM((4, tokens, width), bf16),
            pltpu.VMEM((3, nf, rows, window), bf16),
            pltpu.VMEM((nf,) + vec.shape, bf16),
            DMA((5,)),
            DMA((4,)),
            DMA((3,)),
            DMA((2, steps)),
            peers, peers, stage, stage, stage_aside, stage_aside,
            DMA(()), DMA(()), fine, fine, fine, fine,
            hops, hops, hops, hops,
            DMA((steps,)), DMA((steps,)),
            DMA((tokens // block,)),
            DMA((3,)),
        ],
        compiler_params=params(1),
        name="front",
    )(length, states, wq, wk, wv, vec, wout, up, down)


def plane_gather(nf, shards, outs, z_send, z_recv, h_send, h_recv, n_send, n_recv):
    f = lax.axis_index("fsdp")
    s, near, _, _ = seq_peers()
    side = s % 2
    beside = f + 1 - 2 * (f % 2)
    stages = nf // 2
    count = len(shards)

    def half(ref):
        size = ref.shape[1] // 2
        return ref.at[:, pl.ds(pl.multiple_of(side * size, size), size)]

    def along(d, m):
        return remote(
            half(shards[m]), half(outs[m].at[f]), z_send.at[d - 1, m], z_recv.at[d - 1, m],
            fsdp=(f + 2 * d) % nf,
        )

    def aside(d, m):
        owner = (f + nf - 2 * d) % nf
        source = outs[m].at[owner] if d else shards[m]
        return remote(
            half(source), half(outs[m].at[owner]), h_send.at[d, m], h_recv.at[d, m], fsdp=beside
        )

    def share(e, m):
        owner = (f + nf - 2 * e) % nf if e < stages else (beside + nf - 2 * (e - stages)) % nf
        piece = half(outs[m].at[owner])
        return remote(piece, piece, n_send.at[e - 1, m], n_recv.at[e - 1, m], seq=near)

    def start():
        for d in range(1, stages):
            for m in range(count):
                along(d, m).start()
        for m in range(count):
            aside(0, m).start()

    def first():
        for d in range(1, stages):
            for m in range(count):
                along(d, m).wait_recv()
                aside(d, m).start()
                share(d, m).start()

    def second():
        for d in range(stages):
            for m in range(count):
                aside(d, m).wait_recv()
                share(stages + d, m).start()

    def finish():
        for m in range(count):
            for d in range(1, stages):
                along(d, m).wait_send()
            for d in range(stages):
                aside(d, m).wait_send()
            for e in range(1, nf):
                share(e, m).wait()

    return start, first, second, finish


def feed_kernel(
    nf, block, part, length_ref, states, ctx, wout, vec, upb, up_hbm, down_hbm, cot_hbm,
    wq_s, wk_s, wv_s,
    out, first_grad_out, gctx, up_sum, down_sum, wout_sum, gvec, wq, wk, wv,
    up, down, cot, out_buf, first_buf, act_buf, pre_buf, slope_buf, low_t, down_t, branch_buf,
    g_buf, up_give, down_give, wout_give, up_take, down_take, wout_take,
    load_sem, keep_sem, g_send, g_recv, own_sem, give_send, give_recv, sum_sem, shard_sem,
    z_send, z_recv, h_send, h_recv, n_send, n_recv,
):
    f = lax.axis_index("fsdp")
    s, near, far, cross = seq_peers()
    side = s % 2
    beside = f + 1 - 2 * (f % 2)
    tokens, width = states.shape
    hidden = up.shape[1]
    own = wout.shape[0] // 4
    steps = tokens // block
    wide = ctx.shape[2]
    loads = [
        pltpu.make_async_copy(up_hbm, up, load_sem.at[0]),
        pltpu.make_async_copy(down_hbm, down, load_sem.at[1]),
        pltpu.make_async_copy(cot_hbm, cot, load_sem.at[2]),
    ]
    for copy in loads:
        copy.start()
    shards, outs = (wq_s, wk_s, wv_s), (wq, wk, wv)
    gather = plane_gather(nf, shards, outs, z_send, z_recv, h_send, h_recv, n_send, n_recv)
    greet(
        [{"fsdp": (f + 2 * d) % nf} for d in range(1, nf // 2)]
        + [{"fsdp": beside}, {"seq": near}, {"seq": far}, {"seq": cross}]
    )
    gather[0]()
    kept = [pltpu.make_async_copy(shards[m], outs[m].at[f], shard_sem.at[m]) for m in range(3)]
    for copy in kept:
        copy.start()
    length = length_ref[0]
    gvec[...] = jnp.zeros_like(gvec)
    peers = (s, near, far, cross)

    def line(row):
        return vec[row : row + 1, :]

    def add_line(row, values):
        gvec[row : row + 1, :] += jnp.sum(values, axis=0, keepdims=True)

    def norm(values):
        centred = values - jnp.mean(values, axis=1, keepdims=True)
        scale = lax.rsqrt(jnp.mean(centred * centred, axis=1, keepdims=True) + eps)
        return centred * scale, scale

    def norm_back(grad, gain, normed, scale):
        grad = grad * gain
        return scale * (
            grad
            - jnp.mean(grad, axis=1, keepdims=True)
            - normed * jnp.mean(grad * normed, axis=1, keepdims=True)
        )

    def rows_of(i):
        return pl.ds(pl.multiple_of(i * block, block), block)

    def send(relation, i):
        at = rows_of(i)
        return remote(
            g_buf.at[relation, at],
            gctx.at[s, at],
            g_send.at[relation - 1, i],
            g_recv.at[relation - 1, i],
            seq=peers[relation],
        )

    def keep(i):
        at = rows_of(i)
        return (
            pltpu.make_async_copy(out_buf.at[at], out.at[at], keep_sem.at[0, i]),
            pltpu.make_async_copy(first_buf.at[at], first_grad_out.at[at], keep_sem.at[1, i]),
        )

    def body(i, carry):
        at = rows_of(i)
        attended = None
        for j in range(4):
            term = dims(ctx[j, at, :own], wout[own * j : own * (j + 1), :], NN)
            attended = term if attended is None else attended + term
        normed_first, scale_first = norm(states[at, :].astype(f32) + (attended + line(2)))
        first = normed_first * line(3) + line(4)
        low = first.astype(bf16)
        low_t[:, at] = jnp.transpose(low)

        @pl.when(i == 0)
        def _():
            for copy in loads:
                copy.wait()

        fed = None
        for c in range(hidden // part):
            cut = slice(c * part, (c + 1) * part)
            pre = dims(low, up[:, cut], NN) + upb[:, cut]
            share = 0.5 + 0.5 * lax.erf(pre * (2.0**-0.5))
            slope_buf[:, cut] = share + pre * jnp.exp(-0.5 * pre * pre) * (2.0 * math.pi) ** -0.5
            act = (pre * share).astype(bf16)
            act_buf[at, cut] = act
            term = dims(act, down[cut, :], NN)
            fed = term if fed is None else fed + term
        normed, scale = norm(first + (fed + line(5)))
        place = s * tokens + i * block + lax.broadcasted_iota(jnp.int32, (block, 1), 0)
        valid = jnp.where(place < length, 1.0, 0.0)
        out_buf[at, :] = ((normed * line(6) + line(7)) * valid).astype(bf16)
        grad = cot[at, :].astype(f32) * valid
        add_line(6, grad * normed)
        add_line(7, grad)
        second_grad = norm_back(grad, line(6), normed, scale)
        down_in = second_grad.astype(bf16)
        add_line(5, down_in.astype(f32))
        down_t[:, at] = jnp.transpose(down_in)
        back = second_grad
        for c in range(hidden // part):
            cut = slice(c * part, (c + 1) * part)
            pre_grad = (dims(down_in, down[cut, :], NT) * slope_buf[:, cut]).astype(bf16)
            pre_buf[at, cut] = pre_grad
            row = 8 + c * part // width
            col = c * part % width
            gvec[row : row + 1, col : col + part] += jnp.sum(
                pre_grad.astype(f32), axis=0, keepdims=True
            )
            back = back + dims(pre_grad, up[:, cut], NT)
        add_line(3, back * normed_first)
        add_line(4, back)
        first_grad = norm_back(back, line(3), normed_first, scale_first)
        first_buf[at, :] = first_grad
        branch = first_grad.astype(bf16)
        branch_buf[at, :] = branch
        add_line(2, branch.astype(f32))
        for relation in range(4):
            rows = pl.ds(pl.multiple_of(peers[relation] * own, 64), own)
            g_buf[relation, at, :own] = dims(branch, wout[rows, :], NT).astype(bf16)
            if wide > own:
                g_buf[relation, at, own:] = jnp.zeros((block, wide - own), bf16)
            if relation:
                send(relation, i).start()
        for copy in keep(i):
            copy.start()

        @pl.when(i == min(1, steps - 1))
        def _():
            gather[1]()

        return carry

    lax.fori_loop(0, steps, body, 0)
    mine = pltpu.make_async_copy(g_buf.at[0], gctx.at[s], own_sem)
    mine.start()

    pieces = give_send.shape[1]
    up_cut = hidden // 2 // pieces
    down_cut = hidden // pieces

    def up_part(which, c):
        cut = pl.ds(pl.multiple_of(which * (hidden // 2) + c * up_cut, up_cut), up_cut)
        return dims(low_t[...], pre_buf[:, cut], NN)

    def down_part(which, c):
        rows = pl.ds(pl.multiple_of(which * (width // 2), width // 2), width // 2)
        cut = pl.ds(pl.multiple_of(c * down_cut, down_cut), down_cut)
        return dims(down_t[rows, :], act_buf[:, cut], NN)

    def wout_part(which, j):
        cut = pl.ds(pl.multiple_of(which * (width // 2), width // 2), width // 2)
        return dims(ctx[j, :, :own], branch_buf[:, cut], TN)

    def cols(c, size):
        return (slice(None), pl.ds(pl.multiple_of(c * size, size), size))

    def give(w, c):
        if w == 2:
            pair = wout_give, wout_take
        else:
            at = cols(c, (up_cut, down_cut)[w])
            pair = (up_give, down_give)[w].at[at], (up_take, down_take)[w].at[at]
        return remote(*pair, give_send.at[w, c], give_recv.at[w, c], seq=near)

    def give_away(c, carry):
        up_give[cols(c, up_cut)] = up_part(1 - side, c).astype(bf16)
        give(0, c).start()
        down_give[cols(c, down_cut)] = down_part(1 - side, c).astype(bf16)
        give(1, c).start()
        return carry

    def add_own(c, carry):
        at = cols(c, up_cut)
        total = up_part(side, c)
        give(0, c).wait()
        up_give[at] = (total + up_take[at].astype(f32)).astype(bf16)
        at = cols(c, down_cut)
        total = down_part(side, c)
        give(1, c).wait()
        down_give[at] = (total + down_take[at].astype(f32)).astype(bf16)
        return carry

    lax.fori_loop(0, pieces, give_away, 0)
    for j in range(4):
        wout_give[own * j : own * (j + 1), :] = wout_part(1 - side, j).astype(bf16)
    give(2, 0).start()
    lax.fori_loop(0, pieces, add_own, 0)
    sums = [
        pltpu.make_async_copy(up_give, up_sum, sum_sem.at[0]),
        pltpu.make_async_copy(down_give, down_sum, sum_sem.at[1]),
    ]
    for copy in sums:
        copy.start()
    gather[2]()
    totals = [wout_part(side, j) for j in range(4)]
    give(2, 0).wait()
    for j in range(4):
        at = slice(own * j, own * (j + 1))
        wout_give[at, :] = (totals[j] + wout_take[at, :].astype(f32)).astype(bf16)
    sums.append(pltpu.make_async_copy(wout_give, wout_sum, sum_sem.at[2]))
    sums[-1].start()
    for relation in range(1, 4):
        for i in range(steps):
            send(relation, i).wait()
    for i in range(steps):
        for copy in keep(i):
            copy.wait()
    gather[3]()
    for copy in [mine] + kept + sums:
        copy.wait()


def feed(nf, length, states, cot, ctx, wout, up, down, vec, upb, shards, block=256, part=768):
    tokens, width = states.shape
    hidden = up.shape[1]
    wide = ctx.shape[2]
    pieces = 3
    shape = jax.ShapeDtypeStruct
    halves = ((width, hidden // 2), (width // 2, hidden), (width, width // 2))
    vmem = lambda *size: pltpu.VMEM(size, bf16)
    steps = tokens // block
    staged = DMA((nf // 2 - 1, 3))
    staged_aside = DMA((nf // 2, 3))
    return pl.pallas_call(
        functools.partial(feed_kernel, nf, block, part),
        out_shape=[
            shape((tokens, width), bf16),
            shape((tokens, width), f32),
            shape((4, tokens, wide), bf16),
        ]
        + [shape(x, bf16) for x in halves]
        + [shape((16, width), f32)]
        + [shape((nf,) + w.shape, bf16) for w in shards],
        in_specs=[IN_SMEM] + [IN_VMEM] * 5 + [ANY] * 6,
        out_specs=[ANY] * 6 + [IN_VMEM] + [ANY] * 3,
        scratch_shapes=[
            vmem(width, hidden),
            vmem(hidden, width),
            vmem(tokens, width),
            vmem(tokens, width),
            pltpu.VMEM((tokens, width), f32),
            vmem(tokens, hidden),
            vmem(tokens, hidden),
            pltpu.VMEM((block, hidden), f32),
            vmem(width, tokens),
            vmem(width, tokens),
            vmem(tokens, width),
            vmem(4, tokens, wide),
        ]
        + [vmem(*x) for x in halves] * 2
        + [
            DMA((3,)),
            DMA((2, steps)),
            DMA((3, steps)),
            DMA((3, steps)),
            DMA(()),
            DMA((3, pieces)),
            DMA((3, pieces)),
            DMA((3,)),
            DMA((3,)),
            staged, staged, staged_aside, staged_aside,
            DMA((nf - 1, 3)), DMA((nf - 1, 3)),
        ],
        compiler_params=params(3),
        name="feed",
    )(length, states, ctx, wout, vec, upb, up, down, cot, *shards)


def back_kernel(
    nf, key_block, groups, q_ref, k_ref, v_ref, o_ref, gctx_ref,
    up_sum, down_sum, wout_sum, x_hbm, wq_hbm, wk_hbm, wv_hbm, first_hbm, gvec_hbm,
    states_grad, up_out, down_out, wout_out, qkv_out, vec_out, upb_out,
    k_t, k_acc, v_acc, d_out, g_all, x_all, w_all, first_grad,
    own_up, own_dn, own_wo, ring_up, ring_dn, ring_wo, y_up, y_dn, y_wo, z_up, z_dn, z_wo,
    w_buf, w_came, w_sum, w_parts, v_own, v_came, v_sum, v_parts,
    load_sem, late_sem, hop_send, hop_recv, y_send, y_recv, z_send, z_recv,
    d_send, d_recv, d_own, w_send, w_recv, p_send, p_recv, l_send, l_recv, m_send, m_recv,
):
    h, i = pl.program_id(0), pl.program_id(1)
    heads, blocks = pl.num_programs(0), pl.num_programs(1)
    count = w_buf.shape[0]
    step = h * blocks + i
    final = heads * blocks - 1
    f = lax.axis_index("fsdp")
    s, near, far, cross = seq_peers()
    peers = (s, near, far, cross)
    side = s % 2
    way = 1 - 2 * side
    place = place_of(f, nf)
    ahead = index_at((place + way + nf) % nf, nf)
    block = q_ref.shape[1]
    slots = k_ref.shape[1]
    tokens = slots // 4
    width = x_all.shape[2]
    rows = width // nf
    width_own = count * 64
    full = (up_sum, down_sum, wout_sum)
    own = (own_up, own_dn, own_wo)
    came = (ring_up, ring_dn, ring_wo)
    y_buf = (y_up, y_dn, y_wo)
    z_buf = (z_up, z_dn, z_wo)
    outs = (up_out, down_out, wout_out)
    by_cols = (False, True, False)

    def chunk_at(w, chunk):
        size = came[w].shape[1 + by_cols[w]]
        cut = pl.ds(pl.multiple_of(chunk * size, size), size)
        return (slice(None), cut) if by_cols[w] else (cut, slice(None))

    def hop(w, t, source):
        return remote(source, came[w].at[t], hop_send.at[w, t], hop_recv.at[w, t], fsdp=ahead)

    def chunk_of(t):
        return index_at((place + 2 * nf - way * (1 + t)) % nf, nf)

    def to_far(w):
        return remote(came[w].at[nf - 2], y_buf[w], y_send.at[w], y_recv.at[w], seq=far)

    def to_near(w):
        return remote(y_buf[w], z_buf[w], z_send.at[w], z_recv.at[w], seq=near)

    def loads():
        return [pltpu.make_async_copy(full[w], own[w], load_sem.at[w]) for w in range(3)]

    def late():
        return [
            pltpu.make_async_copy(x_hbm, x_all, late_sem.at[0]),
            pltpu.make_async_copy(wq_hbm, w_all.at[0], late_sem.at[1]),
            pltpu.make_async_copy(wk_hbm, w_all.at[1], late_sem.at[2]),
            pltpu.make_async_copy(wv_hbm, w_all.at[2], late_sem.at[3]),
            pltpu.make_async_copy(first_hbm, first_grad, late_sem.at[4]),
            pltpu.make_async_copy(gvec_hbm, v_own, late_sem.at[5]),
        ]

    @pl.when(step == 0)
    def _():
        greet(
            [{"fsdp": (f + d) % nf} for d in range(1, nf)]
            + [{"seq": near}, {"seq": far}, {"seq": cross}]
        )
        for w in range(3):
            hop(w, 0, full[w].at[chunk_at(w, chunk_of(0))]).start()
        for copy in loads() + late():
            copy.start()

    @pl.when(i == 0)
    def _():
        k_acc[...] = jnp.zeros_like(k_acc)
        v_acc[...] = jnp.zeros_like(v_acc)
        k_t[...] = jnp.transpose(k_ref[0])[:64, :]

    lane = lax.broadcasted_iota(jnp.int32, (block, LANE), 1)
    first = gctx_ref[:, :LANE].astype(f32)
    second = gctx_ref[:, LANE:].astype(f32)
    grad = jnp.where(h == 0, first, jnp.where(h == 1, pltpu.roll(first, 64, 1), second))
    grad = jnp.where(lane < 64, grad, 0.0)
    delta = jnp.sum(grad * o_ref[0].astype(f32), axis=1, keepdims=True)
    high, middle, low = thirds(-delta)
    grad = with_lanes(grad, ((64, high), (65, middle), (66, low))).astype(bf16)
    q = q_ref[0]
    q_total = None
    for c in range(slots // key_block):
        ks = slice(c * key_block, (c + 1) * key_block)
        probs = jnp.exp2(dims(k_ref[0, ks, :], q, NT))
        score = (probs * dims(v_ref[0, ks, :], grad, NT)).astype(bf16)
        v_acc[ks, :] += dims(probs.astype(bf16), grad, NN)
        k_acc[ks, :] += dims(score, q, NN)
        term = dims(k_t[:, ks], score, NN)
        q_total = term if q_total is None else q_total + term
    at_head = pl.ds(pl.multiple_of(h * 64, 64), 64)
    d_out[0, at_head, pl.ds(pl.multiple_of(i * block, block), block)] = (q_total * 0.125).astype(bf16)

    @pl.when(step == 1)
    def _():
        for copy in loads():
            copy.wait()

    for g in range(2):
        t = step // 2

        @pl.when((step % 2 == g) & (t > 0) & (t < nf - 1))
        def _():
            for w in groups[g]:
                hop(w, t - 1, came[w].at[t - 1]).wait_recv()
                here = own[w][chunk_at(w, chunk_of(t))].astype(f32)
                came[w][t - 1] = (here + came[w][t - 1].astype(f32)).astype(bf16)
                hop(w, t, came[w].at[t - 1]).start()

        @pl.when((step % 2 == g) & (t == nf - 1))
        def _():
            for w in groups[g]:
                hop(w, nf - 2, came[w].at[nf - 2]).wait_recv()
                here = own[w][chunk_at(w, f)].astype(f32)
                came[w][nf - 2] = (here + came[w][nf - 2].astype(f32)).astype(bf16)
                to_far(w).start()

    def part(relation, m, head):
        to = peers[relation]
        source = d_out.at[
            m, pl.ds(pl.multiple_of(head * 64, 64), 64), pl.ds(pl.multiple_of(to * tokens, tokens), tokens)
        ]
        target = g_all.at[m, pl.ds(pl.multiple_of(s * width_own + head * 64, 64), 64), :]
        return source, target

    def d_copy(relation, m, head):
        source, target = part(relation, m, head)
        return remote(
            source, target, d_send.at[relation - 1, m, head], d_recv.at[relation - 1, m, head],
            seq=peers[relation],
        )

    def d_local(m, head):
        source, target = part(0, m, head)
        return pltpu.make_async_copy(source, target, d_own.at[m, head])

    def w_copy(head, d):
        to = (f + d) % nf
        at = pl.ds(pl.multiple_of(to * rows, rows), rows)
        return remote(
            w_buf.at[head, at], w_came.at[head, d - 1], w_send.at[head, d - 1],
            w_recv.at[head, d - 1], fsdp=to,
        )

    def p_copy(head, relation):
        return remote(
            w_sum.at[head], w_parts.at[s, head], p_send.at[head, relation - 1],
            p_recv.at[head, relation - 1], seq=peers[relation],
        )

    def v_copy(d):
        return remote(
            v_own, v_came.at[d], l_send.at[d - 1], l_recv.at[d - 1], fsdp=(f + d) % nf
        )

    def m_copy(relation):
        return remote(
            v_sum, v_parts.at[s], m_send.at[relation - 1], m_recv.at[relation - 1],
            seq=peers[relation],
        )

    def settle_head(head):
        for d in range(1, nf):
            w_copy(head, d).wait()
        total = w_buf[head, pl.ds(pl.multiple_of(f * rows, rows), rows), :].astype(f32)
        for d in range(1, nf):
            total = total + w_came[head, d - 1].astype(f32)
        w_sum[head] = total.astype(bf16)
        for relation in (3, 2, 1):
            p_copy(head, relation).start()
        w_parts[s, head] = total.astype(bf16)

    @pl.when(i == blocks - 1)
    def _():
        d_out[1, at_head, :] = jnp.transpose((k_acc[...] * LN2).astype(bf16))[:64, :]
        d_out[2, at_head, :] = jnp.transpose(v_acc[...].astype(bf16))[:64, :]
        for m in range(3):
            for relation in (3, 2, 1):
                d_copy(relation, m, h).start()
            d_local(m, h).start()

        @pl.when(h == 0)
        def _():
            for copy in late():
                copy.wait()

        left = jnp.concatenate([d_out[m, at_head, :] for m in range(3)], axis=0)
        total = None
        for j in range(4):
            term = dims(left[:, j * tokens : (j + 1) * tokens], x_all[j], NN)
            total = term if total is None else total + term
        w_buf[h] = jnp.transpose(total).astype(bf16)
        for d in range(1, nf):
            w_copy(h, d).start()

        @pl.when(h > 0)
        def _():
            settle_head(h - 1)

    @pl.when(step == final)
    def _():
        ones = jnp.ones((8, slots), bf16)
        for row, m in ((0, 0), (1, 2)):
            line = dims(ones, d_out[m], NT)
            line = jnp.concatenate([line, jnp.zeros((8, width - width_own), f32)], axis=1)
            v_own[row : row + 1, :] = pltpu.roll(line, s * width_own, 1)[0:1, :]
        for d in range(1, nf):
            v_copy(d).start()
        for w in range(3):
            to_far(w).wait()
            y_buf[w][...] = (
                came[w][nf - 2].astype(f32) + y_buf[w][...].astype(f32)
            ).astype(bf16)
            to_near(w).start()
        for d in range(1, nf):
            v_copy(d).wait()
        v_came[0] = v_own[...]
        total = None
        for j in range(nf):
            term = v_came[(f + nf - j) % nf]
            total = term if total is None else total + term
        v_sum[...] = total
        for relation in (3, 2, 1):
            m_copy(relation).start()
        v_parts[s] = total
        settle_head(count - 1)
        for w in range(3):
            for t in range(nf - 1):
                hop(w, t, came[w].at[t]).wait_send()
            to_near(w).wait()
            mine, theirs = y_buf[w][...], z_buf[w][...]
            out = outs[w]
            size = out.shape[1] // 2
            if by_cols[w]:
                mine, theirs = jnp.transpose(mine), jnp.transpose(theirs)
            out[:, pl.ds(pl.multiple_of(side * size, size), size)] = mine
            out[:, pl.ds(pl.multiple_of((1 - side) * size, size), size)] = theirs

        def settle(head, carry):
            for m in range(3):
                for relation in range(1, 4):
                    d_copy(relation, m, head).wait()
                d_local(m, head).wait()
            return carry

        lax.fori_loop(0, count, settle, 0)
        cut_size = 256
        mats = [w_all[m].reshape(width, width) for m in range(3)]
        for c in range(width // cut_size):
            cut = slice(c * cut_size, (c + 1) * cut_size)
            total = None
            for m in range(3):
                term = dims(mats[m][cut, :], g_all[m], NN)
                total = term if total is None else total + term
            states_grad[:, cut] = (first_grad[:, cut] + jnp.transpose(total)).astype(bf16)
        for relation in range(1, 4):
            m_copy(relation).wait()
        total = v_parts[0] + v_parts[1] + v_parts[2] + v_parts[3]
        vec_out[...] = pltpu.roll(total, (width - rows * f) % width, 1)[:, :LANE]
        cols = 4 * rows
        lead = f * cols // width
        line = jnp.zeros((1, width), f32)
        for r in range(4):
            line = jnp.where(lead == r, total[8 + r : 9 + r, :], line)
        line = jnp.broadcast_to(line, (8, width))
        upb_out[...] = pltpu.roll(line, (width - f * cols % width) % width, 1)[:, :cols]
        for head in range(count):
            for relation in range(1, 4):
                p_copy(head, relation).wait()
        for m in range(3):
            qkv_out[m] = jnp.concatenate(
                [
                    w_parts[j, head][:, m * 64 : (m + 1) * 64].astype(f32)
                    for j in range(4)
                    for head in range(count)
                ],
                axis=1,
            ).astype(bf16)


def back(nf, qb, k, v, o, gctx, sums, x_all, mats, first_grad, gvec, block, key_block):
    heads, slots, _ = qb.shape
    tokens = slots // 4
    width = x_all.shape[2]
    hidden = sums[0].shape[1] * 2
    rows, cols = width // nf, hidden // nf
    shape = jax.ShapeDtypeStruct
    per_block = pl.BlockSpec((1, block, LANE), lambda h, i: (h, i, 0))
    per_head = pl.BlockSpec((1, slots, LANE), lambda h, i: (h, 0, 0))
    chunk = ((rows, hidden // 2), (width // 2, cols), (rows, width // 2))
    vmem = lambda *size: pltpu.VMEM(size, bf16)
    triple = DMA((3,))
    hops = DMA((3, nf - 1))
    own = heads * 64
    results = [
        shape((tokens, width), bf16),
        shape((rows, hidden), bf16),
        shape((cols, width), bf16),
        shape((rows, width), bf16),
        shape((3, rows, width), bf16),
        shape((16, LANE), f32),
        shape((8, cols), f32),
    ]
    return pl.pallas_call(
        functools.partial(back_kernel, nf, key_block, ((0,), (1, 2))),
        grid=(heads, slots // block),
        out_shape=results,
        in_specs=[
            per_block,
            per_head,
            per_head,
            per_block,
            pl.BlockSpec((block, gctx.shape[1]), lambda h, i: (i, 0)),
        ]
        + [ANY] * 9,
        out_specs=[
            pl.BlockSpec(x.shape, functools.partial(lambda n, h, i: (0,) * n, len(x.shape)))
            for x in results
        ],
        scratch_shapes=[
            vmem(64, slots),
            pltpu.VMEM((slots, LANE), f32),
            pltpu.VMEM((slots, LANE), f32),
            vmem(3, own, slots),
            vmem(3, width, tokens),
            vmem(4, tokens, width),
            vmem(3, nf, rows, width),
            pltpu.VMEM((tokens, width), f32),
        ]
        + [vmem(*x.shape) for x in sums]
        + [vmem(nf - 1, *x) for x in chunk]
        + [vmem(*x) for x in chunk] * 2
        + [
            vmem(heads, width, 192),
            vmem(heads, nf - 1, rows, 192),
            vmem(heads, rows, 192),
            vmem(4, heads, rows, 192),
            pltpu.VMEM((16, width), f32),
            pltpu.VMEM((nf, 16, width), f32),
            pltpu.VMEM((16, width), f32),
            pltpu.VMEM((4, 16, width), f32),
            triple, DMA((6,)), hops, hops, triple, triple, triple, triple,
            DMA((3, 3, heads)), DMA((3, 3, heads)), DMA((3, heads)),
            DMA((heads, nf - 1)), DMA((heads, nf - 1)), DMA((heads, 3)), DMA((heads, 3)),
            DMA((nf - 1,)), DMA((nf - 1,)), triple, triple,
        ],
        compiler_params=params(4),
        name="back",
    )(qb, k, v, o, gctx, *sums, x_all, *mats, first_grad, gvec)


def results_kernel(rows, output, states_grad, up, down, wout, qkv, vec, upb, *outs):
    outs[0][...] = output[...]
    outs[1][...] = states_grad[...]
    for m in range(3):
        outs[2 + m][...] = qkv[m].astype(f32)
    outs[5][...] = wout[...].astype(f32)
    outs[6][...] = up[...].astype(f32)
    outs[7][...] = down[...].astype(f32)
    for r in range(8):
        outs[8 + r][...] = vec[r : r + 1, :rows]
    outs[16][...] = upb[0:1, :]


def results(rows, output, states_grad, up, down, wout, qkv, vec, upb):
    shape = jax.ShapeDtypeStruct
    pieces = 3
    grads = [shape(qkv.shape[1:], f32)] * 3 + [shape(x.shape, f32) for x in (wout, up, down)]
    outs = [shape(output.shape, bf16)] * 2 + grads
    lines = [shape((1, rows), f32)] * 8 + [shape((1, upb.shape[1]), f32)]

    def cut(x):
        n = len(x.shape)
        size = x.shape[: n - 2] + (x.shape[n - 2] // pieces, x.shape[n - 1])
        return pl.BlockSpec(size, functools.partial(lambda n, i: (0,) * (n - 2) + (i, 0), n))

    def same(x):
        return pl.BlockSpec(x.shape, lambda i: (0, 0))

    return pl.pallas_call(
        functools.partial(results_kernel, rows),
        grid=(pieces,),
        out_shape=outs + lines,
        in_specs=[cut(x) for x in (output, states_grad, up, down, wout, qkv)] + [same(vec), same(upb)],
        out_specs=[cut(x) for x in outs] + [same(x) for x in lines],
        compiler_params=params(),
        name="results",
    )(output, states_grad, up, down, wout, qkv, vec, upb)


def fused_device(
    nf, states, query_weight, key_weight, value_weight, out_weight, query_bias, value_bias,
    out_bias, first_gain, first_shift, up_weight, up_bias, down_weight, down_bias, second_gain,
    second_shift, lengths, cotangent,
):
    tokens, width = states.shape
    rows = width // nf
    hidden = up_weight.shape[1]
    heads = width // 4 // 64
    lines = jnp.concatenate(
        [
            x.reshape(-1, rows)
            for x in (
                query_bias, value_bias, out_bias, first_gain, first_shift, down_bias, second_gain,
                second_shift, up_bias,
            )
        ],
        axis=0,
    )
    vec = jnp.pad(lines, ((0, 16 - lines.shape[0]), (0, LANE - rows)))
    qb, o, k, v, x_all, vec_all, ctx, wout, up, down = front(
        nf, heads, lengths, states, query_weight, key_weight, value_weight, vec, out_weight,
        up_weight, down_weight, block=256, key_chunk=1024,
    )
    vec_all = vec_all[:, :, :rows].astype(f32)
    full = vec_all[:, :8].transpose(1, 0, 2).reshape(8, width)
    full_up = vec_all[:, 8:12].reshape(1, hidden)
    output, first_grad, gctx, up_sum, down_sum, wout_sum, gvec, wq, wk, wv = feed(
        nf, lengths, states, cotangent, ctx, wout.reshape(width, width),
        up.reshape(width, hidden), down.reshape(hidden, width), full, full_up,
        (query_weight, key_weight, value_weight),
    )
    states_grad, up_grad, down_grad, out_grad, qkv, vec_grad, upb_grad = back(
        nf, qb, k, v, o, gctx.reshape(4 * tokens, -1), (up_sum, down_sum, wout_sum), x_all,
        (wq, wk, wv), first_grad, gvec, block=512, key_block=512,
    )
    done = results(rows, output, states_grad, up_grad, down_grad, out_grad, qkv, vec_grad, upb_grad)
    output, states_grad, q_grad, k_grad, v_grad, out_grad, up_grad, down_grad = done[:8]
    lines = [x.reshape(-1) for x in done[8:]]
    return (
        output, states_grad, q_grad, k_grad, v_grad, out_grad, *lines[:5], up_grad, lines[8],
        down_grad, *lines[5:8],
    )


def solution(mesh):
    nf, ns = mesh.shape["fsdp"], mesh.shape["seq"]

    def choose(states, query_weight, *rest):
        rows, width = query_weight.shape
        fits = ns == 4 and nf in (4, 6, 8) and rows % 16 == 0 and width == 768 and states.shape[0] % 768 == 0
        device = functools.partial(fused_device, nf) if fits else per_device
        return device(states, query_weight, *rest)

    return jax.shard_map(
        choose,
        mesh=mesh,
        in_specs=(
            P(("fsdp", "seq"), None),
            P("fsdp", None),
            P("fsdp", None),
            P("fsdp", None),
            P("fsdp", None),
            P("fsdp"),
            P("fsdp"),
            P("fsdp"),
            P("fsdp"),
            P("fsdp"),
            P("fsdp", None),
            P("fsdp"),
            P("fsdp", None),
            P("fsdp"),
            P("fsdp"),
            P("fsdp"),
            P("fsdp"),
            P(("fsdp", "seq"), None),
        ),
        out_specs=(
            P(("fsdp", "seq"), None),
            P(("fsdp", "seq"), None),
            P("fsdp", None),
            P("fsdp", None),
            P("fsdp", None),
            P("fsdp", None),
            P("fsdp"),
            P("fsdp"),
            P("fsdp"),
            P("fsdp"),
            P("fsdp"),
            P("fsdp", None),
            P("fsdp"),
            P("fsdp", None),
            P("fsdp"),
            P("fsdp"),
            P("fsdp"),
        ),
        check_vma=False,
    )
```

```python
import functools
import math

import jax
import jax.numpy as jnp
from jax import lax
from jax.experimental import pallas as pl
from jax.experimental.pallas import tpu as pltpu
from jax.sharding import PartitionSpec as P

HEAD_DIM = 64


eps = 1e-12


def product(left, right):
    return jnp.dot(left, right, preferred_element_type=jnp.float32)


def left_product(left, right):
    return lax.dot_general(
        left, right, (((0,), (0,)), ((), ())), preferred_element_type=jnp.float32
    )


def right_product(left, right):
    return lax.dot_general(
        left, right, (((1,), (1,)), ((), ())), preferred_element_type=jnp.float32
    )


def layer_norm(values, gain, shift):
    average = jnp.mean(values, axis=-1, keepdims=True)
    centred = values - average
    spread = jnp.mean(centred * centred, axis=-1, keepdims=True)
    return centred * lax.rsqrt(spread + eps) * gain + shift


def gelu_exact(values):
    return jax.nn.gelu(values, approximate=False)


def column_sums(values):
    return jnp.sum(values.astype(jnp.float32), axis=0)


def per_device(
    states,
    query_weight,
    key_weight,
    value_weight,
    out_weight,
    query_bias,
    value_bias,
    out_bias,
    first_gain,
    first_shift,
    up_weight,
    up_bias,
    down_weight,
    down_bias,
    second_gain,
    second_shift,
    lengths,
    cotangent,
):
    f32 = jnp.float32
    bf16 = jnp.bfloat16
    (
        query_mat,
        key_mat,
        value_mat,
        out_mat,
        query_add,
        value_add,
        out_add,
        gain_first,
        shift_first,
    ) = (
        lax.all_gather(query_weight, "fsdp", axis=0, tiled=True),
        lax.all_gather(key_weight, "fsdp", axis=0, tiled=True),
        lax.all_gather(value_weight, "fsdp", axis=0, tiled=True),
        lax.all_gather(out_weight, "fsdp", axis=0, tiled=True),
        lax.all_gather(query_bias, "fsdp", axis=0, tiled=True),
        lax.all_gather(value_bias, "fsdp", axis=0, tiled=True),
        lax.all_gather(out_bias, "fsdp", axis=0, tiled=True),
        lax.all_gather(first_gain, "fsdp", axis=0, tiled=True),
        lax.all_gather(first_shift, "fsdp", axis=0, tiled=True),
    )
    up_mat, up_add, down_mat, down_add, gain_second, shift_second = (
        lax.all_gather(up_weight, "fsdp", axis=0, tiled=True),
        lax.all_gather(up_bias, "fsdp", axis=0, tiled=True),
        lax.all_gather(down_weight, "fsdp", axis=0, tiled=True),
        lax.all_gather(down_bias, "fsdp", axis=0, tiled=True),
        lax.all_gather(second_gain, "fsdp", axis=0, tiled=True),
        lax.all_gather(second_shift, "fsdp", axis=0, tiled=True),
    )
    tokens = states.shape[0]
    slot_rows = tokens * lax.axis_size("seq")
    length = lengths[0]
    places = lax.axis_index("seq") * tokens + lax.iota(jnp.int32, tokens)
    valid_rows = (places < length).astype(f32)[:, None]
    queries = (product(states, query_mat) + query_add).astype(bf16)
    keys_in = product(states, key_mat).astype(bf16)
    values = (product(states, value_mat) + value_add).astype(bf16)
    head_queries, head_keys, head_values = (
        lax.all_to_all(queries, "seq", split_axis=1, concat_axis=0, tiled=True),
        lax.all_to_all(keys_in, "seq", split_axis=1, concat_axis=0, tiled=True),
        lax.all_to_all(values, "seq", split_axis=1, concat_axis=0, tiled=True),
    )
    local_width = head_queries.shape[1]
    head_count = local_width // HEAD_DIM
    block_rows = min(512, slot_rows)
    blocks = slot_rows // block_rows
    scaling = HEAD_DIM ** (-0.5)
    key_valid = lax.iota(jnp.int32, slot_rows) < length
    keys_heads = head_keys.reshape(slot_rows, head_count, HEAD_DIM)
    values_heads = head_values.reshape(slot_rows, head_count, HEAD_DIM)
    query_blocks = head_queries.reshape(blocks, block_rows, head_count, HEAD_DIM)

    def block_scores(query_block):
        scores = (
            jnp.einsum("qhd,khd->hqk", query_block, keys_heads, preferred_element_type=f32)
            * scaling
        )
        return jnp.where(key_valid[None, None, :], scores, -1000000000.0)

    def forward_block(query_block):
        scores = block_scores(query_block)
        highest = jnp.max(scores, axis=-1, keepdims=True)
        exponent = jnp.exp(scores - highest)
        totals = jnp.sum(exponent, axis=-1, keepdims=True)
        weights_soft = (exponent / totals).astype(bf16)
        context_part = jnp.einsum(
            "hqk,khd->qhd", weights_soft, values_heads, preferred_element_type=f32
        )
        return (context_part.astype(bf16), (highest + jnp.log(totals))[:, :, 0])

    context_blocks, log_totals = lax.map(forward_block, query_blocks)
    context = lax.all_to_all(
        context_blocks.reshape(slot_rows, local_width),
        "seq",
        split_axis=0,
        concat_axis=1,
        tiled=True,
    )
    hidden = states.astype(f32)
    first_sum = hidden + (product(context, out_mat) + out_add)
    first_norm, first_back = jax.vjp(
        layer_norm, first_sum, gain_first.astype(f32), shift_first.astype(f32)
    )
    first_low = first_norm.astype(bf16)
    pre_act = product(first_low, up_mat) + up_add
    activated = gelu_exact(pre_act).astype(bf16)
    second_sum = first_norm + (product(activated, down_mat) + down_add)
    normed, second_back = jax.vjp(
        layer_norm, second_sum, gain_second.astype(f32), shift_second.astype(f32)
    )
    output = (normed * valid_rows).astype(bf16)
    out_grad = cotangent.astype(f32) * valid_rows
    second_grad, gain_second_grad, shift_second_grad = second_back(out_grad)
    down_in = second_grad.astype(bf16)
    down_weight_grad = left_product(activated, down_in)
    down_bias_grad = column_sums(down_in)
    act_grad = right_product(down_in, down_mat)
    pre_grad = jax.vjp(gelu_exact, pre_act)[1](act_grad)[0].astype(bf16)
    up_weight_grad = left_product(first_low, pre_grad)
    up_bias_grad = column_sums(pre_grad)
    norm_grad = second_grad + right_product(pre_grad, up_mat)
    first_grad, gain_first_grad, shift_first_grad = first_back(norm_grad)
    branch_grad = first_grad.astype(bf16)
    out_weight_grad = left_product(context, branch_grad)
    out_bias_grad = column_sums(branch_grad)
    context_grad = right_product(branch_grad, out_mat).astype(bf16)
    head_grad = lax.all_to_all(context_grad, "seq", split_axis=1, concat_axis=0, tiled=True)
    grad_blocks = head_grad.reshape(blocks, block_rows, head_count, HEAD_DIM)

    def backward_step(carry, packed):
        key_acc, value_acc = carry
        query_block, grad_block, log_block = packed
        scores = block_scores(query_block)
        probs_full = jnp.exp(scores - log_block[:, :, None])
        probs_low = probs_full.astype(bf16)
        prob_grad = jnp.einsum("qhd,khd->hqk", grad_block, values_heads, preferred_element_type=f32)
        centre = jnp.sum(prob_grad * probs_full, axis=-1, keepdims=True)
        score_grad = (probs_full * (prob_grad - centre)).astype(bf16)
        query_part = (
            jnp.einsum("hqk,khd->qhd", score_grad, keys_heads, preferred_element_type=f32) * scaling
        )
        key_acc = (
            key_acc
            + jnp.einsum("hqk,qhd->khd", score_grad, query_block, preferred_element_type=f32)
            * scaling
        )
        value_acc = value_acc + jnp.einsum(
            "hqk,qhd->khd", probs_low, grad_block, preferred_element_type=f32
        )
        return ((key_acc, value_acc), query_part.astype(bf16))

    zeros_heads = jnp.zeros((slot_rows, head_count, HEAD_DIM), f32)
    (key_total, value_total), query_parts = lax.scan(
        backward_step, (zeros_heads, zeros_heads), (query_blocks, grad_blocks, log_totals)
    )
    query_back, key_back, value_back = (
        lax.all_to_all(
            query_parts.reshape(slot_rows, local_width),
            "seq",
            split_axis=0,
            concat_axis=1,
            tiled=True,
        ),
        lax.all_to_all(
            key_total.reshape(slot_rows, local_width).astype(bf16),
            "seq",
            split_axis=0,
            concat_axis=1,
            tiled=True,
        ),
        lax.all_to_all(
            value_total.reshape(slot_rows, local_width).astype(bf16),
            "seq",
            split_axis=0,
            concat_axis=1,
            tiled=True,
        ),
    )
    query_weight_grad = left_product(states, query_back)
    key_weight_grad = left_product(states, key_back)
    value_weight_grad = left_product(states, value_back)
    query_bias_grad = column_sums(query_back)
    value_bias_grad = column_sums(value_back)
    states_grad = (
        first_grad
        + right_product(query_back, query_mat)
        + right_product(key_back, key_mat)
        + right_product(value_back, value_mat)
    ).astype(bf16)
    attend_parts = (
        lax.psum_scatter(query_weight_grad, "fsdp", scatter_dimension=0, tiled=True),
        lax.psum_scatter(key_weight_grad, "fsdp", scatter_dimension=0, tiled=True),
        lax.psum_scatter(value_weight_grad, "fsdp", scatter_dimension=0, tiled=True),
        lax.psum_scatter(out_weight_grad, "fsdp", scatter_dimension=0, tiled=True),
        lax.psum_scatter(query_bias_grad, "fsdp", scatter_dimension=0, tiled=True),
        lax.psum_scatter(value_bias_grad, "fsdp", scatter_dimension=0, tiled=True),
        lax.psum_scatter(out_bias_grad, "fsdp", scatter_dimension=0, tiled=True),
        lax.psum_scatter(gain_first_grad, "fsdp", scatter_dimension=0, tiled=True),
        lax.psum_scatter(shift_first_grad, "fsdp", scatter_dimension=0, tiled=True),
    )
    feed_parts = (
        lax.psum_scatter(up_weight_grad, "fsdp", scatter_dimension=0, tiled=True),
        lax.psum_scatter(up_bias_grad, "fsdp", scatter_dimension=0, tiled=True),
        lax.psum_scatter(down_weight_grad, "fsdp", scatter_dimension=0, tiled=True),
        lax.psum_scatter(down_bias_grad, "fsdp", scatter_dimension=0, tiled=True),
        lax.psum_scatter(gain_second_grad, "fsdp", scatter_dimension=0, tiled=True),
        lax.psum_scatter(shift_second_grad, "fsdp", scatter_dimension=0, tiled=True),
    )
    summed = (
        lax.psum(attend_parts[0].astype(jnp.bfloat16), "seq").astype(jnp.float32),
        lax.psum(attend_parts[1].astype(jnp.bfloat16), "seq").astype(jnp.float32),
        lax.psum(attend_parts[2].astype(jnp.bfloat16), "seq").astype(jnp.float32),
        lax.psum(attend_parts[3].astype(jnp.bfloat16), "seq").astype(jnp.float32),
        lax.psum(attend_parts[4].astype(jnp.bfloat16), "seq").astype(jnp.float32),
        lax.psum(attend_parts[5].astype(jnp.bfloat16), "seq").astype(jnp.float32),
        lax.psum(attend_parts[6].astype(jnp.bfloat16), "seq").astype(jnp.float32),
        lax.psum(attend_parts[7].astype(jnp.bfloat16), "seq").astype(jnp.float32),
        lax.psum(attend_parts[8].astype(jnp.bfloat16), "seq").astype(jnp.float32),
        lax.psum(feed_parts[0].astype(jnp.bfloat16), "seq").astype(jnp.float32),
        lax.psum(feed_parts[1].astype(jnp.bfloat16), "seq").astype(jnp.float32),
        lax.psum(feed_parts[2].astype(jnp.bfloat16), "seq").astype(jnp.float32),
        lax.psum(feed_parts[3].astype(jnp.bfloat16), "seq").astype(jnp.float32),
        lax.psum(feed_parts[4].astype(jnp.bfloat16), "seq").astype(jnp.float32),
        lax.psum(feed_parts[5].astype(jnp.bfloat16), "seq").astype(jnp.float32),
    )
    return (
        output,
        states_grad,
        summed[0],
        summed[1],
        summed[2],
        summed[3],
        summed[4],
        summed[5],
        summed[6],
        summed[7],
        summed[8],
        summed[9],
        summed[10],
        summed[11],
        summed[12],
        summed[13],
        summed[14],
    )


LANE = 128
LOG2E = math.log2(math.e)
LN2 = math.log(2.0)
NT = (((1,), (1,)), ((), ()))
NN = (((1,), (0,)), ((), ()))
TN = (((0,), (0,)), ((), ()))
VMEM_BYTES = 66 * 1024 * 1024 - 2 * 1024 * 1024
f32 = jnp.float32
bf16 = jnp.bfloat16
ANY = pl.BlockSpec(memory_space=pl.ANY)
IN_VMEM = pl.BlockSpec(memory_space=pltpu.VMEM)
IN_SMEM = pl.BlockSpec(memory_space=pltpu.SMEM)
DMA = pltpu.SemaphoreType.DMA


def dims(left, right, numbers):
    return lax.dot_general(left, right, numbers, preferred_element_type=f32)


def remote(src, dst, send_sem, recv_sem, **where):
    return pltpu.make_async_remote_copy(
        src_ref=src,
        dst_ref=dst,
        send_sem=send_sem,
        recv_sem=recv_sem,
        device_id=where,
        device_id_type=pl.DeviceIdType.MESH,
    )


def hail(partners):
    barrier = pltpu.get_barrier_semaphore()
    for where in partners:
        pl.semaphore_signal(barrier, inc=1, device_id=where, device_id_type=pl.DeviceIdType.MESH)


def hailed(partners):
    pl.semaphore_wait(pltpu.get_barrier_semaphore(), len(partners))


def greet(partners):
    hail(partners)
    hailed(partners)


def seq_peers():
    me = lax.axis_index("seq")
    across = (me + 2) % 4
    return me, me + 1 - 2 * (me % 2), across, across + 1 - 2 * (across % 2)


def place_of(index, count):
    half = index // 2
    return half + (index % 2) * (count - 1 - 2 * half)


def index_at(place, count):
    upper = place // (count // 2)
    return (1 - upper) * 2 * place + upper * (2 * (count - 1 - place) + 1)


def thirds(values):
    high = values.astype(bf16)
    rest = values - high.astype(f32)
    middle = rest.astype(bf16)
    low = (rest - middle.astype(f32)).astype(bf16)
    return high.astype(f32), middle.astype(f32), low.astype(f32)


def with_lanes(base, columns):
    lane = lax.broadcasted_iota(jnp.int32, base.shape, 1)
    for place, values in columns:
        base = jnp.where(lane == place, values, base)
    return base


def params(collective_id=None):
    if collective_id is None:
        return pltpu.CompilerParams(vmem_limit_bytes=VMEM_BYTES)
    return pltpu.CompilerParams(
        vmem_limit_bytes=VMEM_BYTES, collective_id=collective_id, has_side_effects=True
    )


def ring_gather(nf, shards, halves, outs, ring_send, ring_recv, pair_send, pair_recv):
    f = lax.axis_index("fsdp")
    s, near, _, _ = seq_peers()
    side = s % 2
    step = 1 - 2 * side
    place = place_of(f, nf)
    ahead = index_at((place + step + nf) % nf, nf)

    def half(ref, w):
        axis, size = halves[w]
        cut = pl.ds(pl.multiple_of(side * size, size), size)
        return ref.at[cut, :] if axis == 0 else ref.at[:, cut]

    def slot(hop):
        return index_at((place + nf - step * (hop + 1)) % nf, nf)

    def ring(w, hop, owner, source):
        return remote(
            half(source, w),
            half(outs[w].at[owner], w),
            ring_send.at[w, hop],
            ring_recv.at[w, hop],
            fsdp=ahead,
        )

    def pair(w, hop):
        piece = half(outs[w].at[slot(hop)], w)
        return remote(piece, piece, pair_send.at[w, hop], pair_recv.at[w, hop], seq=near)

    def start(w):
        ring(w, 0, f, shards[w]).start()

    def hop(w, h):
        owner = slot(h)
        ring(w, h, owner, outs[w].at[owner]).wait_recv()

        @pl.when(h < nf - 2)
        def _():
            ring(w, h + 1, owner, outs[w].at[owner]).start()

        pair(w, h).start()

    def finish(w, h):
        ring(w, h, f, shards[w]).wait_send()
        pair(w, h).wait()

    return start, hop, finish


def front_kernel(
    nf, block, key_chunk, halves, groups,
    length_ref, states, wq, wk, wv, vec, wout_s, up_s, down_s,
    qb_out, o_out, k_out, v_out, x_out, vec_out, ctx_out, wout, up, down,
    q_buf, k_buf, v_buf, qb_buf, o_buf, s_buf, top_buf, ctx_buf, x_buf, w_buf, vec_buf,
    local_sem, x_sem, kv_sem, keep_sem, vec_send, vec_recv, z_send, z_recv, h_send, h_recv,
    near_send, near_recv, far_send, far_recv, pass_send, pass_recv,
    ring_send, ring_recv, pair_send, pair_recv, ctx_send, ctx_recv, own_sem, copy_sem,
):
    f = lax.axis_index("fsdp")
    s, near, far, cross = seq_peers()
    tokens, width = states.shape
    heads, slots, _ = q_buf.shape
    rows = wq.shape[0]
    window = w_buf.shape[3]
    own_width = heads * 64
    parts = far_send.shape[0]
    chunk = tokens // parts
    per = tokens // block
    beside = f + 1 - 2 * (f % 2)
    stages = nf // 2
    first_lane = pl.multiple_of((own_width * s // LANE) * LANE, LANE)
    weights = (wq, wk, wv)
    shards, outs = (wout_s, up_s, down_s), (wout, up, down)
    ring_start, ring_hop, ring_finish = ring_gather(
        nf, shards, halves, outs, ring_send, ring_recv, pair_send, pair_recv
    )
    greet(
        [{"fsdp": (f + d) % nf} for d in range(1, nf)]
        + [{"seq": near}, {"seq": far}, {"seq": cross}]
    )

    def windowed(m):
        return weights[m].at[:, pl.ds(first_lane, window)]

    def along(d, m):
        to = (f + 2 * d) % nf
        return remote(windowed(m), w_buf.at[m, f], z_send.at[d - 1, m], z_recv.at[d - 1, m], fsdp=to)

    def aside(d, m):
        owner = (f + nf - 2 * d) % nf
        source = w_buf.at[m, owner] if d else windowed(m)
        return remote(source, w_buf.at[m, owner], h_send.at[d, m], h_recv.at[d, m], fsdp=beside)

    def vec_copy(d):
        return remote(vec, vec_buf.at[f], vec_send.at[d - 1], vec_recv.at[d - 1], fsdp=(f + d) % nf)

    def far_copy(c):
        at = pl.ds(c * chunk, chunk)
        return remote(states.at[at], x_buf.at[2, at], far_send.at[c], far_recv.at[c], seq=far)

    def pass_copy(c):
        at = pl.ds(c * chunk, chunk)
        return remote(
            x_buf.at[2, at], x_buf.at[3, at], pass_send.at[c], pass_recv.at[c], seq=near
        )

    near_copy = remote(states, x_buf.at[1], near_send, near_recv, seq=near)
    for d in range(1, stages):
        for m in range(3):
            along(d, m).start()
    for m in range(3):
        aside(0, m).start()
    for c in range(parts):
        far_copy(c).start()
    near_copy.start()
    for d in range(1, nf):
        vec_copy(d).start()
    for w in groups[0] + groups[1]:
        ring_start(w)
    local = [
        pltpu.make_async_copy(states, x_buf.at[0], local_sem.at[0]),
        pltpu.make_async_copy(vec, vec_buf.at[f], local_sem.at[1]),
    ]
    for m in range(3):
        local.append(pltpu.make_async_copy(windowed(m), w_buf.at[m, f], local_sem.at[2 + m]))
    mine = [
        pltpu.make_async_copy(shards[w], outs[w].at[f], copy_sem.at[w]) for w in range(len(shards))
    ]
    for copy in local + mine:
        copy.start()
    for copy in local:
        copy.wait()
    kept = []

    def keep(slot, index):
        copy = pltpu.make_async_copy(x_buf.at[slot], x_out.at[index], x_sem.at[slot])
        copy.start()
        kept.append(copy)

    def pass_on(c):
        far_copy(c).wait_recv()
        pass_copy(c).start()

    def turn_aside(d):
        for m in range(3):
            along(d, m).wait_recv()
            aside(d, m).start()

    keep(0, s)
    passed = 0
    for d in range(1, stages):
        turn_aside(d)
        if d != 2 and passed < parts - 2:
            pass_on(passed)
            passed += 1
    for d in range(1, nf):
        vec_copy(d).wait_recv()
    for d in range(stages):
        for m in range(3):
            aside(d, m).wait_recv()

    turn = (window - (own_width * s) % LANE) % window
    share = own_width // rows
    wide = lax.broadcasted_iota(jnp.int32, (1, window), 1)
    biases = []
    for row in (0, 1):
        line = jnp.zeros((1, window), f32)
        for i in range(share):
            piece = vec_buf[share * s + i][row : row + 1, :].astype(f32)
            piece = jnp.concatenate([piece, jnp.zeros((1, window - LANE), f32)], axis=1)
            if i:
                piece = pltpu.roll(piece, i * rows, 1)
            line = jnp.where((wide >= i * rows) & (wide < (i + 1) * rows), piece, line)
        biases.append(line)
    length = length_ref[0]
    mats = [w_buf[m].reshape(nf * rows, window) for m in range(3)]
    small = lax.broadcasted_iota(jnp.int32, (chunk, LANE), 1)
    q_tail = jnp.where(small == 64, 1.0, 0.0)
    v_tail = jnp.where((small >= 64) & (small < 67), 1.0, 0.0)

    def heads_of(values, tail):
        found = []
        for h in range(heads):
            tile = values[:, (h // 2) * LANE : (h // 2 + 1) * LANE]
            if h % 2:
                tile = pltpu.roll(tile, 64, 1)
            found.append(jnp.where(small < 64, tile, tail).astype(bf16))
        return found

    def compute(slot, index, part):
        x = x_buf[slot, pl.ds(pl.multiple_of(part * chunk, chunk), chunk), :]
        start = pl.multiple_of(index * tokens + part * chunk, chunk)
        where = start + lax.broadcasted_iota(jnp.int32, (chunk, LANE), 0)
        queries = pltpu.roll(dims(x, mats[0], NN), turn, 1) + biases[0]
        keys = pltpu.roll(dims(x, mats[1], NN), turn, 1)
        k_tail = jnp.where(
            small == 64,
            jnp.where(where < length, 0.0, -1e9),
            jnp.where((small > 64) & (small < 68), 1.0, 0.0),
        )
        values = pltpu.roll(dims(x, mats[2], NN), turn, 1) + biases[1]
        at = pl.ds(start, chunk)
        for ref, found in (
            (q_buf, heads_of(queries * (LOG2E * 0.125), q_tail)),
            (k_buf, heads_of(keys, k_tail)),
            (v_buf, heads_of(values, v_tail)),
        ):
            for h in range(heads):
                ref[h, at, :] = found[h]

    def whole(slot, index, low, high):
        def body(part, carry):
            compute(slot, index, part)
            return carry

        lax.fori_loop(low, high, body, 0)

    def hops(g, h):
        for w in groups[g]:
            ring_hop(w, h)

    hops(0, 0)
    hops(1, 0)
    whole(0, s, 0, parts)
    for c in range(passed, parts - 1):
        pass_on(c)
    near_copy.wait_recv()
    keep(1, near)
    whole(1, near, 0, parts)
    hops(0, 1)
    whole(2, far, 0, parts - 1)
    pass_on(parts - 1)
    hops(1, 1)
    whole(2, far, parts - 1, parts)
    keep(2, far)
    for c in range(parts):
        pass_copy(c).wait_recv()
    keep(3, cross)
    whole(3, cross, 0, parts)
    hops(0, 2)
    saved = [
        pltpu.make_async_copy(k_buf, k_out, kv_sem.at[0]),
        pltpu.make_async_copy(v_buf, v_out, kv_sem.at[1]),
        pltpu.make_async_copy(vec_buf, vec_out, kv_sem.at[2]),
    ]
    for copy in saved:
        copy.start()

    lane = lax.broadcasted_iota(jnp.int32, (block, LANE), 1)

    def partner(round_):
        relation = 3 - round_
        return ((s // 2 + relation // 2) % 2) * 2 + (s % 2 + relation % 2) % 2

    def ctx_copy(step):
        at = pl.ds(pl.multiple_of(step % per * block, block), block)
        return remote(
            ctx_buf.at[step],
            ctx_out.at[s, at],
            ctx_send.at[step],
            ctx_recv.at[step],
            seq=partner(step // per),
        )

    def rows_of(step):
        base = partner(step // per) * tokens + step % per * block
        return pl.ds(pl.multiple_of(base, block), block)

    def keep_copies(step):
        at = rows_of(step)
        return (
            pltpu.make_async_copy(qb_buf.at[:, at], qb_out.at[:, at], keep_sem.at[0, step]),
            pltpu.make_async_copy(o_buf.at[:, at], o_out.at[:, at], keep_sem.at[1, step]),
        )

    chunks = slots // key_chunk

    def score(h, at, c):
        return dims(q_buf[h, at, :], k_buf[h, c * key_chunk : (c + 1) * key_chunk, :], NT)

    def highest(values, top):
        for j in range(key_chunk // LANE):
            tile = values[:, j * LANE : (j + 1) * LANE]
            top = tile if top is None else jnp.maximum(top, tile)
        return top

    top = None
    for c in range(chunks):
        scores = score(0, rows_of(0), c)
        s_buf[:, c * key_chunk : (c + 1) * key_chunk] = scores
        top = highest(scores, top)
    top_buf[...] = top

    def attend(step, carry):
        at = rows_of(step)
        after = rows_of(jnp.minimum(step + 1, 4 * per - 1))
        results = []
        current = [s_buf[:, c * key_chunk : (c + 1) * key_chunk] for c in range(chunks)]
        top = top_buf[...]
        for h in range(heads):
            peak = jnp.max(top, axis=1, keepdims=True)
            total = None
            coming = []
            top = None
            for c in range(chunks):
                scores = score(h + 1, at, c) if h + 1 < heads else score(0, after, c)
                coming.append(scores)
                top = highest(scores, top)
                probs = jnp.exp2(current[c] - peak).astype(bf16)
                term = dims(probs, v_buf[h, c * key_chunk : (c + 1) * key_chunk, :], NN)
                total = term if total is None else total + term
            current = coming
            weight = total[:, 64:65]
            result = jnp.where(lane < 64, total * (1.0 / weight), 0.0)
            o_buf[h, at, :] = result.astype(bf16)
            high, middle, low = thirds(-(peak + jnp.log2(weight)))
            qb_buf[h, at, :] = with_lanes(
                q_buf[h, at, :].astype(f32), ((65, high), (66, middle), (67, low))
            ).astype(bf16)
            results.append(result)
        for c in range(chunks):
            s_buf[:, c * key_chunk : (c + 1) * key_chunk] = current[c]
        top_buf[...] = top
        for t in range((heads + 1) // 2):
            tile = results[2 * t]
            if 2 * t + 1 < heads:
                tile = tile + pltpu.roll(results[2 * t + 1], 64, 1)
            ctx_buf[step, :, t * LANE : (t + 1) * LANE] = tile.astype(bf16)

        @pl.when(step < 3 * per)
        def _():
            ctx_copy(step).start()

        for copy in keep_copies(step):
            copy.start()
        for g in range(2):
            late = 2 * (1 - g)
            h = (2 * step - late + 1) // 5
            @pl.when(((5 * h + late) // 2 == step) & (h + 3 - g < nf - 1))
            def _():
                hops(g, h + 3 - g)

        return carry

    lax.fori_loop(0, 4 * per, attend, 0)
    owns = []
    for i in range(per):
        owns.append(
            pltpu.make_async_copy(
                ctx_buf.at[3 * per + i], ctx_out.at[s, pl.ds(i * block, block)], own_sem.at[i]
            )
        )
        owns[-1].start()

    def rest(h, carry):
        for w in range(len(shards)):
            ring_hop(w, h)
        return carry

    lax.fori_loop(min(7, nf - 1), nf - 1, rest, 0)

    def settle(step, carry):
        @pl.when(step < 3 * per)
        def _():
            ctx_copy(step).wait()

        for copy in keep_copies(step):
            copy.wait()
        return carry

    lax.fori_loop(0, 4 * per, settle, 0)
    for d in range(1, stages):
        for m in range(3):
            along(d, m).wait_send()
    for d in range(stages):
        for m in range(3):
            aside(d, m).wait_send()
    for d in range(1, nf):
        vec_copy(d).wait_send()
    for c in range(parts):
        far_copy(c).wait_send()
        pass_copy(c).wait_send()
    near_copy.wait_send()
    for copy in owns + mine + kept + saved:
        copy.wait()

    def close(h, carry):
        for w in range(len(shards)):
            ring_finish(w, h)
        return carry

    lax.fori_loop(0, nf - 1, close, 0)


def front(nf, heads, length, states, wq, wk, wv, vec, wout, up, down, block, key_chunk):
    tokens, width = states.shape
    rows = wq.shape[0]
    slots = 4 * tokens
    parts = 4
    window = 256
    shards = (wout, up, down)
    halves = tuple((1, w.shape[1] // 2) for w in shards)
    wide = -(-heads // 2) * LANE
    steps = slots // block
    shape = jax.ShapeDtypeStruct
    head_shape = shape((heads, slots, LANE), bf16)
    head_buf = pltpu.VMEM((heads, slots, LANE), bf16)
    hops = DMA((3, nf - 1))
    stage = DMA((nf // 2 - 1, 3))
    stage_aside = DMA((nf // 2, 3))
    peers = DMA((nf - 1,))
    fine = DMA((parts,))
    return pl.pallas_call(
        functools.partial(front_kernel, nf, block, key_chunk, halves, ((1,), (0, 2))),
        out_shape=[head_shape] * 4
        + [
            shape((4, tokens, width), bf16),
            shape((nf,) + vec.shape, bf16),
            shape((4, tokens, wide), bf16),
        ]
        + [shape((nf,) + w.shape, bf16) for w in shards],
        in_specs=[IN_SMEM] + [ANY] * 8,
        out_specs=[ANY] * 10,
        scratch_shapes=[head_buf] * 5
        + [
            pltpu.VMEM((block, slots), f32),
            pltpu.VMEM((block, LANE), f32),
            pltpu.VMEM((steps, block, wide), bf16),
            pltpu.VMEM((4, tokens, width), bf16),
            pltpu.VMEM((3, nf, rows, window), bf16),
            pltpu.VMEM((nf,) + vec.shape, bf16),
            DMA((5,)),
            DMA((4,)),
            DMA((3,)),
            DMA((2, steps)),
            peers, peers, stage, stage, stage_aside, stage_aside,
            DMA(()), DMA(()), fine, fine, fine, fine,
            hops, hops, hops, hops,
            DMA((steps,)), DMA((steps,)),
            DMA((tokens // block,)),
            DMA((3,)),
        ],
        compiler_params=params(1),
        name="front",
    )(length, states, wq, wk, wv, vec, wout, up, down)


def plane_gather(nf, shards, outs, z_send, z_recv, h_send, h_recv, n_send, n_recv):
    f = lax.axis_index("fsdp")
    s, near, _, _ = seq_peers()
    side = s % 2
    beside = f + 1 - 2 * (f % 2)
    stages = nf // 2
    count = len(shards)

    def half(ref):
        size = ref.shape[1] // 2
        return ref.at[:, pl.ds(pl.multiple_of(side * size, size), size)]

    def along(d, m):
        return remote(
            half(shards[m]), half(outs[m].at[f]), z_send.at[d - 1, m], z_recv.at[d - 1, m],
            fsdp=(f + 2 * d) % nf,
        )

    def aside(d, m):
        owner = (f + nf - 2 * d) % nf
        source = outs[m].at[owner] if d else shards[m]
        return remote(
            half(source), half(outs[m].at[owner]), h_send.at[d, m], h_recv.at[d, m], fsdp=beside
        )

    def share(e, m):
        owner = (f + nf - 2 * e) % nf if e < stages else (beside + nf - 2 * (e - stages)) % nf
        piece = half(outs[m].at[owner])
        return remote(piece, piece, n_send.at[e - 1, m], n_recv.at[e - 1, m], seq=near)

    def start():
        for d in range(1, stages):
            for m in range(count):
                along(d, m).start()
        for m in range(count):
            aside(0, m).start()

    def first():
        for d in range(1, stages):
            for m in range(count):
                along(d, m).wait_recv()
                aside(d, m).start()
                share(d, m).start()

    def second():
        for d in range(stages):
            for m in range(count):
                aside(d, m).wait_recv()
                share(stages + d, m).start()

    def finish():
        for m in range(count):
            for d in range(1, stages):
                along(d, m).wait_send()
            for d in range(stages):
                aside(d, m).wait_send()
            for e in range(1, nf):
                share(e, m).wait()

    return start, first, second, finish


def feed_kernel(
    nf, block, part, length_ref, states, ctx, wout, vec, upb, up_hbm, down_hbm, cot_hbm,
    wq_s, wk_s, wv_s,
    out, first_grad_out, gctx, up_sum, down_sum, wout_sum, gvec, wq, wk, wv,
    up, down, cot, out_buf, first_buf, act_buf, pre_buf, slope_buf, low_t, down_t, branch_buf,
    g_buf, up_give, down_give, wout_give, up_take, down_take, wout_take,
    load_sem, keep_sem, g_send, g_recv, own_sem, give_send, give_recv, sum_sem, shard_sem,
    z_send, z_recv, h_send, h_recv, n_send, n_recv,
):
    f = lax.axis_index("fsdp")
    s, near, far, cross = seq_peers()
    side = s % 2
    beside = f + 1 - 2 * (f % 2)
    tokens, width = states.shape
    hidden = up.shape[1]
    own = wout.shape[0] // 4
    steps = tokens // block
    wide = ctx.shape[2]
    loads = [
        pltpu.make_async_copy(up_hbm, up, load_sem.at[0]),
        pltpu.make_async_copy(down_hbm, down, load_sem.at[1]),
        pltpu.make_async_copy(cot_hbm, cot, load_sem.at[2]),
    ]
    for copy in loads:
        copy.start()
    shards, outs = (wq_s, wk_s, wv_s), (wq, wk, wv)
    gather = plane_gather(nf, shards, outs, z_send, z_recv, h_send, h_recv, n_send, n_recv)
    greet(
        [{"fsdp": (f + 2 * d) % nf} for d in range(1, nf // 2)]
        + [{"fsdp": beside}, {"seq": near}, {"seq": far}, {"seq": cross}]
    )
    gather[0]()
    kept = [pltpu.make_async_copy(shards[m], outs[m].at[f], shard_sem.at[m]) for m in range(3)]
    for copy in kept:
        copy.start()
    length = length_ref[0]
    gvec[...] = jnp.zeros_like(gvec)
    peers = (s, near, far, cross)

    def line(row):
        return vec[row : row + 1, :]

    def add_line(row, values):
        gvec[row : row + 1, :] += jnp.sum(values, axis=0, keepdims=True)

    def norm(values):
        centred = values - jnp.mean(values, axis=1, keepdims=True)
        scale = lax.rsqrt(jnp.mean(centred * centred, axis=1, keepdims=True) + eps)
        return centred * scale, scale

    def norm_back(grad, gain, normed, scale):
        grad = grad * gain
        return scale * (
            grad
            - jnp.mean(grad, axis=1, keepdims=True)
            - normed * jnp.mean(grad * normed, axis=1, keepdims=True)
        )

    def rows_of(i):
        return pl.ds(pl.multiple_of(i * block, block), block)

    def send(relation, i):
        at = rows_of(i)
        return remote(
            g_buf.at[relation, at],
            gctx.at[s, at],
            g_send.at[relation - 1, i],
            g_recv.at[relation - 1, i],
            seq=peers[relation],
        )

    def keep(i):
        at = rows_of(i)
        return (
            pltpu.make_async_copy(out_buf.at[at], out.at[at], keep_sem.at[0, i]),
            pltpu.make_async_copy(first_buf.at[at], first_grad_out.at[at], keep_sem.at[1, i]),
        )

    def body(i, carry):
        at = rows_of(i)
        attended = None
        for j in range(4):
            term = dims(ctx[j, at, :own], wout[own * j : own * (j + 1), :], NN)
            attended = term if attended is None else attended + term
        normed_first, scale_first = norm(states[at, :].astype(f32) + (attended + line(2)))
        first = normed_first * line(3) + line(4)
        low = first.astype(bf16)
        low_t[:, at] = jnp.transpose(low)

        @pl.when(i == 0)
        def _():
            for copy in loads:
                copy.wait()

        fed = None
        for c in range(hidden // part):
            cut = slice(c * part, (c + 1) * part)
            pre = dims(low, up[:, cut], NN) + upb[:, cut]
            share = 0.5 + 0.5 * lax.erf(pre * (2.0**-0.5))
            slope_buf[:, cut] = share + pre * jnp.exp(-0.5 * pre * pre) * (2.0 * math.pi) ** -0.5
            act = (pre * share).astype(bf16)
            act_buf[at, cut] = act
            term = dims(act, down[cut, :], NN)
            fed = term if fed is None else fed + term
        normed, scale = norm(first + (fed + line(5)))
        place = s * tokens + i * block + lax.broadcasted_iota(jnp.int32, (block, 1), 0)
        valid = jnp.where(place < length, 1.0, 0.0)
        out_buf[at, :] = ((normed * line(6) + line(7)) * valid).astype(bf16)
        grad = cot[at, :].astype(f32) * valid
        add_line(6, grad * normed)
        add_line(7, grad)
        second_grad = norm_back(grad, line(6), normed, scale)
        down_in = second_grad.astype(bf16)
        add_line(5, down_in.astype(f32))
        down_t[:, at] = jnp.transpose(down_in)
        back = second_grad
        for c in range(hidden // part):
            cut = slice(c * part, (c + 1) * part)
            pre_grad = (dims(down_in, down[cut, :], NT) * slope_buf[:, cut]).astype(bf16)
            pre_buf[at, cut] = pre_grad
            row = 8 + c * part // width
            col = c * part % width
            gvec[row : row + 1, col : col + part] += jnp.sum(
                pre_grad.astype(f32), axis=0, keepdims=True
            )
            back = back + dims(pre_grad, up[:, cut], NT)
        add_line(3, back * normed_first)
        add_line(4, back)
        first_grad = norm_back(back, line(3), normed_first, scale_first)
        first_buf[at, :] = first_grad
        branch = first_grad.astype(bf16)
        branch_buf[at, :] = branch
        add_line(2, branch.astype(f32))
        for relation in range(4):
            rows = pl.ds(pl.multiple_of(peers[relation] * own, 64), own)
            g_buf[relation, at, :own] = dims(branch, wout[rows, :], NT).astype(bf16)
            if wide > own:
                g_buf[relation, at, own:] = jnp.zeros((block, wide - own), bf16)
            if relation:
                send(relation, i).start()
        for copy in keep(i):
            copy.start()

        @pl.when(i == min(1, steps - 1))
        def _():
            gather[1]()

        return carry

    lax.fori_loop(0, steps, body, 0)
    mine = pltpu.make_async_copy(g_buf.at[0], gctx.at[s], own_sem)
    mine.start()

    pieces = give_send.shape[1]
    up_cut = hidden // 2 // pieces
    down_cut = hidden // pieces

    def up_part(which, c):
        cut = pl.ds(pl.multiple_of(which * (hidden // 2) + c * up_cut, up_cut), up_cut)
        return dims(low_t[...], pre_buf[:, cut], NN)

    def down_part(which, c):
        rows = pl.ds(pl.multiple_of(which * (width // 2), width // 2), width // 2)
        cut = pl.ds(pl.multiple_of(c * down_cut, down_cut), down_cut)
        return dims(down_t[rows, :], act_buf[:, cut], NN)

    def wout_part(which, j):
        cut = pl.ds(pl.multiple_of(which * (width // 2), width // 2), width // 2)
        return dims(ctx[j, :, :own], branch_buf[:, cut], TN)

    def cols(c, size):
        return (slice(None), pl.ds(pl.multiple_of(c * size, size), size))

    def give(w, c):
        if w == 2:
            pair = wout_give, wout_take
        else:
            at = cols(c, (up_cut, down_cut)[w])
            pair = (up_give, down_give)[w].at[at], (up_take, down_take)[w].at[at]
        return remote(*pair, give_send.at[w, c], give_recv.at[w, c], seq=near)

    def give_away(c, carry):
        up_give[cols(c, up_cut)] = up_part(1 - side, c).astype(bf16)
        give(0, c).start()
        down_give[cols(c, down_cut)] = down_part(1 - side, c).astype(bf16)
        give(1, c).start()
        return carry

    def add_own(c, carry):
        at = cols(c, up_cut)
        total = up_part(side, c)
        give(0, c).wait()
        up_give[at] = (total + up_take[at].astype(f32)).astype(bf16)
        at = cols(c, down_cut)
        total = down_part(side, c)
        give(1, c).wait()
        down_give[at] = (total + down_take[at].astype(f32)).astype(bf16)
        return carry

    lax.fori_loop(0, pieces, give_away, 0)
    for j in range(4):
        wout_give[own * j : own * (j + 1), :] = wout_part(1 - side, j).astype(bf16)
    give(2, 0).start()
    lax.fori_loop(0, pieces, add_own, 0)
    sums = [
        pltpu.make_async_copy(up_give, up_sum, sum_sem.at[0]),
        pltpu.make_async_copy(down_give, down_sum, sum_sem.at[1]),
    ]
    for copy in sums:
        copy.start()
    gather[2]()
    totals = [wout_part(side, j) for j in range(4)]
    give(2, 0).wait()
    for j in range(4):
        at = slice(own * j, own * (j + 1))
        wout_give[at, :] = (totals[j] + wout_take[at, :].astype(f32)).astype(bf16)
    sums.append(pltpu.make_async_copy(wout_give, wout_sum, sum_sem.at[2]))
    sums[-1].start()
    for relation in range(1, 4):
        for i in range(steps):
            send(relation, i).wait()
    for i in range(steps):
        for copy in keep(i):
            copy.wait()
    gather[3]()
    for copy in [mine] + kept + sums:
        copy.wait()


def feed(nf, length, states, cot, ctx, wout, up, down, vec, upb, shards, block=256, part=768):
    tokens, width = states.shape
    hidden = up.shape[1]
    wide = ctx.shape[2]
    pieces = 3
    shape = jax.ShapeDtypeStruct
    halves = ((width, hidden // 2), (width // 2, hidden), (width, width // 2))
    vmem = lambda *size: pltpu.VMEM(size, bf16)
    steps = tokens // block
    staged = DMA((nf // 2 - 1, 3))
    staged_aside = DMA((nf // 2, 3))
    return pl.pallas_call(
        functools.partial(feed_kernel, nf, block, part),
        out_shape=[
            shape((tokens, width), bf16),
            shape((tokens, width), f32),
            shape((4, tokens, wide), bf16),
        ]
        + [shape(x, bf16) for x in halves]
        + [shape((16, width), f32)]
        + [shape((nf,) + w.shape, bf16) for w in shards],
        in_specs=[IN_SMEM] + [IN_VMEM] * 5 + [ANY] * 6,
        out_specs=[ANY] * 6 + [IN_VMEM] + [ANY] * 3,
        scratch_shapes=[
            vmem(width, hidden),
            vmem(hidden, width),
            vmem(tokens, width),
            vmem(tokens, width),
            pltpu.VMEM((tokens, width), f32),
            vmem(tokens, hidden),
            vmem(tokens, hidden),
            pltpu.VMEM((block, hidden), f32),
            vmem(width, tokens),
            vmem(width, tokens),
            vmem(tokens, width),
            vmem(4, tokens, wide),
        ]
        + [vmem(*x) for x in halves] * 2
        + [
            DMA((3,)),
            DMA((2, steps)),
            DMA((3, steps)),
            DMA((3, steps)),
            DMA(()),
            DMA((3, pieces)),
            DMA((3, pieces)),
            DMA((3,)),
            DMA((3,)),
            staged, staged, staged_aside, staged_aside,
            DMA((nf - 1, 3)), DMA((nf - 1, 3)),
        ],
        compiler_params=params(3),
        name="feed",
    )(length, states, ctx, wout, vec, upb, up, down, cot, *shards)


def back_kernel(
    nf, key_block, groups, q_ref, k_ref, v_ref, o_ref, gctx_ref,
    up_sum, down_sum, wout_sum, x_hbm, wq_hbm, wk_hbm, wv_hbm, first_hbm, gvec_hbm,
    states_grad, up_out, down_out, wout_out, qkv_out, vec_out, upb_out,
    k_acc, v_acc, q_acc, g_buf, q_turned, g_turned, d_out, g_all, x_all, w_all, first_grad,
    own_up, own_dn, own_wo, ring_up, ring_dn, ring_wo, y_up, y_dn, y_wo, z_up, z_dn, z_wo,
    w_buf, w_came, w_sum, w_parts, v_own, v_cut, v_came, v_sum, v_parts,
    load_sem, late_sem, hop_send, hop_recv, y_send, y_recv, z_send, z_recv,
    d_send, d_recv, d_own, w_send, w_recv, p_send, p_recv, l_send, l_recv, m_send, m_recv,
):
    half, h = pl.program_id(0), pl.program_id(1)
    count = w_buf.shape[0]
    f = lax.axis_index("fsdp")
    s, near, far, cross = seq_peers()
    peers = (s, near, far, cross)
    side = s % 2
    way = 1 - 2 * side
    place = place_of(f, nf)
    ahead = index_at((place + way + nf) % nf, nf)
    slots = k_ref.shape[1]
    tokens = slots // 4
    block = tokens
    width = x_all.shape[2]
    rows = width // nf
    width_own = count * 64
    full = (up_sum, down_sum, wout_sum)
    own = (own_up, own_dn, own_wo)
    came = (ring_up, ring_dn, ring_wo)
    y_buf = (y_up, y_dn, y_wo)
    z_buf = (z_up, z_dn, z_wo)
    outs = (up_out, down_out, wout_out)
    by_cols = (False, True, False)

    def chunk_at(w, chunk):
        size = came[w].shape[1 + by_cols[w]]
        cut = pl.ds(pl.multiple_of(chunk * size, size), size)
        return (slice(None), cut) if by_cols[w] else (cut, slice(None))

    def hop(w, t, source):
        return remote(source, came[w].at[t], hop_send.at[w, t], hop_recv.at[w, t], fsdp=ahead)

    def chunk_of(t):
        return index_at((place + 2 * nf - way * (1 + t)) % nf, nf)

    def to_far(w):
        return remote(came[w].at[nf - 2], y_buf[w], y_send.at[w], y_recv.at[w], seq=far)

    def to_near(w):
        return remote(y_buf[w], z_buf[w], z_send.at[w], z_recv.at[w], seq=near)

    def loads():
        return [pltpu.make_async_copy(full[w], own[w], load_sem.at[w]) for w in range(3)]

    def late():
        return [
            pltpu.make_async_copy(x_hbm, x_all, late_sem.at[0]),
            pltpu.make_async_copy(wq_hbm, w_all.at[0], late_sem.at[1]),
            pltpu.make_async_copy(wk_hbm, w_all.at[1], late_sem.at[2]),
            pltpu.make_async_copy(wv_hbm, w_all.at[2], late_sem.at[3]),
            pltpu.make_async_copy(first_hbm, first_grad, late_sem.at[4]),
            pltpu.make_async_copy(gvec_hbm, v_own, late_sem.at[5]),
        ]

    friends = [{"fsdp": (f + d) % nf} for d in range(1, nf)] + [{"seq": p} for p in peers[1:]]

    @pl.when((half == 0) & (h == 0))
    def _():
        hail(friends)
        for copy in loads() + late():
            copy.start()

    k_acc[...] = jnp.zeros_like(k_acc)
    v_acc[...] = jnp.zeros_like(v_acc)
    at_head = pl.ds(pl.multiple_of(h * 64, 64), 64)

    def part(relation, m, head):
        to = peers[relation]
        source = d_out.at[
            m, pl.ds(pl.multiple_of(head * 64, 64), 64), pl.ds(pl.multiple_of(to * tokens, tokens), tokens)
        ]
        target = g_all.at[m, pl.ds(pl.multiple_of(s * width_own + head * 64, 64), 64), :]
        return source, target

    def d_copy(relation, m, head):
        source, target = part(relation, m, head)
        return remote(
            source, target, d_send.at[relation - 1, m, head], d_recv.at[relation - 1, m, head],
            seq=peers[relation],
        )

    def d_local(m, head):
        source, target = part(0, m, head)
        return pltpu.make_async_copy(source, target, d_own.at[m, head])

    def w_copy(head, d):
        to = (f + d) % nf
        return remote(
            w_buf.at[head, to], w_came.at[head, d - 1], w_send.at[head, d - 1],
            w_recv.at[head, d - 1], fsdp=to,
        )

    def p_copy(head, relation):
        return remote(
            w_sum.at[head], w_parts.at[s, head], p_send.at[head, relation - 1],
            p_recv.at[head, relation - 1], seq=peers[relation],
        )

    def v_copy(d):
        to = (f + d) % nf
        return remote(v_cut.at[to], v_came.at[d], l_send.at[d - 1], l_recv.at[d - 1], fsdp=to)

    def m_copy(relation):
        return remote(
            v_sum, v_parts.at[s], m_send.at[relation - 1], m_recv.at[relation - 1],
            seq=peers[relation],
        )

    def settle_head(head):
        for d in range(1, nf):
            w_copy(head, d).wait()
        total = w_buf[head, f].astype(f32)
        for d in range(1, nf):
            total = total + w_came[head, d - 1].astype(f32)
        w_sum[head] = total.astype(bf16)
        for relation in (3, 2, 1):
            p_copy(head, relation).start()
        w_parts[s, head] = total.astype(bf16)

    base = (s // 2 + 1 + half) % 2 * (2 * tokens)

    def round_(turn, carry):
        step = (half * count + h) * 4 + turn
        relation = (1 - turn // 2) * (turn + 2) + turn // 2 * (3 - turn)
        owner = ((s // 2 + relation // 2) % 2) * 2 + (s % 2 + relation % 2) % 2
        at = pl.ds(pl.multiple_of(owner * tokens, tokens), tokens)

        @pl.when(half == 0)
        def _():
            lane = lax.broadcasted_iota(jnp.int32, (block, LANE), 1)
            first = gctx_ref[at, :LANE].astype(f32)
            second = gctx_ref[at, LANE:].astype(f32)
            grad = jnp.where(h == 0, first, jnp.where(h == 1, pltpu.roll(first, 64, 1), second))
            grad = jnp.where(lane < 64, grad, 0.0)
            delta = jnp.sum(grad * o_ref[0, at, :].astype(f32), axis=1, keepdims=True)
            high, middle, low = thirds(-delta)
            grad = with_lanes(grad, ((64, high), (65, middle), (66, low))).astype(bf16)
            g_buf[h, at, :] = grad
            g_turned[h, :, at] = jnp.transpose(grad)[:64, :]
            q_turned[h, :, at] = jnp.transpose(q_ref[0, at, :])[:64, :]

        q, grad = q_ref[0, at, :], g_buf[h, at, :]
        q_side, g_side = q_turned[h, :, at], g_turned[h, :, at]
        q_total = None
        for c in range(2 * tokens // key_block):
            ks = slice(c * key_block, (c + 1) * key_block)
            keys = pl.ds(pl.multiple_of(base + c * key_block, LANE), key_block)
            k = k_ref[0, keys, :]
            probs = jnp.exp2(dims(q, k, NT))
            score = (probs * dims(grad, v_ref[0, keys, :], NT)).astype(bf16)
            v_acc[:, ks] += dims(g_side, probs.astype(bf16), NN)
            k_acc[:, ks] += dims(q_side, score, NN)
            term = dims(score, k, NN)
            q_total = term if q_total is None else q_total + term
        q_total = jnp.transpose(q_total)[:64, :]

        @pl.when(half == 0)
        def _():
            q_acc[h, :, at] = q_total

        @pl.when(half == 1)
        def _():
            d_out[0, at_head, at] = ((q_acc[h, :, at] + q_total) * 0.125).astype(bf16)

        @pl.when(step == 0)
        def _():
            hailed(friends)
            for w in range(3):
                hop(w, 0, full[w].at[chunk_at(w, chunk_of(0))]).start()

        @pl.when(step == 1)
        def _():
            for copy in loads():
                copy.wait()

        for g in range(2):
            t = (2 * (step - g) + 1) // 5
            due = 5 * t // 2 == step - g

            @pl.when(due & (t > 0) & (t < nf - 1))
            def _():
                for w in groups[g]:
                    hop(w, t - 1, came[w].at[t - 1]).wait_recv()
                    here = own[w][chunk_at(w, chunk_of(t))].astype(f32)
                    came[w][t - 1] = (here + came[w][t - 1].astype(f32)).astype(bf16)
                    hop(w, t, came[w].at[t - 1]).start()

            @pl.when(due & (t == nf - 1))
            def _():
                for w in groups[g]:
                    hop(w, nf - 2, came[w].at[nf - 2]).wait_recv()
                    here = own[w][chunk_at(w, f)].astype(f32)
                    came[w][nf - 2] = (here + came[w][nf - 2].astype(f32)).astype(bf16)
                    to_far(w).start()

        for stage, kind in enumerate((2, 3, 1)):
            @pl.when((half == 1) & (turn == stage))
            def _():
                d_copy(kind, 0, h).start()

        @pl.when((half == 1) & (h > 0) & (turn == 1))
        def _():
            settle_head(h - 1)

        return carry

    lax.fori_loop(0, 4, round_, 0)
    keys = pl.ds(pl.multiple_of(base, 2 * tokens), 2 * tokens)
    d_out[1, at_head, keys] = (k_acc[...] * LN2).astype(bf16)
    d_out[2, at_head, keys] = v_acc[...].astype(bf16)

    @pl.when(half == 0)
    def _():
        for m in (1, 2):
            for kind in (2, 3):
                d_copy(kind, m, h).start()

    @pl.when(half == 1)
    def _():
        for m in range(3):
            if m:
                d_copy(1, m, h).start()
            d_local(m, h).start()

        @pl.when(h == 0)
        def _():
            for copy in late():
                copy.wait()

        left = jnp.concatenate([d_out[m, at_head, :] for m in range(3)], axis=0)
        total = None
        for j in range(4):
            term = dims(left[:, j * tokens : (j + 1) * tokens], x_all[j], NN)
            total = term if total is None else total + term
        total = jnp.transpose(total).astype(bf16)
        for j in range(nf):
            w_buf[h, j] = jnp.concatenate(
                [total[rows * j + rows // 2 * e : rows * j + rows // 2 * (e + 1)] for e in range(2)],
                axis=1,
            )
        for d in range(1, nf):
            w_copy(h, d).start()

    @pl.when((half == 1) & (h == count - 1))
    def _():
        ones = jnp.ones((8, slots), bf16)
        for row, m in ((0, 0), (1, 2)):
            line = dims(ones, d_out[m], NT)
            line = jnp.concatenate([line, jnp.zeros((8, width - width_own), f32)], axis=1)
            v_own[row : row + 1, :] = pltpu.roll(line, s * width_own, 1)[0:1, :]
        lines = v_own[...]
        flat = jnp.concatenate([lines[8 + r : 9 + r, :] for r in range(4)], axis=1)
        for j in range(nf):
            piece = lines if j == 0 else pltpu.roll(lines, width - rows * j, 1)
            v_cut[j, 0:8, :] = piece[0:8, :LANE]
            for r in range(4):
                start = rows * (4 * j + r)
                shift = start % LANE
                tile = start - shift
                both = jnp.concatenate(
                    [flat[:, tile : tile + LANE], flat[:, min(tile + LANE, flat.shape[1] - LANE) :][:, :LANE]],
                    axis=1,
                )
                if shift:
                    both = pltpu.roll(both, 2 * LANE - shift, 1)
                v_cut[j, 8 + r : 9 + r, :] = both[:, :LANE]
            v_cut[j, 12:16, :] = jnp.zeros((4, LANE), f32)
        for d in range(1, nf):
            v_copy(d).start()
        for w in range(3):
            to_far(w).wait()
            y_buf[w][...] = (
                came[w][nf - 2].astype(f32) + y_buf[w][...].astype(f32)
            ).astype(bf16)
            to_near(w).start()

        def settle(head, carry):
            for m in range(3):
                for kind in range(1, 4):
                    d_copy(kind, m, head).wait()
                d_local(m, head).wait()
            return carry

        lax.fori_loop(0, count, settle, 0)
        cut_size = 256
        mats = [w_all[m].reshape(width, width) for m in range(3)]
        for c in range(width // cut_size):
            cut = slice(c * cut_size, (c + 1) * cut_size)
            total = None
            for m in range(3):
                term = dims(mats[m][cut, :], g_all[m], NN)
                total = term if total is None else total + term
            states_grad[:, cut] = (first_grad[:, cut] + jnp.transpose(total)).astype(bf16)
        for d in range(1, nf):
            v_copy(d).wait()
        v_came[0] = v_cut[f]
        total = None
        for j in range(nf):
            term = v_came[(f + nf - j) % nf]
            total = term if total is None else total + term
        v_sum[...] = total
        for kind in (3, 2, 1):
            m_copy(kind).start()
        v_parts[s] = total
        settle_head(count - 1)
        for w in range(3):
            for t in range(nf - 1):
                hop(w, t, came[w].at[t]).wait_send()
            to_near(w).wait()
            mine, theirs = y_buf[w][...], z_buf[w][...]
            out = outs[w]
            size = out.shape[1] // 2
            if by_cols[w]:
                mine, theirs = jnp.transpose(mine), jnp.transpose(theirs)
            out[:, pl.ds(pl.multiple_of(side * size, size), size)] = mine
            out[:, pl.ds(pl.multiple_of((1 - side) * size, size), size)] = theirs
        for relation in range(1, 4):
            m_copy(relation).wait()
        total = v_parts[0] + v_parts[1] + v_parts[2] + v_parts[3]
        vec_out[...] = total
        lane = lax.broadcasted_iota(jnp.int32, (1, 4 * rows), 1)
        line = jnp.zeros((1, 4 * rows), f32)
        for r in range(4):
            piece = jnp.concatenate(
                [total[8 + r : 9 + r, :], jnp.zeros((1, 4 * rows - LANE), f32)], axis=1
            )
            if r:
                piece = pltpu.roll(piece, rows * r, 1)
            line = jnp.where((lane >= rows * r) & (lane < rows * (r + 1)), piece, line)
        upb_out[...] = jnp.broadcast_to(line, upb_out.shape)
        for head in range(count):
            for relation in range(1, 4):
                p_copy(head, relation).wait()
        parts = [
            [
                jnp.concatenate([both[:, : 3 * 64], both[:, 3 * 64 :]], axis=0)
                for both in [w_parts[j, head].astype(f32) for head in range(count)]
            ]
            for j in range(4)
        ]
        for m in range(3):
            qkv_out[m] = jnp.concatenate(
                [part[:, m * 64 : (m + 1) * 64] for group in parts for part in group], axis=1
            ).astype(bf16)


def back(nf, qb, k, v, o, gctx, sums, x_all, mats, first_grad, gvec, key_block):
    heads, slots, _ = qb.shape
    tokens = slots // 4
    width = x_all.shape[2]
    hidden = sums[0].shape[1] * 2
    rows, cols = width // nf, hidden // nf
    shape = jax.ShapeDtypeStruct
    per_head = pl.BlockSpec((1, slots, LANE), lambda p, h: (h, 0, 0))
    chunk = ((rows, hidden // 2), (width // 2, cols), (rows, width // 2))
    vmem = lambda *size: pltpu.VMEM(size, bf16)
    triple = DMA((3,))
    hops = DMA((3, nf - 1))
    own = heads * 64
    packed = (rows // 2, 6 * 64)
    results = [
        shape((tokens, width), bf16),
        shape((rows, hidden), bf16),
        shape((cols, width), bf16),
        shape((rows, width), bf16),
        shape((3, rows, width), bf16),
        shape((16, LANE), f32),
        shape((8, cols), f32),
    ]
    return pl.pallas_call(
        functools.partial(back_kernel, nf, key_block, ((0,), (1, 2))),
        grid=(2, heads),
        out_shape=results,
        in_specs=[per_head] * 4 + [IN_VMEM] + [ANY] * 9,
        out_specs=[
            pl.BlockSpec(x.shape, functools.partial(lambda n, *_: (0,) * n, len(x.shape)))
            for x in results
        ],
        scratch_shapes=[
            pltpu.VMEM((64, slots // 2), f32),
            pltpu.VMEM((64, slots // 2), f32),
            pltpu.VMEM((heads, 64, slots), f32),
            vmem(heads, slots, LANE),
            vmem(heads, 64, slots),
            vmem(heads, 64, slots),
            vmem(3, own, slots),
            vmem(3, width, tokens),
            vmem(4, tokens, width),
            vmem(3, nf, rows, width),
            pltpu.VMEM((tokens, width), f32),
        ]
        + [vmem(*x.shape) for x in sums]
        + [vmem(nf - 1, *x) for x in chunk]
        + [vmem(*x) for x in chunk] * 2
        + [
            vmem(heads, nf, *packed),
            vmem(heads, nf - 1, *packed),
            vmem(heads, *packed),
            vmem(4, heads, *packed),
            pltpu.VMEM((16, width), f32),
            pltpu.VMEM((nf, 16, LANE), f32),
            pltpu.VMEM((nf, 16, LANE), f32),
            pltpu.VMEM((16, LANE), f32),
            pltpu.VMEM((4, 16, LANE), f32),
            triple, DMA((6,)), hops, hops, triple, triple, triple, triple,
            DMA((3, 3, heads)), DMA((3, 3, heads)), DMA((3, heads)),
            DMA((heads, nf - 1)), DMA((heads, nf - 1)), DMA((heads, 3)), DMA((heads, 3)),
            DMA((nf - 1,)), DMA((nf - 1,)), triple, triple,
        ],
        compiler_params=params(4),
        name="back",
    )(qb, k, v, o, gctx, *sums, x_all, *mats, first_grad, gvec)


def results_kernel(rows, output, states_grad, up, down, wout, qkv, vec, upb, *outs):
    outs[0][...] = output[...]
    outs[1][...] = states_grad[...]
    for m in range(3):
        outs[2 + m][...] = qkv[m].astype(f32)
    outs[5][...] = wout[...].astype(f32)
    outs[6][...] = up[...].astype(f32)
    outs[7][...] = down[...].astype(f32)
    for r in range(8):
        outs[8 + r][...] = vec[r : r + 1, :rows]
    outs[16][...] = upb[0:1, :]


def results(rows, output, states_grad, up, down, wout, qkv, vec, upb):
    shape = jax.ShapeDtypeStruct
    pieces = 3
    grads = [shape(qkv.shape[1:], f32)] * 3 + [shape(x.shape, f32) for x in (wout, up, down)]
    outs = [shape(output.shape, bf16)] * 2 + grads
    lines = [shape((1, rows), f32)] * 8 + [shape((1, upb.shape[1]), f32)]

    def cut(x):
        n = len(x.shape)
        size = x.shape[: n - 2] + (x.shape[n - 2] // pieces, x.shape[n - 1])
        return pl.BlockSpec(size, functools.partial(lambda n, i: (0,) * (n - 2) + (i, 0), n))

    def same(x):
        return pl.BlockSpec(x.shape, lambda i: (0, 0))

    return pl.pallas_call(
        functools.partial(results_kernel, rows),
        grid=(pieces,),
        out_shape=outs + lines,
        in_specs=[cut(x) for x in (output, states_grad, up, down, wout, qkv)] + [same(vec), same(upb)],
        out_specs=[cut(x) for x in outs] + [same(x) for x in lines],
        compiler_params=params(),
        name="results",
    )(output, states_grad, up, down, wout, qkv, vec, upb)


def fused_device(
    nf, states, query_weight, key_weight, value_weight, out_weight, query_bias, value_bias,
    out_bias, first_gain, first_shift, up_weight, up_bias, down_weight, down_bias, second_gain,
    second_shift, lengths, cotangent,
):
    tokens, width = states.shape
    rows = width // nf
    hidden = up_weight.shape[1]
    heads = width // 4 // 64
    lines = jnp.concatenate(
        [
            x.reshape(-1, rows)
            for x in (
                query_bias, value_bias, out_bias, first_gain, first_shift, down_bias, second_gain,
                second_shift, up_bias,
            )
        ],
        axis=0,
    )
    vec = jnp.pad(lines, ((0, 16 - lines.shape[0]), (0, LANE - rows)))
    qb, o, k, v, x_all, vec_all, ctx, wout, up, down = front(
        nf, heads, lengths, states, query_weight, key_weight, value_weight, vec, out_weight,
        up_weight, down_weight, block=256, key_chunk=512,
    )
    vec_all = vec_all[:, :, :rows].astype(f32)
    full = vec_all[:, :8].transpose(1, 0, 2).reshape(8, width)
    full_up = vec_all[:, 8:12].reshape(1, hidden)
    output, first_grad, gctx, up_sum, down_sum, wout_sum, gvec, wq, wk, wv = feed(
        nf, lengths, states, cotangent, ctx, wout.reshape(width, width),
        up.reshape(width, hidden), down.reshape(hidden, width), full, full_up,
        (query_weight, key_weight, value_weight),
    )
    states_grad, up_grad, down_grad, out_grad, qkv, vec_grad, upb_grad = back(
        nf, qb, k, v, o, gctx.reshape(4 * tokens, -1), (up_sum, down_sum, wout_sum), x_all,
        (wq, wk, wv), first_grad, gvec, key_block=384,
    )
    done = results(rows, output, states_grad, up_grad, down_grad, out_grad, qkv, vec_grad, upb_grad)
    output, states_grad, q_grad, k_grad, v_grad, out_grad, up_grad, down_grad = done[:8]
    lines = [x.reshape(-1) for x in done[8:]]
    return (
        output, states_grad, q_grad, k_grad, v_grad, out_grad, *lines[:5], up_grad, lines[8],
        down_grad, *lines[5:8],
    )


def solution(mesh):
    nf, ns = mesh.shape["fsdp"], mesh.shape["seq"]

    def choose(states, query_weight, *rest):
        rows, width = query_weight.shape
        fits = ns == 4 and nf in (4, 6, 8) and rows % 16 == 0 and width == 768 and states.shape[0] % 768 == 0
        device = functools.partial(fused_device, nf) if fits else per_device
        return device(states, query_weight, *rest)

    return jax.shard_map(
        choose,
        mesh=mesh,
        in_specs=(
            P(("fsdp", "seq"), None),
            P("fsdp", None),
            P("fsdp", None),
            P("fsdp", None),
            P("fsdp", None),
            P("fsdp"),
            P("fsdp"),
            P("fsdp"),
            P("fsdp"),
            P("fsdp"),
            P("fsdp", None),
            P("fsdp"),
            P("fsdp", None),
            P("fsdp"),
            P("fsdp"),
            P("fsdp"),
            P("fsdp"),
            P(("fsdp", "seq"), None),
        ),
        out_specs=(
            P(("fsdp", "seq"), None),
            P(("fsdp", "seq"), None),
            P("fsdp", None),
            P("fsdp", None),
            P("fsdp", None),
            P("fsdp", None),
            P("fsdp"),
            P("fsdp"),
            P("fsdp"),
            P("fsdp"),
            P("fsdp"),
            P("fsdp", None),
            P("fsdp"),
            P("fsdp", None),
            P("fsdp"),
            P("fsdp"),
            P("fsdp"),
        ),
        check_vma=False,
    )
```

```python
import functools
import math

import jax
import jax.numpy as jnp
from jax import lax
from jax.experimental import pallas as pl
from jax.experimental.pallas import tpu as pltpu
from jax.sharding import PartitionSpec as P

HEAD_DIM = 64


eps = 1e-12


def product(left, right):
    return jnp.dot(left, right, preferred_element_type=jnp.float32)


def left_product(left, right):
    return lax.dot_general(
        left, right, (((0,), (0,)), ((), ())), preferred_element_type=jnp.float32
    )


def right_product(left, right):
    return lax.dot_general(
        left, right, (((1,), (1,)), ((), ())), preferred_element_type=jnp.float32
    )


def layer_norm(values, gain, shift):
    average = jnp.mean(values, axis=-1, keepdims=True)
    centred = values - average
    spread = jnp.mean(centred * centred, axis=-1, keepdims=True)
    return centred * lax.rsqrt(spread + eps) * gain + shift


def gelu_exact(values):
    return jax.nn.gelu(values, approximate=False)


def column_sums(values):
    return jnp.sum(values.astype(jnp.float32), axis=0)


def per_device(
    states,
    query_weight,
    key_weight,
    value_weight,
    out_weight,
    query_bias,
    value_bias,
    out_bias,
    first_gain,
    first_shift,
    up_weight,
    up_bias,
    down_weight,
    down_bias,
    second_gain,
    second_shift,
    lengths,
    cotangent,
):
    f32 = jnp.float32
    bf16 = jnp.bfloat16
    (
        query_mat,
        key_mat,
        value_mat,
        out_mat,
        query_add,
        value_add,
        out_add,
        gain_first,
        shift_first,
    ) = (
        lax.all_gather(query_weight, "fsdp", axis=0, tiled=True),
        lax.all_gather(key_weight, "fsdp", axis=0, tiled=True),
        lax.all_gather(value_weight, "fsdp", axis=0, tiled=True),
        lax.all_gather(out_weight, "fsdp", axis=0, tiled=True),
        lax.all_gather(query_bias, "fsdp", axis=0, tiled=True),
        lax.all_gather(value_bias, "fsdp", axis=0, tiled=True),
        lax.all_gather(out_bias, "fsdp", axis=0, tiled=True),
        lax.all_gather(first_gain, "fsdp", axis=0, tiled=True),
        lax.all_gather(first_shift, "fsdp", axis=0, tiled=True),
    )
    up_mat, up_add, down_mat, down_add, gain_second, shift_second = (
        lax.all_gather(up_weight, "fsdp", axis=0, tiled=True),
        lax.all_gather(up_bias, "fsdp", axis=0, tiled=True),
        lax.all_gather(down_weight, "fsdp", axis=0, tiled=True),
        lax.all_gather(down_bias, "fsdp", axis=0, tiled=True),
        lax.all_gather(second_gain, "fsdp", axis=0, tiled=True),
        lax.all_gather(second_shift, "fsdp", axis=0, tiled=True),
    )
    tokens = states.shape[0]
    slot_rows = tokens * lax.axis_size("seq")
    length = lengths[0]
    places = lax.axis_index("seq") * tokens + lax.iota(jnp.int32, tokens)
    valid_rows = (places < length).astype(f32)[:, None]
    queries = (product(states, query_mat) + query_add).astype(bf16)
    keys_in = product(states, key_mat).astype(bf16)
    values = (product(states, value_mat) + value_add).astype(bf16)
    head_queries, head_keys, head_values = (
        lax.all_to_all(queries, "seq", split_axis=1, concat_axis=0, tiled=True),
        lax.all_to_all(keys_in, "seq", split_axis=1, concat_axis=0, tiled=True),
        lax.all_to_all(values, "seq", split_axis=1, concat_axis=0, tiled=True),
    )
    local_width = head_queries.shape[1]
    head_count = local_width // HEAD_DIM
    block_rows = min(512, slot_rows)
    blocks = slot_rows // block_rows
    scaling = HEAD_DIM ** (-0.5)
    key_valid = lax.iota(jnp.int32, slot_rows) < length
    keys_heads = head_keys.reshape(slot_rows, head_count, HEAD_DIM)
    values_heads = head_values.reshape(slot_rows, head_count, HEAD_DIM)
    query_blocks = head_queries.reshape(blocks, block_rows, head_count, HEAD_DIM)

    def block_scores(query_block):
        scores = (
            jnp.einsum("qhd,khd->hqk", query_block, keys_heads, preferred_element_type=f32)
            * scaling
        )
        return jnp.where(key_valid[None, None, :], scores, -1000000000.0)

    def forward_block(query_block):
        scores = block_scores(query_block)
        highest = jnp.max(scores, axis=-1, keepdims=True)
        exponent = jnp.exp(scores - highest)
        totals = jnp.sum(exponent, axis=-1, keepdims=True)
        weights_soft = (exponent / totals).astype(bf16)
        context_part = jnp.einsum(
            "hqk,khd->qhd", weights_soft, values_heads, preferred_element_type=f32
        )
        return (context_part.astype(bf16), (highest + jnp.log(totals))[:, :, 0])

    context_blocks, log_totals = lax.map(forward_block, query_blocks)
    context = lax.all_to_all(
        context_blocks.reshape(slot_rows, local_width),
        "seq",
        split_axis=0,
        concat_axis=1,
        tiled=True,
    )
    hidden = states.astype(f32)
    first_sum = hidden + (product(context, out_mat) + out_add)
    first_norm, first_back = jax.vjp(
        layer_norm, first_sum, gain_first.astype(f32), shift_first.astype(f32)
    )
    first_low = first_norm.astype(bf16)
    pre_act = product(first_low, up_mat) + up_add
    activated = gelu_exact(pre_act).astype(bf16)
    second_sum = first_norm + (product(activated, down_mat) + down_add)
    normed, second_back = jax.vjp(
        layer_norm, second_sum, gain_second.astype(f32), shift_second.astype(f32)
    )
    output = (normed * valid_rows).astype(bf16)
    out_grad = cotangent.astype(f32) * valid_rows
    second_grad, gain_second_grad, shift_second_grad = second_back(out_grad)
    down_in = second_grad.astype(bf16)
    down_weight_grad = left_product(activated, down_in)
    down_bias_grad = column_sums(down_in)
    act_grad = right_product(down_in, down_mat)
    pre_grad = jax.vjp(gelu_exact, pre_act)[1](act_grad)[0].astype(bf16)
    up_weight_grad = left_product(first_low, pre_grad)
    up_bias_grad = column_sums(pre_grad)
    norm_grad = second_grad + right_product(pre_grad, up_mat)
    first_grad, gain_first_grad, shift_first_grad = first_back(norm_grad)
    branch_grad = first_grad.astype(bf16)
    out_weight_grad = left_product(context, branch_grad)
    out_bias_grad = column_sums(branch_grad)
    context_grad = right_product(branch_grad, out_mat).astype(bf16)
    head_grad = lax.all_to_all(context_grad, "seq", split_axis=1, concat_axis=0, tiled=True)
    grad_blocks = head_grad.reshape(blocks, block_rows, head_count, HEAD_DIM)

    def backward_step(carry, packed):
        key_acc, value_acc = carry
        query_block, grad_block, log_block = packed
        scores = block_scores(query_block)
        probs_full = jnp.exp(scores - log_block[:, :, None])
        probs_low = probs_full.astype(bf16)
        prob_grad = jnp.einsum("qhd,khd->hqk", grad_block, values_heads, preferred_element_type=f32)
        centre = jnp.sum(prob_grad * probs_full, axis=-1, keepdims=True)
        score_grad = (probs_full * (prob_grad - centre)).astype(bf16)
        query_part = (
            jnp.einsum("hqk,khd->qhd", score_grad, keys_heads, preferred_element_type=f32) * scaling
        )
        key_acc = (
            key_acc
            + jnp.einsum("hqk,qhd->khd", score_grad, query_block, preferred_element_type=f32)
            * scaling
        )
        value_acc = value_acc + jnp.einsum(
            "hqk,qhd->khd", probs_low, grad_block, preferred_element_type=f32
        )
        return ((key_acc, value_acc), query_part.astype(bf16))

    zeros_heads = jnp.zeros((slot_rows, head_count, HEAD_DIM), f32)
    (key_total, value_total), query_parts = lax.scan(
        backward_step, (zeros_heads, zeros_heads), (query_blocks, grad_blocks, log_totals)
    )
    query_back, key_back, value_back = (
        lax.all_to_all(
            query_parts.reshape(slot_rows, local_width),
            "seq",
            split_axis=0,
            concat_axis=1,
            tiled=True,
        ),
        lax.all_to_all(
            key_total.reshape(slot_rows, local_width).astype(bf16),
            "seq",
            split_axis=0,
            concat_axis=1,
            tiled=True,
        ),
        lax.all_to_all(
            value_total.reshape(slot_rows, local_width).astype(bf16),
            "seq",
            split_axis=0,
            concat_axis=1,
            tiled=True,
        ),
    )
    query_weight_grad = left_product(states, query_back)
    key_weight_grad = left_product(states, key_back)
    value_weight_grad = left_product(states, value_back)
    query_bias_grad = column_sums(query_back)
    value_bias_grad = column_sums(value_back)
    states_grad = (
        first_grad
        + right_product(query_back, query_mat)
        + right_product(key_back, key_mat)
        + right_product(value_back, value_mat)
    ).astype(bf16)
    attend_parts = (
        lax.psum_scatter(query_weight_grad, "fsdp", scatter_dimension=0, tiled=True),
        lax.psum_scatter(key_weight_grad, "fsdp", scatter_dimension=0, tiled=True),
        lax.psum_scatter(value_weight_grad, "fsdp", scatter_dimension=0, tiled=True),
        lax.psum_scatter(out_weight_grad, "fsdp", scatter_dimension=0, tiled=True),
        lax.psum_scatter(query_bias_grad, "fsdp", scatter_dimension=0, tiled=True),
        lax.psum_scatter(value_bias_grad, "fsdp", scatter_dimension=0, tiled=True),
        lax.psum_scatter(out_bias_grad, "fsdp", scatter_dimension=0, tiled=True),
        lax.psum_scatter(gain_first_grad, "fsdp", scatter_dimension=0, tiled=True),
        lax.psum_scatter(shift_first_grad, "fsdp", scatter_dimension=0, tiled=True),
    )
    feed_parts = (
        lax.psum_scatter(up_weight_grad, "fsdp", scatter_dimension=0, tiled=True),
        lax.psum_scatter(up_bias_grad, "fsdp", scatter_dimension=0, tiled=True),
        lax.psum_scatter(down_weight_grad, "fsdp", scatter_dimension=0, tiled=True),
        lax.psum_scatter(down_bias_grad, "fsdp", scatter_dimension=0, tiled=True),
        lax.psum_scatter(gain_second_grad, "fsdp", scatter_dimension=0, tiled=True),
        lax.psum_scatter(shift_second_grad, "fsdp", scatter_dimension=0, tiled=True),
    )
    summed = (
        lax.psum(attend_parts[0].astype(jnp.bfloat16), "seq").astype(jnp.float32),
        lax.psum(attend_parts[1].astype(jnp.bfloat16), "seq").astype(jnp.float32),
        lax.psum(attend_parts[2].astype(jnp.bfloat16), "seq").astype(jnp.float32),
        lax.psum(attend_parts[3].astype(jnp.bfloat16), "seq").astype(jnp.float32),
        lax.psum(attend_parts[4].astype(jnp.bfloat16), "seq").astype(jnp.float32),
        lax.psum(attend_parts[5].astype(jnp.bfloat16), "seq").astype(jnp.float32),
        lax.psum(attend_parts[6].astype(jnp.bfloat16), "seq").astype(jnp.float32),
        lax.psum(attend_parts[7].astype(jnp.bfloat16), "seq").astype(jnp.float32),
        lax.psum(attend_parts[8].astype(jnp.bfloat16), "seq").astype(jnp.float32),
        lax.psum(feed_parts[0].astype(jnp.bfloat16), "seq").astype(jnp.float32),
        lax.psum(feed_parts[1].astype(jnp.bfloat16), "seq").astype(jnp.float32),
        lax.psum(feed_parts[2].astype(jnp.bfloat16), "seq").astype(jnp.float32),
        lax.psum(feed_parts[3].astype(jnp.bfloat16), "seq").astype(jnp.float32),
        lax.psum(feed_parts[4].astype(jnp.bfloat16), "seq").astype(jnp.float32),
        lax.psum(feed_parts[5].astype(jnp.bfloat16), "seq").astype(jnp.float32),
    )
    return (
        output,
        states_grad,
        summed[0],
        summed[1],
        summed[2],
        summed[3],
        summed[4],
        summed[5],
        summed[6],
        summed[7],
        summed[8],
        summed[9],
        summed[10],
        summed[11],
        summed[12],
        summed[13],
        summed[14],
    )


LANE = 128
LOG2E = math.log2(math.e)
LN2 = math.log(2.0)
NT = (((1,), (1,)), ((), ()))
NN = (((1,), (0,)), ((), ()))
TN = (((0,), (0,)), ((), ()))
VMEM_BYTES = 66 * 1024 * 1024 - 2 * 1024 * 1024
f32 = jnp.float32
bf16 = jnp.bfloat16
ANY = pl.BlockSpec(memory_space=pl.ANY)
IN_VMEM = pl.BlockSpec(memory_space=pltpu.VMEM)
IN_SMEM = pl.BlockSpec(memory_space=pltpu.SMEM)
DMA = pltpu.SemaphoreType.DMA


def dims(left, right, numbers):
    return lax.dot_general(left, right, numbers, preferred_element_type=f32)


def remote(src, dst, send_sem, recv_sem, **where):
    return pltpu.make_async_remote_copy(
        src_ref=src,
        dst_ref=dst,
        send_sem=send_sem,
        recv_sem=recv_sem,
        device_id=where,
        device_id_type=pl.DeviceIdType.MESH,
    )


def hail(partners):
    barrier = pltpu.get_barrier_semaphore()
    for where in partners:
        pl.semaphore_signal(barrier, inc=1, device_id=where, device_id_type=pl.DeviceIdType.MESH)


def hailed(partners):
    pl.semaphore_wait(pltpu.get_barrier_semaphore(), len(partners))


def greet(partners):
    hail(partners)
    hailed(partners)


def seq_peers():
    me = lax.axis_index("seq")
    across = (me + 2) % 4
    return me, me + 1 - 2 * (me % 2), across, across + 1 - 2 * (across % 2)


def place_of(index, count):
    half = index // 2
    return half + (index % 2) * (count - 1 - 2 * half)


def index_at(place, count):
    upper = place // (count // 2)
    return (1 - upper) * 2 * place + upper * (2 * (count - 1 - place) + 1)


def thirds(values):
    high = values.astype(bf16)
    rest = values - high.astype(f32)
    middle = rest.astype(bf16)
    low = (rest - middle.astype(f32)).astype(bf16)
    return high.astype(f32), middle.astype(f32), low.astype(f32)


def with_lanes(base, columns):
    lane = lax.broadcasted_iota(jnp.int32, base.shape, 1)
    for place, values in columns:
        base = jnp.where(lane == place, values, base)
    return base


def params(collective_id=None):
    if collective_id is None:
        return pltpu.CompilerParams(vmem_limit_bytes=VMEM_BYTES)
    return pltpu.CompilerParams(
        vmem_limit_bytes=VMEM_BYTES, collective_id=collective_id, has_side_effects=True
    )


def ring_gather(nf, shards, halves, outs, ring_send, ring_recv, pair_send, pair_recv):
    f = lax.axis_index("fsdp")
    s, near, _, _ = seq_peers()
    side = s % 2
    step = 1 - 2 * side
    place = place_of(f, nf)
    ahead = index_at((place + step + nf) % nf, nf)

    def half(ref, w):
        axis, size = halves[w]
        cut = pl.ds(pl.multiple_of(side * size, size), size)
        return ref.at[cut, :] if axis == 0 else ref.at[:, cut]

    def slot(hop):
        return index_at((place + nf - step * (hop + 1)) % nf, nf)

    def ring(w, hop, owner, source):
        return remote(
            half(source, w),
            half(outs[w].at[owner], w),
            ring_send.at[w, hop],
            ring_recv.at[w, hop],
            fsdp=ahead,
        )

    def pair(w, hop):
        piece = half(outs[w].at[slot(hop)], w)
        return remote(piece, piece, pair_send.at[w, hop], pair_recv.at[w, hop], seq=near)

    def start(w):
        ring(w, 0, f, shards[w]).start()

    def hop(w, h):
        owner = slot(h)
        ring(w, h, owner, outs[w].at[owner]).wait_recv()

        @pl.when(h < nf - 2)
        def _():
            ring(w, h + 1, owner, outs[w].at[owner]).start()

        pair(w, h).start()

    def finish(w, h):
        ring(w, h, f, shards[w]).wait_send()
        pair(w, h).wait()

    return start, hop, finish


def front_kernel(
    nf, block, key_chunk, halves, groups,
    length_ref, states, wq, wk, wv, wout_s, up_s, down_s, *refs,
):
    small_params, refs = refs[:9], refs[9:]
    (
qb_out, o_out, k_out, v_out, x_out, vec_out, ctx_out, wout, up, down,
        q_buf, k_buf, v_buf, qb_buf, o_buf, s_buf, top_buf, ctx_buf, x_buf, w_buf, w_own, packed, vec_own, vec_buf,
        wout_buf, up_buf, down_buf, local_sem, x_sem, kv_sem, keep_sem, vec_send, vec_recv, z_send, z_recv, h_send, h_recv,
        near_send, near_recv, far_send, far_recv, pass_send, pass_recv,
        ring_send, ring_recv, pair_send, pair_recv, ctx_send, ctx_recv, own_sem, copy_sem,
    ) = refs
    f = lax.axis_index("fsdp")
    s, near, far, cross = seq_peers()
    tokens, width = states.shape
    heads, slots, _ = q_buf.shape
    rows = wq.shape[0]
    window = w_buf.shape[2]
    vec_rows = vec_buf.shape[1]
    own_width = heads * 64
    parts = far_send.shape[0]
    chunk = tokens // parts
    per = tokens // block
    beside = f + 1 - 2 * (f % 2)
    stages = nf // 2
    first_lane = pl.multiple_of((own_width * s // LANE) * LANE, LANE)
    weights = (wq, wk, wv)
    shards, outs = (wout_s, up_s, down_s), (wout, up, down)
    ring_start, ring_hop, ring_finish = ring_gather(
        nf, shards, halves, outs, ring_send, ring_recv, pair_send, pair_recv
    )
    friends = [{"fsdp": (f + d) % nf} for d in range(1, nf)] + [
        {"seq": near}, {"seq": far}, {"seq": cross},
    ]
    hail(friends)

    def along(d):
        to = (f + 2 * d) % nf
        return remote(packed.at[f], packed.at[f], z_send.at[d - 1], z_recv.at[d - 1], fsdp=to)

    def aside(d):
        owner = (f + nf - 2 * d) % nf
        return remote(packed.at[owner], packed.at[owner], h_send.at[d], h_recv.at[d], fsdp=beside)

    def vec_copy(d):
        return remote(
            vec_buf.at[f], vec_buf.at[f], vec_send.at[d - 1], vec_recv.at[d - 1],
            fsdp=(f + d) % nf,
        )

    def far_copy(c):
        at = pl.ds(c * chunk, chunk)
        return remote(states.at[at], x_buf.at[2, at], far_send.at[c], far_recv.at[c], seq=far)

    def pass_copy(c):
        at = pl.ds(c * chunk, chunk)
        return remote(
            x_buf.at[2, at], x_buf.at[3, at], pass_send.at[c], pass_recv.at[c], seq=near
        )

    near_copy = remote(states, x_buf.at[1], near_send, near_recv, seq=near)
    windows = [
        pltpu.make_async_copy(
            weights[m].at[:, pl.ds(first_lane, window)], w_own.at[m], local_sem.at[1 + m]
        )
        for m in range(3)
    ]
    local = [pltpu.make_async_copy(states, x_buf.at[0], local_sem.at[0])]
    for copy in windows + local:
        copy.start()
    vec_own[...] = jnp.zeros_like(vec_own)
    for r in range(8):
        vec_own[r : r + 1, :rows] = small_params[r][...].astype(f32).reshape(1, rows)
    line = small_params[8][...].astype(f32).reshape(1, 4 * rows)
    for r in range(4):
        vec_own[8 + r : 9 + r, :rows] = line[:, rows * r : rows * (r + 1)]
    vec_buf[f] = vec_own[...].astype(bf16)
    turn = (window - (own_width * s) % LANE) % window
    for m in range(3):
        windows[m].wait()
        columns = pltpu.roll(w_own[m].astype(f32), turn, 1)[:, :own_width]
        packed[f, m] = jnp.concatenate(
            [columns[: rows // 2], columns[rows // 2 :]], axis=1
        ).astype(bf16)
    hailed(friends)
    for d in range(1, stages):
        along(d).start()
    aside(0).start()
    for c in range(parts):
        far_copy(c).start()
    near_copy.start()
    for d in range(1, nf):
        vec_copy(d).start()
    for w in groups[0] + groups[1]:
        ring_start(w)
    held = (wout_buf, up_buf, down_buf)
    mine = [
        pltpu.make_async_copy(shards[w], held[w], copy_sem.at[0, w]) for w in range(len(shards))
    ]
    for copy in mine:
        copy.start()
    for copy in local:
        copy.wait()
    kept = []

    def keep(slot, index):
        copy = pltpu.make_async_copy(x_buf.at[slot], x_out.at[index], x_sem.at[slot])
        copy.start()
        kept.append(copy)

    def pass_on(c):
        far_copy(c).wait_recv()
        pass_copy(c).start()

    def turn_aside(d):
        along(d).wait_recv()
        aside(d).start()

    keep(0, s)
    for copy in mine:
        copy.wait()
    mine = [
        pltpu.make_async_copy(held[w], outs[w].at[f], copy_sem.at[1, w]) for w in range(len(shards))
    ]
    for copy in mine:
        copy.start()
    passed = 0
    for d in range(1, stages):
        turn_aside(d)
        if d != 2 and passed < parts - 2:
            pass_on(passed)
            passed += 1
    for d in range(1, nf):
        vec_copy(d).wait_recv()
    for d in range(stages):
        aside(d).wait_recv()
    gap = jnp.zeros((rows // 2, window - own_width), f32)
    for j in range(nf):
        for m in range(3):
            both = packed[j, m].astype(f32)
            for e in range(2):
                at = pl.ds(rows * j + rows // 2 * e, rows // 2)
                columns = both[:, own_width * e : own_width * (e + 1)]
                w_buf[m, at, :] = jnp.concatenate([columns, gap], axis=1).astype(bf16)
    share = own_width // rows
    wide = lax.broadcasted_iota(jnp.int32, (1, window), 1)
    biases = []
    for row in (0, 1):
        line = jnp.zeros((1, window), f32)
        for i in range(share):
            piece = vec_buf[share * s + i][row : row + 1, :].astype(f32)
            piece = jnp.concatenate([piece, jnp.zeros((1, window - LANE), f32)], axis=1)
            if i:
                piece = pltpu.roll(piece, i * rows, 1)
            line = jnp.where((wide >= i * rows) & (wide < (i + 1) * rows), piece, line)
        biases.append(line)
    length = length_ref[0]
    mats = [w_buf[m] for m in range(3)]
    small = lax.broadcasted_iota(jnp.int32, (chunk, LANE), 1)
    q_tail = jnp.where(small == 64, 1.0, 0.0)
    v_tail = jnp.where((small >= 64) & (small < 67), 1.0, 0.0)

    def heads_of(values, tail):
        found = []
        for h in range(heads):
            tile = values[:, (h // 2) * LANE : (h // 2 + 1) * LANE]
            if h % 2:
                tile = pltpu.roll(tile, 64, 1)
            found.append(jnp.where(small < 64, tile, tail).astype(bf16))
        return found

    def compute(slot, index, part):
        x = x_buf[slot, pl.ds(pl.multiple_of(part * chunk, chunk), chunk), :]
        start = pl.multiple_of(index * tokens + part * chunk, chunk)
        where = start + lax.broadcasted_iota(jnp.int32, (chunk, LANE), 0)
        queries = dims(x, mats[0], NN) + biases[0]
        keys = dims(x, mats[1], NN)
        k_tail = jnp.where(
            small == 64,
            jnp.where(where < length, 0.0, -1e9),
            jnp.where((small > 64) & (small < 68), 1.0, 0.0),
        )
        values = dims(x, mats[2], NN) + biases[1]
        at = pl.ds(start, chunk)
        for ref, found in (
            (q_buf, heads_of(queries * (LOG2E * 0.125), q_tail)),
            (k_buf, heads_of(keys, k_tail)),
            (v_buf, heads_of(values, v_tail)),
        ):
            for h in range(heads):
                ref[h, at, :] = found[h]

    def whole(slot, index, low, high):
        def body(part, carry):
            compute(slot, index, part)
            return carry

        lax.fori_loop(low, high, body, 0)

    def hops(g, h):
        for w in groups[g]:
            ring_hop(w, h)

    hops(0, 0)
    hops(1, 0)
    whole(0, s, 0, parts)
    for c in range(passed, parts - 1):
        pass_on(c)
    near_copy.wait_recv()
    keep(1, near)
    whole(1, near, 0, parts)
    hops(0, 1)
    whole(2, far, 0, parts - 1)
    pass_on(parts - 1)
    hops(1, 1)
    whole(2, far, parts - 1, parts)
    keep(2, far)
    for c in range(parts):
        pass_copy(c).wait_recv()
    keep(3, cross)
    whole(3, cross, 0, parts)
    hops(0, 2)
    saved = [
        pltpu.make_async_copy(k_buf, k_out, kv_sem.at[0]),
        pltpu.make_async_copy(v_buf, v_out, kv_sem.at[1]),
        pltpu.make_async_copy(vec_buf, vec_out, kv_sem.at[2]),
    ]
    for copy in saved:
        copy.start()

    lane = lax.broadcasted_iota(jnp.int32, (block, LANE), 1)

    def partner(round_):
        relation = 3 - round_
        return ((s // 2 + relation // 2) % 2) * 2 + (s % 2 + relation % 2) % 2

    def ctx_copy(step):
        at = pl.ds(pl.multiple_of(step % per * block, block), block)
        return remote(
            ctx_buf.at[step],
            ctx_out.at[s, at],
            ctx_send.at[step],
            ctx_recv.at[step],
            seq=partner(step // per),
        )

    def rows_of(step):
        base = partner(step // per) * tokens + step % per * block
        return pl.ds(pl.multiple_of(base, block), block)

    def keep_copies(step):
        at = rows_of(step)
        return (
            pltpu.make_async_copy(qb_buf.at[:, at], qb_out.at[:, at], keep_sem.at[0, step]),
            pltpu.make_async_copy(o_buf.at[:, at], o_out.at[:, at], keep_sem.at[1, step]),
        )

    chunks = slots // key_chunk

    def score(h, at, c):
        return dims(q_buf[h, at, :], k_buf[h, c * key_chunk : (c + 1) * key_chunk, :], NT)

    def highest(values, top):
        for j in range(key_chunk // LANE):
            tile = values[:, j * LANE : (j + 1) * LANE]
            top = tile if top is None else jnp.maximum(top, tile)
        return top

    top = None
    for c in range(chunks):
        scores = score(0, rows_of(0), c)
        s_buf[:, c * key_chunk : (c + 1) * key_chunk] = scores
        top = highest(scores, top)
    top_buf[...] = top

    def attend(step, carry):
        at = rows_of(step)
        after = rows_of(jnp.minimum(step + 1, 4 * per - 1))
        results = []
        current = [s_buf[:, c * key_chunk : (c + 1) * key_chunk] for c in range(chunks)]
        top = top_buf[...]
        for h in range(heads):
            peak = jnp.max(top, axis=1, keepdims=True)
            total = None
            coming = []
            top = None
            for c in range(chunks):
                scores = score(h + 1, at, c) if h + 1 < heads else score(0, after, c)
                coming.append(scores)
                top = highest(scores, top)
                probs = jnp.exp2(current[c] - peak).astype(bf16)
                term = dims(probs, v_buf[h, c * key_chunk : (c + 1) * key_chunk, :], NN)
                total = term if total is None else total + term
            current = coming
            weight = total[:, 64:65]
            result = jnp.where(lane < 64, total * (1.0 / weight), 0.0)
            o_buf[h, at, :] = result.astype(bf16)
            high, middle, low = thirds(-(peak + jnp.log2(weight)))
            qb_buf[h, at, :] = with_lanes(
                q_buf[h, at, :].astype(f32), ((65, high), (66, middle), (67, low))
            ).astype(bf16)
            results.append(result)
        for c in range(chunks):
            s_buf[:, c * key_chunk : (c + 1) * key_chunk] = current[c]
        top_buf[...] = top
        for t in range((heads + 1) // 2):
            tile = results[2 * t]
            if 2 * t + 1 < heads:
                tile = tile + pltpu.roll(results[2 * t + 1], 64, 1)
            ctx_buf[step, :, t * LANE : (t + 1) * LANE] = tile.astype(bf16)

        @pl.when(step < 3 * per)
        def _():
            ctx_copy(step).start()

        for copy in keep_copies(step):
            copy.start()
        for g in range(2):
            late = 2 * (1 - g)
            h = (2 * step - late + 1) // 5
            @pl.when(((5 * h + late) // 2 == step) & (h + 3 - g < nf - 1))
            def _():
                hops(g, h + 3 - g)

        return carry

    lax.fori_loop(0, 4 * per, attend, 0)
    owns = []
    for i in range(per):
        owns.append(
            pltpu.make_async_copy(
                ctx_buf.at[3 * per + i], ctx_out.at[s, pl.ds(i * block, block)], own_sem.at[i]
            )
        )
        owns[-1].start()

    def rest(h, carry):
        for w in range(len(shards)):
            ring_hop(w, h)
        return carry

    lax.fori_loop(min(7, nf - 1), nf - 1, rest, 0)

    def settle(step, carry):
        @pl.when(step < 3 * per)
        def _():
            ctx_copy(step).wait()

        for copy in keep_copies(step):
            copy.wait()
        return carry

    lax.fori_loop(0, 4 * per, settle, 0)
    for d in range(1, stages):
        along(d).wait_send()
    for d in range(stages):
        aside(d).wait_send()
    for d in range(1, nf):
        vec_copy(d).wait_send()
    for c in range(parts):
        far_copy(c).wait_send()
        pass_copy(c).wait_send()
    near_copy.wait_send()
    for copy in owns + mine + kept + saved:
        copy.wait()

    def close(h, carry):
        for w in range(len(shards)):
            ring_finish(w, h)
        return carry

    lax.fori_loop(0, nf - 1, close, 0)


def front(nf, heads, length, states, wq, wk, wv, wout, up, down, small_params, block, key_chunk):
    tokens, width = states.shape
    rows = wq.shape[0]
    slots = 4 * tokens
    parts = 4
    window = 256
    shards = (wout, up, down)
    halves = tuple((1, w.shape[1] // 2) for w in shards)
    wide = -(-heads // 2) * LANE
    steps = slots // block
    shape = jax.ShapeDtypeStruct
    head_shape = shape((heads, slots, LANE), bf16)
    head_buf = pltpu.VMEM((heads, slots, LANE), bf16)
    hops = DMA((3, nf - 1))
    stage = DMA((nf // 2 - 1,))
    stage_aside = DMA((nf // 2,))
    peers = DMA((nf - 1,))
    fine = DMA((parts,))
    return pl.pallas_call(
        functools.partial(front_kernel, nf, block, key_chunk, halves, ((1,), (0, 2))),
        out_shape=[head_shape] * 4
        + [
            shape((4, tokens, width), bf16),
            shape((nf, 16, LANE), bf16),
            shape((4, tokens, wide), bf16),
        ]
        + [shape((nf,) + w.shape, bf16) for w in shards],
        in_specs=[IN_SMEM] + [ANY] * 7 + [IN_VMEM] * 9,
        out_specs=[ANY] * 10,
        scratch_shapes=[head_buf] * 5
        + [
            pltpu.VMEM((block, slots), f32),
            pltpu.VMEM((block, LANE), f32),
            pltpu.VMEM((steps, block, wide), bf16),
            pltpu.VMEM((4, tokens, width), bf16),
            pltpu.VMEM((3, width, window), bf16),
            pltpu.VMEM((3, rows, window), bf16),
            pltpu.VMEM((nf, 3, rows // 2, heads * 128), bf16),
            pltpu.VMEM((16, LANE), f32),
            pltpu.VMEM((nf, 16, LANE), bf16),
        ]
        + [pltpu.VMEM(w.shape, bf16) for w in shards]
        + [
            DMA((5,)),
            DMA((4,)),
            DMA((3,)),
            DMA((2, steps)),
            peers, peers, stage, stage, stage_aside, stage_aside,
            DMA(()), DMA(()), fine, fine, fine, fine,
            hops, hops, hops, hops,
            DMA((steps,)), DMA((steps,)),
            DMA((tokens // block,)),
            DMA((2, 3)),
        ],
        compiler_params=params(1),
        name="front",
    )(length, states, wq, wk, wv, wout, up, down, *small_params)


def plane_gather(nf, shards, outs, z_send, z_recv, h_send, h_recv, n_send, n_recv):
    f = lax.axis_index("fsdp")
    s, near, _, _ = seq_peers()
    side = s % 2
    beside = f + 1 - 2 * (f % 2)
    stages = nf // 2
    count = len(shards)

    def half(ref):
        size = ref.shape[1] // 2
        return ref.at[:, pl.ds(pl.multiple_of(side * size, size), size)]

    def along(d, m):
        return remote(
            half(shards[m]), half(outs[m].at[f]), z_send.at[d - 1, m], z_recv.at[d - 1, m],
            fsdp=(f + 2 * d) % nf,
        )

    def aside(d, m):
        owner = (f + nf - 2 * d) % nf
        source = outs[m].at[owner] if d else shards[m]
        return remote(
            half(source), half(outs[m].at[owner]), h_send.at[d, m], h_recv.at[d, m], fsdp=beside
        )

    def share(e, m):
        owner = (f + nf - 2 * e) % nf if e < stages else (beside + nf - 2 * (e - stages)) % nf
        piece = half(outs[m].at[owner])
        return remote(piece, piece, n_send.at[e - 1, m], n_recv.at[e - 1, m], seq=near)

    def start():
        for d in range(1, stages):
            for m in range(count):
                along(d, m).start()
        for m in range(count):
            aside(0, m).start()

    def first():
        for d in range(1, stages):
            for m in range(count):
                along(d, m).wait_recv()
                aside(d, m).start()
                share(d, m).start()

    def second():
        for d in range(stages):
            for m in range(count):
                aside(d, m).wait_recv()
                share(stages + d, m).start()

    def finish():
        for m in range(count):
            for d in range(1, stages):
                along(d, m).wait_send()
            for d in range(stages):
                aside(d, m).wait_send()
            for e in range(1, nf):
                share(e, m).wait()

    return start, first, second, finish


def feed_kernel(
    nf, block, part, length_ref, states, ctx, wout, vec_all, up_hbm, down_hbm, cot_hbm,
    wq_s, wk_s, wv_s,
    out, first_grad_out, gctx, up_sum, down_sum, wout_sum, gvec, wq, wk, wv,
    up, down, cot, held, vec, upb, out_buf, first_buf, act_buf, pre_buf, slope_buf, low_t, down_t, branch_buf,
    g_buf, up_give, down_give, wout_give, up_take, down_take, wout_take,
    load_sem, keep_sem, g_send, g_recv, own_sem, give_send, give_recv, sum_sem, shard_sem,
    z_send, z_recv, h_send, h_recv, n_send, n_recv,
):
    f = lax.axis_index("fsdp")
    s, near, far, cross = seq_peers()
    side = s % 2
    beside = f + 1 - 2 * (f % 2)
    tokens, width = states.shape
    hidden = up.shape[1]
    own = wout.shape[0] // 4
    steps = tokens // block
    wide = ctx.shape[2]
    loads = [
        pltpu.make_async_copy(up_hbm, up, load_sem.at[0]),
        pltpu.make_async_copy(down_hbm, down, load_sem.at[1]),
        pltpu.make_async_copy(cot_hbm, cot, load_sem.at[2]),
    ]
    for copy in loads:
        copy.start()
    shards, outs = (wq_s, wk_s, wv_s), (wq, wk, wv)
    gather = plane_gather(nf, shards, outs, z_send, z_recv, h_send, h_recv, n_send, n_recv)
    friends = [{"fsdp": (f + 2 * d) % nf} for d in range(1, nf // 2)] + [
        {"fsdp": beside}, {"seq": near}, {"seq": far}, {"seq": cross},
    ]
    hail(friends)
    rows = width // nf
    short = lax.broadcasted_iota(jnp.int32, vec_all.shape[1:], 1) < rows
    lines = jnp.zeros((vec_all.shape[1], width), f32)
    blank = jnp.zeros((vec_all.shape[1], width - LANE), f32)
    tiles = [jnp.zeros((1, LANE), f32) for _ in range(hidden // LANE)]
    for j in range(nf):
        piece = jnp.where(short, vec_all[j].astype(f32), 0.0)
        both = jnp.concatenate([piece, blank], axis=1)
        lines = lines + (pltpu.roll(both, rows * j, 1) if j else both)
        for r in range(4):
            first_lane = rows * (4 * j + r)
            tile, shift = first_lane // LANE, first_lane % LANE
            both = jnp.concatenate([piece[8 + r : 9 + r, :], blank[:1, :LANE]], axis=1)
            if shift:
                both = pltpu.roll(both, shift, 1)
            tiles[tile] = tiles[tile] + both[:, :LANE]
            if tile + 1 < len(tiles):
                tiles[tile + 1] = tiles[tile + 1] + both[:, LANE:]
    vec[...] = lines[:8]
    upb[...] = jnp.concatenate(tiles, axis=1)
    kept = [pltpu.make_async_copy(shards[m], held.at[m], shard_sem.at[0, m]) for m in range(3)]
    for copy in kept:
        copy.start()
    kept_out = [
        pltpu.make_async_copy(held.at[m], outs[m].at[f], shard_sem.at[1, m]) for m in range(3)
    ]
    length = length_ref[0]
    gvec[...] = jnp.zeros_like(gvec)
    peers = (s, near, far, cross)

    def line(row):
        return vec[row : row + 1, :]

    def add_line(row, values):
        gvec[row : row + 1, :] += jnp.sum(values, axis=0, keepdims=True)

    def norm(values):
        centred = values - jnp.mean(values, axis=1, keepdims=True)
        scale = lax.rsqrt(jnp.mean(centred * centred, axis=1, keepdims=True) + eps)
        return centred * scale, scale

    def norm_back(grad, gain, normed, scale):
        grad = grad * gain
        return scale * (
            grad
            - jnp.mean(grad, axis=1, keepdims=True)
            - normed * jnp.mean(grad * normed, axis=1, keepdims=True)
        )

    def rows_of(i):
        return pl.ds(pl.multiple_of(i * block, block), block)

    def send(relation, i):
        at = rows_of(i)
        return remote(
            g_buf.at[relation, at],
            gctx.at[s, at],
            g_send.at[relation - 1, i],
            g_recv.at[relation - 1, i],
            seq=peers[relation],
        )

    def keep(i):
        at = rows_of(i)
        return (
            pltpu.make_async_copy(out_buf.at[at], out.at[at], keep_sem.at[0, i]),
            pltpu.make_async_copy(first_buf.at[at], first_grad_out.at[at], keep_sem.at[1, i]),
        )

    def body(i, carry):
        at = rows_of(i)
        attended = None
        for j in range(4):
            term = dims(ctx[j, at, :own], wout[own * j : own * (j + 1), :], NN)
            attended = term if attended is None else attended + term
        normed_first, scale_first = norm(states[at, :].astype(f32) + (attended + line(2)))
        first = normed_first * line(3) + line(4)
        low = first.astype(bf16)
        low_t[:, at] = jnp.transpose(low)

        @pl.when(i == 0)
        def _():
            hailed(friends)
            gather[0]()
            for copy in kept + loads:
                copy.wait()
            for copy in kept_out:
                copy.start()

        fed = None
        for c in range(hidden // part):
            cut = slice(c * part, (c + 1) * part)
            pre = dims(low, up[:, cut], NN) + upb[:, cut]
            share = 0.5 + 0.5 * lax.erf(pre * (2.0**-0.5))
            slope_buf[:, cut] = share + pre * jnp.exp(-0.5 * pre * pre) * (2.0 * math.pi) ** -0.5
            act = (pre * share).astype(bf16)
            act_buf[at, cut] = act
            term = dims(act, down[cut, :], NN)
            fed = term if fed is None else fed + term
        normed, scale = norm(first + (fed + line(5)))
        place = s * tokens + i * block + lax.broadcasted_iota(jnp.int32, (block, 1), 0)
        valid = jnp.where(place < length, 1.0, 0.0)
        out_buf[at, :] = ((normed * line(6) + line(7)) * valid).astype(bf16)
        grad = cot[at, :].astype(f32) * valid
        add_line(6, grad * normed)
        add_line(7, grad)
        second_grad = norm_back(grad, line(6), normed, scale)
        down_in = second_grad.astype(bf16)
        add_line(5, down_in.astype(f32))
        down_t[:, at] = jnp.transpose(down_in)
        back = second_grad
        for c in range(hidden // part):
            cut = slice(c * part, (c + 1) * part)
            pre_grad = (dims(down_in, down[cut, :], NT) * slope_buf[:, cut]).astype(bf16)
            pre_buf[at, cut] = pre_grad
            row = 8 + c * part // width
            col = c * part % width
            gvec[row : row + 1, col : col + part] += jnp.sum(
                pre_grad.astype(f32), axis=0, keepdims=True
            )
            back = back + dims(pre_grad, up[:, cut], NT)
        add_line(3, back * normed_first)
        add_line(4, back)
        first_grad = norm_back(back, line(3), normed_first, scale_first)
        first_buf[at, :] = first_grad
        branch = first_grad.astype(bf16)
        branch_buf[at, :] = branch
        add_line(2, branch.astype(f32))
        for relation in range(4):
            rows = pl.ds(pl.multiple_of(peers[relation] * own, 64), own)
            g_buf[relation, at, :own] = dims(branch, wout[rows, :], NT).astype(bf16)
            if wide > own:
                g_buf[relation, at, own:] = jnp.zeros((block, wide - own), bf16)
            if relation:
                send(relation, i).start()
        for copy in keep(i):
            copy.start()

        @pl.when(i == min(1, steps - 1))
        def _():
            gather[1]()

        return carry

    lax.fori_loop(0, steps, body, 0)
    mine = pltpu.make_async_copy(g_buf.at[0], gctx.at[s], own_sem)
    mine.start()

    pieces = give_send.shape[1]
    up_cut = hidden // 2 // pieces
    down_cut = hidden // pieces

    def up_part(which, c):
        cut = pl.ds(pl.multiple_of(which * (hidden // 2) + c * up_cut, up_cut), up_cut)
        return dims(low_t[...], pre_buf[:, cut], NN)

    def down_part(which, c):
        rows = pl.ds(pl.multiple_of(which * (width // 2), width // 2), width // 2)
        cut = pl.ds(pl.multiple_of(c * down_cut, down_cut), down_cut)
        return dims(down_t[rows, :], act_buf[:, cut], NN)

    def wout_part(which, j):
        cut = pl.ds(pl.multiple_of(which * (width // 2), width // 2), width // 2)
        return dims(ctx[j, :, :own], branch_buf[:, cut], TN)

    def cols(c, size):
        return (slice(None), pl.ds(pl.multiple_of(c * size, size), size))

    def give(w, c):
        if w == 2:
            pair = wout_give, wout_take
        else:
            at = cols(c, (up_cut, down_cut)[w])
            pair = (up_give, down_give)[w].at[at], (up_take, down_take)[w].at[at]
        return remote(*pair, give_send.at[w, c], give_recv.at[w, c], seq=near)

    def give_away(c, carry):
        up_give[cols(c, up_cut)] = up_part(1 - side, c).astype(bf16)
        give(0, c).start()
        down_give[cols(c, down_cut)] = down_part(1 - side, c).astype(bf16)
        give(1, c).start()
        return carry

    def add_own(c, carry):
        at = cols(c, up_cut)
        total = up_part(side, c)
        give(0, c).wait()
        up_give[at] = (total + up_take[at].astype(f32)).astype(bf16)
        at = cols(c, down_cut)
        total = down_part(side, c)
        give(1, c).wait()
        down_give[at] = (total + down_take[at].astype(f32)).astype(bf16)
        return carry

    lax.fori_loop(0, pieces, give_away, 0)
    for j in range(4):
        wout_give[own * j : own * (j + 1), :] = wout_part(1 - side, j).astype(bf16)
    give(2, 0).start()
    lax.fori_loop(0, pieces, add_own, 0)
    sums = [
        pltpu.make_async_copy(up_give, up_sum, sum_sem.at[0]),
        pltpu.make_async_copy(down_give, down_sum, sum_sem.at[1]),
    ]
    for copy in sums:
        copy.start()
    gather[2]()
    totals = [wout_part(side, j) for j in range(4)]
    give(2, 0).wait()
    for j in range(4):
        at = slice(own * j, own * (j + 1))
        wout_give[at, :] = (totals[j] + wout_take[at, :].astype(f32)).astype(bf16)
    sums.append(pltpu.make_async_copy(wout_give, wout_sum, sum_sem.at[2]))
    sums[-1].start()
    for relation in range(1, 4):
        for i in range(steps):
            send(relation, i).wait()
    for i in range(steps):
        for copy in keep(i):
            copy.wait()
    gather[3]()
    for copy in [mine] + kept_out + sums:
        copy.wait()


def feed(nf, length, states, cot, ctx, wout, up, down, vec_all, shards, block=256, part=768):
    tokens, width = states.shape
    hidden = up.shape[1]
    wide = ctx.shape[2]
    pieces = 3
    shape = jax.ShapeDtypeStruct
    halves = ((width, hidden // 2), (width // 2, hidden), (width, width // 2))
    vmem = lambda *size: pltpu.VMEM(size, bf16)
    steps = tokens // block
    staged = DMA((nf // 2 - 1, 3))
    staged_aside = DMA((nf // 2, 3))
    return pl.pallas_call(
        functools.partial(feed_kernel, nf, block, part),
        out_shape=[
            shape((tokens, width), bf16),
            shape((tokens, width), f32),
            shape((4, tokens, wide), bf16),
        ]
        + [shape(x, bf16) for x in halves]
        + [shape((16, width), f32)]
        + [shape((nf,) + w.shape, bf16) for w in shards],
        in_specs=[IN_SMEM] + [IN_VMEM] * 4 + [ANY] * 6,
        out_specs=[ANY] * 6 + [IN_VMEM] + [ANY] * 3,
        scratch_shapes=[
            vmem(width, hidden),
            vmem(hidden, width),
            vmem(tokens, width),
            vmem(3, *shards[0].shape),
            pltpu.VMEM((8, width), f32),
            pltpu.VMEM((1, hidden), f32),
            vmem(tokens, width),
            pltpu.VMEM((tokens, width), f32),
            vmem(tokens, hidden),
            vmem(tokens, hidden),
            pltpu.VMEM((block, hidden), f32),
            vmem(width, tokens),
            vmem(width, tokens),
            vmem(tokens, width),
            vmem(4, tokens, wide),
        ]
        + [vmem(*x) for x in halves] * 2
        + [
            DMA((3,)),
            DMA((2, steps)),
            DMA((3, steps)),
            DMA((3, steps)),
            DMA(()),
            DMA((3, pieces)),
            DMA((3, pieces)),
            DMA((3,)),
            DMA((2, 3)),
            staged, staged, staged_aside, staged_aside,
            DMA((nf - 1, 3)), DMA((nf - 1, 3)),
        ],
        compiler_params=params(3),
        name="feed",
    )(length, states, ctx, wout, vec_all, up, down, cot, *shards)


def back_kernel(
    nf, key_block, groups, q_ref, k_ref, v_ref, o_ref, gctx_ref,
    up_sum, down_sum, wout_sum, x_hbm, wq_hbm, wk_hbm, wv_hbm, first_hbm, gvec_hbm,
    states_grad, up_out, down_out, wout_out, qkv_out, vec_out, upb_out,
    k_acc, v_acc, q_acc, g_buf, q_turned, g_turned, d_out, g_all, x_all, w_all, first_grad,
    own_up, own_dn, own_wo, ring_up, ring_dn, ring_wo, y_up, y_dn, y_wo, z_up, z_dn, z_wo,
    w_buf, w_came, w_sum, w_parts, v_own, v_cut, v_came, v_sum, v_parts,
    load_sem, late_sem, hop_send, hop_recv, y_send, y_recv, z_send, z_recv,
    d_send, d_recv, d_own, w_send, w_recv, p_send, p_recv, l_send, l_recv, m_send, m_recv,
):
    half, h = pl.program_id(0), pl.program_id(1)
    count = w_buf.shape[0]
    f = lax.axis_index("fsdp")
    s, near, far, cross = seq_peers()
    peers = (s, near, far, cross)
    side = s % 2
    way = 1 - 2 * side
    place = place_of(f, nf)
    ahead = index_at((place + way + nf) % nf, nf)
    slots = k_ref.shape[1]
    tokens = slots // 4
    block = tokens
    width = x_all.shape[2]
    rows = width // nf
    width_own = count * 64
    full = (up_sum, down_sum, wout_sum)
    own = (own_up, own_dn, own_wo)
    came = (ring_up, ring_dn, ring_wo)
    y_buf = (y_up, y_dn, y_wo)
    z_buf = (z_up, z_dn, z_wo)
    outs = (up_out, down_out, wout_out)
    by_cols = (False, True, False)

    def chunk_at(w, chunk):
        size = came[w].shape[1 + by_cols[w]]
        cut = pl.ds(pl.multiple_of(chunk * size, size), size)
        return (slice(None), cut) if by_cols[w] else (cut, slice(None))

    def hop(w, t, source):
        return remote(source, came[w].at[t], hop_send.at[w, t], hop_recv.at[w, t], fsdp=ahead)

    def chunk_of(t):
        return index_at((place + 2 * nf - way * (1 + t)) % nf, nf)

    def to_far(w):
        return remote(came[w].at[nf - 2], y_buf[w], y_send.at[w], y_recv.at[w], seq=far)

    def to_near(w):
        return remote(y_buf[w], z_buf[w], z_send.at[w], z_recv.at[w], seq=near)

    def loads():
        return [pltpu.make_async_copy(full[w], own[w], load_sem.at[w]) for w in range(3)]

    def late():
        return [
            pltpu.make_async_copy(x_hbm, x_all, late_sem.at[0]),
            pltpu.make_async_copy(wq_hbm, w_all.at[0], late_sem.at[1]),
            pltpu.make_async_copy(wk_hbm, w_all.at[1], late_sem.at[2]),
            pltpu.make_async_copy(wv_hbm, w_all.at[2], late_sem.at[3]),
            pltpu.make_async_copy(first_hbm, first_grad, late_sem.at[4]),
            pltpu.make_async_copy(gvec_hbm, v_own, late_sem.at[5]),
        ]

    friends = [{"fsdp": (f + d) % nf} for d in range(1, nf)] + [{"seq": p} for p in peers[1:]]

    @pl.when((half == 0) & (h == 0))
    def _():
        hail(friends)
        for copy in loads() + late():
            copy.start()

    k_acc[...] = jnp.zeros_like(k_acc)
    v_acc[...] = jnp.zeros_like(v_acc)
    at_head = pl.ds(pl.multiple_of(h * 64, 64), 64)

    def part(relation, m, head):
        to = peers[relation]
        source = d_out.at[
            m, pl.ds(pl.multiple_of(head * 64, 64), 64), pl.ds(pl.multiple_of(to * tokens, tokens), tokens)
        ]
        target = g_all.at[m, pl.ds(pl.multiple_of(s * width_own + head * 64, 64), 64), :]
        return source, target

    def d_copy(relation, m, head):
        source, target = part(relation, m, head)
        return remote(
            source, target, d_send.at[relation - 1, m, head], d_recv.at[relation - 1, m, head],
            seq=peers[relation],
        )

    def d_local(m, head):
        source, target = part(0, m, head)
        return pltpu.make_async_copy(source, target, d_own.at[m, head])

    def w_copy(head, d):
        to = (f + d) % nf
        return remote(
            w_buf.at[head, to], w_came.at[head, d - 1], w_send.at[head, d - 1],
            w_recv.at[head, d - 1], fsdp=to,
        )

    def p_copy(head, relation):
        return remote(
            w_sum.at[head], w_parts.at[s, head], p_send.at[head, relation - 1],
            p_recv.at[head, relation - 1], seq=peers[relation],
        )

    def v_copy(d):
        to = (f + d) % nf
        return remote(v_cut.at[to], v_came.at[d], l_send.at[d - 1], l_recv.at[d - 1], fsdp=to)

    def m_copy(relation):
        return remote(
            v_sum, v_parts.at[s], m_send.at[relation - 1], m_recv.at[relation - 1],
            seq=peers[relation],
        )

    def settle_head(head):
        for d in range(1, nf):
            w_copy(head, d).wait()
        total = w_buf[head, f].astype(f32)
        for d in range(1, nf):
            total = total + w_came[head, d - 1].astype(f32)
        w_sum[head] = total.astype(bf16)
        for relation in (3, 2, 1):
            p_copy(head, relation).start()
        w_parts[s, head] = total.astype(bf16)

    base = (s // 2 + 1 + half) % 2 * (2 * tokens)

    def round_(turn, carry):
        step = (half * count + h) * 4 + turn
        relation = (1 - turn // 2) * (turn + 2) + turn // 2 * (3 - turn)
        owner = ((s // 2 + relation // 2) % 2) * 2 + (s % 2 + relation % 2) % 2
        at = pl.ds(pl.multiple_of(owner * tokens, tokens), tokens)

        @pl.when(half == 0)
        def _():
            lane = lax.broadcasted_iota(jnp.int32, (block, LANE), 1)
            first = gctx_ref[at, :LANE].astype(f32)
            second = gctx_ref[at, LANE:].astype(f32)
            grad = jnp.where(h == 0, first, jnp.where(h == 1, pltpu.roll(first, 64, 1), second))
            grad = jnp.where(lane < 64, grad, 0.0)
            delta = jnp.sum(grad * o_ref[0, at, :].astype(f32), axis=1, keepdims=True)
            high, middle, low = thirds(-delta)
            grad = with_lanes(grad, ((64, high), (65, middle), (66, low))).astype(bf16)
            g_buf[h, at, :] = grad
            g_turned[h, :, at] = jnp.transpose(grad)[:64, :]
            q_turned[h, :, at] = jnp.transpose(q_ref[0, at, :])[:64, :]

        q, grad = q_ref[0, at, :], g_buf[h, at, :]
        q_side, g_side = q_turned[h, :, at], g_turned[h, :, at]
        q_total = None
        for c in range(2 * tokens // key_block):
            ks = slice(c * key_block, (c + 1) * key_block)
            keys = pl.ds(pl.multiple_of(base + c * key_block, LANE), key_block)
            k = k_ref[0, keys, :]
            probs = jnp.exp2(dims(q, k, NT))
            score = (probs * dims(grad, v_ref[0, keys, :], NT)).astype(bf16)
            v_acc[:, ks] += dims(g_side, probs.astype(bf16), NN)
            k_acc[:, ks] += dims(q_side, score, NN)
            term = dims(score, k, NN)
            q_total = term if q_total is None else q_total + term
        q_total = jnp.transpose(q_total)[:64, :]

        @pl.when(half == 0)
        def _():
            q_acc[h, :, at] = q_total

        @pl.when(half == 1)
        def _():
            d_out[0, at_head, at] = ((q_acc[h, :, at] + q_total) * 0.125).astype(bf16)

        @pl.when(step == 0)
        def _():
            hailed(friends)
            for w in range(3):
                hop(w, 0, full[w].at[chunk_at(w, chunk_of(0))]).start()

        @pl.when(step == 1)
        def _():
            for copy in loads():
                copy.wait()

        for g in range(2):
            t = (2 * (step - g) + 1) // 5
            due = 5 * t // 2 == step - g

            @pl.when(due & (t > 0) & (t < nf - 1))
            def _():
                for w in groups[g]:
                    hop(w, t - 1, came[w].at[t - 1]).wait_recv()
                    here = own[w][chunk_at(w, chunk_of(t))].astype(f32)
                    came[w][t - 1] = (here + came[w][t - 1].astype(f32)).astype(bf16)
                    hop(w, t, came[w].at[t - 1]).start()

            @pl.when(due & (t == nf - 1))
            def _():
                for w in groups[g]:
                    hop(w, nf - 2, came[w].at[nf - 2]).wait_recv()
                    here = own[w][chunk_at(w, f)].astype(f32)
                    came[w][nf - 2] = (here + came[w][nf - 2].astype(f32)).astype(bf16)
                    to_far(w).start()

        for stage, kind in enumerate((2, 3, 1)):
            @pl.when((half == 1) & (turn == stage))
            def _():
                d_copy(kind, 0, h).start()

        @pl.when((half == 1) & (h > 0) & (turn == 1))
        def _():
            settle_head(h - 1)

        return carry

    lax.fori_loop(0, 4, round_, 0)
    keys = pl.ds(pl.multiple_of(base, 2 * tokens), 2 * tokens)
    d_out[1, at_head, keys] = (k_acc[...] * LN2).astype(bf16)
    d_out[2, at_head, keys] = v_acc[...].astype(bf16)

    @pl.when(half == 0)
    def _():
        for m in (1, 2):
            for kind in (2, 3):
                d_copy(kind, m, h).start()

    @pl.when(half == 1)
    def _():
        for m in range(3):
            if m:
                d_copy(1, m, h).start()
            d_local(m, h).start()

        @pl.when(h == 0)
        def _():
            for copy in late():
                copy.wait()

        left = jnp.concatenate([d_out[m, at_head, :] for m in range(3)], axis=0)
        total = None
        for j in range(4):
            term = dims(left[:, j * tokens : (j + 1) * tokens], x_all[j], NN)
            total = term if total is None else total + term
        total = jnp.transpose(total).astype(bf16)
        for j in range(nf):
            w_buf[h, j] = jnp.concatenate(
                [total[rows * j + rows // 2 * e : rows * j + rows // 2 * (e + 1)] for e in range(2)],
                axis=1,
            )
        for d in range(1, nf):
            w_copy(h, d).start()

    @pl.when((half == 1) & (h == count - 1))
    def _():
        ones = jnp.ones((8, slots), bf16)
        for row, m in ((0, 0), (1, 2)):
            line = dims(ones, d_out[m], NT)
            line = jnp.concatenate([line, jnp.zeros((8, width - width_own), f32)], axis=1)
            v_own[row : row + 1, :] = pltpu.roll(line, s * width_own, 1)[0:1, :]
        lines = v_own[...]
        flat = jnp.concatenate([lines[8 + r : 9 + r, :] for r in range(4)], axis=1)
        for j in range(nf):
            piece = lines if j == 0 else pltpu.roll(lines, width - rows * j, 1)
            v_cut[j, 0:8, :] = piece[0:8, :LANE]
            for r in range(4):
                start = rows * (4 * j + r)
                shift = start % LANE
                tile = start - shift
                both = jnp.concatenate(
                    [flat[:, tile : tile + LANE], flat[:, min(tile + LANE, flat.shape[1] - LANE) :][:, :LANE]],
                    axis=1,
                )
                if shift:
                    both = pltpu.roll(both, 2 * LANE - shift, 1)
                v_cut[j, 8 + r : 9 + r, :] = both[:, :LANE]
            v_cut[j, 12:16, :] = jnp.zeros((4, LANE), f32)
        for d in range(1, nf):
            v_copy(d).start()
        for w in range(3):
            to_far(w).wait()
            y_buf[w][...] = (
                came[w][nf - 2].astype(f32) + y_buf[w][...].astype(f32)
            ).astype(bf16)
            to_near(w).start()

        def settle(head, carry):
            for m in range(3):
                for kind in range(1, 4):
                    d_copy(kind, m, head).wait()
                d_local(m, head).wait()
            return carry

        lax.fori_loop(0, count, settle, 0)
        cut_size = 256
        mats = [w_all[m].reshape(width, width) for m in range(3)]
        for c in range(width // cut_size):
            cut = slice(c * cut_size, (c + 1) * cut_size)
            total = None
            for m in range(3):
                term = dims(mats[m][cut, :], g_all[m], NN)
                total = term if total is None else total + term
            states_grad[:, cut] = (first_grad[:, cut] + jnp.transpose(total)).astype(bf16)
        for d in range(1, nf):
            v_copy(d).wait()
        v_came[0] = v_cut[f]
        total = None
        for j in range(nf):
            term = v_came[(f + nf - j) % nf]
            total = term if total is None else total + term
        v_sum[...] = total
        for kind in (3, 2, 1):
            m_copy(kind).start()
        v_parts[s] = total
        settle_head(count - 1)
        for w in range(3):
            for t in range(nf - 1):
                hop(w, t, came[w].at[t]).wait_send()
            to_near(w).wait()
            mine, theirs = y_buf[w][...], z_buf[w][...]
            out = outs[w]
            size = out.shape[1] // 2
            if by_cols[w]:
                mine, theirs = jnp.transpose(mine), jnp.transpose(theirs)
            out[:, pl.ds(pl.multiple_of(side * size, size), size)] = mine
            out[:, pl.ds(pl.multiple_of((1 - side) * size, size), size)] = theirs
        for relation in range(1, 4):
            m_copy(relation).wait()
        total = v_parts[0] + v_parts[1] + v_parts[2] + v_parts[3]
        vec_out[...] = total
        lane = lax.broadcasted_iota(jnp.int32, (1, 4 * rows), 1)
        line = jnp.zeros((1, 4 * rows), f32)
        for r in range(4):
            piece = jnp.concatenate(
                [total[8 + r : 9 + r, :], jnp.zeros((1, 4 * rows - LANE), f32)], axis=1
            )
            if r:
                piece = pltpu.roll(piece, rows * r, 1)
            line = jnp.where((lane >= rows * r) & (lane < rows * (r + 1)), piece, line)
        upb_out[...] = jnp.broadcast_to(line, upb_out.shape)
        for head in range(count):
            for relation in range(1, 4):
                p_copy(head, relation).wait()
        parts = [
            [
                jnp.concatenate([both[:, : 3 * 64], both[:, 3 * 64 :]], axis=0)
                for both in [w_parts[j, head].astype(f32) for head in range(count)]
            ]
            for j in range(4)
        ]
        for m in range(3):
            qkv_out[m] = jnp.concatenate(
                [part[:, m * 64 : (m + 1) * 64] for group in parts for part in group], axis=1
            ).astype(bf16)


def back(nf, qb, k, v, o, gctx, sums, x_all, mats, first_grad, gvec, key_block):
    heads, slots, _ = qb.shape
    tokens = slots // 4
    width = x_all.shape[2]
    hidden = sums[0].shape[1] * 2
    rows, cols = width // nf, hidden // nf
    shape = jax.ShapeDtypeStruct
    per_head = pl.BlockSpec((1, slots, LANE), lambda p, h: (h, 0, 0))
    chunk = ((rows, hidden // 2), (width // 2, cols), (rows, width // 2))
    vmem = lambda *size: pltpu.VMEM(size, bf16)
    triple = DMA((3,))
    hops = DMA((3, nf - 1))
    own = heads * 64
    packed = (rows // 2, 6 * 64)
    results = [
        shape((tokens, width), bf16),
        shape((rows, hidden), bf16),
        shape((cols, width), bf16),
        shape((rows, width), bf16),
        shape((3, rows, width), bf16),
        shape((16, LANE), f32),
        shape((8, cols), f32),
    ]
    return pl.pallas_call(
        functools.partial(back_kernel, nf, key_block, ((0,), (1, 2))),
        grid=(2, heads),
        out_shape=results,
        in_specs=[per_head] * 4 + [IN_VMEM] + [ANY] * 9,
        out_specs=[
            pl.BlockSpec(x.shape, functools.partial(lambda n, *_: (0,) * n, len(x.shape)))
            for x in results
        ],
        scratch_shapes=[
            pltpu.VMEM((64, slots // 2), f32),
            pltpu.VMEM((64, slots // 2), f32),
            pltpu.VMEM((heads, 64, slots), f32),
            vmem(heads, slots, LANE),
            vmem(heads, 64, slots),
            vmem(heads, 64, slots),
            vmem(3, own, slots),
            vmem(3, width, tokens),
            vmem(4, tokens, width),
            vmem(3, nf, rows, width),
            pltpu.VMEM((tokens, width), f32),
        ]
        + [vmem(*x.shape) for x in sums]
        + [vmem(nf - 1, *x) for x in chunk]
        + [vmem(*x) for x in chunk] * 2
        + [
            vmem(heads, nf, *packed),
            vmem(heads, nf - 1, *packed),
            vmem(heads, *packed),
            vmem(4, heads, *packed),
            pltpu.VMEM((16, width), f32),
            pltpu.VMEM((nf, 16, LANE), f32),
            pltpu.VMEM((nf, 16, LANE), f32),
            pltpu.VMEM((16, LANE), f32),
            pltpu.VMEM((4, 16, LANE), f32),
            triple, DMA((6,)), hops, hops, triple, triple, triple, triple,
            DMA((3, 3, heads)), DMA((3, 3, heads)), DMA((3, heads)),
            DMA((heads, nf - 1)), DMA((heads, nf - 1)), DMA((heads, 3)), DMA((heads, 3)),
            DMA((nf - 1,)), DMA((nf - 1,)), triple, triple,
        ],
        compiler_params=params(4),
        name="back",
    )(qb, k, v, o, gctx, *sums, x_all, *mats, first_grad, gvec)


def results_kernel(rows, output, states_grad, up, down, wout, qkv, vec, upb, *outs):
    outs[0][...] = output[...]
    outs[1][...] = states_grad[...]
    for m in range(3):
        outs[2 + m][...] = qkv[m].astype(f32)
    outs[5][...] = wout[...].astype(f32)
    outs[6][...] = up[...].astype(f32)
    outs[7][...] = down[...].astype(f32)
    for r in range(8):
        outs[8 + r][...] = vec[r, :rows]
    outs[16][...] = upb[0, :]


def results(rows, output, states_grad, up, down, wout, qkv, vec, upb):
    shape = jax.ShapeDtypeStruct
    pieces = 3
    grads = [shape(qkv.shape[1:], f32)] * 3 + [shape(x.shape, f32) for x in (wout, up, down)]
    outs = [shape(output.shape, bf16)] * 2 + grads
    lines = [shape((rows,), f32)] * 8 + [shape((upb.shape[1],), f32)]

    def cut(x):
        n = len(x.shape)
        size = x.shape[: n - 2] + (x.shape[n - 2] // pieces, x.shape[n - 1])
        return pl.BlockSpec(size, functools.partial(lambda n, i: (0,) * (n - 2) + (i, 0), n))

    def same(x):
        return pl.BlockSpec(x.shape, lambda i: (0,) * len(x.shape))

    return pl.pallas_call(
        functools.partial(results_kernel, rows),
        grid=(pieces,),
        out_shape=outs + lines,
        in_specs=[cut(x) for x in (output, states_grad, up, down, wout, qkv)] + [same(vec), same(upb)],
        out_specs=[cut(x) for x in outs] + [same(x) for x in lines],
        compiler_params=params(),
        name="results",
    )(output, states_grad, up, down, wout, qkv, vec, upb)


def fused_device(
    nf, states, query_weight, key_weight, value_weight, out_weight, query_bias, value_bias,
    out_bias, first_gain, first_shift, up_weight, up_bias, down_weight, down_bias, second_gain,
    second_shift, lengths, cotangent,
):
    tokens, width = states.shape
    rows = width // nf
    hidden = up_weight.shape[1]
    heads = width // 4 // 64
    qb, o, k, v, x_all, vec_all, ctx, wout, up, down = front(
        nf, heads, lengths, states, query_weight, key_weight, value_weight, out_weight, up_weight,
        down_weight,
        (
            query_bias, value_bias, out_bias, first_gain, first_shift, down_bias, second_gain,
            second_shift, up_bias,
        ),
        block=256, key_chunk=512,
    )
    output, first_grad, gctx, up_sum, down_sum, wout_sum, gvec, wq, wk, wv = feed(
        nf, lengths, states, cotangent, ctx, wout.reshape(width, width),
        up.reshape(width, hidden), down.reshape(hidden, width), vec_all,
        (query_weight, key_weight, value_weight),
    )
    states_grad, up_grad, down_grad, out_grad, qkv, vec_grad, upb_grad = back(
        nf, qb, k, v, o, gctx.reshape(4 * tokens, -1), (up_sum, down_sum, wout_sum), x_all,
        (wq, wk, wv), first_grad, gvec, key_block=384,
    )
    done = results(rows, output, states_grad, up_grad, down_grad, out_grad, qkv, vec_grad, upb_grad)
    output, states_grad, q_grad, k_grad, v_grad, out_grad, up_grad, down_grad = done[:8]
    lines = done[8:]
    return (
        output, states_grad, q_grad, k_grad, v_grad, out_grad, *lines[:5], up_grad, lines[8],
        down_grad, *lines[5:8],
    )


def solution(mesh):
    nf, ns = mesh.shape["fsdp"], mesh.shape["seq"]

    def choose(states, query_weight, *rest):
        rows, width = query_weight.shape
        fits = ns == 4 and nf in (4, 6, 8) and rows % 16 == 0 and width == 768 and states.shape[0] % 768 == 0
        device = functools.partial(fused_device, nf) if fits else per_device
        return device(states, query_weight, *rest)

    return jax.shard_map(
        choose,
        mesh=mesh,
        in_specs=(
            P(("fsdp", "seq"), None),
            P("fsdp", None),
            P("fsdp", None),
            P("fsdp", None),
            P("fsdp", None),
            P("fsdp"),
            P("fsdp"),
            P("fsdp"),
            P("fsdp"),
            P("fsdp"),
            P("fsdp", None),
            P("fsdp"),
            P("fsdp", None),
            P("fsdp"),
            P("fsdp"),
            P("fsdp"),
            P("fsdp"),
            P(("fsdp", "seq"), None),
        ),
        out_specs=(
            P(("fsdp", "seq"), None),
            P(("fsdp", "seq"), None),
            P("fsdp", None),
            P("fsdp", None),
            P("fsdp", None),
            P("fsdp", None),
            P("fsdp"),
            P("fsdp"),
            P("fsdp"),
            P("fsdp"),
            P("fsdp"),
            P("fsdp", None),
            P("fsdp"),
            P("fsdp", None),
            P("fsdp"),
            P("fsdp"),
            P("fsdp"),
        ),
        check_vma=False,
    )
```

```python
import functools
import math

import jax
import jax.numpy as jnp
from jax import lax
from jax.experimental import pallas as pl
from jax.experimental.pallas import tpu as pltpu
from jax.sharding import PartitionSpec as P

HEAD_DIM = 64


eps = 1e-12


def product(left, right):
    return jnp.dot(left, right, preferred_element_type=jnp.float32)


def left_product(left, right):
    return lax.dot_general(
        left, right, (((0,), (0,)), ((), ())), preferred_element_type=jnp.float32
    )


def right_product(left, right):
    return lax.dot_general(
        left, right, (((1,), (1,)), ((), ())), preferred_element_type=jnp.float32
    )


def layer_norm(values, gain, shift):
    average = jnp.mean(values, axis=-1, keepdims=True)
    centred = values - average
    spread = jnp.mean(centred * centred, axis=-1, keepdims=True)
    return centred * lax.rsqrt(spread + eps) * gain + shift


def gelu_exact(values):
    return jax.nn.gelu(values, approximate=False)


def column_sums(values):
    return jnp.sum(values.astype(jnp.float32), axis=0)


def per_device(
    states,
    query_weight,
    key_weight,
    value_weight,
    out_weight,
    query_bias,
    value_bias,
    out_bias,
    first_gain,
    first_shift,
    up_weight,
    up_bias,
    down_weight,
    down_bias,
    second_gain,
    second_shift,
    lengths,
    cotangent,
):
    f32 = jnp.float32
    bf16 = jnp.bfloat16
    (
        query_mat,
        key_mat,
        value_mat,
        out_mat,
        query_add,
        value_add,
        out_add,
        gain_first,
        shift_first,
    ) = (
        lax.all_gather(query_weight, "fsdp", axis=0, tiled=True),
        lax.all_gather(key_weight, "fsdp", axis=0, tiled=True),
        lax.all_gather(value_weight, "fsdp", axis=0, tiled=True),
        lax.all_gather(out_weight, "fsdp", axis=0, tiled=True),
        lax.all_gather(query_bias, "fsdp", axis=0, tiled=True),
        lax.all_gather(value_bias, "fsdp", axis=0, tiled=True),
        lax.all_gather(out_bias, "fsdp", axis=0, tiled=True),
        lax.all_gather(first_gain, "fsdp", axis=0, tiled=True),
        lax.all_gather(first_shift, "fsdp", axis=0, tiled=True),
    )
    up_mat, up_add, down_mat, down_add, gain_second, shift_second = (
        lax.all_gather(up_weight, "fsdp", axis=0, tiled=True),
        lax.all_gather(up_bias, "fsdp", axis=0, tiled=True),
        lax.all_gather(down_weight, "fsdp", axis=0, tiled=True),
        lax.all_gather(down_bias, "fsdp", axis=0, tiled=True),
        lax.all_gather(second_gain, "fsdp", axis=0, tiled=True),
        lax.all_gather(second_shift, "fsdp", axis=0, tiled=True),
    )
    tokens = states.shape[0]
    slot_rows = tokens * lax.axis_size("seq")
    length = lengths[0]
    places = lax.axis_index("seq") * tokens + lax.iota(jnp.int32, tokens)
    valid_rows = (places < length).astype(f32)[:, None]
    queries = (product(states, query_mat) + query_add).astype(bf16)
    keys_in = product(states, key_mat).astype(bf16)
    values = (product(states, value_mat) + value_add).astype(bf16)
    head_queries, head_keys, head_values = (
        lax.all_to_all(queries, "seq", split_axis=1, concat_axis=0, tiled=True),
        lax.all_to_all(keys_in, "seq", split_axis=1, concat_axis=0, tiled=True),
        lax.all_to_all(values, "seq", split_axis=1, concat_axis=0, tiled=True),
    )
    local_width = head_queries.shape[1]
    head_count = local_width // HEAD_DIM
    block_rows = min(512, slot_rows)
    blocks = slot_rows // block_rows
    scaling = HEAD_DIM ** (-0.5)
    key_valid = lax.iota(jnp.int32, slot_rows) < length
    keys_heads = head_keys.reshape(slot_rows, head_count, HEAD_DIM)
    values_heads = head_values.reshape(slot_rows, head_count, HEAD_DIM)
    query_blocks = head_queries.reshape(blocks, block_rows, head_count, HEAD_DIM)

    def block_scores(query_block):
        scores = (
            jnp.einsum("qhd,khd->hqk", query_block, keys_heads, preferred_element_type=f32)
            * scaling
        )
        return jnp.where(key_valid[None, None, :], scores, -1000000000.0)

    def forward_block(query_block):
        scores = block_scores(query_block)
        highest = jnp.max(scores, axis=-1, keepdims=True)
        exponent = jnp.exp(scores - highest)
        totals = jnp.sum(exponent, axis=-1, keepdims=True)
        weights_soft = (exponent / totals).astype(bf16)
        context_part = jnp.einsum(
            "hqk,khd->qhd", weights_soft, values_heads, preferred_element_type=f32
        )
        return (context_part.astype(bf16), (highest + jnp.log(totals))[:, :, 0])

    context_blocks, log_totals = lax.map(forward_block, query_blocks)
    context = lax.all_to_all(
        context_blocks.reshape(slot_rows, local_width),
        "seq",
        split_axis=0,
        concat_axis=1,
        tiled=True,
    )
    hidden = states.astype(f32)
    first_sum = hidden + (product(context, out_mat) + out_add)
    first_norm, first_back = jax.vjp(
        layer_norm, first_sum, gain_first.astype(f32), shift_first.astype(f32)
    )
    first_low = first_norm.astype(bf16)
    pre_act = product(first_low, up_mat) + up_add
    activated = gelu_exact(pre_act).astype(bf16)
    second_sum = first_norm + (product(activated, down_mat) + down_add)
    normed, second_back = jax.vjp(
        layer_norm, second_sum, gain_second.astype(f32), shift_second.astype(f32)
    )
    output = (normed * valid_rows).astype(bf16)
    out_grad = cotangent.astype(f32) * valid_rows
    second_grad, gain_second_grad, shift_second_grad = second_back(out_grad)
    down_in = second_grad.astype(bf16)
    down_weight_grad = left_product(activated, down_in)
    down_bias_grad = column_sums(down_in)
    act_grad = right_product(down_in, down_mat)
    pre_grad = jax.vjp(gelu_exact, pre_act)[1](act_grad)[0].astype(bf16)
    up_weight_grad = left_product(first_low, pre_grad)
    up_bias_grad = column_sums(pre_grad)
    norm_grad = second_grad + right_product(pre_grad, up_mat)
    first_grad, gain_first_grad, shift_first_grad = first_back(norm_grad)
    branch_grad = first_grad.astype(bf16)
    out_weight_grad = left_product(context, branch_grad)
    out_bias_grad = column_sums(branch_grad)
    context_grad = right_product(branch_grad, out_mat).astype(bf16)
    head_grad = lax.all_to_all(context_grad, "seq", split_axis=1, concat_axis=0, tiled=True)
    grad_blocks = head_grad.reshape(blocks, block_rows, head_count, HEAD_DIM)

    def backward_step(carry, packed):
        key_acc, value_acc = carry
        query_block, grad_block, log_block = packed
        scores = block_scores(query_block)
        probs_full = jnp.exp(scores - log_block[:, :, None])
        probs_low = probs_full.astype(bf16)
        prob_grad = jnp.einsum("qhd,khd->hqk", grad_block, values_heads, preferred_element_type=f32)
        centre = jnp.sum(prob_grad * probs_full, axis=-1, keepdims=True)
        score_grad = (probs_full * (prob_grad - centre)).astype(bf16)
        query_part = (
            jnp.einsum("hqk,khd->qhd", score_grad, keys_heads, preferred_element_type=f32) * scaling
        )
        key_acc = (
            key_acc
            + jnp.einsum("hqk,qhd->khd", score_grad, query_block, preferred_element_type=f32)
            * scaling
        )
        value_acc = value_acc + jnp.einsum(
            "hqk,qhd->khd", probs_low, grad_block, preferred_element_type=f32
        )
        return ((key_acc, value_acc), query_part.astype(bf16))

    zeros_heads = jnp.zeros((slot_rows, head_count, HEAD_DIM), f32)
    (key_total, value_total), query_parts = lax.scan(
        backward_step, (zeros_heads, zeros_heads), (query_blocks, grad_blocks, log_totals)
    )
    query_back, key_back, value_back = (
        lax.all_to_all(
            query_parts.reshape(slot_rows, local_width),
            "seq",
            split_axis=0,
            concat_axis=1,
            tiled=True,
        ),
        lax.all_to_all(
            key_total.reshape(slot_rows, local_width).astype(bf16),
            "seq",
            split_axis=0,
            concat_axis=1,
            tiled=True,
        ),
        lax.all_to_all(
            value_total.reshape(slot_rows, local_width).astype(bf16),
            "seq",
            split_axis=0,
            concat_axis=1,
            tiled=True,
        ),
    )
    query_weight_grad = left_product(states, query_back)
    key_weight_grad = left_product(states, key_back)
    value_weight_grad = left_product(states, value_back)
    query_bias_grad = column_sums(query_back)
    value_bias_grad = column_sums(value_back)
    states_grad = (
        first_grad
        + right_product(query_back, query_mat)
        + right_product(key_back, key_mat)
        + right_product(value_back, value_mat)
    ).astype(bf16)
    attend_parts = (
        lax.psum_scatter(query_weight_grad, "fsdp", scatter_dimension=0, tiled=True),
        lax.psum_scatter(key_weight_grad, "fsdp", scatter_dimension=0, tiled=True),
        lax.psum_scatter(value_weight_grad, "fsdp", scatter_dimension=0, tiled=True),
        lax.psum_scatter(out_weight_grad, "fsdp", scatter_dimension=0, tiled=True),
        lax.psum_scatter(query_bias_grad, "fsdp", scatter_dimension=0, tiled=True),
        lax.psum_scatter(value_bias_grad, "fsdp", scatter_dimension=0, tiled=True),
        lax.psum_scatter(out_bias_grad, "fsdp", scatter_dimension=0, tiled=True),
        lax.psum_scatter(gain_first_grad, "fsdp", scatter_dimension=0, tiled=True),
        lax.psum_scatter(shift_first_grad, "fsdp", scatter_dimension=0, tiled=True),
    )
    feed_parts = (
        lax.psum_scatter(up_weight_grad, "fsdp", scatter_dimension=0, tiled=True),
        lax.psum_scatter(up_bias_grad, "fsdp", scatter_dimension=0, tiled=True),
        lax.psum_scatter(down_weight_grad, "fsdp", scatter_dimension=0, tiled=True),
        lax.psum_scatter(down_bias_grad, "fsdp", scatter_dimension=0, tiled=True),
        lax.psum_scatter(gain_second_grad, "fsdp", scatter_dimension=0, tiled=True),
        lax.psum_scatter(shift_second_grad, "fsdp", scatter_dimension=0, tiled=True),
    )
    summed = (
        lax.psum(attend_parts[0].astype(jnp.bfloat16), "seq").astype(jnp.float32),
        lax.psum(attend_parts[1].astype(jnp.bfloat16), "seq").astype(jnp.float32),
        lax.psum(attend_parts[2].astype(jnp.bfloat16), "seq").astype(jnp.float32),
        lax.psum(attend_parts[3].astype(jnp.bfloat16), "seq").astype(jnp.float32),
        lax.psum(attend_parts[4].astype(jnp.bfloat16), "seq").astype(jnp.float32),
        lax.psum(attend_parts[5].astype(jnp.bfloat16), "seq").astype(jnp.float32),
        lax.psum(attend_parts[6].astype(jnp.bfloat16), "seq").astype(jnp.float32),
        lax.psum(attend_parts[7].astype(jnp.bfloat16), "seq").astype(jnp.float32),
        lax.psum(attend_parts[8].astype(jnp.bfloat16), "seq").astype(jnp.float32),
        lax.psum(feed_parts[0].astype(jnp.bfloat16), "seq").astype(jnp.float32),
        lax.psum(feed_parts[1].astype(jnp.bfloat16), "seq").astype(jnp.float32),
        lax.psum(feed_parts[2].astype(jnp.bfloat16), "seq").astype(jnp.float32),
        lax.psum(feed_parts[3].astype(jnp.bfloat16), "seq").astype(jnp.float32),
        lax.psum(feed_parts[4].astype(jnp.bfloat16), "seq").astype(jnp.float32),
        lax.psum(feed_parts[5].astype(jnp.bfloat16), "seq").astype(jnp.float32),
    )
    return (
        output,
        states_grad,
        summed[0],
        summed[1],
        summed[2],
        summed[3],
        summed[4],
        summed[5],
        summed[6],
        summed[7],
        summed[8],
        summed[9],
        summed[10],
        summed[11],
        summed[12],
        summed[13],
        summed[14],
    )


LANE = 128
LOG2E = math.log2(math.e)
LN2 = math.log(2.0)
NT = (((1,), (1,)), ((), ()))
NN = (((1,), (0,)), ((), ()))
TN = (((0,), (0,)), ((), ()))
VMEM_BYTES = 66 * 1024 * 1024 - 2 * 1024 * 1024
f32 = jnp.float32
bf16 = jnp.bfloat16
ANY = pl.BlockSpec(memory_space=pl.ANY)
IN_VMEM = pl.BlockSpec(memory_space=pltpu.VMEM)
IN_SMEM = pl.BlockSpec(memory_space=pltpu.SMEM)
DMA = pltpu.SemaphoreType.DMA


def dims(left, right, numbers):
    return lax.dot_general(left, right, numbers, preferred_element_type=f32)


def remote(src, dst, send_sem, recv_sem, **where):
    return pltpu.make_async_remote_copy(
        src_ref=src,
        dst_ref=dst,
        send_sem=send_sem,
        recv_sem=recv_sem,
        device_id=where,
        device_id_type=pl.DeviceIdType.MESH,
    )


def hail(partners):
    barrier = pltpu.get_barrier_semaphore()
    for where in partners:
        pl.semaphore_signal(barrier, inc=1, device_id=where, device_id_type=pl.DeviceIdType.MESH)


def hailed(partners):
    pl.semaphore_wait(pltpu.get_barrier_semaphore(), len(partners))


def greet(partners):
    hail(partners)
    hailed(partners)


def seq_peers():
    me = lax.axis_index("seq")
    across = (me + 2) % 4
    return me, me + 1 - 2 * (me % 2), across, across + 1 - 2 * (across % 2)


def place_of(index, count):
    half = index // 2
    return half + (index % 2) * (count - 1 - 2 * half)


def index_at(place, count):
    upper = place // (count // 2)
    return (1 - upper) * 2 * place + upper * (2 * (count - 1 - place) + 1)


def thirds(values):
    high = values.astype(bf16)
    rest = values - high.astype(f32)
    middle = rest.astype(bf16)
    low = (rest - middle.astype(f32)).astype(bf16)
    return high.astype(f32), middle.astype(f32), low.astype(f32)


def with_lanes(base, columns):
    lane = lax.broadcasted_iota(jnp.int32, base.shape, 1)
    for place, values in columns:
        base = jnp.where(lane == place, values, base)
    return base


def params(collective_id=None):
    if collective_id is None:
        return pltpu.CompilerParams(vmem_limit_bytes=VMEM_BYTES)
    return pltpu.CompilerParams(
        vmem_limit_bytes=VMEM_BYTES, collective_id=collective_id, has_side_effects=True
    )


def ring_gather(nf, shards, halves, outs, ring_send, ring_recv, pair_send, pair_recv):
    f = lax.axis_index("fsdp")
    s, near, _, _ = seq_peers()
    side = s % 2
    step = 1 - 2 * side
    place = place_of(f, nf)
    ahead = index_at((place + step + nf) % nf, nf)

    def half(ref, w):
        axis, size = halves[w]
        cut = pl.ds(pl.multiple_of(side * size, size), size)
        return ref.at[cut, :] if axis == 0 else ref.at[:, cut]

    def slot(hop):
        return index_at((place + nf - step * (hop + 1)) % nf, nf)

    def ring(w, hop, owner, source):
        return remote(
            half(source, w),
            half(outs[w].at[owner], w),
            ring_send.at[w, hop],
            ring_recv.at[w, hop],
            fsdp=ahead,
        )

    def pair(w, hop):
        piece = half(outs[w].at[slot(hop)], w)
        return remote(piece, piece, pair_send.at[w, hop], pair_recv.at[w, hop], seq=near)

    def start(w):
        ring(w, 0, f, shards[w]).start()

    def hop(w, h):
        owner = slot(h)
        ring(w, h, owner, outs[w].at[owner]).wait_recv()

        @pl.when(h < nf - 2)
        def _():
            ring(w, h + 1, owner, outs[w].at[owner]).start()

        pair(w, h).start()

    def finish(w, h):
        ring(w, h, f, shards[w]).wait_send()
        pair(w, h).wait()

    return start, hop, finish


def front_kernel(
    nf, block, key_chunk, halves, groups,
    length_ref, states, wq, wk, wv, wout_s, up_s, down_s, *refs,
):
    small_params, refs = refs[:9], refs[9:]
    (
qb_out, o_out, k_out, v_out, x_out, vec_out, ctx_out, wout, up, down,
        q_buf, k_buf, v_buf, qb_buf, o_buf, s_buf, top_buf, ctx_buf, x_buf, w_buf, w_own, packed, vec_own, vec_buf,
        wout_buf, up_buf, down_buf, local_sem, x_sem, kv_sem, keep_sem, vec_send, vec_recv, z_send, z_recv, h_send, h_recv,
        near_send, near_recv, far_send, far_recv, pass_send, pass_recv,
        ring_send, ring_recv, pair_send, pair_recv, ctx_send, ctx_recv, own_sem, copy_sem,
    ) = refs
    f = lax.axis_index("fsdp")
    s, near, far, cross = seq_peers()
    tokens, width = states.shape
    heads, slots, _ = q_buf.shape
    rows = wq.shape[0]
    window = w_buf.shape[2]
    vec_rows = vec_buf.shape[1]
    own_width = heads * 64
    parts = far_send.shape[0]
    chunk = tokens // parts
    per = tokens // block
    beside = f + 1 - 2 * (f % 2)
    stages = nf // 2
    first_lane = pl.multiple_of((own_width * s // LANE) * LANE, LANE)
    weights = (wq, wk, wv)
    shards, outs = (wout_s, up_s, down_s), (wout, up, down)
    ring_start, ring_hop, ring_finish = ring_gather(
        nf, shards, halves, outs, ring_send, ring_recv, pair_send, pair_recv
    )
    friends = [{"fsdp": (f + d) % nf} for d in range(1, nf)] + [
        {"seq": near}, {"seq": far}, {"seq": cross},
    ]
    hail(friends)

    def along(d):
        to = (f + 2 * d) % nf
        return remote(packed.at[f], packed.at[f], z_send.at[d - 1], z_recv.at[d - 1], fsdp=to)

    def aside(d):
        owner = (f + nf - 2 * d) % nf
        return remote(packed.at[owner], packed.at[owner], h_send.at[d], h_recv.at[d], fsdp=beside)

    def vec_copy(d):
        return remote(
            vec_buf.at[f], vec_buf.at[f], vec_send.at[d - 1], vec_recv.at[d - 1],
            fsdp=(f + d) % nf,
        )

    def far_copy(c):
        at = pl.ds(c * chunk, chunk)
        return remote(states.at[at], x_buf.at[2, at], far_send.at[c], far_recv.at[c], seq=far)

    def pass_copy(c):
        at = pl.ds(c * chunk, chunk)
        return remote(
            x_buf.at[2, at], x_buf.at[3, at], pass_send.at[c], pass_recv.at[c], seq=near
        )

    near_copy = remote(states, x_buf.at[1], near_send, near_recv, seq=near)
    windows = [
        pltpu.make_async_copy(
            weights[m].at[:, pl.ds(first_lane, window)], w_own.at[m], local_sem.at[1 + m]
        )
        for m in range(3)
    ]
    local = [pltpu.make_async_copy(states, x_buf.at[0], local_sem.at[0])]
    for copy in windows + local:
        copy.start()
    vec_own[...] = jnp.zeros_like(vec_own)
    for r in range(8):
        vec_own[r : r + 1, :rows] = small_params[r][...].astype(f32).reshape(1, rows)
    line = small_params[8][...].astype(f32).reshape(1, 4 * rows)
    for r in range(4):
        vec_own[8 + r : 9 + r, :rows] = line[:, rows * r : rows * (r + 1)]
    vec_buf[f] = vec_own[...].astype(bf16)
    turn = (window - (own_width * s) % LANE) % window
    for m in range(3):
        windows[m].wait()
        columns = pltpu.roll(w_own[m].astype(f32), turn, 1)[:, :own_width]
        packed[f, m] = jnp.concatenate(
            [columns[: rows // 2], columns[rows // 2 :]], axis=1
        ).astype(bf16)
    hailed(friends)
    for d in range(1, stages):
        along(d).start()
    aside(0).start()
    for c in range(parts):
        far_copy(c).start()
    near_copy.start()
    for d in range(1, nf):
        vec_copy(d).start()
    for w in groups[0] + groups[1]:
        ring_start(w)
    held = (wout_buf, up_buf, down_buf)
    mine = [
        pltpu.make_async_copy(shards[w], held[w], copy_sem.at[0, w]) for w in range(len(shards))
    ]
    for copy in mine:
        copy.start()
    for copy in local:
        copy.wait()
    kept = []

    def keep(slot, index):
        copy = pltpu.make_async_copy(x_buf.at[slot], x_out.at[index], x_sem.at[slot])
        copy.start()
        kept.append(copy)

    def pass_on(c):
        far_copy(c).wait_recv()
        pass_copy(c).start()

    def turn_aside(d):
        along(d).wait_recv()
        aside(d).start()

    keep(0, s)
    for copy in mine:
        copy.wait()
    mine = [
        pltpu.make_async_copy(held[w], outs[w].at[f], copy_sem.at[1, w]) for w in range(len(shards))
    ]
    for copy in mine:
        copy.start()
    passed = 0
    for d in range(1, stages):
        turn_aside(d)
        if d != 2 and passed < parts - 2:
            pass_on(passed)
            passed += 1
    for d in range(1, nf):
        vec_copy(d).wait_recv()
    for d in range(stages):
        aside(d).wait_recv()
    gap = jnp.zeros((rows // 2, window - own_width), f32)
    for j in range(nf):
        for m in range(3):
            both = packed[j, m].astype(f32)
            for e in range(2):
                at = pl.ds(rows * j + rows // 2 * e, rows // 2)
                columns = both[:, own_width * e : own_width * (e + 1)]
                w_buf[m, at, :] = jnp.concatenate([columns, gap], axis=1).astype(bf16)
    share = own_width // rows
    wide = lax.broadcasted_iota(jnp.int32, (1, window), 1)
    biases = []
    for row in (0, 1):
        line = jnp.zeros((1, window), f32)
        for i in range(share):
            piece = vec_buf[share * s + i][row : row + 1, :].astype(f32)
            piece = jnp.concatenate([piece, jnp.zeros((1, window - LANE), f32)], axis=1)
            if i:
                piece = pltpu.roll(piece, i * rows, 1)
            line = jnp.where((wide >= i * rows) & (wide < (i + 1) * rows), piece, line)
        biases.append(line)
    length = length_ref[0]
    mats = [w_buf[m] for m in range(3)]
    small = lax.broadcasted_iota(jnp.int32, (chunk, LANE), 1)
    q_tail = jnp.where(small == 64, 1.0, 0.0)
    v_tail = jnp.where((small >= 64) & (small < 67), 1.0, 0.0)

    def heads_of(values, tail):
        found = []
        for h in range(heads):
            tile = values[:, (h // 2) * LANE : (h // 2 + 1) * LANE]
            if h % 2:
                tile = pltpu.roll(tile, 64, 1)
            found.append(jnp.where(small < 64, tile, tail).astype(bf16))
        return found

    def compute(slot, index, part):
        x = x_buf[slot, pl.ds(pl.multiple_of(part * chunk, chunk), chunk), :]
        start = pl.multiple_of(index * tokens + part * chunk, chunk)
        where = start + lax.broadcasted_iota(jnp.int32, (chunk, LANE), 0)
        queries = dims(x, mats[0], NN) + biases[0]
        keys = dims(x, mats[1], NN)
        k_tail = jnp.where(
            small == 64,
            jnp.where(where < length, 0.0, -1e9),
            jnp.where((small > 64) & (small < 68), 1.0, 0.0),
        )
        values = dims(x, mats[2], NN) + biases[1]
        at = pl.ds(start, chunk)
        for ref, found in (
            (q_buf, heads_of(queries * (LOG2E * 0.125), q_tail)),
            (k_buf, heads_of(keys, k_tail)),
            (v_buf, heads_of(values, v_tail)),
        ):
            for h in range(heads):
                ref[h, at, :] = found[h]

    def whole(slot, index, low, high):
        def body(part, carry):
            compute(slot, index, part)
            return carry

        lax.fori_loop(low, high, body, 0)

    def hops(g, h):
        for w in groups[g]:
            ring_hop(w, h)

    hops(0, 0)
    hops(1, 0)
    whole(0, s, 0, parts)
    for c in range(passed, parts - 1):
        pass_on(c)
    near_copy.wait_recv()
    keep(1, near)
    whole(1, near, 0, parts)
    hops(0, 1)
    whole(2, far, 0, parts - 1)
    pass_on(parts - 1)
    hops(1, 1)
    whole(2, far, parts - 1, parts)
    keep(2, far)
    for c in range(parts):
        pass_copy(c).wait_recv()
    keep(3, cross)
    whole(3, cross, 0, parts)
    hops(0, 2)
    saved = [
        pltpu.make_async_copy(k_buf, k_out, kv_sem.at[0]),
        pltpu.make_async_copy(v_buf, v_out, kv_sem.at[1]),
        pltpu.make_async_copy(vec_buf, vec_out, kv_sem.at[2]),
    ]
    for copy in saved:
        copy.start()

    lane = lax.broadcasted_iota(jnp.int32, (block, LANE), 1)

    def partner(round_):
        relation = 3 - round_
        return ((s // 2 + relation // 2) % 2) * 2 + (s % 2 + relation % 2) % 2

    def ctx_copy(step):
        at = pl.ds(pl.multiple_of(step % per * block, block), block)
        return remote(
            ctx_buf.at[step],
            ctx_out.at[s, at],
            ctx_send.at[step],
            ctx_recv.at[step],
            seq=partner(step // per),
        )

    def rows_of(step):
        base = partner(step // per) * tokens + step % per * block
        return pl.ds(pl.multiple_of(base, block), block)

    def keep_copies(step):
        at = rows_of(step)
        return (
            pltpu.make_async_copy(qb_buf.at[:, at], qb_out.at[:, at], keep_sem.at[0, step]),
            pltpu.make_async_copy(o_buf.at[:, at], o_out.at[:, at], keep_sem.at[1, step]),
        )

    chunks = slots // key_chunk

    def score(h, at, c):
        return dims(q_buf[h, at, :], k_buf[h, c * key_chunk : (c + 1) * key_chunk, :], NT)

    def highest(values, top):
        for j in range(key_chunk // LANE):
            tile = values[:, j * LANE : (j + 1) * LANE]
            top = tile if top is None else jnp.maximum(top, tile)
        return top

    top = None
    for c in range(chunks):
        scores = score(0, rows_of(0), c)
        s_buf[:, c * key_chunk : (c + 1) * key_chunk] = scores
        top = highest(scores, top)
    top_buf[...] = top

    def attend(step, carry):
        at = rows_of(step)
        after = rows_of(jnp.minimum(step + 1, 4 * per - 1))
        results = []
        current = [s_buf[:, c * key_chunk : (c + 1) * key_chunk] for c in range(chunks)]
        top = top_buf[...]
        for h in range(heads):
            peak = jnp.max(top, axis=1, keepdims=True)
            total = None
            coming = []
            top = None
            for c in range(chunks):
                scores = score(h + 1, at, c) if h + 1 < heads else score(0, after, c)
                coming.append(scores)
                top = highest(scores, top)
                probs = jnp.exp2(current[c] - peak).astype(bf16)
                term = dims(probs, v_buf[h, c * key_chunk : (c + 1) * key_chunk, :], NN)
                total = term if total is None else total + term
            current = coming
            weight = total[:, 64:65]
            result = jnp.where(lane < 64, total * (1.0 / weight), 0.0)
            o_buf[h, at, :] = result.astype(bf16)
            high, middle, low = thirds(-(peak + jnp.log2(weight)))
            qb_buf[h, at, :] = with_lanes(
                q_buf[h, at, :].astype(f32), ((65, high), (66, middle), (67, low))
            ).astype(bf16)
            results.append(result)
        for c in range(chunks):
            s_buf[:, c * key_chunk : (c + 1) * key_chunk] = current[c]
        top_buf[...] = top
        for t in range((heads + 1) // 2):
            tile = results[2 * t]
            if 2 * t + 1 < heads:
                tile = tile + pltpu.roll(results[2 * t + 1], 64, 1)
            ctx_buf[step, :, t * LANE : (t + 1) * LANE] = tile.astype(bf16)

        @pl.when(step < 3 * per)
        def _():
            ctx_copy(step).start()

        for copy in keep_copies(step):
            copy.start()
        for g in range(2):
            late = 2 * (1 - g)
            h = (2 * step - late + 1) // 5
            @pl.when(((5 * h + late) // 2 == step) & (h + 3 - g < nf - 1))
            def _():
                hops(g, h + 3 - g)

        return carry

    lax.fori_loop(0, 4 * per, attend, 0)
    owns = []
    for i in range(per):
        owns.append(
            pltpu.make_async_copy(
                ctx_buf.at[3 * per + i], ctx_out.at[s, pl.ds(i * block, block)], own_sem.at[i]
            )
        )
        owns[-1].start()

    def rest(h, carry):
        for w in range(len(shards)):
            ring_hop(w, h)
        return carry

    lax.fori_loop(min(7, nf - 1), nf - 1, rest, 0)

    def settle(step, carry):
        @pl.when(step < 3 * per)
        def _():
            ctx_copy(step).wait()

        for copy in keep_copies(step):
            copy.wait()
        return carry

    lax.fori_loop(0, 4 * per, settle, 0)
    for d in range(1, stages):
        along(d).wait_send()
    for d in range(stages):
        aside(d).wait_send()
    for d in range(1, nf):
        vec_copy(d).wait_send()
    for c in range(parts):
        far_copy(c).wait_send()
        pass_copy(c).wait_send()
    near_copy.wait_send()
    for copy in owns + mine + kept + saved:
        copy.wait()

    def close(h, carry):
        for w in range(len(shards)):
            ring_finish(w, h)
        return carry

    lax.fori_loop(0, nf - 1, close, 0)


def front(nf, heads, length, states, wq, wk, wv, wout, up, down, small_params, block, key_chunk):
    tokens, width = states.shape
    rows = wq.shape[0]
    slots = 4 * tokens
    parts = 4
    window = 256
    shards = (wout, up, down)
    halves = tuple((1, w.shape[1] // 2) for w in shards)
    wide = -(-heads // 2) * LANE
    steps = slots // block
    shape = jax.ShapeDtypeStruct
    head_shape = shape((heads, slots, LANE), bf16)
    head_buf = pltpu.VMEM((heads, slots, LANE), bf16)
    hops = DMA((3, nf - 1))
    stage = DMA((nf // 2 - 1,))
    stage_aside = DMA((nf // 2,))
    peers = DMA((nf - 1,))
    fine = DMA((parts,))
    return pl.pallas_call(
        functools.partial(front_kernel, nf, block, key_chunk, halves, ((1,), (0, 2))),
        out_shape=[head_shape] * 4
        + [
            shape((4, tokens, width), bf16),
            shape((nf, 16, LANE), bf16),
            shape((4, tokens, wide), bf16),
        ]
        + [shape((nf,) + w.shape, bf16) for w in shards],
        in_specs=[IN_SMEM] + [ANY] * 7 + [IN_VMEM] * 9,
        out_specs=[ANY] * 10,
        scratch_shapes=[head_buf] * 5
        + [
            pltpu.VMEM((block, slots), f32),
            pltpu.VMEM((block, LANE), f32),
            pltpu.VMEM((steps, block, wide), bf16),
            pltpu.VMEM((4, tokens, width), bf16),
            pltpu.VMEM((3, width, window), bf16),
            pltpu.VMEM((3, rows, window), bf16),
            pltpu.VMEM((nf, 3, rows // 2, heads * 128), bf16),
            pltpu.VMEM((16, LANE), f32),
            pltpu.VMEM((nf, 16, LANE), bf16),
        ]
        + [pltpu.VMEM(w.shape, bf16) for w in shards]
        + [
            DMA((5,)),
            DMA((4,)),
            DMA((3,)),
            DMA((2, steps)),
            peers, peers, stage, stage, stage_aside, stage_aside,
            DMA(()), DMA(()), fine, fine, fine, fine,
            hops, hops, hops, hops,
            DMA((steps,)), DMA((steps,)),
            DMA((tokens // block,)),
            DMA((2, 3)),
        ],
        compiler_params=params(1),
        name="front",
    )(length, states, wq, wk, wv, wout, up, down, *small_params)


def plane_gather(nf, shards, outs, z_send, z_recv, h_send, h_recv, n_send, n_recv):
    f = lax.axis_index("fsdp")
    s, near, _, _ = seq_peers()
    side = s % 2
    beside = f + 1 - 2 * (f % 2)
    stages = nf // 2
    count = len(shards)

    def half(ref):
        size = ref.shape[1] // 2
        return ref.at[:, pl.ds(pl.multiple_of(side * size, size), size)]

    def along(d, m):
        return remote(
            half(shards[m]), half(outs[m].at[f]), z_send.at[d - 1, m], z_recv.at[d - 1, m],
            fsdp=(f + 2 * d) % nf,
        )

    def aside(d, m):
        owner = (f + nf - 2 * d) % nf
        source = outs[m].at[owner] if d else shards[m]
        return remote(
            half(source), half(outs[m].at[owner]), h_send.at[d, m], h_recv.at[d, m], fsdp=beside
        )

    def share(e, m):
        owner = (f + nf - 2 * e) % nf if e < stages else (beside + nf - 2 * (e - stages)) % nf
        piece = half(outs[m].at[owner])
        return remote(piece, piece, n_send.at[e - 1, m], n_recv.at[e - 1, m], seq=near)

    def start():
        for d in range(1, stages):
            for m in range(count):
                along(d, m).start()
        for m in range(count):
            aside(0, m).start()

    def first():
        for d in range(1, stages):
            for m in range(count):
                along(d, m).wait_recv()
                aside(d, m).start()
                share(d, m).start()

    def second():
        for d in range(stages):
            for m in range(count):
                aside(d, m).wait_recv()
                share(stages + d, m).start()

    def finish():
        for m in range(count):
            for d in range(1, stages):
                along(d, m).wait_send()
            for d in range(stages):
                aside(d, m).wait_send()
            for e in range(1, nf):
                share(e, m).wait()

    return start, first, second, finish


def feed_kernel(
    nf, block, part, length_ref, vec_all, states_hbm, ctx_hbm, wout_hbm, up_hbm, down_hbm, cot_hbm,
    wq_s, wk_s, wv_s,
    out, first_grad_out, gctx, up_sum, down_sum, wout_sum, gvec, wq, wk, wv,
    states, ctx, wout, up, down, cot, held, vec, upb, out_buf, first_buf, act_buf, pre_buf, slope_buf, low_t, down_t, branch_buf,
    g_buf, up_give, down_give, wout_give, up_take, down_take, wout_take,
    load_sem, keep_sem, g_send, g_recv, own_sem, give_send, give_recv, sum_sem, shard_sem,
    z_send, z_recv, h_send, h_recv, n_send, n_recv,
):
    f = lax.axis_index("fsdp")
    s, near, far, cross = seq_peers()
    side = s % 2
    beside = f + 1 - 2 * (f % 2)
    tokens, width = states.shape
    hidden = up.shape[1]
    own = wout.shape[0] // 4
    steps = tokens // block
    wide = ctx.shape[2]
    loads = [
        pltpu.make_async_copy(up_hbm, up, load_sem.at[0]),
        pltpu.make_async_copy(down_hbm, down, load_sem.at[1]),
        pltpu.make_async_copy(cot_hbm, cot, load_sem.at[2]),
    ]
    early = [
        pltpu.make_async_copy(wout_hbm, wout, load_sem.at[3]),
        pltpu.make_async_copy(ctx_hbm, ctx, load_sem.at[4]),
        pltpu.make_async_copy(states_hbm, states, load_sem.at[5]),
    ]
    for copy in early + loads:
        copy.start()
    shards, outs = (wq_s, wk_s, wv_s), (wq, wk, wv)
    gather = plane_gather(nf, shards, outs, z_send, z_recv, h_send, h_recv, n_send, n_recv)
    friends = [{"fsdp": (f + 2 * d) % nf} for d in range(1, nf // 2)] + [
        {"fsdp": beside}, {"seq": near}, {"seq": far}, {"seq": cross},
    ]
    hail(friends)
    rows = width // nf
    short = lax.broadcasted_iota(jnp.int32, vec_all.shape[1:], 1) < rows
    lines = jnp.zeros((vec_all.shape[1], width), f32)
    blank = jnp.zeros((vec_all.shape[1], width - LANE), f32)
    tiles = [jnp.zeros((1, LANE), f32) for _ in range(hidden // LANE)]
    for j in range(nf):
        piece = jnp.where(short, vec_all[j].astype(f32), 0.0)
        both = jnp.concatenate([piece, blank], axis=1)
        lines = lines + (pltpu.roll(both, rows * j, 1) if j else both)
        for r in range(4):
            first_lane = rows * (4 * j + r)
            tile, shift = first_lane // LANE, first_lane % LANE
            both = jnp.concatenate([piece[8 + r : 9 + r, :], blank[:1, :LANE]], axis=1)
            if shift:
                both = pltpu.roll(both, shift, 1)
            tiles[tile] = tiles[tile] + both[:, :LANE]
            if tile + 1 < len(tiles):
                tiles[tile + 1] = tiles[tile + 1] + both[:, LANE:]
    vec[...] = lines[:8]
    upb[...] = jnp.concatenate(tiles, axis=1)
    kept = [pltpu.make_async_copy(shards[m], held.at[m], shard_sem.at[0, m]) for m in range(3)]
    for copy in kept:
        copy.start()
    kept_out = [
        pltpu.make_async_copy(held.at[m], outs[m].at[f], shard_sem.at[1, m]) for m in range(3)
    ]
    length = length_ref[0]
    gvec[...] = jnp.zeros_like(gvec)
    peers = (s, near, far, cross)

    def line(row):
        return vec[row : row + 1, :]

    def add_line(row, values):
        gvec[row : row + 1, :] += jnp.sum(values, axis=0, keepdims=True)

    def norm(values):
        centred = values - jnp.mean(values, axis=1, keepdims=True)
        scale = lax.rsqrt(jnp.mean(centred * centred, axis=1, keepdims=True) + eps)
        return centred * scale, scale

    def norm_back(grad, gain, normed, scale):
        grad = grad * gain
        return scale * (
            grad
            - jnp.mean(grad, axis=1, keepdims=True)
            - normed * jnp.mean(grad * normed, axis=1, keepdims=True)
        )

    def rows_of(i):
        return pl.ds(pl.multiple_of(i * block, block), block)

    def send(relation, i):
        at = rows_of(i)
        return remote(
            g_buf.at[relation, at],
            gctx.at[s, at],
            g_send.at[relation - 1, i],
            g_recv.at[relation - 1, i],
            seq=peers[relation],
        )

    def keep(i):
        at = rows_of(i)
        return (
            pltpu.make_async_copy(out_buf.at[at], out.at[at], keep_sem.at[0, i]),
            pltpu.make_async_copy(first_buf.at[at], first_grad_out.at[at], keep_sem.at[1, i]),
        )

    def body(i, carry):
        at = rows_of(i)
        attended = None
        for j in range(4):
            term = dims(ctx[j, at, :own], wout[own * j : own * (j + 1), :], NN)
            attended = term if attended is None else attended + term
        normed_first, scale_first = norm(states[at, :].astype(f32) + (attended + line(2)))
        first = normed_first * line(3) + line(4)
        low = first.astype(bf16)
        low_t[:, at] = jnp.transpose(low)

        @pl.when(i == 0)
        def _():
            hailed(friends)
            gather[0]()
            for copy in kept + loads:
                copy.wait()
            for copy in kept_out:
                copy.start()

        fed = None
        for c in range(hidden // part):
            cut = slice(c * part, (c + 1) * part)
            pre = dims(low, up[:, cut], NN) + upb[:, cut]
            share = 0.5 + 0.5 * lax.erf(pre * (2.0**-0.5))
            slope_buf[:, cut] = share + pre * jnp.exp(-0.5 * pre * pre) * (2.0 * math.pi) ** -0.5
            act = (pre * share).astype(bf16)
            act_buf[at, cut] = act
            term = dims(act, down[cut, :], NN)
            fed = term if fed is None else fed + term
        normed, scale = norm(first + (fed + line(5)))
        place = s * tokens + i * block + lax.broadcasted_iota(jnp.int32, (block, 1), 0)
        valid = jnp.where(place < length, 1.0, 0.0)
        out_buf[at, :] = ((normed * line(6) + line(7)) * valid).astype(bf16)
        grad = cot[at, :].astype(f32) * valid
        add_line(6, grad * normed)
        add_line(7, grad)
        second_grad = norm_back(grad, line(6), normed, scale)
        down_in = second_grad.astype(bf16)
        add_line(5, down_in.astype(f32))
        down_t[:, at] = jnp.transpose(down_in)
        back = second_grad
        for c in range(hidden // part):
            cut = slice(c * part, (c + 1) * part)
            pre_grad = (dims(down_in, down[cut, :], NT) * slope_buf[:, cut]).astype(bf16)
            pre_buf[at, cut] = pre_grad
            row = 8 + c * part // width
            col = c * part % width
            gvec[row : row + 1, col : col + part] += jnp.sum(
                pre_grad.astype(f32), axis=0, keepdims=True
            )
            back = back + dims(pre_grad, up[:, cut], NT)
        add_line(3, back * normed_first)
        add_line(4, back)
        first_grad = norm_back(back, line(3), normed_first, scale_first)
        first_buf[at, :] = first_grad
        branch = first_grad.astype(bf16)
        branch_buf[at, :] = branch
        add_line(2, branch.astype(f32))
        for relation in range(4):
            rows = pl.ds(pl.multiple_of(peers[relation] * own, 64), own)
            g_buf[relation, at, :own] = dims(branch, wout[rows, :], NT).astype(bf16)
            if wide > own:
                g_buf[relation, at, own:] = jnp.zeros((block, wide - own), bf16)
            if relation:
                send(relation, i).start()
        for copy in keep(i):
            copy.start()

        @pl.when(i == min(1, steps - 1))
        def _():
            gather[1]()

        return carry

    for copy in early:
        copy.wait()
    lax.fori_loop(0, steps, body, 0)
    mine = pltpu.make_async_copy(g_buf.at[0], gctx.at[s], own_sem)
    mine.start()

    pieces = give_send.shape[1]
    up_cut = hidden // 2 // pieces
    down_cut = hidden // pieces

    def up_part(which, c):
        cut = pl.ds(pl.multiple_of(which * (hidden // 2) + c * up_cut, up_cut), up_cut)
        return dims(low_t[...], pre_buf[:, cut], NN)

    def down_part(which, c):
        rows = pl.ds(pl.multiple_of(which * (width // 2), width // 2), width // 2)
        cut = pl.ds(pl.multiple_of(c * down_cut, down_cut), down_cut)
        return dims(down_t[rows, :], act_buf[:, cut], NN)

    def wout_part(which, j):
        cut = pl.ds(pl.multiple_of(which * (width // 2), width // 2), width // 2)
        return dims(ctx[j, :, :own], branch_buf[:, cut], TN)

    def cols(c, size):
        return (slice(None), pl.ds(pl.multiple_of(c * size, size), size))

    def give(w, c):
        if w == 2:
            pair = wout_give, wout_take
        else:
            at = cols(c, (up_cut, down_cut)[w])
            pair = (up_give, down_give)[w].at[at], (up_take, down_take)[w].at[at]
        return remote(*pair, give_send.at[w, c], give_recv.at[w, c], seq=near)

    def give_away(c, carry):
        up_give[cols(c, up_cut)] = up_part(1 - side, c).astype(bf16)
        give(0, c).start()
        down_give[cols(c, down_cut)] = down_part(1 - side, c).astype(bf16)
        give(1, c).start()
        return carry

    def add_own(c, carry):
        at = cols(c, up_cut)
        total = up_part(side, c)
        give(0, c).wait()
        up_give[at] = (total + up_take[at].astype(f32)).astype(bf16)
        at = cols(c, down_cut)
        total = down_part(side, c)
        give(1, c).wait()
        down_give[at] = (total + down_take[at].astype(f32)).astype(bf16)
        return carry

    lax.fori_loop(0, pieces, give_away, 0)
    for j in range(4):
        wout_give[own * j : own * (j + 1), :] = wout_part(1 - side, j).astype(bf16)
    give(2, 0).start()
    gather[2]()
    lax.fori_loop(0, pieces, add_own, 0)
    sums = [
        pltpu.make_async_copy(up_give, up_sum, sum_sem.at[0]),
        pltpu.make_async_copy(down_give, down_sum, sum_sem.at[1]),
    ]
    for copy in sums:
        copy.start()
    totals = [wout_part(side, j) for j in range(4)]
    give(2, 0).wait()
    for j in range(4):
        at = slice(own * j, own * (j + 1))
        wout_give[at, :] = (totals[j] + wout_take[at, :].astype(f32)).astype(bf16)
    sums.append(pltpu.make_async_copy(wout_give, wout_sum, sum_sem.at[2]))
    sums[-1].start()
    for relation in range(1, 4):
        for i in range(steps):
            send(relation, i).wait()
    for i in range(steps):
        for copy in keep(i):
            copy.wait()
    gather[3]()
    for copy in [mine] + kept_out + sums:
        copy.wait()


def feed(nf, length, states, cot, ctx, wout, up, down, vec_all, shards, block=256, part=768):
    tokens, width = states.shape
    hidden = up.shape[1]
    wide = ctx.shape[2]
    pieces = 3
    shape = jax.ShapeDtypeStruct
    halves = ((width, hidden // 2), (width // 2, hidden), (width, width // 2))
    vmem = lambda *size: pltpu.VMEM(size, bf16)
    steps = tokens // block
    staged = DMA((nf // 2 - 1, 3))
    staged_aside = DMA((nf // 2, 3))
    return pl.pallas_call(
        functools.partial(feed_kernel, nf, block, part),
        out_shape=[
            shape((tokens, width), bf16),
            shape((tokens, width), f32),
            shape((4, tokens, wide), bf16),
        ]
        + [shape(x, bf16) for x in halves]
        + [shape((16, width), f32)]
        + [shape((nf,) + w.shape, bf16) for w in shards],
        in_specs=[IN_SMEM, IN_VMEM] + [ANY] * 9,
        out_specs=[ANY] * 6 + [IN_VMEM] + [ANY] * 3,
        scratch_shapes=[
            vmem(*states.shape),
            vmem(*ctx.shape),
            vmem(*wout.shape),
            vmem(width, hidden),
            vmem(hidden, width),
            vmem(tokens, width),
            vmem(3, *shards[0].shape),
            pltpu.VMEM((8, width), f32),
            pltpu.VMEM((1, hidden), f32),
            vmem(tokens, width),
            pltpu.VMEM((tokens, width), f32),
            vmem(tokens, hidden),
            vmem(tokens, hidden),
            pltpu.VMEM((block, hidden), f32),
            vmem(width, tokens),
            vmem(width, tokens),
            vmem(tokens, width),
            vmem(4, tokens, wide),
        ]
        + [vmem(*x) for x in halves] * 2
        + [
            DMA((6,)),
            DMA((2, steps)),
            DMA((3, steps)),
            DMA((3, steps)),
            DMA(()),
            DMA((3, pieces)),
            DMA((3, pieces)),
            DMA((3,)),
            DMA((2, 3)),
            staged, staged, staged_aside, staged_aside,
            DMA((nf - 1, 3)), DMA((nf - 1, 3)),
        ],
        compiler_params=params(3),
        name="feed",
    )(length, vec_all, states, ctx, wout, up, down, cot, *shards)


def back_kernel(
    nf, key_block, groups, q_ref, k_ref, v_ref, o_ref, gctx_ref,
    up_sum, down_sum, wout_sum, x_hbm, wq_hbm, wk_hbm, wv_hbm, first_hbm, gvec_hbm,
    states_grad, up_out, down_out, wout_out, qkv_out, vec_out, upb_out,
    k_acc, v_acc, q_acc, g_buf, q_turned, g_turned, d_out, g_all, x_all, w_all, first_grad,
    own_up, own_dn, own_wo, ring_up, ring_dn, ring_wo, y_up, y_dn, y_wo, z_up, z_dn, z_wo,
    w_buf, w_came, w_sum, w_parts, v_own, v_cut, v_came, v_sum, v_parts,
    load_sem, late_sem, hop_send, hop_recv, y_send, y_recv, z_send, z_recv,
    d_send, d_recv, d_own, w_send, w_recv, p_send, p_recv, l_send, l_recv, m_send, m_recv,
):
    half, h = pl.program_id(0), pl.program_id(1)
    count = w_buf.shape[0]
    f = lax.axis_index("fsdp")
    s, near, far, cross = seq_peers()
    peers = (s, near, far, cross)
    side = s % 2
    way = 1 - 2 * side
    place = place_of(f, nf)
    ahead = index_at((place + way + nf) % nf, nf)
    slots = k_ref.shape[1]
    tokens = slots // 4
    block = tokens
    width = x_all.shape[2]
    rows = width // nf
    width_own = count * 64
    full = (up_sum, down_sum, wout_sum)
    own = (own_up, own_dn, own_wo)
    came = (ring_up, ring_dn, ring_wo)
    y_buf = (y_up, y_dn, y_wo)
    z_buf = (z_up, z_dn, z_wo)
    outs = (up_out, down_out, wout_out)
    by_cols = (False, True, False)

    def chunk_at(w, chunk):
        size = came[w].shape[1 + by_cols[w]]
        cut = pl.ds(pl.multiple_of(chunk * size, size), size)
        return (slice(None), cut) if by_cols[w] else (cut, slice(None))

    def hop(w, t, source):
        return remote(source, came[w].at[t], hop_send.at[w, t], hop_recv.at[w, t], fsdp=ahead)

    def chunk_of(t):
        return index_at((place + 2 * nf - way * (1 + t)) % nf, nf)

    def to_far(w):
        return remote(came[w].at[nf - 2], y_buf[w], y_send.at[w], y_recv.at[w], seq=far)

    def to_near(w):
        return remote(y_buf[w], z_buf[w], z_send.at[w], z_recv.at[w], seq=near)

    def loads():
        return [pltpu.make_async_copy(full[w], own[w], load_sem.at[w]) for w in range(3)]

    def late():
        return [
            pltpu.make_async_copy(x_hbm, x_all, late_sem.at[0]),
            pltpu.make_async_copy(wq_hbm, w_all.at[0], late_sem.at[1]),
            pltpu.make_async_copy(wk_hbm, w_all.at[1], late_sem.at[2]),
            pltpu.make_async_copy(wv_hbm, w_all.at[2], late_sem.at[3]),
            pltpu.make_async_copy(first_hbm, first_grad, late_sem.at[4]),
            pltpu.make_async_copy(gvec_hbm, v_own, late_sem.at[5]),
        ]

    friends = [{"fsdp": (f + d) % nf} for d in range(1, nf)] + [{"seq": p} for p in peers[1:]]

    @pl.when((half == 0) & (h == 0))
    def _():
        hail(friends)
        for copy in loads() + late():
            copy.start()

    k_acc[...] = jnp.zeros_like(k_acc)
    v_acc[...] = jnp.zeros_like(v_acc)
    at_head = pl.ds(pl.multiple_of(h * 64, 64), 64)

    def part(relation, m, head):
        to = peers[relation]
        source = d_out.at[
            m, pl.ds(pl.multiple_of(head * 64, 64), 64), pl.ds(pl.multiple_of(to * tokens, tokens), tokens)
        ]
        target = g_all.at[m, pl.ds(pl.multiple_of(s * width_own + head * 64, 64), 64), :]
        return source, target

    def d_copy(relation, m, head):
        source, target = part(relation, m, head)
        return remote(
            source, target, d_send.at[relation - 1, m, head], d_recv.at[relation - 1, m, head],
            seq=peers[relation],
        )

    def d_local(m, head):
        source, target = part(0, m, head)
        return pltpu.make_async_copy(source, target, d_own.at[m, head])

    def w_copy(head, d):
        to = (f + d) % nf
        return remote(
            w_buf.at[head, to], w_came.at[head, d - 1], w_send.at[head, d - 1],
            w_recv.at[head, d - 1], fsdp=to,
        )

    def p_copy(head, relation):
        return remote(
            w_sum.at[head], w_parts.at[s, head], p_send.at[head, relation - 1],
            p_recv.at[head, relation - 1], seq=peers[relation],
        )

    def v_copy(d):
        to = (f + d) % nf
        return remote(v_cut.at[to], v_came.at[d], l_send.at[d - 1], l_recv.at[d - 1], fsdp=to)

    def m_copy(relation):
        return remote(
            v_sum, v_parts.at[s], m_send.at[relation - 1], m_recv.at[relation - 1],
            seq=peers[relation],
        )

    def settle_head(head):
        for d in range(1, nf):
            w_copy(head, d).wait()
        total = w_buf[head, f].astype(f32)
        for d in range(1, nf):
            total = total + w_came[head, d - 1].astype(f32)
        w_sum[head] = total.astype(bf16)
        for relation in (3, 2, 1):
            p_copy(head, relation).start()
        w_parts[s, head] = total.astype(bf16)

    base = (s // 2 + 1 + half) % 2 * (2 * tokens)

    def round_(early, turn, carry):
        step = (half * count + h) * 4 + turn
        relation = (1 - turn // 2) * (turn + 2) + turn // 2 * (3 - turn)
        owner = ((s // 2 + relation // 2) % 2) * 2 + (s % 2 + relation % 2) % 2
        at = pl.ds(pl.multiple_of(owner * tokens, tokens), tokens)

        q = q_ref[0, at, :]
        if early:
            lane = lax.broadcasted_iota(jnp.int32, (block, LANE), 1)
            first = gctx_ref[at, :LANE].astype(f32)
            second = gctx_ref[at, LANE:].astype(f32)
            grad = jnp.where(h == 0, first, jnp.where(h == 1, pltpu.roll(first, 64, 1), second))
            grad = jnp.where(lane < 64, grad, 0.0)
            delta = jnp.sum(grad * o_ref[0, at, :].astype(f32), axis=1, keepdims=True)
            high, middle, low = thirds(-delta)
            grad = with_lanes(grad, ((64, high), (65, middle), (66, low))).astype(bf16)
            g_side = jnp.transpose(grad)[:64, :]
            q_side = jnp.transpose(q)[:64, :]
            g_buf[h, at, :] = grad
            g_turned[h, :, at] = g_side
            q_turned[h, :, at] = q_side
        else:
            grad = g_buf[h, at, :]
            g_side, q_side = g_turned[h, :, at], q_turned[h, :, at]
        q_total = None
        for c in range(2 * tokens // key_block):
            ks = slice(c * key_block, (c + 1) * key_block)
            keys = pl.ds(pl.multiple_of(base + c * key_block, LANE), key_block)
            k = k_ref[0, keys, :]
            probs = jnp.exp2(dims(q, k, NT))
            score = (probs * dims(grad, v_ref[0, keys, :], NT)).astype(bf16)
            v_acc[:, ks] += dims(g_side, probs.astype(bf16), NN)
            k_acc[:, ks] += dims(q_side, score, NN)
            term = dims(score, k, NN)
            q_total = term if q_total is None else q_total + term
        q_total = jnp.transpose(q_total)[:64, :]

        if early:
            q_acc[h, :, at] = q_total
        else:
            d_out[0, at_head, at] = ((q_total + q_acc[h, :, at]) * 0.125).astype(bf16)

        if early:
            @pl.when(step == 0)
            def _():
                hailed(friends)
                for w in range(3):
                    hop(w, 0, full[w].at[chunk_at(w, chunk_of(0))]).start()

            @pl.when(step == 1)
            def _():
                for copy in loads():
                    copy.wait()

        for g in range(2):
            t = (2 * (step - g) + 1) // 5
            due = 5 * t // 2 == step - g

            @pl.when(due & (t > 0) & (t < nf - 1))
            def _():
                for w in groups[g]:
                    hop(w, t - 1, came[w].at[t - 1]).wait_recv()
                    here = own[w][chunk_at(w, chunk_of(t))].astype(f32)
                    came[w][t - 1] = (here + came[w][t - 1].astype(f32)).astype(bf16)
                    hop(w, t, came[w].at[t - 1]).start()

            if early:
                continue

            @pl.when(due & (t == nf - 1))
            def _():
                for w in groups[g]:
                    hop(w, nf - 2, came[w].at[nf - 2]).wait_recv()
                    here = own[w][chunk_at(w, f)].astype(f32)
                    came[w][nf - 2] = (here + came[w][nf - 2].astype(f32)).astype(bf16)
                    to_far(w).start()

        if early:
            return carry
        for stage, kind in enumerate((2, 3, 1)):
            @pl.when(turn == stage)
            def _():
                d_copy(kind, 0, h).start()

        @pl.when((h > 0) & (turn == 1))
        def _():
            settle_head(h - 1)

        return carry

    for early in (True, False):
        @pl.when(half == (0 if early else 1))
        def _():
            lax.fori_loop(0, 4, functools.partial(round_, early), 0)

    keys = pl.ds(pl.multiple_of(base, 2 * tokens), 2 * tokens)
    d_out[1, at_head, keys] = (k_acc[...] * LN2).astype(bf16)
    d_out[2, at_head, keys] = v_acc[...].astype(bf16)

    @pl.when(half == 0)
    def _():
        for m in (1, 2):
            for kind in (2, 3):
                d_copy(kind, m, h).start()

    @pl.when(half == 1)
    def _():
        for m in range(3):
            if m:
                d_copy(1, m, h).start()
            d_local(m, h).start()

        @pl.when(h == 0)
        def _():
            for copy in late():
                copy.wait()

        left = jnp.concatenate([d_out[m, at_head, :] for m in range(3)], axis=0)
        total = None
        for j in range(4):
            term = dims(left[:, j * tokens : (j + 1) * tokens], x_all[j], NN)
            total = term if total is None else total + term
        total = jnp.transpose(total).astype(bf16)
        for j in range(nf):
            w_buf[h, j] = jnp.concatenate(
                [total[rows * j + rows // 2 * e : rows * j + rows // 2 * (e + 1)] for e in range(2)],
                axis=1,
            )
        for d in range(1, nf):
            w_copy(h, d).start()

    @pl.when((half == 1) & (h == count - 1))
    def _():
        ones = jnp.ones((8, slots), bf16)
        for row, m in ((0, 0), (1, 2)):
            line = dims(ones, d_out[m], NT)
            line = jnp.concatenate([line, jnp.zeros((8, width - width_own), f32)], axis=1)
            v_own[row : row + 1, :] = pltpu.roll(line, s * width_own, 1)[0:1, :]
        lines = v_own[...]
        flat = jnp.concatenate([lines[8 + r : 9 + r, :] for r in range(4)], axis=1)
        for j in range(nf):
            piece = lines if j == 0 else pltpu.roll(lines, width - rows * j, 1)
            v_cut[j, 0:8, :] = piece[0:8, :LANE]
            for r in range(4):
                start = rows * (4 * j + r)
                shift = start % LANE
                tile = start - shift
                both = jnp.concatenate(
                    [flat[:, tile : tile + LANE], flat[:, min(tile + LANE, flat.shape[1] - LANE) :][:, :LANE]],
                    axis=1,
                )
                if shift:
                    both = pltpu.roll(both, 2 * LANE - shift, 1)
                v_cut[j, 8 + r : 9 + r, :] = both[:, :LANE]
            v_cut[j, 12:16, :] = jnp.zeros((4, LANE), f32)
        for d in range(1, nf):
            v_copy(d).start()
        for w in range(3):
            to_far(w).wait()
            y_buf[w][...] = (
                came[w][nf - 2].astype(f32) + y_buf[w][...].astype(f32)
            ).astype(bf16)
            to_near(w).start()

        def settle(head, carry):
            for m in range(3):
                for kind in range(1, 4):
                    d_copy(kind, m, head).wait()
                d_local(m, head).wait()
            return carry

        lax.fori_loop(0, count, settle, 0)
        cut_size = 256
        mats = [w_all[m].reshape(width, width) for m in range(3)]
        for c in range(width // cut_size):
            cut = slice(c * cut_size, (c + 1) * cut_size)
            total = None
            for m in range(3):
                term = dims(mats[m][cut, :], g_all[m], NN)
                total = term if total is None else total + term
            states_grad[:, cut] = (first_grad[:, cut] + jnp.transpose(total)).astype(bf16)
        for d in range(1, nf):
            v_copy(d).wait()
        v_came[0] = v_cut[f]
        total = None
        for j in range(nf):
            term = v_came[(f + nf - j) % nf]
            total = term if total is None else total + term
        v_sum[...] = total
        for kind in (3, 2, 1):
            m_copy(kind).start()
        v_parts[s] = total
        settle_head(count - 1)
        for w in range(3):
            for t in range(nf - 1):
                hop(w, t, came[w].at[t]).wait_send()
            to_near(w).wait()
            mine, theirs = y_buf[w][...], z_buf[w][...]
            out = outs[w]
            size = out.shape[1] // 2
            if by_cols[w]:
                mine, theirs = jnp.transpose(mine), jnp.transpose(theirs)
            out[:, pl.ds(pl.multiple_of(side * size, size), size)] = mine
            out[:, pl.ds(pl.multiple_of((1 - side) * size, size), size)] = theirs
        for relation in range(1, 4):
            m_copy(relation).wait()
        total = v_parts[0] + v_parts[1] + v_parts[2] + v_parts[3]
        vec_out[...] = total
        lane = lax.broadcasted_iota(jnp.int32, (1, 4 * rows), 1)
        line = jnp.zeros((1, 4 * rows), f32)
        for r in range(4):
            piece = jnp.concatenate(
                [total[8 + r : 9 + r, :], jnp.zeros((1, 4 * rows - LANE), f32)], axis=1
            )
            if r:
                piece = pltpu.roll(piece, rows * r, 1)
            line = jnp.where((lane >= rows * r) & (lane < rows * (r + 1)), piece, line)
        upb_out[...] = jnp.broadcast_to(line, upb_out.shape)
        for head in range(count):
            for relation in range(1, 4):
                p_copy(head, relation).wait()
        parts = [
            [
                jnp.concatenate([both[:, : 3 * 64], both[:, 3 * 64 :]], axis=0)
                for both in [w_parts[j, head].astype(f32) for head in range(count)]
            ]
            for j in range(4)
        ]
        for m in range(3):
            qkv_out[m] = jnp.concatenate(
                [part[:, m * 64 : (m + 1) * 64] for group in parts for part in group], axis=1
            ).astype(bf16)


def back(nf, qb, k, v, o, gctx, sums, x_all, mats, first_grad, gvec, key_block):
    heads, slots, _ = qb.shape
    tokens = slots // 4
    width = x_all.shape[2]
    hidden = sums[0].shape[1] * 2
    rows, cols = width // nf, hidden // nf
    shape = jax.ShapeDtypeStruct
    per_head = pl.BlockSpec((1, slots, LANE), lambda p, h: (h, 0, 0))
    chunk = ((rows, hidden // 2), (width // 2, cols), (rows, width // 2))
    vmem = lambda *size: pltpu.VMEM(size, bf16)
    triple = DMA((3,))
    hops = DMA((3, nf - 1))
    own = heads * 64
    packed = (rows // 2, 6 * 64)
    results = [
        shape((tokens, width), bf16),
        shape((rows, hidden), bf16),
        shape((cols, width), bf16),
        shape((rows, width), bf16),
        shape((3, rows, width), bf16),
        shape((16, LANE), f32),
        shape((8, cols), f32),
    ]
    return pl.pallas_call(
        functools.partial(back_kernel, nf, key_block, ((0,), (1, 2))),
        grid=(2, heads),
        out_shape=results,
        in_specs=[per_head] * 4 + [IN_VMEM] + [ANY] * 9,
        out_specs=[
            pl.BlockSpec(x.shape, functools.partial(lambda n, *_: (0,) * n, len(x.shape)))
            for x in results
        ],
        scratch_shapes=[
            pltpu.VMEM((64, slots // 2), f32),
            pltpu.VMEM((64, slots // 2), f32),
            pltpu.VMEM((heads, 64, slots), f32),
            vmem(heads, slots, LANE),
            vmem(heads, 64, slots),
            vmem(heads, 64, slots),
            vmem(3, own, slots),
            vmem(3, width, tokens),
            vmem(4, tokens, width),
            vmem(3, nf, rows, width),
            pltpu.VMEM((tokens, width), f32),
        ]
        + [vmem(*x.shape) for x in sums]
        + [vmem(nf - 1, *x) for x in chunk]
        + [vmem(*x) for x in chunk] * 2
        + [
            vmem(heads, nf, *packed),
            vmem(heads, nf - 1, *packed),
            vmem(heads, *packed),
            vmem(4, heads, *packed),
            pltpu.VMEM((16, width), f32),
            pltpu.VMEM((nf, 16, LANE), f32),
            pltpu.VMEM((nf, 16, LANE), f32),
            pltpu.VMEM((16, LANE), f32),
            pltpu.VMEM((4, 16, LANE), f32),
            triple, DMA((6,)), hops, hops, triple, triple, triple, triple,
            DMA((3, 3, heads)), DMA((3, 3, heads)), DMA((3, heads)),
            DMA((heads, nf - 1)), DMA((heads, nf - 1)), DMA((heads, 3)), DMA((heads, 3)),
            DMA((nf - 1,)), DMA((nf - 1,)), triple, triple,
        ],
        compiler_params=params(4),
        name="back",
    )(qb, k, v, o, gctx, *sums, x_all, *mats, first_grad, gvec)


def results_kernel(rows, output, states_grad, up, down, wout, qkv, vec, upb, *outs):
    outs[0][...] = output[...]
    outs[1][...] = states_grad[...]
    for m in range(3):
        outs[2 + m][...] = qkv[m].astype(f32)
    outs[5][...] = wout[...].astype(f32)
    outs[6][...] = up[...].astype(f32)
    outs[7][...] = down[...].astype(f32)
    for r in range(8):
        outs[8 + r][...] = vec[r, :rows]
    outs[16][...] = upb[0, :]


def results(rows, output, states_grad, up, down, wout, qkv, vec, upb):
    shape = jax.ShapeDtypeStruct
    pieces = 2
    grads = [shape(qkv.shape[1:], f32)] * 3 + [shape(x.shape, f32) for x in (wout, up, down)]
    outs = [shape(output.shape, bf16)] * 2 + grads
    lines = [shape((rows,), f32)] * 8 + [shape((upb.shape[1],), f32)]

    def cut(x):
        n = len(x.shape)
        size = x.shape[: n - 2] + (x.shape[n - 2] // pieces, x.shape[n - 1])
        return pl.BlockSpec(size, functools.partial(lambda n, i: (0,) * (n - 2) + (i, 0), n))

    def same(x):
        return pl.BlockSpec(x.shape, lambda i: (0,) * len(x.shape))

    return pl.pallas_call(
        functools.partial(results_kernel, rows),
        grid=(pieces,),
        out_shape=outs + lines,
        in_specs=[cut(x) for x in (output, states_grad, up, down, wout, qkv)] + [same(vec), same(upb)],
        out_specs=[cut(x) for x in outs] + [same(x) for x in lines],
        compiler_params=params(),
        name="results",
    )(output, states_grad, up, down, wout, qkv, vec, upb)


def fused_device(
    nf, states, query_weight, key_weight, value_weight, out_weight, query_bias, value_bias,
    out_bias, first_gain, first_shift, up_weight, up_bias, down_weight, down_bias, second_gain,
    second_shift, lengths, cotangent,
):
    tokens, width = states.shape
    rows = width // nf
    hidden = up_weight.shape[1]
    heads = width // 4 // 64
    qb, o, k, v, x_all, vec_all, ctx, wout, up, down = front(
        nf, heads, lengths, states, query_weight, key_weight, value_weight, out_weight, up_weight,
        down_weight,
        (
            query_bias, value_bias, out_bias, first_gain, first_shift, down_bias, second_gain,
            second_shift, up_bias,
        ),
        block=256, key_chunk=512,
    )
    output, first_grad, gctx, up_sum, down_sum, wout_sum, gvec, wq, wk, wv = feed(
        nf, lengths, states, cotangent, ctx, wout.reshape(width, width),
        up.reshape(width, hidden), down.reshape(hidden, width), vec_all,
        (query_weight, key_weight, value_weight),
    )
    states_grad, up_grad, down_grad, out_grad, qkv, vec_grad, upb_grad = back(
        nf, qb, k, v, o, gctx.reshape(4 * tokens, -1), (up_sum, down_sum, wout_sum), x_all,
        (wq, wk, wv), first_grad, gvec, key_block=384,
    )
    done = results(rows, output, states_grad, up_grad, down_grad, out_grad, qkv, vec_grad, upb_grad)
    output, states_grad, q_grad, k_grad, v_grad, out_grad, up_grad, down_grad = done[:8]
    lines = done[8:]
    return (
        output, states_grad, q_grad, k_grad, v_grad, out_grad, *lines[:5], up_grad, lines[8],
        down_grad, *lines[5:8],
    )


def solution(mesh):
    nf, ns = mesh.shape["fsdp"], mesh.shape["seq"]

    def choose(states, query_weight, *rest):
        rows, width = query_weight.shape
        fits = ns == 4 and nf == 8 and rows % 16 == 0 and width == 768 and states.shape[0] % 768 == 0
        device = functools.partial(fused_device, nf) if fits else per_device
        return device(states, query_weight, *rest)

    return jax.shard_map(
        choose,
        mesh=mesh,
        in_specs=(
            P(("fsdp", "seq"), None),
            P("fsdp", None),
            P("fsdp", None),
            P("fsdp", None),
            P("fsdp", None),
            P("fsdp"),
            P("fsdp"),
            P("fsdp"),
            P("fsdp"),
            P("fsdp"),
            P("fsdp", None),
            P("fsdp"),
            P("fsdp", None),
            P("fsdp"),
            P("fsdp"),
            P("fsdp"),
            P("fsdp"),
            P(("fsdp", "seq"), None),
        ),
        out_specs=(
            P(("fsdp", "seq"), None),
            P(("fsdp", "seq"), None),
            P("fsdp", None),
            P("fsdp", None),
            P("fsdp", None),
            P("fsdp", None),
            P("fsdp"),
            P("fsdp"),
            P("fsdp"),
            P("fsdp"),
            P("fsdp"),
            P("fsdp", None),
            P("fsdp"),
            P("fsdp", None),
            P("fsdp"),
            P("fsdp"),
            P("fsdp"),
        ),
        check_vma=False,
    )
```

```python
import functools
import math

import jax
import jax.numpy as jnp
from jax import lax
from jax.experimental import pallas as pl
from jax.experimental.pallas import tpu as pltpu
from jax.sharding import PartitionSpec as P

HEAD_DIM = 64


eps = 1e-12


def product(left, right):
    return jnp.dot(left, right, preferred_element_type=jnp.float32)


def left_product(left, right):
    return lax.dot_general(
        left, right, (((0,), (0,)), ((), ())), preferred_element_type=jnp.float32
    )


def right_product(left, right):
    return lax.dot_general(
        left, right, (((1,), (1,)), ((), ())), preferred_element_type=jnp.float32
    )


def layer_norm(values, gain, shift):
    average = jnp.mean(values, axis=-1, keepdims=True)
    centred = values - average
    spread = jnp.mean(centred * centred, axis=-1, keepdims=True)
    return centred * lax.rsqrt(spread + eps) * gain + shift


def gelu_exact(values):
    return jax.nn.gelu(values, approximate=False)


def column_sums(values):
    return jnp.sum(values.astype(jnp.float32), axis=0)


def per_device(
    states,
    query_weight,
    key_weight,
    value_weight,
    out_weight,
    query_bias,
    value_bias,
    out_bias,
    first_gain,
    first_shift,
    up_weight,
    up_bias,
    down_weight,
    down_bias,
    second_gain,
    second_shift,
    lengths,
    cotangent,
):
    f32 = jnp.float32
    bf16 = jnp.bfloat16
    (
        query_mat,
        key_mat,
        value_mat,
        out_mat,
        query_add,
        value_add,
        out_add,
        gain_first,
        shift_first,
    ) = (
        lax.all_gather(query_weight, "fsdp", axis=0, tiled=True),
        lax.all_gather(key_weight, "fsdp", axis=0, tiled=True),
        lax.all_gather(value_weight, "fsdp", axis=0, tiled=True),
        lax.all_gather(out_weight, "fsdp", axis=0, tiled=True),
        lax.all_gather(query_bias, "fsdp", axis=0, tiled=True),
        lax.all_gather(value_bias, "fsdp", axis=0, tiled=True),
        lax.all_gather(out_bias, "fsdp", axis=0, tiled=True),
        lax.all_gather(first_gain, "fsdp", axis=0, tiled=True),
        lax.all_gather(first_shift, "fsdp", axis=0, tiled=True),
    )
    up_mat, up_add, down_mat, down_add, gain_second, shift_second = (
        lax.all_gather(up_weight, "fsdp", axis=0, tiled=True),
        lax.all_gather(up_bias, "fsdp", axis=0, tiled=True),
        lax.all_gather(down_weight, "fsdp", axis=0, tiled=True),
        lax.all_gather(down_bias, "fsdp", axis=0, tiled=True),
        lax.all_gather(second_gain, "fsdp", axis=0, tiled=True),
        lax.all_gather(second_shift, "fsdp", axis=0, tiled=True),
    )
    tokens = states.shape[0]
    slot_rows = tokens * lax.axis_size("seq")
    length = lengths[0]
    places = lax.axis_index("seq") * tokens + lax.iota(jnp.int32, tokens)
    valid_rows = (places < length).astype(f32)[:, None]
    queries = (product(states, query_mat) + query_add).astype(bf16)
    keys_in = product(states, key_mat).astype(bf16)
    values = (product(states, value_mat) + value_add).astype(bf16)
    head_queries, head_keys, head_values = (
        lax.all_to_all(queries, "seq", split_axis=1, concat_axis=0, tiled=True),
        lax.all_to_all(keys_in, "seq", split_axis=1, concat_axis=0, tiled=True),
        lax.all_to_all(values, "seq", split_axis=1, concat_axis=0, tiled=True),
    )
    local_width = head_queries.shape[1]
    head_count = local_width // HEAD_DIM
    block_rows = min(512, slot_rows)
    blocks = slot_rows // block_rows
    scaling = HEAD_DIM ** (-0.5)
    key_valid = lax.iota(jnp.int32, slot_rows) < length
    keys_heads = head_keys.reshape(slot_rows, head_count, HEAD_DIM)
    values_heads = head_values.reshape(slot_rows, head_count, HEAD_DIM)
    query_blocks = head_queries.reshape(blocks, block_rows, head_count, HEAD_DIM)

    def block_scores(query_block):
        scores = (
            jnp.einsum("qhd,khd->hqk", query_block, keys_heads, preferred_element_type=f32)
            * scaling
        )
        return jnp.where(key_valid[None, None, :], scores, -1000000000.0)

    def forward_block(query_block):
        scores = block_scores(query_block)
        highest = jnp.max(scores, axis=-1, keepdims=True)
        exponent = jnp.exp(scores - highest)
        totals = jnp.sum(exponent, axis=-1, keepdims=True)
        weights_soft = (exponent / totals).astype(bf16)
        context_part = jnp.einsum(
            "hqk,khd->qhd", weights_soft, values_heads, preferred_element_type=f32
        )
        return (context_part.astype(bf16), (highest + jnp.log(totals))[:, :, 0])

    context_blocks, log_totals = lax.map(forward_block, query_blocks)
    context = lax.all_to_all(
        context_blocks.reshape(slot_rows, local_width),
        "seq",
        split_axis=0,
        concat_axis=1,
        tiled=True,
    )
    hidden = states.astype(f32)
    first_sum = hidden + (product(context, out_mat) + out_add)
    first_norm, first_back = jax.vjp(
        layer_norm, first_sum, gain_first.astype(f32), shift_first.astype(f32)
    )
    first_low = first_norm.astype(bf16)
    pre_act = product(first_low, up_mat) + up_add
    activated = gelu_exact(pre_act).astype(bf16)
    second_sum = first_norm + (product(activated, down_mat) + down_add)
    normed, second_back = jax.vjp(
        layer_norm, second_sum, gain_second.astype(f32), shift_second.astype(f32)
    )
    output = (normed * valid_rows).astype(bf16)
    out_grad = cotangent.astype(f32) * valid_rows
    second_grad, gain_second_grad, shift_second_grad = second_back(out_grad)
    down_in = second_grad.astype(bf16)
    down_weight_grad = left_product(activated, down_in)
    down_bias_grad = column_sums(down_in)
    act_grad = right_product(down_in, down_mat)
    pre_grad = jax.vjp(gelu_exact, pre_act)[1](act_grad)[0].astype(bf16)
    up_weight_grad = left_product(first_low, pre_grad)
    up_bias_grad = column_sums(pre_grad)
    norm_grad = second_grad + right_product(pre_grad, up_mat)
    first_grad, gain_first_grad, shift_first_grad = first_back(norm_grad)
    branch_grad = first_grad.astype(bf16)
    out_weight_grad = left_product(context, branch_grad)
    out_bias_grad = column_sums(branch_grad)
    context_grad = right_product(branch_grad, out_mat).astype(bf16)
    head_grad = lax.all_to_all(context_grad, "seq", split_axis=1, concat_axis=0, tiled=True)
    grad_blocks = head_grad.reshape(blocks, block_rows, head_count, HEAD_DIM)

    def backward_step(carry, packed):
        key_acc, value_acc = carry
        query_block, grad_block, log_block = packed
        scores = block_scores(query_block)
        probs_full = jnp.exp(scores - log_block[:, :, None])
        probs_low = probs_full.astype(bf16)
        prob_grad = jnp.einsum("qhd,khd->hqk", grad_block, values_heads, preferred_element_type=f32)
        centre = jnp.sum(prob_grad * probs_full, axis=-1, keepdims=True)
        score_grad = (probs_full * (prob_grad - centre)).astype(bf16)
        query_part = (
            jnp.einsum("hqk,khd->qhd", score_grad, keys_heads, preferred_element_type=f32) * scaling
        )
        key_acc = (
            key_acc
            + jnp.einsum("hqk,qhd->khd", score_grad, query_block, preferred_element_type=f32)
            * scaling
        )
        value_acc = value_acc + jnp.einsum(
            "hqk,qhd->khd", probs_low, grad_block, preferred_element_type=f32
        )
        return ((key_acc, value_acc), query_part.astype(bf16))

    zeros_heads = jnp.zeros((slot_rows, head_count, HEAD_DIM), f32)
    (key_total, value_total), query_parts = lax.scan(
        backward_step, (zeros_heads, zeros_heads), (query_blocks, grad_blocks, log_totals)
    )
    query_back, key_back, value_back = (
        lax.all_to_all(
            query_parts.reshape(slot_rows, local_width),
            "seq",
            split_axis=0,
            concat_axis=1,
            tiled=True,
        ),
        lax.all_to_all(
            key_total.reshape(slot_rows, local_width).astype(bf16),
            "seq",
            split_axis=0,
            concat_axis=1,
            tiled=True,
        ),
        lax.all_to_all(
            value_total.reshape(slot_rows, local_width).astype(bf16),
            "seq",
            split_axis=0,
            concat_axis=1,
            tiled=True,
        ),
    )
    query_weight_grad = left_product(states, query_back)
    key_weight_grad = left_product(states, key_back)
    value_weight_grad = left_product(states, value_back)
    query_bias_grad = column_sums(query_back)
    value_bias_grad = column_sums(value_back)
    states_grad = (
        first_grad
        + right_product(query_back, query_mat)
        + right_product(key_back, key_mat)
        + right_product(value_back, value_mat)
    ).astype(bf16)
    attend_parts = (
        lax.psum_scatter(query_weight_grad, "fsdp", scatter_dimension=0, tiled=True),
        lax.psum_scatter(key_weight_grad, "fsdp", scatter_dimension=0, tiled=True),
        lax.psum_scatter(value_weight_grad, "fsdp", scatter_dimension=0, tiled=True),
        lax.psum_scatter(out_weight_grad, "fsdp", scatter_dimension=0, tiled=True),
        lax.psum_scatter(query_bias_grad, "fsdp", scatter_dimension=0, tiled=True),
        lax.psum_scatter(value_bias_grad, "fsdp", scatter_dimension=0, tiled=True),
        lax.psum_scatter(out_bias_grad, "fsdp", scatter_dimension=0, tiled=True),
        lax.psum_scatter(gain_first_grad, "fsdp", scatter_dimension=0, tiled=True),
        lax.psum_scatter(shift_first_grad, "fsdp", scatter_dimension=0, tiled=True),
    )
    feed_parts = (
        lax.psum_scatter(up_weight_grad, "fsdp", scatter_dimension=0, tiled=True),
        lax.psum_scatter(up_bias_grad, "fsdp", scatter_dimension=0, tiled=True),
        lax.psum_scatter(down_weight_grad, "fsdp", scatter_dimension=0, tiled=True),
        lax.psum_scatter(down_bias_grad, "fsdp", scatter_dimension=0, tiled=True),
        lax.psum_scatter(gain_second_grad, "fsdp", scatter_dimension=0, tiled=True),
        lax.psum_scatter(shift_second_grad, "fsdp", scatter_dimension=0, tiled=True),
    )
    summed = (
        lax.psum(attend_parts[0].astype(jnp.bfloat16), "seq").astype(jnp.float32),
        lax.psum(attend_parts[1].astype(jnp.bfloat16), "seq").astype(jnp.float32),
        lax.psum(attend_parts[2].astype(jnp.bfloat16), "seq").astype(jnp.float32),
        lax.psum(attend_parts[3].astype(jnp.bfloat16), "seq").astype(jnp.float32),
        lax.psum(attend_parts[4].astype(jnp.bfloat16), "seq").astype(jnp.float32),
        lax.psum(attend_parts[5].astype(jnp.bfloat16), "seq").astype(jnp.float32),
        lax.psum(attend_parts[6].astype(jnp.bfloat16), "seq").astype(jnp.float32),
        lax.psum(attend_parts[7].astype(jnp.bfloat16), "seq").astype(jnp.float32),
        lax.psum(attend_parts[8].astype(jnp.bfloat16), "seq").astype(jnp.float32),
        lax.psum(feed_parts[0].astype(jnp.bfloat16), "seq").astype(jnp.float32),
        lax.psum(feed_parts[1].astype(jnp.bfloat16), "seq").astype(jnp.float32),
        lax.psum(feed_parts[2].astype(jnp.bfloat16), "seq").astype(jnp.float32),
        lax.psum(feed_parts[3].astype(jnp.bfloat16), "seq").astype(jnp.float32),
        lax.psum(feed_parts[4].astype(jnp.bfloat16), "seq").astype(jnp.float32),
        lax.psum(feed_parts[5].astype(jnp.bfloat16), "seq").astype(jnp.float32),
    )
    return (
        output,
        states_grad,
        summed[0],
        summed[1],
        summed[2],
        summed[3],
        summed[4],
        summed[5],
        summed[6],
        summed[7],
        summed[8],
        summed[9],
        summed[10],
        summed[11],
        summed[12],
        summed[13],
        summed[14],
    )


LANE = 128
LOG2E = math.log2(math.e)
LN2 = math.log(2.0)
NT = (((1,), (1,)), ((), ()))
NN = (((1,), (0,)), ((), ()))
TN = (((0,), (0,)), ((), ()))
VMEM_BYTES = 66 * 1024 * 1024 - 2 * 1024 * 1024
f32 = jnp.float32
bf16 = jnp.bfloat16
ANY = pl.BlockSpec(memory_space=pl.ANY)
IN_VMEM = pl.BlockSpec(memory_space=pltpu.VMEM)
IN_SMEM = pl.BlockSpec(memory_space=pltpu.SMEM)
DMA = pltpu.SemaphoreType.DMA


def dims(left, right, numbers):
    return lax.dot_general(left, right, numbers, preferred_element_type=f32)


def remote(src, dst, send_sem, recv_sem, **where):
    return pltpu.make_async_remote_copy(
        src_ref=src,
        dst_ref=dst,
        send_sem=send_sem,
        recv_sem=recv_sem,
        device_id=where,
        device_id_type=pl.DeviceIdType.MESH,
    )


def hail(partners):
    barrier = pltpu.get_barrier_semaphore()
    for where in partners:
        pl.semaphore_signal(barrier, inc=1, device_id=where, device_id_type=pl.DeviceIdType.MESH)


def hailed(partners):
    pl.semaphore_wait(pltpu.get_barrier_semaphore(), len(partners))


def greet(partners):
    hail(partners)
    hailed(partners)


def seq_peers():
    me = lax.axis_index("seq")
    across = (me + 2) % 4
    return me, me + 1 - 2 * (me % 2), across, across + 1 - 2 * (across % 2)


def place_of(index, count):
    half = index // 2
    return half + (index % 2) * (count - 1 - 2 * half)


def index_at(place, count):
    upper = place // (count // 2)
    return (1 - upper) * 2 * place + upper * (2 * (count - 1 - place) + 1)


def thirds(values):
    high = values.astype(bf16)
    rest = values - high.astype(f32)
    middle = rest.astype(bf16)
    low = (rest - middle.astype(f32)).astype(bf16)
    return high.astype(f32), middle.astype(f32), low.astype(f32)


def with_lanes(base, columns):
    lane = lax.broadcasted_iota(jnp.int32, base.shape, 1)
    for place, values in columns:
        base = jnp.where(lane == place, values, base)
    return base


def params(collective_id=None):
    if collective_id is None:
        return pltpu.CompilerParams(vmem_limit_bytes=VMEM_BYTES)
    return pltpu.CompilerParams(
        vmem_limit_bytes=VMEM_BYTES, collective_id=collective_id, has_side_effects=True
    )


def ring_gather(nf, shards, halves, outs, ring_send, ring_recv, pair_send, pair_recv):
    f = lax.axis_index("fsdp")
    s, near, _, _ = seq_peers()
    side = s % 2
    step = 1 - 2 * side
    place = place_of(f, nf)
    ahead = index_at((place + step + nf) % nf, nf)

    def half(ref, w):
        axis, size = halves[w]
        cut = pl.ds(pl.multiple_of(side * size, size), size)
        return ref.at[cut, :] if axis == 0 else ref.at[:, cut]

    def slot(hop):
        return index_at((place + nf - step * (hop + 1)) % nf, nf)

    def ring(w, hop, owner, source):
        return remote(
            half(source, w),
            half(outs[w].at[owner], w),
            ring_send.at[w, hop],
            ring_recv.at[w, hop],
            fsdp=ahead,
        )

    def pair(w, hop):
        piece = half(outs[w].at[slot(hop)], w)
        return remote(piece, piece, pair_send.at[w, hop], pair_recv.at[w, hop], seq=near)

    def start(w):
        ring(w, 0, f, shards[w]).start()

    def hop(w, h):
        owner = slot(h)
        ring(w, h, owner, outs[w].at[owner]).wait_recv()

        @pl.when(h < nf - 2)
        def _():
            ring(w, h + 1, owner, outs[w].at[owner]).start()

        pair(w, h).start()

    def finish(w, h):
        ring(w, h, f, shards[w]).wait_send()
        pair(w, h).wait()

    return start, hop, finish


def front_kernel(
    nf, block, key_chunk, halves, groups,
    length_ref, states, wq, wk, wv, wout_s, up_s, down_s, *refs,
):
    small_params, refs = refs[:9], refs[9:]
    (
qb_out, o_out, k_out, v_out, x_out, vec_out, ctx_out, wout, up, down,
        q_buf, k_buf, v_buf, qb_buf, o_buf, s_buf, top_buf, ctx_buf, x_buf, w_buf, w_own, packed, vec_own, vec_buf,
        wout_buf, up_buf, down_buf, local_sem, x_sem, kv_sem, keep_sem, vec_send, vec_recv, z_send, z_recv, h_send, h_recv,
        near_send, near_recv, far_send, far_recv, pass_send, pass_recv,
        ring_send, ring_recv, pair_send, pair_recv, ctx_send, ctx_recv, own_sem, copy_sem,
    ) = refs
    f = lax.axis_index("fsdp")
    s, near, far, cross = seq_peers()
    tokens, width = states.shape
    heads, slots, _ = q_buf.shape
    rows = wq.shape[0]
    window = w_buf.shape[2]
    vec_rows = vec_buf.shape[1]
    own_width = heads * 64
    parts = far_send.shape[0]
    chunk = tokens // parts
    per = tokens // block
    beside = f + 1 - 2 * (f % 2)
    stages = nf // 2
    first_lane = pl.multiple_of((own_width * s // LANE) * LANE, LANE)
    weights = (wq, wk, wv)
    shards, outs = (wout_s, up_s, down_s), (wout, up, down)
    ring_start, ring_hop, ring_finish = ring_gather(
        nf, shards, halves, outs, ring_send, ring_recv, pair_send, pair_recv
    )
    friends = [{"fsdp": (f + d) % nf} for d in range(1, nf)] + [
        {"seq": near}, {"seq": far}, {"seq": cross},
    ]
    hail(friends)

    def along(d):
        to = (f + 2 * d) % nf
        return remote(packed.at[f], packed.at[f], z_send.at[d - 1], z_recv.at[d - 1], fsdp=to)

    def aside(d):
        owner = (f + nf - 2 * d) % nf
        return remote(packed.at[owner], packed.at[owner], h_send.at[d], h_recv.at[d], fsdp=beside)

    def vec_copy(d):
        return remote(
            vec_buf.at[f], vec_buf.at[f], vec_send.at[d - 1], vec_recv.at[d - 1],
            fsdp=(f + d) % nf,
        )

    def far_copy(c):
        at = pl.ds(c * chunk, chunk)
        return remote(states.at[at], x_buf.at[2, at], far_send.at[c], far_recv.at[c], seq=far)

    def pass_copy(c):
        at = pl.ds(c * chunk, chunk)
        return remote(
            x_buf.at[2, at], x_buf.at[3, at], pass_send.at[c], pass_recv.at[c], seq=near
        )

    near_copy = remote(states, x_buf.at[1], near_send, near_recv, seq=near)
    windows = [
        pltpu.make_async_copy(
            weights[m].at[:, pl.ds(first_lane, window)], w_own.at[m], local_sem.at[1 + m]
        )
        for m in range(3)
    ]
    local = [pltpu.make_async_copy(states, x_buf.at[0], local_sem.at[0])]
    for copy in windows + local:
        copy.start()
    vec_own[...] = jnp.zeros_like(vec_own)
    for r in range(8):
        vec_own[r : r + 1, :rows] = small_params[r][...].astype(f32).reshape(1, rows)
    line = small_params[8][...].astype(f32).reshape(1, 4 * rows)
    for r in range(4):
        vec_own[8 + r : 9 + r, :rows] = line[:, rows * r : rows * (r + 1)]
    vec_buf[f] = vec_own[...].astype(bf16)
    turn = (window - (own_width * s) % LANE) % window
    for m in range(3):
        windows[m].wait()
        columns = pltpu.roll(w_own[m].astype(f32), turn, 1)[:, :own_width]
        packed[f, m] = jnp.concatenate(
            [columns[: rows // 2], columns[rows // 2 :]], axis=1
        ).astype(bf16)
    hailed(friends)
    for d in range(1, stages):
        along(d).start()
    aside(0).start()
    for c in range(parts):
        far_copy(c).start()
    near_copy.start()
    for d in range(1, nf):
        vec_copy(d).start()
    for w in groups[0] + groups[1]:
        ring_start(w)
    held = (wout_buf, up_buf, down_buf)
    mine = [
        pltpu.make_async_copy(shards[w], held[w], copy_sem.at[0, w]) for w in range(len(shards))
    ]
    for copy in mine:
        copy.start()
    for copy in local:
        copy.wait()
    kept = []

    def keep(slot, index):
        copy = pltpu.make_async_copy(x_buf.at[slot], x_out.at[index], x_sem.at[slot])
        copy.start()
        kept.append(copy)

    def pass_on(c):
        far_copy(c).wait_recv()
        pass_copy(c).start()

    def turn_aside(d):
        along(d).wait_recv()
        aside(d).start()

    keep(0, s)
    for copy in mine:
        copy.wait()
    mine = [
        pltpu.make_async_copy(held[w], outs[w].at[f], copy_sem.at[1, w]) for w in range(len(shards))
    ]
    for copy in mine:
        copy.start()
    passed = 0
    for d in range(1, stages):
        turn_aside(d)
        if d != 2 and passed < parts - 2:
            pass_on(passed)
            passed += 1
    for d in range(1, nf):
        vec_copy(d).wait_recv()
    for d in range(stages):
        aside(d).wait_recv()
    gap = jnp.zeros((rows // 2, window - own_width), f32)
    for j in range(nf):
        for m in range(3):
            both = packed[j, m].astype(f32)
            for e in range(2):
                at = pl.ds(rows * j + rows // 2 * e, rows // 2)
                columns = both[:, own_width * e : own_width * (e + 1)]
                w_buf[m, at, :] = jnp.concatenate([columns, gap], axis=1).astype(bf16)
    share = own_width // rows
    wide = lax.broadcasted_iota(jnp.int32, (1, window), 1)
    biases = []
    for row in (0, 1):
        line = jnp.zeros((1, window), f32)
        for i in range(share):
            piece = vec_buf[share * s + i][row : row + 1, :].astype(f32)
            piece = jnp.concatenate([piece, jnp.zeros((1, window - LANE), f32)], axis=1)
            if i:
                piece = pltpu.roll(piece, i * rows, 1)
            line = jnp.where((wide >= i * rows) & (wide < (i + 1) * rows), piece, line)
        biases.append(line)
    length = length_ref[0]
    mats = [w_buf[m] for m in range(3)]
    small = lax.broadcasted_iota(jnp.int32, (chunk, LANE), 1)
    q_tail = jnp.where(small == 64, 1.0, 0.0)
    v_tail = jnp.where((small >= 64) & (small < 67), 1.0, 0.0)

    def heads_of(values, tail):
        found = []
        for h in range(heads):
            tile = values[:, (h // 2) * LANE : (h // 2 + 1) * LANE]
            if h % 2:
                tile = pltpu.roll(tile, 64, 1)
            found.append(jnp.where(small < 64, tile, tail).astype(bf16))
        return found

    def compute(slot, index, part):
        x = x_buf[slot, pl.ds(pl.multiple_of(part * chunk, chunk), chunk), :]
        start = pl.multiple_of(index * tokens + part * chunk, chunk)
        where = start + lax.broadcasted_iota(jnp.int32, (chunk, LANE), 0)
        queries = dims(x, mats[0], NN) + biases[0]
        keys = dims(x, mats[1], NN)
        k_tail = jnp.where(
            small == 64,
            jnp.where(where < length, 0.0, -1e9),
            jnp.where((small > 64) & (small < 68), 1.0, 0.0),
        )
        values = dims(x, mats[2], NN) + biases[1]
        at = pl.ds(start, chunk)
        for ref, found in (
            (q_buf, heads_of(queries * (LOG2E * 0.125), q_tail)),
            (k_buf, heads_of(keys, k_tail)),
            (v_buf, heads_of(values, v_tail)),
        ):
            for h in range(heads):
                ref[h, at, :] = found[h]

    def whole(slot, index, low, high):
        def body(part, carry):
            compute(slot, index, part)
            return carry

        lax.fori_loop(low, high, body, 0)

    def hops(g, h):
        for w in groups[g]:
            ring_hop(w, h)

    hops(0, 0)
    hops(1, 0)
    whole(0, s, 0, parts)
    for c in range(passed, parts - 1):
        pass_on(c)
    near_copy.wait_recv()
    keep(1, near)
    whole(1, near, 0, parts)
    hops(0, 1)
    whole(2, far, 0, parts - 1)
    pass_on(parts - 1)
    hops(1, 1)
    whole(2, far, parts - 1, parts)
    keep(2, far)
    for c in range(parts):
        pass_copy(c).wait_recv()
    keep(3, cross)
    whole(3, cross, 0, parts)
    hops(0, 2)
    saved = [
        pltpu.make_async_copy(k_buf, k_out, kv_sem.at[0]),
        pltpu.make_async_copy(v_buf, v_out, kv_sem.at[1]),
        pltpu.make_async_copy(vec_buf, vec_out, kv_sem.at[2]),
    ]
    for copy in saved:
        copy.start()

    lane = lax.broadcasted_iota(jnp.int32, (block, LANE), 1)

    def partner(round_):
        relation = 3 - round_
        return ((s // 2 + relation // 2) % 2) * 2 + (s % 2 + relation % 2) % 2

    def ctx_copy(step):
        at = pl.ds(pl.multiple_of(step % per * block, block), block)
        return remote(
            ctx_buf.at[step],
            ctx_out.at[s, at],
            ctx_send.at[step],
            ctx_recv.at[step],
            seq=partner(step // per),
        )

    def rows_of(step):
        base = partner(step // per) * tokens + step % per * block
        return pl.ds(pl.multiple_of(base, block), block)

    def keep_copies(step):
        at = rows_of(step)
        return (
            pltpu.make_async_copy(qb_buf.at[:, at], qb_out.at[:, at], keep_sem.at[0, step]),
            pltpu.make_async_copy(o_buf.at[:, at], o_out.at[:, at], keep_sem.at[1, step]),
        )

    chunks = slots // key_chunk

    def score(h, at, c):
        return dims(q_buf[h, at, :], k_buf[h, c * key_chunk : (c + 1) * key_chunk, :], NT)

    def highest(values, top):
        for j in range(key_chunk // LANE):
            tile = values[:, j * LANE : (j + 1) * LANE]
            top = tile if top is None else jnp.maximum(top, tile)
        return top

    top = None
    for c in range(chunks):
        scores = score(0, rows_of(0), c)
        s_buf[:, c * key_chunk : (c + 1) * key_chunk] = scores
        top = highest(scores, top)
    top_buf[...] = top

    def attend(step, carry):
        at = rows_of(step)
        after = rows_of(jnp.minimum(step + 1, 4 * per - 1))
        results = []
        current = [s_buf[:, c * key_chunk : (c + 1) * key_chunk] for c in range(chunks)]
        top = top_buf[...]
        for h in range(heads):
            peak = jnp.max(top, axis=1, keepdims=True)
            total = None
            coming = []
            top = None
            for c in range(chunks):
                scores = score(h + 1, at, c) if h + 1 < heads else score(0, after, c)
                coming.append(scores)
                top = highest(scores, top)
                probs = jnp.exp2(current[c] - peak).astype(bf16)
                term = dims(probs, v_buf[h, c * key_chunk : (c + 1) * key_chunk, :], NN)
                total = term if total is None else total + term
            current = coming
            weight = total[:, 64:65]
            result = jnp.where(lane < 64, total * (1.0 / weight), 0.0)
            o_buf[h, at, :] = result.astype(bf16)
            high, middle, low = thirds(-(peak + jnp.log2(weight)))
            qb_buf[h, at, :] = with_lanes(
                q_buf[h, at, :].astype(f32), ((65, high), (66, middle), (67, low))
            ).astype(bf16)
            results.append(result)
        for c in range(chunks):
            s_buf[:, c * key_chunk : (c + 1) * key_chunk] = current[c]
        top_buf[...] = top
        for t in range((heads + 1) // 2):
            tile = results[2 * t]
            if 2 * t + 1 < heads:
                tile = tile + pltpu.roll(results[2 * t + 1], 64, 1)
            ctx_buf[step, :, t * LANE : (t + 1) * LANE] = tile.astype(bf16)

        @pl.when(step < 3 * per)
        def _():
            ctx_copy(step).start()

        for copy in keep_copies(step):
            copy.start()
        for g in range(2):
            late = 2 * (1 - g)
            h = (2 * step - late + 1) // 5
            @pl.when(((5 * h + late) // 2 == step) & (h + 3 - g < nf - 1))
            def _():
                hops(g, h + 3 - g)

        return carry

    lax.fori_loop(0, 4 * per, attend, 0)
    owns = []
    for i in range(per):
        owns.append(
            pltpu.make_async_copy(
                ctx_buf.at[3 * per + i], ctx_out.at[s, pl.ds(i * block, block)], own_sem.at[i]
            )
        )
        owns[-1].start()

    def rest(h, carry):
        for w in range(len(shards)):
            ring_hop(w, h)
        return carry

    lax.fori_loop(min(7, nf - 1), nf - 1, rest, 0)

    def settle(step, carry):
        @pl.when(step < 3 * per)
        def _():
            ctx_copy(step).wait()

        for copy in keep_copies(step):
            copy.wait()
        return carry

    lax.fori_loop(0, 4 * per, settle, 0)
    for d in range(1, stages):
        along(d).wait_send()
    for d in range(stages):
        aside(d).wait_send()
    for d in range(1, nf):
        vec_copy(d).wait_send()
    for c in range(parts):
        far_copy(c).wait_send()
        pass_copy(c).wait_send()
    near_copy.wait_send()
    for copy in owns + mine + kept + saved:
        copy.wait()

    def close(h, carry):
        for w in range(len(shards)):
            ring_finish(w, h)
        return carry

    lax.fori_loop(0, nf - 1, close, 0)


def front(nf, heads, length, states, wq, wk, wv, wout, up, down, small_params, block, key_chunk):
    tokens, width = states.shape
    rows = wq.shape[0]
    slots = 4 * tokens
    parts = 4
    window = 256
    shards = (wout, up, down)
    halves = tuple((1, w.shape[1] // 2) for w in shards)
    wide = -(-heads // 2) * LANE
    steps = slots // block
    shape = jax.ShapeDtypeStruct
    head_shape = shape((heads, slots, LANE), bf16)
    head_buf = pltpu.VMEM((heads, slots, LANE), bf16)
    hops = DMA((3, nf - 1))
    stage = DMA((nf // 2 - 1,))
    stage_aside = DMA((nf // 2,))
    peers = DMA((nf - 1,))
    fine = DMA((parts,))
    return pl.pallas_call(
        functools.partial(front_kernel, nf, block, key_chunk, halves, ((1,), (0, 2))),
        out_shape=[head_shape] * 4
        + [
            shape((4, tokens, width), bf16),
            shape((nf, 16, LANE), bf16),
            shape((4, tokens, wide), bf16),
        ]
        + [shape((nf,) + w.shape, bf16) for w in shards],
        in_specs=[IN_SMEM] + [ANY] * 7 + [IN_VMEM] * 9,
        out_specs=[ANY] * 10,
        scratch_shapes=[head_buf] * 5
        + [
            pltpu.VMEM((block, slots), f32),
            pltpu.VMEM((block, LANE), f32),
            pltpu.VMEM((steps, block, wide), bf16),
            pltpu.VMEM((4, tokens, width), bf16),
            pltpu.VMEM((3, width, window), bf16),
            pltpu.VMEM((3, rows, window), bf16),
            pltpu.VMEM((nf, 3, rows // 2, heads * 128), bf16),
            pltpu.VMEM((16, LANE), f32),
            pltpu.VMEM((nf, 16, LANE), bf16),
        ]
        + [pltpu.VMEM(w.shape, bf16) for w in shards]
        + [
            DMA((5,)),
            DMA((4,)),
            DMA((3,)),
            DMA((2, steps)),
            peers, peers, stage, stage, stage_aside, stage_aside,
            DMA(()), DMA(()), fine, fine, fine, fine,
            hops, hops, hops, hops,
            DMA((steps,)), DMA((steps,)),
            DMA((tokens // block,)),
            DMA((2, 3)),
        ],
        compiler_params=params(1),
        name="front",
    )(length, states, wq, wk, wv, wout, up, down, *small_params)


def plane_gather(nf, shards, outs, z_send, z_recv, h_send, h_recv, n_send, n_recv):
    f = lax.axis_index("fsdp")
    s, near, _, _ = seq_peers()
    side = s % 2
    beside = f + 1 - 2 * (f % 2)
    stages = nf // 2
    count = len(shards)

    def half(ref):
        size = ref.shape[1] // 2
        return ref.at[:, pl.ds(pl.multiple_of(side * size, size), size)]

    def along(d, m):
        return remote(
            half(shards[m]), half(outs[m].at[f]), z_send.at[d - 1, m], z_recv.at[d - 1, m],
            fsdp=(f + 2 * d) % nf,
        )

    def aside(d, m):
        owner = (f + nf - 2 * d) % nf
        source = outs[m].at[owner] if d else shards[m]
        return remote(
            half(source), half(outs[m].at[owner]), h_send.at[d, m], h_recv.at[d, m], fsdp=beside
        )

    def share(e, m):
        owner = (f + nf - 2 * e) % nf if e < stages else (beside + nf - 2 * (e - stages)) % nf
        piece = half(outs[m].at[owner])
        return remote(piece, piece, n_send.at[e - 1, m], n_recv.at[e - 1, m], seq=near)

    def start():
        for d in range(1, stages):
            for m in range(count):
                along(d, m).start()
        for m in range(count):
            aside(0, m).start()

    def first():
        for d in range(1, stages):
            for m in range(count):
                along(d, m).wait_recv()
                aside(d, m).start()
                share(d, m).start()

    def second():
        for d in range(stages):
            for m in range(count):
                aside(d, m).wait_recv()
                share(stages + d, m).start()

    def finish():
        for m in range(count):
            for d in range(1, stages):
                along(d, m).wait_send()
            for d in range(stages):
                aside(d, m).wait_send()
            for e in range(1, nf):
                share(e, m).wait()

    return start, first, second, finish


def feed_kernel(
    nf, block, part, length_ref, vec_all, states_hbm, ctx_hbm, wout_hbm, up_hbm, down_hbm, cot_hbm,
    wq_s, wk_s, wv_s,
    out, first_grad_out, gctx, up_sum, down_sum, wout_sum, gvec, wq, wk, wv,
    states, ctx, wout, up, down, cot, held, vec, upb, out_buf, first_buf, act_buf, pre_buf, slope_buf, low_t, down_t, branch_buf,
    g_buf, up_give, down_give, wout_give, up_take, down_take, wout_take,
    load_sem, keep_sem, g_send, g_recv, own_sem, give_send, give_recv, sum_sem, shard_sem,
    z_send, z_recv, h_send, h_recv, n_send, n_recv,
):
    f = lax.axis_index("fsdp")
    s, near, far, cross = seq_peers()
    side = s % 2
    beside = f + 1 - 2 * (f % 2)
    tokens, width = states.shape
    hidden = up.shape[1]
    own = wout.shape[0] // 4
    steps = tokens // block
    wide = ctx.shape[2]
    loads = [
        pltpu.make_async_copy(up_hbm, up, load_sem.at[0]),
        pltpu.make_async_copy(down_hbm, down, load_sem.at[1]),
        pltpu.make_async_copy(cot_hbm, cot, load_sem.at[2]),
    ]
    early = [
        pltpu.make_async_copy(wout_hbm, wout, load_sem.at[3]),
        pltpu.make_async_copy(ctx_hbm, ctx, load_sem.at[4]),
        pltpu.make_async_copy(states_hbm, states, load_sem.at[5]),
    ]
    for copy in early + loads:
        copy.start()
    shards, outs = (wq_s, wk_s, wv_s), (wq, wk, wv)
    gather = plane_gather(nf, shards, outs, z_send, z_recv, h_send, h_recv, n_send, n_recv)
    friends = [{"fsdp": (f + 2 * d) % nf} for d in range(1, nf // 2)] + [
        {"fsdp": beside}, {"seq": near}, {"seq": far}, {"seq": cross},
    ]
    hail(friends)
    rows = width // nf
    short = lax.broadcasted_iota(jnp.int32, vec_all.shape[1:], 1) < rows
    lines = jnp.zeros((vec_all.shape[1], width), f32)
    blank = jnp.zeros((vec_all.shape[1], width - LANE), f32)
    tiles = [jnp.zeros((1, LANE), f32) for _ in range(hidden // LANE)]
    for j in range(nf):
        piece = jnp.where(short, vec_all[j].astype(f32), 0.0)
        both = jnp.concatenate([piece, blank], axis=1)
        lines = lines + (pltpu.roll(both, rows * j, 1) if j else both)
        for r in range(4):
            first_lane = rows * (4 * j + r)
            tile, shift = first_lane // LANE, first_lane % LANE
            both = jnp.concatenate([piece[8 + r : 9 + r, :], blank[:1, :LANE]], axis=1)
            if shift:
                both = pltpu.roll(both, shift, 1)
            tiles[tile] = tiles[tile] + both[:, :LANE]
            if tile + 1 < len(tiles):
                tiles[tile + 1] = tiles[tile + 1] + both[:, LANE:]
    vec[...] = lines[:8]
    upb[...] = jnp.concatenate(tiles, axis=1)
    kept = [pltpu.make_async_copy(shards[m], held.at[m], shard_sem.at[0, m]) for m in range(3)]
    for copy in kept:
        copy.start()
    kept_out = [
        pltpu.make_async_copy(held.at[m], outs[m].at[f], shard_sem.at[1, m]) for m in range(3)
    ]
    length = length_ref[0]
    gvec[...] = jnp.zeros_like(gvec)
    peers = (s, near, far, cross)

    def line(row):
        return vec[row : row + 1, :]

    def add_line(row, values):
        gvec[row : row + 1, :] += jnp.sum(values, axis=0, keepdims=True)

    def norm(values):
        centred = values - jnp.mean(values, axis=1, keepdims=True)
        scale = lax.rsqrt(jnp.mean(centred * centred, axis=1, keepdims=True) + eps)
        return centred * scale, scale

    def norm_back(grad, gain, normed, scale):
        grad = grad * gain
        return scale * (
            grad
            - jnp.mean(grad, axis=1, keepdims=True)
            - normed * jnp.mean(grad * normed, axis=1, keepdims=True)
        )

    def rows_of(i):
        return pl.ds(pl.multiple_of(i * block, block), block)

    def send(relation, i):
        at = rows_of(i)
        return remote(
            g_buf.at[relation, at],
            gctx.at[s, at],
            g_send.at[relation - 1, i],
            g_recv.at[relation - 1, i],
            seq=peers[relation],
        )

    def keep(i):
        at = rows_of(i)
        return (
            pltpu.make_async_copy(out_buf.at[at], out.at[at], keep_sem.at[0, i]),
            pltpu.make_async_copy(first_buf.at[at], first_grad_out.at[at], keep_sem.at[1, i]),
        )

    def body(i, carry):
        at = rows_of(i)
        attended = None
        for j in range(4):
            term = dims(ctx[j, at, :own], wout[own * j : own * (j + 1), :], NN)
            attended = term if attended is None else attended + term
        normed_first, scale_first = norm(states[at, :].astype(f32) + (attended + line(2)))
        first = normed_first * line(3) + line(4)
        low = first.astype(bf16)
        low_t[:, at] = jnp.transpose(low)

        @pl.when(i == 0)
        def _():
            hailed(friends)
            gather[0]()
            for copy in kept + loads:
                copy.wait()
            for copy in kept_out:
                copy.start()

        fed = None
        for c in range(hidden // part):
            cut = slice(c * part, (c + 1) * part)
            pre = dims(low, up[:, cut], NN) + upb[:, cut]
            share = 0.5 + 0.5 * lax.erf(pre * (2.0**-0.5))
            slope_buf[:, cut] = share + pre * jnp.exp(-0.5 * pre * pre) * (2.0 * math.pi) ** -0.5
            act = (pre * share).astype(bf16)
            act_buf[at, cut] = act
            term = dims(act, down[cut, :], NN)
            fed = term if fed is None else fed + term
        normed, scale = norm(first + (fed + line(5)))
        place = s * tokens + i * block + lax.broadcasted_iota(jnp.int32, (block, 1), 0)
        valid = jnp.where(place < length, 1.0, 0.0)
        out_buf[at, :] = ((normed * line(6) + line(7)) * valid).astype(bf16)
        grad = cot[at, :].astype(f32) * valid
        add_line(6, grad * normed)
        add_line(7, grad)
        second_grad = norm_back(grad, line(6), normed, scale)
        down_in = second_grad.astype(bf16)
        add_line(5, down_in.astype(f32))
        down_t[:, at] = jnp.transpose(down_in)
        back = second_grad
        for c in range(hidden // part):
            cut = slice(c * part, (c + 1) * part)
            pre_grad = (dims(down_in, down[cut, :], NT) * slope_buf[:, cut]).astype(bf16)
            pre_buf[at, cut] = pre_grad
            row = 8 + c * part // width
            col = c * part % width
            gvec[row : row + 1, col : col + part] += jnp.sum(
                pre_grad.astype(f32), axis=0, keepdims=True
            )
            back = back + dims(pre_grad, up[:, cut], NT)
        add_line(3, back * normed_first)
        add_line(4, back)
        first_grad = norm_back(back, line(3), normed_first, scale_first)
        first_buf[at, :] = first_grad
        branch = first_grad.astype(bf16)
        branch_buf[at, :] = branch
        add_line(2, branch.astype(f32))
        for relation in range(4):
            rows = pl.ds(pl.multiple_of(peers[relation] * own, 64), own)
            g_buf[relation, at, :own] = dims(branch, wout[rows, :], NT).astype(bf16)
            if wide > own:
                g_buf[relation, at, own:] = jnp.zeros((block, wide - own), bf16)
            if relation:
                send(relation, i).start()
        for copy in keep(i):
            copy.start()

        @pl.when(i == min(1, steps - 1))
        def _():
            gather[1]()

        return carry

    for copy in early:
        copy.wait()
    lax.fori_loop(0, steps, body, 0)
    mine = pltpu.make_async_copy(g_buf.at[0], gctx.at[s], own_sem)
    mine.start()

    pieces = give_send.shape[1]
    up_cut = hidden // 2 // pieces
    down_cut = hidden // pieces

    def up_part(which, c):
        cut = pl.ds(pl.multiple_of(which * (hidden // 2) + c * up_cut, up_cut), up_cut)
        return dims(low_t[...], pre_buf[:, cut], NN)

    def down_part(which, c):
        rows = pl.ds(pl.multiple_of(which * (width // 2), width // 2), width // 2)
        cut = pl.ds(pl.multiple_of(c * down_cut, down_cut), down_cut)
        return dims(down_t[rows, :], act_buf[:, cut], NN)

    def wout_part(which, j):
        cut = pl.ds(pl.multiple_of(which * (width // 2), width // 2), width // 2)
        return dims(ctx[j, :, :own], branch_buf[:, cut], TN)

    def cols(c, size):
        return (slice(None), pl.ds(pl.multiple_of(c * size, size), size))

    def give(w, c):
        if w == 2:
            pair = wout_give, wout_take
        else:
            at = cols(c, (up_cut, down_cut)[w])
            pair = (up_give, down_give)[w].at[at], (up_take, down_take)[w].at[at]
        return remote(*pair, give_send.at[w, c], give_recv.at[w, c], seq=near)

    def give_away(c, carry):
        up_give[cols(c, up_cut)] = up_part(1 - side, c).astype(bf16)
        give(0, c).start()
        down_give[cols(c, down_cut)] = down_part(1 - side, c).astype(bf16)
        give(1, c).start()
        return carry

    def add_own(c, carry):
        at = cols(c, up_cut)
        total = up_part(side, c)
        give(0, c).wait()
        up_give[at] = (total + up_take[at].astype(f32)).astype(bf16)
        at = cols(c, down_cut)
        total = down_part(side, c)
        give(1, c).wait()
        down_give[at] = (total + down_take[at].astype(f32)).astype(bf16)
        return carry

    lax.fori_loop(0, pieces, give_away, 0)
    for j in range(4):
        wout_give[own * j : own * (j + 1), :] = wout_part(1 - side, j).astype(bf16)
    give(2, 0).start()
    gather[2]()
    lax.fori_loop(0, pieces, add_own, 0)
    sums = [
        pltpu.make_async_copy(up_give, up_sum, sum_sem.at[0]),
        pltpu.make_async_copy(down_give, down_sum, sum_sem.at[1]),
    ]
    for copy in sums:
        copy.start()
    totals = [wout_part(side, j) for j in range(4)]
    give(2, 0).wait()
    for j in range(4):
        at = slice(own * j, own * (j + 1))
        wout_give[at, :] = (totals[j] + wout_take[at, :].astype(f32)).astype(bf16)
    sums.append(pltpu.make_async_copy(wout_give, wout_sum, sum_sem.at[2]))
    sums[-1].start()
    for relation in range(1, 4):
        for i in range(steps):
            send(relation, i).wait()
    for i in range(steps):
        for copy in keep(i):
            copy.wait()
    gather[3]()
    for copy in [mine] + kept_out + sums:
        copy.wait()


def feed(nf, length, states, cot, ctx, wout, up, down, vec_all, shards, block=256, part=768):
    tokens, width = states.shape
    hidden = up.shape[1]
    wide = ctx.shape[2]
    pieces = 3
    shape = jax.ShapeDtypeStruct
    halves = ((width, hidden // 2), (width // 2, hidden), (width, width // 2))
    vmem = lambda *size: pltpu.VMEM(size, bf16)
    steps = tokens // block
    staged = DMA((nf // 2 - 1, 3))
    staged_aside = DMA((nf // 2, 3))
    return pl.pallas_call(
        functools.partial(feed_kernel, nf, block, part),
        out_shape=[
            shape((tokens, width), bf16),
            shape((tokens, width), f32),
            shape((4, tokens, wide), bf16),
        ]
        + [shape(x, bf16) for x in halves]
        + [shape((16, width), f32)]
        + [shape((nf,) + w.shape, bf16) for w in shards],
        in_specs=[IN_SMEM, IN_VMEM] + [ANY] * 9,
        out_specs=[ANY] * 6 + [IN_VMEM] + [ANY] * 3,
        scratch_shapes=[
            vmem(*states.shape),
            vmem(*ctx.shape),
            vmem(*wout.shape),
            vmem(width, hidden),
            vmem(hidden, width),
            vmem(tokens, width),
            vmem(3, *shards[0].shape),
            pltpu.VMEM((8, width), f32),
            pltpu.VMEM((1, hidden), f32),
            vmem(tokens, width),
            pltpu.VMEM((tokens, width), f32),
            vmem(tokens, hidden),
            vmem(tokens, hidden),
            pltpu.VMEM((block, hidden), f32),
            vmem(width, tokens),
            vmem(width, tokens),
            vmem(tokens, width),
            vmem(4, tokens, wide),
        ]
        + [vmem(*x) for x in halves] * 2
        + [
            DMA((6,)),
            DMA((2, steps)),
            DMA((3, steps)),
            DMA((3, steps)),
            DMA(()),
            DMA((3, pieces)),
            DMA((3, pieces)),
            DMA((3,)),
            DMA((2, 3)),
            staged, staged, staged_aside, staged_aside,
            DMA((nf - 1, 3)), DMA((nf - 1, 3)),
        ],
        compiler_params=params(3),
        name="feed",
    )(length, vec_all, states, ctx, wout, up, down, cot, *shards)


def back_kernel(
    nf, key_block, groups, q_ref, k_ref, v_ref, o_ref, gctx_ref,
    up_sum, down_sum, wout_sum, x_hbm, wq_hbm, wk_hbm, wv_hbm, first_hbm, gvec_hbm,
    states_grad, up_out, down_out, wout_out, qkv_out, vec_out, upb_out,
    k_acc, v_acc, q_acc, g_buf, q_turned, g_turned, d_out, g_all, x_all, w_all, first_grad,
    own_up, own_dn, own_wo, ring_up, ring_dn, ring_wo, y_up, y_dn, y_wo, z_up, z_dn, z_wo,
    w_buf, w_came, w_sum, w_parts, v_own, v_cut, v_came, v_sum, v_parts,
    load_sem, late_sem, hop_send, hop_recv, y_send, y_recv, z_send, z_recv,
    d_send, d_recv, d_own, w_send, w_recv, p_send, p_recv, l_send, l_recv, m_send, m_recv,
):
    half, h = pl.program_id(0), pl.program_id(1)
    count = w_buf.shape[0]
    f = lax.axis_index("fsdp")
    s, near, far, cross = seq_peers()
    peers = (s, near, far, cross)
    side = s % 2
    way = 1 - 2 * side
    place = place_of(f, nf)
    ahead = index_at((place + way + nf) % nf, nf)
    slots = k_ref.shape[1]
    tokens = slots // 4
    block = tokens
    width = x_all.shape[2]
    rows = width // nf
    width_own = count * 64
    full = (up_sum, down_sum, wout_sum)
    own = (own_up, own_dn, own_wo)
    came = (ring_up, ring_dn, ring_wo)
    y_buf = (y_up, y_dn, y_wo)
    z_buf = (z_up, z_dn, z_wo)
    outs = (up_out, down_out, wout_out)
    by_cols = (False, True, False)

    def chunk_at(w, chunk):
        size = came[w].shape[1 + by_cols[w]]
        cut = pl.ds(pl.multiple_of(chunk * size, size), size)
        return (slice(None), cut) if by_cols[w] else (cut, slice(None))

    def hop(w, t, source):
        return remote(source, came[w].at[t], hop_send.at[w, t], hop_recv.at[w, t], fsdp=ahead)

    def chunk_of(t):
        return index_at((place + 2 * nf - way * (1 + t)) % nf, nf)

    def to_far(w):
        return remote(came[w].at[nf - 2], y_buf[w], y_send.at[w], y_recv.at[w], seq=far)

    def to_near(w):
        return remote(y_buf[w], z_buf[w], z_send.at[w], z_recv.at[w], seq=near)

    def loads():
        return [pltpu.make_async_copy(full[w], own[w], load_sem.at[w]) for w in range(3)]

    def late():
        return [
            pltpu.make_async_copy(x_hbm, x_all, late_sem.at[0]),
            pltpu.make_async_copy(wq_hbm, w_all.at[0], late_sem.at[1]),
            pltpu.make_async_copy(wk_hbm, w_all.at[1], late_sem.at[2]),
            pltpu.make_async_copy(wv_hbm, w_all.at[2], late_sem.at[3]),
            pltpu.make_async_copy(first_hbm, first_grad, late_sem.at[4]),
            pltpu.make_async_copy(gvec_hbm, v_own, late_sem.at[5]),
        ]

    friends = [{"fsdp": (f + d) % nf} for d in range(1, nf)] + [{"seq": p} for p in peers[1:]]

    @pl.when((half == 0) & (h == 0))
    def _():
        hail(friends)
        for copy in loads() + late():
            copy.start()

    k_acc[...] = jnp.zeros_like(k_acc)
    v_acc[...] = jnp.zeros_like(v_acc)
    at_head = pl.ds(pl.multiple_of(h * 64, 64), 64)

    def part(relation, m, head):
        to = peers[relation]
        source = d_out.at[
            m, pl.ds(pl.multiple_of(head * 64, 64), 64), pl.ds(pl.multiple_of(to * tokens, tokens), tokens)
        ]
        target = g_all.at[m, pl.ds(pl.multiple_of(s * width_own + head * 64, 64), 64), :]
        return source, target

    def d_copy(relation, m, head):
        source, target = part(relation, m, head)
        return remote(
            source, target, d_send.at[relation - 1, m, head], d_recv.at[relation - 1, m, head],
            seq=peers[relation],
        )

    def d_local(m, head):
        source, target = part(0, m, head)
        return pltpu.make_async_copy(source, target, d_own.at[m, head])

    def w_copy(head, d):
        to = (f + d) % nf
        return remote(
            w_buf.at[head, to], w_came.at[head, d - 1], w_send.at[head, d - 1],
            w_recv.at[head, d - 1], fsdp=to,
        )

    def p_copy(head, relation):
        return remote(
            w_sum.at[head], w_parts.at[s, head], p_send.at[head, relation - 1],
            p_recv.at[head, relation - 1], seq=peers[relation],
        )

    def v_copy(d):
        to = (f + d) % nf
        return remote(v_cut.at[to], v_came.at[d], l_send.at[d - 1], l_recv.at[d - 1], fsdp=to)

    def m_copy(relation):
        return remote(
            v_sum, v_parts.at[s], m_send.at[relation - 1], m_recv.at[relation - 1],
            seq=peers[relation],
        )

    def settle_head(head):
        for d in range(1, nf):
            w_copy(head, d).wait()
        total = w_buf[head, f].astype(f32)
        for d in range(1, nf):
            total = total + w_came[head, d - 1].astype(f32)
        w_sum[head] = total.astype(bf16)
        for relation in (3, 2, 1):
            p_copy(head, relation).start()
        w_parts[s, head] = total.astype(bf16)

    base = (s // 2 + 1 + half) % 2 * (2 * tokens)

    def round_(early, turn, carry):
        step = (half * count + h) * 4 + turn
        relation = (1 - turn // 2) * (turn + 2) + turn // 2 * (3 - turn)
        owner = ((s // 2 + relation // 2) % 2) * 2 + (s % 2 + relation % 2) % 2
        at = pl.ds(pl.multiple_of(owner * tokens, tokens), tokens)

        q = q_ref[0, at, :]
        if early:
            lane = lax.broadcasted_iota(jnp.int32, (block, LANE), 1)
            first = gctx_ref[at, :LANE].astype(f32)
            second = gctx_ref[at, LANE:].astype(f32)
            grad = jnp.where(h == 0, first, jnp.where(h == 1, pltpu.roll(first, 64, 1), second))
            grad = jnp.where(lane < 64, grad, 0.0)
            delta = jnp.sum(grad * o_ref[0, at, :].astype(f32), axis=1, keepdims=True)
            high, middle, low = thirds(-delta)
            grad = with_lanes(grad, ((64, high), (65, middle), (66, low))).astype(bf16)
            g_side = jnp.transpose(grad)[:64, :]
            q_side = jnp.transpose(q)[:64, :]
            g_buf[h, at, :] = grad
            g_turned[h, :, at] = g_side
            q_turned[h, :, at] = q_side
        else:
            grad = g_buf[h, at, :]
            g_side, q_side = g_turned[h, :, at], q_turned[h, :, at]
        q_total = None
        for c in range(2 * tokens // key_block):
            ks = slice(c * key_block, (c + 1) * key_block)
            keys = pl.ds(pl.multiple_of(base + c * key_block, LANE), key_block)
            k = k_ref[0, keys, :]
            probs = jnp.exp2(dims(q, k, NT))
            score = (probs * dims(grad, v_ref[0, keys, :], NT)).astype(bf16)
            v_acc[:, ks] += dims(g_side, probs.astype(bf16), NN)
            k_acc[:, ks] += dims(q_side, score, NN)
            term = dims(score, k, NN)
            q_total = term if q_total is None else q_total + term
        q_total = jnp.transpose(q_total)[:64, :]

        if early:
            q_acc[h, :, at] = q_total
        else:
            d_out[0, at_head, at] = ((q_total + q_acc[h, :, at]) * 0.125).astype(bf16)

        if early:
            @pl.when(step == 0)
            def _():
                hailed(friends)
                for w in range(3):
                    hop(w, 0, full[w].at[chunk_at(w, chunk_of(0))]).start()

            @pl.when(step == 1)
            def _():
                for copy in loads():
                    copy.wait()

        for g in range(2):
            t = (4 * (step - g) + 3) // 11
            due = 11 * t // 4 == step - g

            @pl.when(due & (t > 0) & (t < nf - 1))
            def _():
                for w in groups[g]:
                    hop(w, t - 1, came[w].at[t - 1]).wait_recv()
                    here = own[w][chunk_at(w, chunk_of(t))].astype(f32)
                    came[w][t - 1] = (here + came[w][t - 1].astype(f32)).astype(bf16)
                    hop(w, t, came[w].at[t - 1]).start()

            if early:
                continue

            @pl.when(due & (t == nf - 1))
            def _():
                for w in groups[g]:
                    hop(w, nf - 2, came[w].at[nf - 2]).wait_recv()
                    here = own[w][chunk_at(w, f)].astype(f32)
                    came[w][nf - 2] = (here + came[w][nf - 2].astype(f32)).astype(bf16)
                    to_far(w).start()

        if early:
            return carry
        for stage, kind in enumerate((2, 3, 1)):
            @pl.when(turn == stage)
            def _():
                d_copy(kind, 0, h).start()

        @pl.when((h > 0) & (turn == 3))
        def _():
            settle_head(h - 1)

        return carry

    for early in (True, False):
        @pl.when(half == (0 if early else 1))
        def _():
            lax.fori_loop(0, 4, functools.partial(round_, early), 0)

    keys = pl.ds(pl.multiple_of(base, 2 * tokens), 2 * tokens)
    d_out[1, at_head, keys] = (k_acc[...] * LN2).astype(bf16)
    d_out[2, at_head, keys] = v_acc[...].astype(bf16)

    @pl.when(half == 0)
    def _():
        for m in (1, 2):
            for kind in (2, 3):
                d_copy(kind, m, h).start()

    @pl.when(half == 1)
    def _():
        for m in range(3):
            if m:
                d_copy(1, m, h).start()
            d_local(m, h).start()

        @pl.when(h == 0)
        def _():
            for copy in late():
                copy.wait()

        left = jnp.concatenate([d_out[m, at_head, :] for m in range(3)], axis=0)
        total = None
        for j in range(4):
            term = dims(left[:, j * tokens : (j + 1) * tokens], x_all[j], NN)
            total = term if total is None else total + term
        total = jnp.transpose(total).astype(bf16)
        for j in range(nf):
            w_buf[h, j] = jnp.concatenate(
                [total[rows * j + rows // 2 * e : rows * j + rows // 2 * (e + 1)] for e in range(2)],
                axis=1,
            )
        for d in range(1, nf):
            w_copy(h, d).start()

    @pl.when((half == 1) & (h == count - 1))
    def _():
        ones = jnp.ones((8, slots), bf16)
        for row, m in ((0, 0), (1, 2)):
            line = dims(ones, d_out[m], NT)
            line = jnp.concatenate([line, jnp.zeros((8, width - width_own), f32)], axis=1)
            v_own[row : row + 1, :] = pltpu.roll(line, s * width_own, 1)[0:1, :]
        lines = v_own[...]
        flat = jnp.concatenate([lines[8 + r : 9 + r, :] for r in range(4)], axis=1)
        for j in range(nf):
            piece = lines if j == 0 else pltpu.roll(lines, width - rows * j, 1)
            v_cut[j, 0:8, :] = piece[0:8, :LANE]
            for r in range(4):
                start = rows * (4 * j + r)
                shift = start % LANE
                tile = start - shift
                both = jnp.concatenate(
                    [flat[:, tile : tile + LANE], flat[:, min(tile + LANE, flat.shape[1] - LANE) :][:, :LANE]],
                    axis=1,
                )
                if shift:
                    both = pltpu.roll(both, 2 * LANE - shift, 1)
                v_cut[j, 8 + r : 9 + r, :] = both[:, :LANE]
            v_cut[j, 12:16, :] = jnp.zeros((4, LANE), f32)
        for d in range(1, nf):
            v_copy(d).start()
        for w in range(3):
            to_far(w).wait()
            y_buf[w][...] = (
                came[w][nf - 2].astype(f32) + y_buf[w][...].astype(f32)
            ).astype(bf16)
            to_near(w).start()

        def settle(head, carry):
            for m in range(3):
                for kind in range(1, 4):
                    d_copy(kind, m, head).wait()
                d_local(m, head).wait()
            return carry

        lax.fori_loop(0, count, settle, 0)
        cut_size = 256
        mats = [w_all[m].reshape(width, width) for m in range(3)]
        for c in range(width // cut_size):
            cut = slice(c * cut_size, (c + 1) * cut_size)
            total = None
            for m in range(3):
                term = dims(mats[m][cut, :], g_all[m], NN)
                total = term if total is None else total + term
            states_grad[:, cut] = (first_grad[:, cut] + jnp.transpose(total)).astype(bf16)
        for d in range(1, nf):
            v_copy(d).wait()
        v_came[0] = v_cut[f]
        total = None
        for j in range(nf):
            term = v_came[(f + nf - j) % nf]
            total = term if total is None else total + term
        v_sum[...] = total
        for kind in (3, 2, 1):
            m_copy(kind).start()
        v_parts[s] = total
        settle_head(count - 1)
        for w in range(3):
            for t in range(nf - 1):
                hop(w, t, came[w].at[t]).wait_send()
            to_near(w).wait()
            mine, theirs = y_buf[w][...], z_buf[w][...]
            out = outs[w]
            size = out.shape[1] // 2
            if by_cols[w]:
                mine, theirs = jnp.transpose(mine), jnp.transpose(theirs)
            out[:, pl.ds(pl.multiple_of(side * size, size), size)] = mine
            out[:, pl.ds(pl.multiple_of((1 - side) * size, size), size)] = theirs
        for relation in range(1, 4):
            m_copy(relation).wait()
        total = v_parts[0] + v_parts[1] + v_parts[2] + v_parts[3]
        vec_out[...] = total
        lane = lax.broadcasted_iota(jnp.int32, (1, 4 * rows), 1)
        line = jnp.zeros((1, 4 * rows), f32)
        for r in range(4):
            piece = jnp.concatenate(
                [total[8 + r : 9 + r, :], jnp.zeros((1, 4 * rows - LANE), f32)], axis=1
            )
            if r:
                piece = pltpu.roll(piece, rows * r, 1)
            line = jnp.where((lane >= rows * r) & (lane < rows * (r + 1)), piece, line)
        upb_out[...] = jnp.broadcast_to(line, upb_out.shape)
        for head in range(count):
            for relation in range(1, 4):
                p_copy(head, relation).wait()
        parts = [
            [
                jnp.concatenate([both[:, : 3 * 64], both[:, 3 * 64 :]], axis=0)
                for both in [w_parts[j, head].astype(f32) for head in range(count)]
            ]
            for j in range(4)
        ]
        for m in range(3):
            qkv_out[m] = jnp.concatenate(
                [part[:, m * 64 : (m + 1) * 64] for group in parts for part in group], axis=1
            ).astype(bf16)


def back(nf, qb, k, v, o, gctx, sums, x_all, mats, first_grad, gvec, key_block):
    heads, slots, _ = qb.shape
    tokens = slots // 4
    width = x_all.shape[2]
    hidden = sums[0].shape[1] * 2
    rows, cols = width // nf, hidden // nf
    shape = jax.ShapeDtypeStruct
    per_head = pl.BlockSpec((1, slots, LANE), lambda p, h: (h, 0, 0))
    chunk = ((rows, hidden // 2), (width // 2, cols), (rows, width // 2))
    vmem = lambda *size: pltpu.VMEM(size, bf16)
    triple = DMA((3,))
    hops = DMA((3, nf - 1))
    own = heads * 64
    packed = (rows // 2, 6 * 64)
    results = [
        shape((tokens, width), bf16),
        shape((rows, hidden), bf16),
        shape((cols, width), bf16),
        shape((rows, width), bf16),
        shape((3, rows, width), bf16),
        shape((16, LANE), f32),
        shape((8, cols), f32),
    ]
    return pl.pallas_call(
        functools.partial(back_kernel, nf, key_block, ((0,), (1, 2))),
        grid=(2, heads),
        out_shape=results,
        in_specs=[per_head] * 4 + [IN_VMEM] + [ANY] * 9,
        out_specs=[
            pl.BlockSpec(x.shape, functools.partial(lambda n, *_: (0,) * n, len(x.shape)))
            for x in results
        ],
        scratch_shapes=[
            pltpu.VMEM((64, slots // 2), f32),
            pltpu.VMEM((64, slots // 2), f32),
            pltpu.VMEM((heads, 64, slots), f32),
            vmem(heads, slots, LANE),
            vmem(heads, 64, slots),
            vmem(heads, 64, slots),
            vmem(3, own, slots),
            vmem(3, width, tokens),
            vmem(4, tokens, width),
            vmem(3, nf, rows, width),
            pltpu.VMEM((tokens, width), f32),
        ]
        + [vmem(*x.shape) for x in sums]
        + [vmem(nf - 1, *x) for x in chunk]
        + [vmem(*x) for x in chunk] * 2
        + [
            vmem(heads, nf, *packed),
            vmem(heads, nf - 1, *packed),
            vmem(heads, *packed),
            vmem(4, heads, *packed),
            pltpu.VMEM((16, width), f32),
            pltpu.VMEM((nf, 16, LANE), f32),
            pltpu.VMEM((nf, 16, LANE), f32),
            pltpu.VMEM((16, LANE), f32),
            pltpu.VMEM((4, 16, LANE), f32),
            triple, DMA((6,)), hops, hops, triple, triple, triple, triple,
            DMA((3, 3, heads)), DMA((3, 3, heads)), DMA((3, heads)),
            DMA((heads, nf - 1)), DMA((heads, nf - 1)), DMA((heads, 3)), DMA((heads, 3)),
            DMA((nf - 1,)), DMA((nf - 1,)), triple, triple,
        ],
        compiler_params=params(4),
        name="back",
    )(qb, k, v, o, gctx, *sums, x_all, *mats, first_grad, gvec)


def results_kernel(rows, output, states_grad, up, down, wout, qkv, vec, upb, *outs):
    outs[0][...] = output[...]
    outs[1][...] = states_grad[...]
    for m in range(3):
        outs[2 + m][...] = qkv[m].astype(f32)
    outs[5][...] = wout[...].astype(f32)
    outs[6][...] = up[...].astype(f32)
    outs[7][...] = down[...].astype(f32)
    for r in range(8):
        outs[8 + r][...] = vec[r, :rows]
    outs[16][...] = upb[0, :]


def results(rows, output, states_grad, up, down, wout, qkv, vec, upb):
    shape = jax.ShapeDtypeStruct
    pieces = 2
    grads = [shape(qkv.shape[1:], f32)] * 3 + [shape(x.shape, f32) for x in (wout, up, down)]
    outs = [shape(output.shape, bf16)] * 2 + grads
    lines = [shape((rows,), f32)] * 8 + [shape((upb.shape[1],), f32)]

    def cut(x):
        n = len(x.shape)
        size = x.shape[: n - 2] + (x.shape[n - 2] // pieces, x.shape[n - 1])
        return pl.BlockSpec(size, functools.partial(lambda n, i: (0,) * (n - 2) + (i, 0), n))

    def same(x):
        return pl.BlockSpec(x.shape, lambda i: (0,) * len(x.shape))

    return pl.pallas_call(
        functools.partial(results_kernel, rows),
        grid=(pieces,),
        out_shape=outs + lines,
        in_specs=[cut(x) for x in (output, states_grad, up, down, wout, qkv)] + [same(vec), same(upb)],
        out_specs=[cut(x) for x in outs] + [same(x) for x in lines],
        compiler_params=params(),
        name="results",
    )(output, states_grad, up, down, wout, qkv, vec, upb)


def fused_device(
    nf, states, query_weight, key_weight, value_weight, out_weight, query_bias, value_bias,
    out_bias, first_gain, first_shift, up_weight, up_bias, down_weight, down_bias, second_gain,
    second_shift, lengths, cotangent,
):
    tokens, width = states.shape
    rows = width // nf
    hidden = up_weight.shape[1]
    heads = width // 4 // 64
    qb, o, k, v, x_all, vec_all, ctx, wout, up, down = front(
        nf, heads, lengths, states, query_weight, key_weight, value_weight, out_weight, up_weight,
        down_weight,
        (
            query_bias, value_bias, out_bias, first_gain, first_shift, down_bias, second_gain,
            second_shift, up_bias,
        ),
        block=256, key_chunk=512,
    )
    output, first_grad, gctx, up_sum, down_sum, wout_sum, gvec, wq, wk, wv = feed(
        nf, lengths, states, cotangent, ctx, wout.reshape(width, width),
        up.reshape(width, hidden), down.reshape(hidden, width), vec_all,
        (query_weight, key_weight, value_weight),
    )
    states_grad, up_grad, down_grad, out_grad, qkv, vec_grad, upb_grad = back(
        nf, qb, k, v, o, gctx.reshape(4 * tokens, -1), (up_sum, down_sum, wout_sum), x_all,
        (wq, wk, wv), first_grad, gvec, key_block=384,
    )
    done = results(rows, output, states_grad, up_grad, down_grad, out_grad, qkv, vec_grad, upb_grad)
    output, states_grad, q_grad, k_grad, v_grad, out_grad, up_grad, down_grad = done[:8]
    lines = done[8:]
    return (
        output, states_grad, q_grad, k_grad, v_grad, out_grad, *lines[:5], up_grad, lines[8],
        down_grad, *lines[5:8],
    )


def solution(mesh):
    nf, ns = mesh.shape["fsdp"], mesh.shape["seq"]

    def choose(states, query_weight, *rest):
        rows, width = query_weight.shape
        fits = ns == 4 and nf == 8 and rows % 16 == 0 and width == 768 and states.shape[0] % 768 == 0
        device = functools.partial(fused_device, nf) if fits else per_device
        return device(states, query_weight, *rest)

    return jax.shard_map(
        choose,
        mesh=mesh,
        in_specs=(
            P(("fsdp", "seq"), None),
            P("fsdp", None),
            P("fsdp", None),
            P("fsdp", None),
            P("fsdp", None),
            P("fsdp"),
            P("fsdp"),
            P("fsdp"),
            P("fsdp"),
            P("fsdp"),
            P("fsdp", None),
            P("fsdp"),
            P("fsdp", None),
            P("fsdp"),
            P("fsdp"),
            P("fsdp"),
            P("fsdp"),
            P(("fsdp", "seq"), None),
        ),
        out_specs=(
            P(("fsdp", "seq"), None),
            P(("fsdp", "seq"), None),
            P("fsdp", None),
            P("fsdp", None),
            P("fsdp", None),
            P("fsdp", None),
            P("fsdp"),
            P("fsdp"),
            P("fsdp"),
            P("fsdp"),
            P("fsdp"),
            P("fsdp", None),
            P("fsdp"),
            P("fsdp", None),
            P("fsdp"),
            P("fsdp"),
            P("fsdp"),
        ),
        check_vma=False,
    )
```

```python
import functools
import math

import jax
import jax.numpy as jnp
from jax import lax
from jax.experimental import pallas as pl
from jax.experimental.pallas import tpu as pltpu
from jax.sharding import PartitionSpec as P

HEAD_DIM = 64


eps = 1e-12


def product(left, right):
    return jnp.dot(left, right, preferred_element_type=jnp.float32)


def left_product(left, right):
    return lax.dot_general(
        left, right, (((0,), (0,)), ((), ())), preferred_element_type=jnp.float32
    )


def right_product(left, right):
    return lax.dot_general(
        left, right, (((1,), (1,)), ((), ())), preferred_element_type=jnp.float32
    )


def layer_norm(values, gain, shift):
    average = jnp.mean(values, axis=-1, keepdims=True)
    centred = values - average
    spread = jnp.mean(centred * centred, axis=-1, keepdims=True)
    return centred * lax.rsqrt(spread + eps) * gain + shift


def gelu_exact(values):
    return jax.nn.gelu(values, approximate=False)


def column_sums(values):
    return jnp.sum(values.astype(jnp.float32), axis=0)


def per_device(
    states,
    query_weight,
    key_weight,
    value_weight,
    out_weight,
    query_bias,
    value_bias,
    out_bias,
    first_gain,
    first_shift,
    up_weight,
    up_bias,
    down_weight,
    down_bias,
    second_gain,
    second_shift,
    lengths,
    cotangent,
):
    f32 = jnp.float32
    bf16 = jnp.bfloat16
    (
        query_mat,
        key_mat,
        value_mat,
        out_mat,
        query_add,
        value_add,
        out_add,
        gain_first,
        shift_first,
    ) = (
        lax.all_gather(query_weight, "fsdp", axis=0, tiled=True),
        lax.all_gather(key_weight, "fsdp", axis=0, tiled=True),
        lax.all_gather(value_weight, "fsdp", axis=0, tiled=True),
        lax.all_gather(out_weight, "fsdp", axis=0, tiled=True),
        lax.all_gather(query_bias, "fsdp", axis=0, tiled=True),
        lax.all_gather(value_bias, "fsdp", axis=0, tiled=True),
        lax.all_gather(out_bias, "fsdp", axis=0, tiled=True),
        lax.all_gather(first_gain, "fsdp", axis=0, tiled=True),
        lax.all_gather(first_shift, "fsdp", axis=0, tiled=True),
    )
    up_mat, up_add, down_mat, down_add, gain_second, shift_second = (
        lax.all_gather(up_weight, "fsdp", axis=0, tiled=True),
        lax.all_gather(up_bias, "fsdp", axis=0, tiled=True),
        lax.all_gather(down_weight, "fsdp", axis=0, tiled=True),
        lax.all_gather(down_bias, "fsdp", axis=0, tiled=True),
        lax.all_gather(second_gain, "fsdp", axis=0, tiled=True),
        lax.all_gather(second_shift, "fsdp", axis=0, tiled=True),
    )
    tokens = states.shape[0]
    slot_rows = tokens * lax.axis_size("seq")
    length = lengths[0]
    places = lax.axis_index("seq") * tokens + lax.iota(jnp.int32, tokens)
    valid_rows = (places < length).astype(f32)[:, None]
    queries = (product(states, query_mat) + query_add).astype(bf16)
    keys_in = product(states, key_mat).astype(bf16)
    values = (product(states, value_mat) + value_add).astype(bf16)
    head_queries, head_keys, head_values = (
        lax.all_to_all(queries, "seq", split_axis=1, concat_axis=0, tiled=True),
        lax.all_to_all(keys_in, "seq", split_axis=1, concat_axis=0, tiled=True),
        lax.all_to_all(values, "seq", split_axis=1, concat_axis=0, tiled=True),
    )
    local_width = head_queries.shape[1]
    head_count = local_width // HEAD_DIM
    block_rows = min(512, slot_rows)
    blocks = slot_rows // block_rows
    scaling = HEAD_DIM ** (-0.5)
    key_valid = lax.iota(jnp.int32, slot_rows) < length
    keys_heads = head_keys.reshape(slot_rows, head_count, HEAD_DIM)
    values_heads = head_values.reshape(slot_rows, head_count, HEAD_DIM)
    query_blocks = head_queries.reshape(blocks, block_rows, head_count, HEAD_DIM)

    def block_scores(query_block):
        scores = (
            jnp.einsum("qhd,khd->hqk", query_block, keys_heads, preferred_element_type=f32)
            * scaling
        )
        return jnp.where(key_valid[None, None, :], scores, -1000000000.0)

    def forward_block(query_block):
        scores = block_scores(query_block)
        highest = jnp.max(scores, axis=-1, keepdims=True)
        exponent = jnp.exp(scores - highest)
        totals = jnp.sum(exponent, axis=-1, keepdims=True)
        weights_soft = (exponent / totals).astype(bf16)
        context_part = jnp.einsum(
            "hqk,khd->qhd", weights_soft, values_heads, preferred_element_type=f32
        )
        return (context_part.astype(bf16), (highest + jnp.log(totals))[:, :, 0])

    context_blocks, log_totals = lax.map(forward_block, query_blocks)
    context = lax.all_to_all(
        context_blocks.reshape(slot_rows, local_width),
        "seq",
        split_axis=0,
        concat_axis=1,
        tiled=True,
    )
    hidden = states.astype(f32)
    first_sum = hidden + (product(context, out_mat) + out_add)
    first_norm, first_back = jax.vjp(
        layer_norm, first_sum, gain_first.astype(f32), shift_first.astype(f32)
    )
    first_low = first_norm.astype(bf16)
    pre_act = product(first_low, up_mat) + up_add
    activated = gelu_exact(pre_act).astype(bf16)
    second_sum = first_norm + (product(activated, down_mat) + down_add)
    normed, second_back = jax.vjp(
        layer_norm, second_sum, gain_second.astype(f32), shift_second.astype(f32)
    )
    output = (normed * valid_rows).astype(bf16)
    out_grad = cotangent.astype(f32) * valid_rows
    second_grad, gain_second_grad, shift_second_grad = second_back(out_grad)
    down_in = second_grad.astype(bf16)
    down_weight_grad = left_product(activated, down_in)
    down_bias_grad = column_sums(down_in)
    act_grad = right_product(down_in, down_mat)
    pre_grad = jax.vjp(gelu_exact, pre_act)[1](act_grad)[0].astype(bf16)
    up_weight_grad = left_product(first_low, pre_grad)
    up_bias_grad = column_sums(pre_grad)
    norm_grad = second_grad + right_product(pre_grad, up_mat)
    first_grad, gain_first_grad, shift_first_grad = first_back(norm_grad)
    branch_grad = first_grad.astype(bf16)
    out_weight_grad = left_product(context, branch_grad)
    out_bias_grad = column_sums(branch_grad)
    context_grad = right_product(branch_grad, out_mat).astype(bf16)
    head_grad = lax.all_to_all(context_grad, "seq", split_axis=1, concat_axis=0, tiled=True)
    grad_blocks = head_grad.reshape(blocks, block_rows, head_count, HEAD_DIM)

    def backward_step(carry, packed):
        key_acc, value_acc = carry
        query_block, grad_block, log_block = packed
        scores = block_scores(query_block)
        probs_full = jnp.exp(scores - log_block[:, :, None])
        probs_low = probs_full.astype(bf16)
        prob_grad = jnp.einsum("qhd,khd->hqk", grad_block, values_heads, preferred_element_type=f32)
        centre = jnp.sum(prob_grad * probs_full, axis=-1, keepdims=True)
        score_grad = (probs_full * (prob_grad - centre)).astype(bf16)
        query_part = (
            jnp.einsum("hqk,khd->qhd", score_grad, keys_heads, preferred_element_type=f32) * scaling
        )
        key_acc = (
            key_acc
            + jnp.einsum("hqk,qhd->khd", score_grad, query_block, preferred_element_type=f32)
            * scaling
        )
        value_acc = value_acc + jnp.einsum(
            "hqk,qhd->khd", probs_low, grad_block, preferred_element_type=f32
        )
        return ((key_acc, value_acc), query_part.astype(bf16))

    zeros_heads = jnp.zeros((slot_rows, head_count, HEAD_DIM), f32)
    (key_total, value_total), query_parts = lax.scan(
        backward_step, (zeros_heads, zeros_heads), (query_blocks, grad_blocks, log_totals)
    )
    query_back, key_back, value_back = (
        lax.all_to_all(
            query_parts.reshape(slot_rows, local_width),
            "seq",
            split_axis=0,
            concat_axis=1,
            tiled=True,
        ),
        lax.all_to_all(
            key_total.reshape(slot_rows, local_width).astype(bf16),
            "seq",
            split_axis=0,
            concat_axis=1,
            tiled=True,
        ),
        lax.all_to_all(
            value_total.reshape(slot_rows, local_width).astype(bf16),
            "seq",
            split_axis=0,
            concat_axis=1,
            tiled=True,
        ),
    )
    query_weight_grad = left_product(states, query_back)
    key_weight_grad = left_product(states, key_back)
    value_weight_grad = left_product(states, value_back)
    query_bias_grad = column_sums(query_back)
    value_bias_grad = column_sums(value_back)
    states_grad = (
        first_grad
        + right_product(query_back, query_mat)
        + right_product(key_back, key_mat)
        + right_product(value_back, value_mat)
    ).astype(bf16)
    attend_parts = (
        lax.psum_scatter(query_weight_grad, "fsdp", scatter_dimension=0, tiled=True),
        lax.psum_scatter(key_weight_grad, "fsdp", scatter_dimension=0, tiled=True),
        lax.psum_scatter(value_weight_grad, "fsdp", scatter_dimension=0, tiled=True),
        lax.psum_scatter(out_weight_grad, "fsdp", scatter_dimension=0, tiled=True),
        lax.psum_scatter(query_bias_grad, "fsdp", scatter_dimension=0, tiled=True),
        lax.psum_scatter(value_bias_grad, "fsdp", scatter_dimension=0, tiled=True),
        lax.psum_scatter(out_bias_grad, "fsdp", scatter_dimension=0, tiled=True),
        lax.psum_scatter(gain_first_grad, "fsdp", scatter_dimension=0, tiled=True),
        lax.psum_scatter(shift_first_grad, "fsdp", scatter_dimension=0, tiled=True),
    )
    feed_parts = (
        lax.psum_scatter(up_weight_grad, "fsdp", scatter_dimension=0, tiled=True),
        lax.psum_scatter(up_bias_grad, "fsdp", scatter_dimension=0, tiled=True),
        lax.psum_scatter(down_weight_grad, "fsdp", scatter_dimension=0, tiled=True),
        lax.psum_scatter(down_bias_grad, "fsdp", scatter_dimension=0, tiled=True),
        lax.psum_scatter(gain_second_grad, "fsdp", scatter_dimension=0, tiled=True),
        lax.psum_scatter(shift_second_grad, "fsdp", scatter_dimension=0, tiled=True),
    )
    summed = (
        lax.psum(attend_parts[0].astype(jnp.bfloat16), "seq").astype(jnp.float32),
        lax.psum(attend_parts[1].astype(jnp.bfloat16), "seq").astype(jnp.float32),
        lax.psum(attend_parts[2].astype(jnp.bfloat16), "seq").astype(jnp.float32),
        lax.psum(attend_parts[3].astype(jnp.bfloat16), "seq").astype(jnp.float32),
        lax.psum(attend_parts[4].astype(jnp.bfloat16), "seq").astype(jnp.float32),
        lax.psum(attend_parts[5].astype(jnp.bfloat16), "seq").astype(jnp.float32),
        lax.psum(attend_parts[6].astype(jnp.bfloat16), "seq").astype(jnp.float32),
        lax.psum(attend_parts[7].astype(jnp.bfloat16), "seq").astype(jnp.float32),
        lax.psum(attend_parts[8].astype(jnp.bfloat16), "seq").astype(jnp.float32),
        lax.psum(feed_parts[0].astype(jnp.bfloat16), "seq").astype(jnp.float32),
        lax.psum(feed_parts[1].astype(jnp.bfloat16), "seq").astype(jnp.float32),
        lax.psum(feed_parts[2].astype(jnp.bfloat16), "seq").astype(jnp.float32),
        lax.psum(feed_parts[3].astype(jnp.bfloat16), "seq").astype(jnp.float32),
        lax.psum(feed_parts[4].astype(jnp.bfloat16), "seq").astype(jnp.float32),
        lax.psum(feed_parts[5].astype(jnp.bfloat16), "seq").astype(jnp.float32),
    )
    return (
        output,
        states_grad,
        summed[0],
        summed[1],
        summed[2],
        summed[3],
        summed[4],
        summed[5],
        summed[6],
        summed[7],
        summed[8],
        summed[9],
        summed[10],
        summed[11],
        summed[12],
        summed[13],
        summed[14],
    )


LANE = 128
LOG2E = math.log2(math.e)
LN2 = math.log(2.0)
NT = (((1,), (1,)), ((), ()))
NN = (((1,), (0,)), ((), ()))
TN = (((0,), (0,)), ((), ()))
VMEM_BYTES = 66 * 1024 * 1024 - 2 * 1024 * 1024
f32 = jnp.float32
bf16 = jnp.bfloat16
ANY = pl.BlockSpec(memory_space=pl.ANY)
IN_VMEM = pl.BlockSpec(memory_space=pltpu.VMEM)
IN_SMEM = pl.BlockSpec(memory_space=pltpu.SMEM)
DMA = pltpu.SemaphoreType.DMA


def dims(left, right, numbers):
    return lax.dot_general(left, right, numbers, preferred_element_type=f32)


def remote(src, dst, send_sem, recv_sem, **where):
    return pltpu.make_async_remote_copy(
        src_ref=src,
        dst_ref=dst,
        send_sem=send_sem,
        recv_sem=recv_sem,
        device_id=where,
        device_id_type=pl.DeviceIdType.MESH,
    )


def hail(partners):
    barrier = pltpu.get_barrier_semaphore()
    for where in partners:
        pl.semaphore_signal(barrier, inc=1, device_id=where, device_id_type=pl.DeviceIdType.MESH)


def hailed(partners):
    pl.semaphore_wait(pltpu.get_barrier_semaphore(), len(partners))


def greet(partners):
    hail(partners)
    hailed(partners)


def seq_peers():
    me = lax.axis_index("seq")
    across = (me + 2) % 4
    return me, me + 1 - 2 * (me % 2), across, across + 1 - 2 * (across % 2)


def place_of(index, count):
    half = index // 2
    return half + (index % 2) * (count - 1 - 2 * half)


def index_at(place, count):
    upper = place // (count // 2)
    return (1 - upper) * 2 * place + upper * (2 * (count - 1 - place) + 1)


def thirds(values):
    high = values.astype(bf16)
    rest = values - high.astype(f32)
    middle = rest.astype(bf16)
    low = (rest - middle.astype(f32)).astype(bf16)
    return high.astype(f32), middle.astype(f32), low.astype(f32)


def with_lanes(base, columns):
    lane = lax.broadcasted_iota(jnp.int32, base.shape, 1)
    for place, values in columns:
        base = jnp.where(lane == place, values, base)
    return base


def params(collective_id=None):
    if collective_id is None:
        return pltpu.CompilerParams(vmem_limit_bytes=VMEM_BYTES)
    return pltpu.CompilerParams(
        vmem_limit_bytes=VMEM_BYTES, collective_id=collective_id, has_side_effects=True
    )


def ring_gather(nf, shards, halves, outs, ring_send, ring_recv, pair_send, pair_recv):
    f = lax.axis_index("fsdp")
    s, near, _, _ = seq_peers()
    side = s % 2
    step = 1 - 2 * side
    place = place_of(f, nf)
    ahead = index_at((place + step + nf) % nf, nf)

    def half(ref, w):
        axis, size = halves[w]
        cut = pl.ds(pl.multiple_of(side * size, size), size)
        return ref.at[cut, :] if axis == 0 else ref.at[:, cut]

    def slot(hop):
        return index_at((place + nf - step * (hop + 1)) % nf, nf)

    def ring(w, hop, owner, source):
        return remote(
            half(source, w),
            half(outs[w].at[owner], w),
            ring_send.at[w, hop],
            ring_recv.at[w, hop],
            fsdp=ahead,
        )

    def pair(w, hop):
        piece = half(outs[w].at[slot(hop)], w)
        return remote(piece, piece, pair_send.at[w, hop], pair_recv.at[w, hop], seq=near)

    def start(w):
        ring(w, 0, f, shards[w]).start()

    def hop(w, h):
        owner = slot(h)
        ring(w, h, owner, outs[w].at[owner]).wait_recv()

        @pl.when(h < nf - 2)
        def _():
            ring(w, h + 1, owner, outs[w].at[owner]).start()

        pair(w, h).start()

    def finish(w, h):
        ring(w, h, f, shards[w]).wait_send()
        pair(w, h).wait()

    return start, hop, finish


def front_kernel(
    nf, block, key_chunk, halves, groups,
    length_ref, states, wq, wk, wv, wout_s, up_s, down_s, *refs,
):
    small_params, refs = refs[:9], refs[9:]
    (
qb_out, o_out, k_out, v_out, x_out, vec_out, ctx_out, wout, up, down,
        q_buf, k_buf, v_buf, qb_buf, o_buf, s_buf, top_buf, ctx_buf, x_buf, w_buf, w_own, packed, vec_own, vec_buf,
        wout_buf, up_buf, down_buf, local_sem, x_sem, kv_sem, keep_sem, vec_send, vec_recv, z_send, z_recv, h_send, h_recv,
        near_send, near_recv, far_send, far_recv, pass_send, pass_recv,
        ring_send, ring_recv, pair_send, pair_recv, ctx_send, ctx_recv, own_sem, copy_sem,
    ) = refs
    f = lax.axis_index("fsdp")
    s, near, far, cross = seq_peers()
    tokens, width = states.shape
    heads, slots, _ = q_buf.shape
    rows = wq.shape[0]
    window = w_buf.shape[2]
    vec_rows = vec_buf.shape[1]
    own_width = heads * 64
    parts = far_send.shape[0]
    chunk = tokens // parts
    per = tokens // block
    beside = f + 1 - 2 * (f % 2)
    stages = nf // 2
    first_lane = pl.multiple_of((own_width * s // LANE) * LANE, LANE)
    weights = (wq, wk, wv)
    shards, outs = (wout_s, up_s, down_s), (wout, up, down)
    ring_start, ring_hop, ring_finish = ring_gather(
        nf, shards, halves, outs, ring_send, ring_recv, pair_send, pair_recv
    )
    friends = [{"fsdp": (f + d) % nf} for d in range(1, nf)] + [
        {"seq": near}, {"seq": far}, {"seq": cross},
    ]
    hail(friends)

    def along(d):
        to = (f + 2 * d) % nf
        return remote(packed.at[f], packed.at[f], z_send.at[d - 1], z_recv.at[d - 1], fsdp=to)

    def aside(d):
        owner = (f + nf - 2 * d) % nf
        return remote(packed.at[owner], packed.at[owner], h_send.at[d], h_recv.at[d], fsdp=beside)

    def vec_copy(d):
        return remote(
            vec_buf.at[f], vec_buf.at[f], vec_send.at[d - 1], vec_recv.at[d - 1],
            fsdp=(f + d) % nf,
        )

    def far_copy(c):
        at = pl.ds(c * chunk, chunk)
        return remote(states.at[at], x_buf.at[2, at], far_send.at[c], far_recv.at[c], seq=far)

    def pass_copy(c):
        at = pl.ds(c * chunk, chunk)
        return remote(
            x_buf.at[2, at], x_buf.at[3, at], pass_send.at[c], pass_recv.at[c], seq=near
        )

    near_copy = remote(states, x_buf.at[1], near_send, near_recv, seq=near)
    windows = [
        pltpu.make_async_copy(
            weights[m].at[:, pl.ds(first_lane, window)], w_own.at[m], local_sem.at[1 + m]
        )
        for m in range(3)
    ]
    local = [pltpu.make_async_copy(states, x_buf.at[0], local_sem.at[0])]
    for copy in windows + local:
        copy.start()
    vec_own[...] = jnp.zeros_like(vec_own)
    for r in range(8):
        vec_own[r : r + 1, :rows] = small_params[r][...].astype(f32).reshape(1, rows)
    line = small_params[8][...].astype(f32).reshape(1, 4 * rows)
    for r in range(4):
        vec_own[8 + r : 9 + r, :rows] = line[:, rows * r : rows * (r + 1)]
    vec_buf[f] = vec_own[...].astype(bf16)
    turn = (window - (own_width * s) % LANE) % window
    for m in range(3):
        windows[m].wait()
        columns = pltpu.roll(w_own[m].astype(f32), turn, 1)[:, :own_width]
        packed[f, m] = jnp.concatenate(
            [columns[: rows // 2], columns[rows // 2 :]], axis=1
        ).astype(bf16)
    hailed(friends)
    for d in range(1, stages):
        along(d).start()
    aside(0).start()
    for c in range(parts):
        far_copy(c).start()
    near_copy.start()
    for d in range(1, nf):
        vec_copy(d).start()
    for w in groups[0] + groups[1]:
        ring_start(w)
    held = (wout_buf, up_buf, down_buf)
    mine = [
        pltpu.make_async_copy(shards[w], held[w], copy_sem.at[0, w]) for w in range(len(shards))
    ]
    for copy in mine:
        copy.start()
    for copy in local:
        copy.wait()
    kept = []

    def keep(slot, index):
        copy = pltpu.make_async_copy(x_buf.at[slot], x_out.at[index], x_sem.at[slot])
        copy.start()
        kept.append(copy)

    def pass_on(c):
        far_copy(c).wait_recv()
        pass_copy(c).start()

    def turn_aside(d):
        along(d).wait_recv()
        aside(d).start()

    keep(0, s)
    for copy in mine:
        copy.wait()
    mine = [
        pltpu.make_async_copy(held[w], outs[w].at[f], copy_sem.at[1, w]) for w in range(len(shards))
    ]
    for copy in mine:
        copy.start()
    passed = 0
    for d in range(1, stages):
        turn_aside(d)
        if d != 2 and passed < parts - 2:
            pass_on(passed)
            passed += 1
    for d in range(1, nf):
        vec_copy(d).wait_recv()
    for d in range(stages):
        aside(d).wait_recv()
    gap = jnp.zeros((rows // 2, window - own_width), f32)
    for j in range(nf):
        for m in range(3):
            both = packed[j, m].astype(f32)
            for e in range(2):
                at = pl.ds(rows * j + rows // 2 * e, rows // 2)
                columns = both[:, own_width * e : own_width * (e + 1)]
                w_buf[m, at, :] = jnp.concatenate([columns, gap], axis=1).astype(bf16)
    share = own_width // rows
    wide = lax.broadcasted_iota(jnp.int32, (1, window), 1)
    biases = []
    for row in (0, 1):
        line = jnp.zeros((1, window), f32)
        for i in range(share):
            piece = vec_buf[share * s + i][row : row + 1, :].astype(f32)
            piece = jnp.concatenate([piece, jnp.zeros((1, window - LANE), f32)], axis=1)
            if i:
                piece = pltpu.roll(piece, i * rows, 1)
            line = jnp.where((wide >= i * rows) & (wide < (i + 1) * rows), piece, line)
        biases.append(line)
    length = length_ref[0]
    mats = [w_buf[m] for m in range(3)]
    small = lax.broadcasted_iota(jnp.int32, (chunk, LANE), 1)
    q_tail = jnp.where(small == 64, 1.0, 0.0)
    v_tail = jnp.where((small >= 64) & (small < 67), 1.0, 0.0)

    def heads_of(values, tail):
        found = []
        for h in range(heads):
            tile = values[:, (h // 2) * LANE : (h // 2 + 1) * LANE]
            if h % 2:
                tile = pltpu.roll(tile, 64, 1)
            found.append(jnp.where(small < 64, tile, tail).astype(bf16))
        return found

    def compute(slot, index, part):
        x = x_buf[slot, pl.ds(pl.multiple_of(part * chunk, chunk), chunk), :]
        start = pl.multiple_of(index * tokens + part * chunk, chunk)
        where = start + lax.broadcasted_iota(jnp.int32, (chunk, LANE), 0)
        queries = dims(x, mats[0], NN) + biases[0]
        keys = dims(x, mats[1], NN)
        k_tail = jnp.where(
            small == 64,
            jnp.where(where < length, 0.0, -1e9),
            jnp.where((small > 64) & (small < 68), 1.0, 0.0),
        )
        values = dims(x, mats[2], NN) + biases[1]
        at = pl.ds(start, chunk)
        for ref, found in (
            (q_buf, heads_of(queries * (LOG2E * 0.125), q_tail)),
            (k_buf, heads_of(keys, k_tail)),
            (v_buf, heads_of(values, v_tail)),
        ):
            for h in range(heads):
                ref[h, at, :] = found[h]

    def whole(slot, index, low, high):
        def body(part, carry):
            compute(slot, index, part)
            return carry

        lax.fori_loop(low, high, body, 0)

    def hops(g, h):
        for w in groups[g]:
            ring_hop(w, h)

    hops(0, 0)
    hops(1, 0)
    whole(0, s, 0, parts)
    for c in range(passed, parts - 1):
        pass_on(c)
    near_copy.wait_recv()
    keep(1, near)
    whole(1, near, 0, parts)
    hops(0, 1)
    whole(2, far, 0, parts - 1)
    pass_on(parts - 1)
    hops(1, 1)
    whole(2, far, parts - 1, parts)
    keep(2, far)
    for c in range(parts):
        pass_copy(c).wait_recv()
    keep(3, cross)
    whole(3, cross, 0, parts)
    hops(0, 2)
    saved = [
        pltpu.make_async_copy(k_buf, k_out, kv_sem.at[0]),
        pltpu.make_async_copy(v_buf, v_out, kv_sem.at[1]),
        pltpu.make_async_copy(vec_buf, vec_out, kv_sem.at[2]),
    ]
    for copy in saved:
        copy.start()

    lane = lax.broadcasted_iota(jnp.int32, (block, LANE), 1)

    def partner(round_):
        relation = 3 - round_
        return ((s // 2 + relation // 2) % 2) * 2 + (s % 2 + relation % 2) % 2

    def ctx_copy(step):
        at = pl.ds(pl.multiple_of(step % per * block, block), block)
        return remote(
            ctx_buf.at[step],
            ctx_out.at[s, at],
            ctx_send.at[step],
            ctx_recv.at[step],
            seq=partner(step // per),
        )

    def rows_of(step):
        base = partner(step // per) * tokens + step % per * block
        return pl.ds(pl.multiple_of(base, block), block)

    def keep_copies(step):
        at = rows_of(step)
        return (
            pltpu.make_async_copy(qb_buf.at[:, at], qb_out.at[:, at], keep_sem.at[0, step]),
            pltpu.make_async_copy(o_buf.at[:, at], o_out.at[:, at], keep_sem.at[1, step]),
        )

    chunks = slots // key_chunk

    def score(h, at, c):
        return dims(q_buf[h, at, :], k_buf[h, c * key_chunk : (c + 1) * key_chunk, :], NT)

    def highest(values, top):
        for j in range(key_chunk // LANE):
            tile = values[:, j * LANE : (j + 1) * LANE]
            top = tile if top is None else jnp.maximum(top, tile)
        return top

    top = None
    for c in range(chunks):
        scores = score(0, rows_of(0), c)
        s_buf[:, c * key_chunk : (c + 1) * key_chunk] = scores
        top = highest(scores, top)
    top_buf[...] = top

    def attend(step, carry):
        at = rows_of(step)
        after = rows_of(jnp.minimum(step + 1, 4 * per - 1))
        results = []
        current = [s_buf[:, c * key_chunk : (c + 1) * key_chunk] for c in range(chunks)]
        top = top_buf[...]
        for h in range(heads):
            peak = jnp.max(top, axis=1, keepdims=True)
            total = None
            coming = []
            top = None
            for c in range(chunks):
                scores = score(h + 1, at, c) if h + 1 < heads else score(0, after, c)
                coming.append(scores)
                top = highest(scores, top)
                probs = jnp.exp2(current[c] - peak).astype(bf16)
                term = dims(probs, v_buf[h, c * key_chunk : (c + 1) * key_chunk, :], NN)
                total = term if total is None else total + term
            current = coming
            weight = total[:, 64:65]
            result = jnp.where(lane < 64, total * (1.0 / weight), 0.0)
            o_buf[h, at, :] = result.astype(bf16)
            high, middle, low = thirds(-(peak + jnp.log2(weight)))
            qb_buf[h, at, :] = with_lanes(
                q_buf[h, at, :].astype(f32), ((65, high), (66, middle), (67, low))
            ).astype(bf16)
            results.append(result)
        for c in range(chunks):
            s_buf[:, c * key_chunk : (c + 1) * key_chunk] = current[c]
        top_buf[...] = top
        for t in range((heads + 1) // 2):
            tile = results[2 * t]
            if 2 * t + 1 < heads:
                tile = tile + pltpu.roll(results[2 * t + 1], 64, 1)
            ctx_buf[step, :, t * LANE : (t + 1) * LANE] = tile.astype(bf16)

        @pl.when(step < 3 * per)
        def _():
            ctx_copy(step).start()

        for copy in keep_copies(step):
            copy.start()
        for g in range(2):
            late = 2 * (1 - g)
            h = (2 * step - late + 1) // 5
            @pl.when(((5 * h + late) // 2 == step) & (h + 3 - g < nf - 1))
            def _():
                hops(g, h + 3 - g)

        return carry

    lax.fori_loop(0, 4 * per, attend, 0)
    owns = []
    for i in range(per):
        owns.append(
            pltpu.make_async_copy(
                ctx_buf.at[3 * per + i], ctx_out.at[s, pl.ds(i * block, block)], own_sem.at[i]
            )
        )
        owns[-1].start()

    def rest(h, carry):
        for w in range(len(shards)):
            ring_hop(w, h)
        return carry

    lax.fori_loop(min(7, nf - 1), nf - 1, rest, 0)

    def settle(step, carry):
        @pl.when(step < 3 * per)
        def _():
            ctx_copy(step).wait()

        for copy in keep_copies(step):
            copy.wait()
        return carry

    lax.fori_loop(0, 4 * per, settle, 0)
    for d in range(1, stages):
        along(d).wait_send()
    for d in range(stages):
        aside(d).wait_send()
    for d in range(1, nf):
        vec_copy(d).wait_send()
    for c in range(parts):
        far_copy(c).wait_send()
        pass_copy(c).wait_send()
    near_copy.wait_send()
    for copy in owns + mine + kept + saved:
        copy.wait()

    def close(h, carry):
        for w in range(len(shards)):
            ring_finish(w, h)
        return carry

    lax.fori_loop(0, nf - 1, close, 0)


def front(nf, heads, length, states, wq, wk, wv, wout, up, down, small_params, block, key_chunk):
    tokens, width = states.shape
    rows = wq.shape[0]
    slots = 4 * tokens
    parts = 4
    window = 256
    shards = (wout, up, down)
    halves = tuple((1, w.shape[1] // 2) for w in shards)
    wide = -(-heads // 2) * LANE
    steps = slots // block
    shape = jax.ShapeDtypeStruct
    head_shape = shape((heads, slots, LANE), bf16)
    head_buf = pltpu.VMEM((heads, slots, LANE), bf16)
    hops = DMA((3, nf - 1))
    stage = DMA((nf // 2 - 1,))
    stage_aside = DMA((nf // 2,))
    peers = DMA((nf - 1,))
    fine = DMA((parts,))
    return pl.pallas_call(
        functools.partial(front_kernel, nf, block, key_chunk, halves, ((1,), (0, 2))),
        out_shape=[head_shape] * 4
        + [
            shape((4, tokens, width), bf16),
            shape((nf, 16, LANE), bf16),
            shape((4, tokens, wide), bf16),
        ]
        + [shape((nf,) + w.shape, bf16) for w in shards],
        in_specs=[IN_SMEM] + [ANY] * 7 + [IN_VMEM] * 9,
        out_specs=[ANY] * 10,
        scratch_shapes=[head_buf] * 5
        + [
            pltpu.VMEM((block, slots), f32),
            pltpu.VMEM((block, LANE), f32),
            pltpu.VMEM((steps, block, wide), bf16),
            pltpu.VMEM((4, tokens, width), bf16),
            pltpu.VMEM((3, width, window), bf16),
            pltpu.VMEM((3, rows, window), bf16),
            pltpu.VMEM((nf, 3, rows // 2, heads * 128), bf16),
            pltpu.VMEM((16, LANE), f32),
            pltpu.VMEM((nf, 16, LANE), bf16),
        ]
        + [pltpu.VMEM(w.shape, bf16) for w in shards]
        + [
            DMA((5,)),
            DMA((4,)),
            DMA((3,)),
            DMA((2, steps)),
            peers, peers, stage, stage, stage_aside, stage_aside,
            DMA(()), DMA(()), fine, fine, fine, fine,
            hops, hops, hops, hops,
            DMA((steps,)), DMA((steps,)),
            DMA((tokens // block,)),
            DMA((2, 3)),
        ],
        compiler_params=params(1),
        name="front",
    )(length, states, wq, wk, wv, wout, up, down, *small_params)


def plane_gather(nf, shards, outs, z_send, z_recv, h_send, h_recv, n_send, n_recv):
    f = lax.axis_index("fsdp")
    s, near, _, _ = seq_peers()
    side = s % 2
    beside = f + 1 - 2 * (f % 2)
    stages = nf // 2
    count = len(shards)

    def half(ref):
        size = ref.shape[1] // 2
        return ref.at[:, pl.ds(pl.multiple_of(side * size, size), size)]

    def along(d, m):
        return remote(
            half(shards[m]), half(outs[m].at[f]), z_send.at[d - 1, m], z_recv.at[d - 1, m],
            fsdp=(f + 2 * d) % nf,
        )

    def aside(d, m):
        owner = (f + nf - 2 * d) % nf
        source = outs[m].at[owner] if d else shards[m]
        return remote(
            half(source), half(outs[m].at[owner]), h_send.at[d, m], h_recv.at[d, m], fsdp=beside
        )

    def share(e, m):
        owner = (f + nf - 2 * e) % nf if e < stages else (beside + nf - 2 * (e - stages)) % nf
        piece = half(outs[m].at[owner])
        return remote(piece, piece, n_send.at[e - 1, m], n_recv.at[e - 1, m], seq=near)

    def start():
        for d in range(1, stages):
            for m in range(count):
                along(d, m).start()
        for m in range(count):
            aside(0, m).start()

    def first():
        for d in range(1, stages):
            for m in range(count):
                along(d, m).wait_recv()
                aside(d, m).start()
                share(d, m).start()

    def second():
        for d in range(stages):
            for m in range(count):
                aside(d, m).wait_recv()
                share(stages + d, m).start()

    def finish():
        for m in range(count):
            for d in range(1, stages):
                along(d, m).wait_send()
            for d in range(stages):
                aside(d, m).wait_send()
            for e in range(1, nf):
                share(e, m).wait()

    return start, first, second, finish


def feed_kernel(
    nf, block, part, length_ref, vec_all, states_hbm, ctx_hbm, wout_hbm, up_hbm, down_hbm, cot_hbm,
    wq_s, wk_s, wv_s,
    out, first_grad_out, gctx, up_sum, down_sum, wout_sum, gvec, wq, wk, wv,
    states, ctx, wout, up, down, cot, held, vec, upb, out_buf, first_buf, act_buf, pre_buf, slope_buf, low_t, down_t, branch_buf,
    g_buf, up_give, down_give, wout_give, up_take, down_take, wout_take,
    load_sem, keep_sem, g_send, g_recv, own_sem, give_send, give_recv, sum_sem, shard_sem,
    z_send, z_recv, h_send, h_recv, n_send, n_recv,
):
    f = lax.axis_index("fsdp")
    s, near, far, cross = seq_peers()
    side = s % 2
    beside = f + 1 - 2 * (f % 2)
    tokens, width = states.shape
    hidden = up.shape[1]
    own = wout.shape[0] // 4
    steps = tokens // block
    wide = ctx.shape[2]
    loads = [
        pltpu.make_async_copy(up_hbm, up, load_sem.at[0]),
        pltpu.make_async_copy(down_hbm, down, load_sem.at[1]),
        pltpu.make_async_copy(cot_hbm, cot, load_sem.at[2]),
    ]
    early = [
        pltpu.make_async_copy(wout_hbm, wout, load_sem.at[3]),
        pltpu.make_async_copy(ctx_hbm, ctx, load_sem.at[4]),
        pltpu.make_async_copy(states_hbm, states, load_sem.at[5]),
    ]
    for copy in early + loads:
        copy.start()
    shards, outs = (wq_s, wk_s, wv_s), (wq, wk, wv)
    gather = plane_gather(nf, shards, outs, z_send, z_recv, h_send, h_recv, n_send, n_recv)
    friends = [{"fsdp": (f + 2 * d) % nf} for d in range(1, nf // 2)] + [
        {"fsdp": beside}, {"seq": near}, {"seq": far}, {"seq": cross},
    ]
    hail(friends)
    rows = width // nf
    short = lax.broadcasted_iota(jnp.int32, vec_all.shape[1:], 1) < rows
    lines = jnp.zeros((vec_all.shape[1], width), f32)
    blank = jnp.zeros((vec_all.shape[1], width - LANE), f32)
    tiles = [jnp.zeros((1, LANE), f32) for _ in range(hidden // LANE)]
    for j in range(nf):
        piece = jnp.where(short, vec_all[j].astype(f32), 0.0)
        both = jnp.concatenate([piece, blank], axis=1)
        lines = lines + (pltpu.roll(both, rows * j, 1) if j else both)
        for r in range(4):
            first_lane = rows * (4 * j + r)
            tile, shift = first_lane // LANE, first_lane % LANE
            both = jnp.concatenate([piece[8 + r : 9 + r, :], blank[:1, :LANE]], axis=1)
            if shift:
                both = pltpu.roll(both, shift, 1)
            tiles[tile] = tiles[tile] + both[:, :LANE]
            if tile + 1 < len(tiles):
                tiles[tile + 1] = tiles[tile + 1] + both[:, LANE:]
    vec[...] = lines[:8]
    upb[...] = jnp.concatenate(tiles, axis=1)
    kept = [pltpu.make_async_copy(shards[m], held.at[m], shard_sem.at[0, m]) for m in range(3)]
    for copy in kept:
        copy.start()
    kept_out = [
        pltpu.make_async_copy(held.at[m], outs[m].at[f], shard_sem.at[1, m]) for m in range(3)
    ]
    length = length_ref[0]
    gvec[...] = jnp.zeros_like(gvec)
    peers = (s, near, far, cross)

    def line(row):
        return vec[row : row + 1, :]

    def add_line(row, values):
        gvec[row : row + 1, :] += jnp.sum(values, axis=0, keepdims=True)

    def norm(values):
        centred = values - jnp.mean(values, axis=1, keepdims=True)
        scale = lax.rsqrt(jnp.mean(centred * centred, axis=1, keepdims=True) + eps)
        return centred * scale, scale

    def norm_back(grad, gain, normed, scale):
        grad = grad * gain
        return scale * (
            grad
            - jnp.mean(grad, axis=1, keepdims=True)
            - normed * jnp.mean(grad * normed, axis=1, keepdims=True)
        )

    def rows_of(i):
        return pl.ds(pl.multiple_of(i * block, block), block)

    def send(relation, i):
        at = rows_of(i)
        return remote(
            g_buf.at[relation, at],
            gctx.at[s, at],
            g_send.at[relation - 1, i],
            g_recv.at[relation - 1, i],
            seq=peers[relation],
        )

    def keep(i):
        at = rows_of(i)
        return (
            pltpu.make_async_copy(out_buf.at[at], out.at[at], keep_sem.at[0, i]),
            pltpu.make_async_copy(first_buf.at[at], first_grad_out.at[at], keep_sem.at[1, i]),
        )

    def body(i, carry):
        at = rows_of(i)
        attended = None
        for j in range(4):
            term = dims(ctx[j, at, :own], wout[own * j : own * (j + 1), :], NN)
            attended = term if attended is None else attended + term
        normed_first, scale_first = norm(states[at, :].astype(f32) + (attended + line(2)))
        first = normed_first * line(3) + line(4)
        low = first.astype(bf16)
        low_t[:, at] = jnp.transpose(low)

        @pl.when(i == 0)
        def _():
            hailed(friends)
            gather[0]()
            for copy in kept + loads:
                copy.wait()
            for copy in kept_out:
                copy.start()

        fed = None
        for c in range(hidden // part):
            cut = slice(c * part, (c + 1) * part)
            pre = dims(low, up[:, cut], NN) + upb[:, cut]
            share = 0.5 + 0.5 * lax.erf(pre * (2.0**-0.5))
            slope_buf[:, cut] = share + pre * jnp.exp(-0.5 * pre * pre) * (2.0 * math.pi) ** -0.5
            act = (pre * share).astype(bf16)
            act_buf[at, cut] = act
            term = dims(act, down[cut, :], NN)
            fed = term if fed is None else fed + term
        normed, scale = norm(first + (fed + line(5)))
        place = s * tokens + i * block + lax.broadcasted_iota(jnp.int32, (block, 1), 0)
        valid = jnp.where(place < length, 1.0, 0.0)
        out_buf[at, :] = ((normed * line(6) + line(7)) * valid).astype(bf16)
        grad = cot[at, :].astype(f32) * valid
        add_line(6, grad * normed)
        add_line(7, grad)
        second_grad = norm_back(grad, line(6), normed, scale)
        down_in = second_grad.astype(bf16)
        add_line(5, down_in.astype(f32))
        down_t[:, at] = jnp.transpose(down_in)
        back = second_grad
        for c in range(hidden // part):
            cut = slice(c * part, (c + 1) * part)
            pre_grad = (dims(down_in, down[cut, :], NT) * slope_buf[:, cut]).astype(bf16)
            pre_buf[at, cut] = pre_grad
            row = 8 + c * part // width
            col = c * part % width
            gvec[row : row + 1, col : col + part] += jnp.sum(
                pre_grad.astype(f32), axis=0, keepdims=True
            )
            back = back + dims(pre_grad, up[:, cut], NT)
        add_line(3, back * normed_first)
        add_line(4, back)
        first_grad = norm_back(back, line(3), normed_first, scale_first)
        first_buf[at, :] = first_grad
        branch = first_grad.astype(bf16)
        branch_buf[at, :] = branch
        add_line(2, branch.astype(f32))
        for relation in range(4):
            rows = pl.ds(pl.multiple_of(peers[relation] * own, 64), own)
            g_buf[relation, at, :own] = dims(branch, wout[rows, :], NT).astype(bf16)
            if wide > own:
                g_buf[relation, at, own:] = jnp.zeros((block, wide - own), bf16)
            if relation:
                send(relation, i).start()
        for copy in keep(i):
            copy.start()

        @pl.when(i == min(1, steps - 1))
        def _():
            gather[1]()

        return carry

    for copy in early:
        copy.wait()
    lax.fori_loop(0, steps, body, 0)
    mine = pltpu.make_async_copy(g_buf.at[0], gctx.at[s], own_sem)
    mine.start()

    pieces = give_send.shape[1]
    up_cut = hidden // 2 // pieces
    down_cut = hidden // pieces

    def up_part(which, c):
        cut = pl.ds(pl.multiple_of(which * (hidden // 2) + c * up_cut, up_cut), up_cut)
        return dims(low_t[...], pre_buf[:, cut], NN)

    def down_part(which, c):
        rows = pl.ds(pl.multiple_of(which * (width // 2), width // 2), width // 2)
        cut = pl.ds(pl.multiple_of(c * down_cut, down_cut), down_cut)
        return dims(down_t[rows, :], act_buf[:, cut], NN)

    def wout_part(which, j):
        cut = pl.ds(pl.multiple_of(which * (width // 2), width // 2), width // 2)
        return dims(ctx[j, :, :own], branch_buf[:, cut], TN)

    def cols(c, size):
        return (slice(None), pl.ds(pl.multiple_of(c * size, size), size))

    def give(w, c):
        if w == 2:
            pair = wout_give, wout_take
        else:
            at = cols(c, (up_cut, down_cut)[w])
            pair = (up_give, down_give)[w].at[at], (up_take, down_take)[w].at[at]
        return remote(*pair, give_send.at[w, c], give_recv.at[w, c], seq=near)

    def give_away(c, carry):
        up_give[cols(c, up_cut)] = up_part(1 - side, c).astype(bf16)
        give(0, c).start()
        down_give[cols(c, down_cut)] = down_part(1 - side, c).astype(bf16)
        give(1, c).start()
        return carry

    def add_own(c, carry):
        at = cols(c, up_cut)
        total = up_part(side, c)
        give(0, c).wait()
        up_give[at] = (total + up_take[at].astype(f32)).astype(bf16)
        at = cols(c, down_cut)
        total = down_part(side, c)
        give(1, c).wait()
        down_give[at] = (total + down_take[at].astype(f32)).astype(bf16)
        return carry

    lax.fori_loop(0, pieces, give_away, 0)
    for j in range(4):
        wout_give[own * j : own * (j + 1), :] = wout_part(1 - side, j).astype(bf16)
    give(2, 0).start()
    gather[2]()
    lax.fori_loop(0, pieces, add_own, 0)
    sums = [
        pltpu.make_async_copy(up_give, up_sum, sum_sem.at[0]),
        pltpu.make_async_copy(down_give, down_sum, sum_sem.at[1]),
    ]
    for copy in sums:
        copy.start()
    totals = [wout_part(side, j) for j in range(4)]
    give(2, 0).wait()
    for j in range(4):
        at = slice(own * j, own * (j + 1))
        wout_give[at, :] = (totals[j] + wout_take[at, :].astype(f32)).astype(bf16)
    sums.append(pltpu.make_async_copy(wout_give, wout_sum, sum_sem.at[2]))
    sums[-1].start()
    for relation in range(1, 4):
        for i in range(steps):
            send(relation, i).wait()
    for i in range(steps):
        for copy in keep(i):
            copy.wait()
    gather[3]()
    for copy in [mine] + kept_out + sums:
        copy.wait()


def feed(nf, length, states, cot, ctx, wout, up, down, vec_all, shards, block=256, part=768):
    tokens, width = states.shape
    hidden = up.shape[1]
    wide = ctx.shape[2]
    pieces = 2
    shape = jax.ShapeDtypeStruct
    halves = ((width, hidden // 2), (width // 2, hidden), (width, width // 2))
    vmem = lambda *size: pltpu.VMEM(size, bf16)
    steps = tokens // block
    staged = DMA((nf // 2 - 1, 3))
    staged_aside = DMA((nf // 2, 3))
    return pl.pallas_call(
        functools.partial(feed_kernel, nf, block, part),
        out_shape=[
            shape((tokens, width), bf16),
            shape((tokens, width), f32),
            shape((4, tokens, wide), bf16),
        ]
        + [shape(x, bf16) for x in halves]
        + [shape((16, width), f32)]
        + [shape((nf,) + w.shape, bf16) for w in shards],
        in_specs=[IN_SMEM, IN_VMEM] + [ANY] * 9,
        out_specs=[ANY] * 6 + [IN_VMEM] + [ANY] * 3,
        scratch_shapes=[
            vmem(*states.shape),
            vmem(*ctx.shape),
            vmem(*wout.shape),
            vmem(width, hidden),
            vmem(hidden, width),
            vmem(tokens, width),
            vmem(3, *shards[0].shape),
            pltpu.VMEM((8, width), f32),
            pltpu.VMEM((1, hidden), f32),
            vmem(tokens, width),
            pltpu.VMEM((tokens, width), f32),
            vmem(tokens, hidden),
            vmem(tokens, hidden),
            pltpu.VMEM((block, hidden), f32),
            vmem(width, tokens),
            vmem(width, tokens),
            vmem(tokens, width),
            vmem(4, tokens, wide),
        ]
        + [vmem(*x) for x in halves] * 2
        + [
            DMA((6,)),
            DMA((2, steps)),
            DMA((3, steps)),
            DMA((3, steps)),
            DMA(()),
            DMA((3, pieces)),
            DMA((3, pieces)),
            DMA((3,)),
            DMA((2, 3)),
            staged, staged, staged_aside, staged_aside,
            DMA((nf - 1, 3)), DMA((nf - 1, 3)),
        ],
        compiler_params=params(3),
        name="feed",
    )(length, vec_all, states, ctx, wout, up, down, cot, *shards)


def back_kernel(
    nf, key_block, groups, q_ref, k_ref, v_ref, o_ref, gctx_ref,
    up_sum, down_sum, wout_sum, x_hbm, wq_hbm, wk_hbm, wv_hbm, first_hbm, gvec_hbm,
    states_grad, up_out, down_out, wout_out, qkv_out, vec_out, upb_out,
    k_acc, v_acc, q_acc, g_buf, q_turned, g_turned, d_out, g_all, x_all, w_all, first_grad,
    own_up, own_dn, own_wo, ring_up, ring_dn, ring_wo, y_up, y_dn, y_wo, z_up, z_dn, z_wo,
    w_buf, w_came, w_sum, w_parts, v_own, v_cut, v_came, v_sum, v_parts,
    load_sem, late_sem, hop_send, hop_recv, y_send, y_recv, z_send, z_recv,
    d_send, d_recv, d_own, w_send, w_recv, p_send, p_recv, l_send, l_recv, m_send, m_recv,
):
    half, h = pl.program_id(0), pl.program_id(1)
    count = w_buf.shape[0]
    f = lax.axis_index("fsdp")
    s, near, far, cross = seq_peers()
    peers = (s, near, far, cross)
    side = s % 2
    way = 1 - 2 * side
    place = place_of(f, nf)
    ahead = index_at((place + way + nf) % nf, nf)
    slots = k_ref.shape[1]
    tokens = slots // 4
    block = tokens
    width = x_all.shape[2]
    rows = width // nf
    width_own = count * 64
    full = (up_sum, down_sum, wout_sum)
    own = (own_up, own_dn, own_wo)
    came = (ring_up, ring_dn, ring_wo)
    y_buf = (y_up, y_dn, y_wo)
    z_buf = (z_up, z_dn, z_wo)
    outs = (up_out, down_out, wout_out)
    by_cols = (False, True, False)

    def chunk_at(w, chunk):
        size = came[w].shape[1 + by_cols[w]]
        cut = pl.ds(pl.multiple_of(chunk * size, size), size)
        return (slice(None), cut) if by_cols[w] else (cut, slice(None))

    def hop(w, t, source):
        return remote(source, came[w].at[t], hop_send.at[w, t], hop_recv.at[w, t], fsdp=ahead)

    def chunk_of(t):
        return index_at((place + 2 * nf - way * (1 + t)) % nf, nf)

    def to_far(w):
        return remote(came[w].at[nf - 2], y_buf[w], y_send.at[w], y_recv.at[w], seq=far)

    def to_near(w):
        return remote(y_buf[w], z_buf[w], z_send.at[w], z_recv.at[w], seq=near)

    def loads():
        return [pltpu.make_async_copy(full[w], own[w], load_sem.at[w]) for w in range(3)]

    def late():
        return [
            pltpu.make_async_copy(x_hbm, x_all, late_sem.at[0]),
            pltpu.make_async_copy(wq_hbm, w_all.at[0], late_sem.at[1]),
            pltpu.make_async_copy(wk_hbm, w_all.at[1], late_sem.at[2]),
            pltpu.make_async_copy(wv_hbm, w_all.at[2], late_sem.at[3]),
            pltpu.make_async_copy(first_hbm, first_grad, late_sem.at[4]),
            pltpu.make_async_copy(gvec_hbm, v_own, late_sem.at[5]),
        ]

    friends = [{"fsdp": (f + d) % nf} for d in range(1, nf)] + [{"seq": p} for p in peers[1:]]

    @pl.when((half == 0) & (h == 0))
    def _():
        hail(friends)
        for copy in loads() + late():
            copy.start()

    k_acc[...] = jnp.zeros_like(k_acc)
    v_acc[...] = jnp.zeros_like(v_acc)
    at_head = pl.ds(pl.multiple_of(h * 64, 64), 64)

    def part(relation, m, head):
        to = peers[relation]
        source = d_out.at[
            m, pl.ds(pl.multiple_of(head * 64, 64), 64), pl.ds(pl.multiple_of(to * tokens, tokens), tokens)
        ]
        target = g_all.at[m, pl.ds(pl.multiple_of(s * width_own + head * 64, 64), 64), :]
        return source, target

    def d_copy(relation, m, head):
        source, target = part(relation, m, head)
        return remote(
            source, target, d_send.at[relation - 1, m, head], d_recv.at[relation - 1, m, head],
            seq=peers[relation],
        )

    def d_local(m, head):
        source, target = part(0, m, head)
        return pltpu.make_async_copy(source, target, d_own.at[m, head])

    def w_copy(head, d):
        to = (f + d) % nf
        return remote(
            w_buf.at[head, to], w_came.at[head, d - 1], w_send.at[head, d - 1],
            w_recv.at[head, d - 1], fsdp=to,
        )

    def p_copy(head, relation):
        return remote(
            w_sum.at[head], w_parts.at[s, head], p_send.at[head, relation - 1],
            p_recv.at[head, relation - 1], seq=peers[relation],
        )

    def v_copy(d):
        to = (f + d) % nf
        return remote(v_cut.at[to], v_came.at[d], l_send.at[d - 1], l_recv.at[d - 1], fsdp=to)

    def m_copy(relation):
        return remote(
            v_sum, v_parts.at[s], m_send.at[relation - 1], m_recv.at[relation - 1],
            seq=peers[relation],
        )

    def settle_head(head):
        for d in range(1, nf):
            w_copy(head, d).wait()
        total = w_buf[head, f].astype(f32)
        for d in range(1, nf):
            total = total + w_came[head, d - 1].astype(f32)
        w_sum[head] = total.astype(bf16)
        for relation in (3, 2, 1):
            p_copy(head, relation).start()
        w_parts[s, head] = total.astype(bf16)

    base = (s // 2 + 1 + half) % 2 * (2 * tokens)

    def round_(early, turn, carry):
        step = (half * count + h) * 4 + turn
        relation = (1 - turn // 2) * (turn + 2) + turn // 2 * (3 - turn)
        owner = ((s // 2 + relation // 2) % 2) * 2 + (s % 2 + relation % 2) % 2
        at = pl.ds(pl.multiple_of(owner * tokens, tokens), tokens)

        q = q_ref[0, at, :]
        if early:
            lane = lax.broadcasted_iota(jnp.int32, (block, LANE), 1)
            first = gctx_ref[at, :LANE].astype(f32)
            second = gctx_ref[at, LANE:].astype(f32)
            grad = jnp.where(h == 0, first, jnp.where(h == 1, pltpu.roll(first, 64, 1), second))
            grad = jnp.where(lane < 64, grad, 0.0)
            delta = jnp.sum(grad * o_ref[0, at, :].astype(f32), axis=1, keepdims=True)
            high, middle, low = thirds(-delta)
            grad = with_lanes(grad, ((64, high), (65, middle), (66, low))).astype(bf16)
            g_side = jnp.transpose(grad)[:64, :]
            q_side = jnp.transpose(q)[:64, :]
            g_buf[h, at, :] = grad
            g_turned[h, :, at] = g_side
            q_turned[h, :, at] = q_side
        else:
            grad = g_buf[h, at, :]
            g_side, q_side = g_turned[h, :, at], q_turned[h, :, at]
        q_total = None
        for c in range(2 * tokens // key_block):
            ks = slice(c * key_block, (c + 1) * key_block)
            keys = pl.ds(pl.multiple_of(base + c * key_block, LANE), key_block)
            k = k_ref[0, keys, :]
            probs = jnp.exp2(dims(q, k, NT))
            score = (probs * dims(grad, v_ref[0, keys, :], NT)).astype(bf16)
            v_acc[:, ks] += dims(g_side, probs.astype(bf16), NN)
            k_acc[:, ks] += dims(q_side, score, NN)
            term = dims(score, k, NN)
            q_total = term if q_total is None else q_total + term
        q_total = jnp.transpose(q_total)[:64, :]

        if early:
            q_acc[h, :, at] = q_total
        else:
            d_out[0, at_head, at] = ((q_total + q_acc[h, :, at]) * 0.125).astype(bf16)

        if early:
            @pl.when(step == 0)
            def _():
                hailed(friends)
                for w in range(3):
                    hop(w, 0, full[w].at[chunk_at(w, chunk_of(0))]).start()

            @pl.when(step == 1)
            def _():
                for copy in loads():
                    copy.wait()

        for g in range(2):
            t = (4 * (step - g) + 3) // 11
            due = 11 * t // 4 == step - g

            @pl.when(due & (t > 0) & (t < nf - 1))
            def _():
                for w in groups[g]:
                    hop(w, t - 1, came[w].at[t - 1]).wait_recv()
                    here = own[w][chunk_at(w, chunk_of(t))].astype(f32)
                    came[w][t - 1] = (here + came[w][t - 1].astype(f32)).astype(bf16)
                    hop(w, t, came[w].at[t - 1]).start()

            if early:
                continue

            @pl.when(due & (t == nf - 1))
            def _():
                for w in groups[g]:
                    hop(w, nf - 2, came[w].at[nf - 2]).wait_recv()
                    here = own[w][chunk_at(w, f)].astype(f32)
                    came[w][nf - 2] = (here + came[w][nf - 2].astype(f32)).astype(bf16)
                    to_far(w).start()

        if early:
            return carry
        for stage, kind in enumerate((2, 3, 1)):
            @pl.when(turn == stage)
            def _():
                d_copy(kind, 0, h).start()

        @pl.when((h > 0) & (turn == 3))
        def _():
            settle_head(h - 1)

        return carry

    for early in (True, False):
        @pl.when(half == (0 if early else 1))
        def _():
            lax.fori_loop(0, 4, functools.partial(round_, early), 0)

    keys = pl.ds(pl.multiple_of(base, 2 * tokens), 2 * tokens)
    d_out[1, at_head, keys] = (k_acc[...] * LN2).astype(bf16)
    d_out[2, at_head, keys] = v_acc[...].astype(bf16)

    @pl.when(half == 0)
    def _():
        for m in (1, 2):
            for kind in (2, 3):
                d_copy(kind, m, h).start()

    @pl.when(half == 1)
    def _():
        for m in range(3):
            if m:
                d_copy(1, m, h).start()
            d_local(m, h).start()

        @pl.when(h == 0)
        def _():
            for copy in late():
                copy.wait()

        left = jnp.concatenate([d_out[m, at_head, :] for m in range(3)], axis=0)
        total = None
        for j in range(4):
            term = dims(left[:, j * tokens : (j + 1) * tokens], x_all[j], NN)
            total = term if total is None else total + term
        total = jnp.transpose(total).astype(bf16)
        for j in range(nf):
            w_buf[h, j] = jnp.concatenate(
                [total[rows * j + rows // 2 * e : rows * j + rows // 2 * (e + 1)] for e in range(2)],
                axis=1,
            )
        for d in range(1, nf):
            w_copy(h, d).start()

    @pl.when((half == 1) & (h == count - 1))
    def _():
        ones = jnp.ones((8, slots), bf16)
        for row, m in ((0, 0), (1, 2)):
            line = dims(ones, d_out[m], NT)
            line = jnp.concatenate([line, jnp.zeros((8, width - width_own), f32)], axis=1)
            v_own[row : row + 1, :] = pltpu.roll(line, s * width_own, 1)[0:1, :]
        lines = v_own[...]
        flat = jnp.concatenate([lines[8 + r : 9 + r, :] for r in range(4)], axis=1)
        for j in range(nf):
            piece = lines if j == 0 else pltpu.roll(lines, width - rows * j, 1)
            v_cut[j, 0:8, :] = piece[0:8, :LANE]
            for r in range(4):
                start = rows * (4 * j + r)
                shift = start % LANE
                tile = start - shift
                both = jnp.concatenate(
                    [flat[:, tile : tile + LANE], flat[:, min(tile + LANE, flat.shape[1] - LANE) :][:, :LANE]],
                    axis=1,
                )
                if shift:
                    both = pltpu.roll(both, 2 * LANE - shift, 1)
                v_cut[j, 8 + r : 9 + r, :] = both[:, :LANE]
            v_cut[j, 12:16, :] = jnp.zeros((4, LANE), f32)
        for d in range(1, nf):
            v_copy(d).start()
        for w in range(3):
            to_far(w).wait()
            y_buf[w][...] = (
                came[w][nf - 2].astype(f32) + y_buf[w][...].astype(f32)
            ).astype(bf16)
            to_near(w).start()

        def settle(head, carry):
            for m in range(3):
                for kind in range(1, 4):
                    d_copy(kind, m, head).wait()
                d_local(m, head).wait()
            return carry

        lax.fori_loop(0, count, settle, 0)
        cut_size = 256
        mats = [w_all[m].reshape(width, width) for m in range(3)]
        for c in range(width // cut_size):
            cut = slice(c * cut_size, (c + 1) * cut_size)
            total = None
            for m in range(3):
                term = dims(mats[m][cut, :], g_all[m], NN)
                total = term if total is None else total + term
            states_grad[:, cut] = (first_grad[:, cut] + jnp.transpose(total)).astype(bf16)
        for d in range(1, nf):
            v_copy(d).wait()
        v_came[0] = v_cut[f]
        total = None
        for j in range(nf):
            term = v_came[(f + nf - j) % nf]
            total = term if total is None else total + term
        v_sum[...] = total
        for kind in (3, 2, 1):
            m_copy(kind).start()
        v_parts[s] = total
        settle_head(count - 1)
        for w in range(3):
            for t in range(nf - 1):
                hop(w, t, came[w].at[t]).wait_send()
            to_near(w).wait()
            mine, theirs = y_buf[w][...], z_buf[w][...]
            out = outs[w]
            size = out.shape[1] // 2
            if by_cols[w]:
                mine, theirs = jnp.transpose(mine), jnp.transpose(theirs)
            out[:, pl.ds(pl.multiple_of(side * size, size), size)] = mine
            out[:, pl.ds(pl.multiple_of((1 - side) * size, size), size)] = theirs
        for relation in range(1, 4):
            m_copy(relation).wait()
        total = v_parts[0] + v_parts[1] + v_parts[2] + v_parts[3]
        vec_out[...] = total
        lane = lax.broadcasted_iota(jnp.int32, (1, 4 * rows), 1)
        line = jnp.zeros((1, 4 * rows), f32)
        for r in range(4):
            piece = jnp.concatenate(
                [total[8 + r : 9 + r, :], jnp.zeros((1, 4 * rows - LANE), f32)], axis=1
            )
            if r:
                piece = pltpu.roll(piece, rows * r, 1)
            line = jnp.where((lane >= rows * r) & (lane < rows * (r + 1)), piece, line)
        upb_out[...] = jnp.broadcast_to(line, upb_out.shape)
        for head in range(count):
            for relation in range(1, 4):
                p_copy(head, relation).wait()
        parts = [
            [
                jnp.concatenate([both[:, : 3 * 64], both[:, 3 * 64 :]], axis=0)
                for both in [w_parts[j, head].astype(f32) for head in range(count)]
            ]
            for j in range(4)
        ]
        for m in range(3):
            qkv_out[m] = jnp.concatenate(
                [part[:, m * 64 : (m + 1) * 64] for group in parts for part in group], axis=1
            ).astype(bf16)


def back(nf, qb, k, v, o, gctx, sums, x_all, mats, first_grad, gvec, key_block):
    heads, slots, _ = qb.shape
    tokens = slots // 4
    width = x_all.shape[2]
    hidden = sums[0].shape[1] * 2
    rows, cols = width // nf, hidden // nf
    shape = jax.ShapeDtypeStruct
    per_head = pl.BlockSpec((1, slots, LANE), lambda p, h: (h, 0, 0))
    chunk = ((rows, hidden // 2), (width // 2, cols), (rows, width // 2))
    vmem = lambda *size: pltpu.VMEM(size, bf16)
    triple = DMA((3,))
    hops = DMA((3, nf - 1))
    own = heads * 64
    packed = (rows // 2, 6 * 64)
    results = [
        shape((tokens, width), bf16),
        shape((rows, hidden), bf16),
        shape((cols, width), bf16),
        shape((rows, width), bf16),
        shape((3, rows, width), bf16),
        shape((16, LANE), f32),
        shape((8, cols), f32),
    ]
    return pl.pallas_call(
        functools.partial(back_kernel, nf, key_block, ((0,), (1, 2))),
        grid=(2, heads),
        out_shape=results,
        in_specs=[per_head] * 4 + [IN_VMEM] + [ANY] * 9,
        out_specs=[
            pl.BlockSpec(x.shape, functools.partial(lambda n, *_: (0,) * n, len(x.shape)))
            for x in results
        ],
        scratch_shapes=[
            pltpu.VMEM((64, slots // 2), f32),
            pltpu.VMEM((64, slots // 2), f32),
            pltpu.VMEM((heads, 64, slots), f32),
            vmem(heads, slots, LANE),
            vmem(heads, 64, slots),
            vmem(heads, 64, slots),
            vmem(3, own, slots),
            vmem(3, width, tokens),
            vmem(4, tokens, width),
            vmem(3, nf, rows, width),
            pltpu.VMEM((tokens, width), f32),
        ]
        + [vmem(*x.shape) for x in sums]
        + [vmem(nf - 1, *x) for x in chunk]
        + [vmem(*x) for x in chunk] * 2
        + [
            vmem(heads, nf, *packed),
            vmem(heads, nf - 1, *packed),
            vmem(heads, *packed),
            vmem(4, heads, *packed),
            pltpu.VMEM((16, width), f32),
            pltpu.VMEM((nf, 16, LANE), f32),
            pltpu.VMEM((nf, 16, LANE), f32),
            pltpu.VMEM((16, LANE), f32),
            pltpu.VMEM((4, 16, LANE), f32),
            triple, DMA((6,)), hops, hops, triple, triple, triple, triple,
            DMA((3, 3, heads)), DMA((3, 3, heads)), DMA((3, heads)),
            DMA((heads, nf - 1)), DMA((heads, nf - 1)), DMA((heads, 3)), DMA((heads, 3)),
            DMA((nf - 1,)), DMA((nf - 1,)), triple, triple,
        ],
        compiler_params=params(4),
        name="back",
    )(qb, k, v, o, gctx, *sums, x_all, *mats, first_grad, gvec)


def results_kernel(rows, output, states_grad, up, down, wout, qkv, vec, upb, *outs):
    outs[0][...] = output[...]
    outs[1][...] = states_grad[...]
    for m in range(3):
        outs[2 + m][...] = qkv[m].astype(f32)
    outs[5][...] = wout[...].astype(f32)
    outs[6][...] = up[...].astype(f32)
    outs[7][...] = down[...].astype(f32)
    for r in range(8):
        outs[8 + r][...] = vec[r, :rows]
    outs[16][...] = upb[0, :]


def results(rows, output, states_grad, up, down, wout, qkv, vec, upb):
    shape = jax.ShapeDtypeStruct
    pieces = 2
    grads = [shape(qkv.shape[1:], f32)] * 3 + [shape(x.shape, f32) for x in (wout, up, down)]
    outs = [shape(output.shape, bf16)] * 2 + grads
    lines = [shape((rows,), f32)] * 8 + [shape((upb.shape[1],), f32)]

    def cut(x):
        n = len(x.shape)
        size = x.shape[: n - 2] + (x.shape[n - 2] // pieces, x.shape[n - 1])
        return pl.BlockSpec(size, functools.partial(lambda n, i: (0,) * (n - 2) + (i, 0), n))

    def same(x):
        return pl.BlockSpec(x.shape, lambda i: (0,) * len(x.shape))

    return pl.pallas_call(
        functools.partial(results_kernel, rows),
        grid=(pieces,),
        out_shape=outs + lines,
        in_specs=[cut(x) for x in (output, states_grad, up, down, wout, qkv)] + [same(vec), same(upb)],
        out_specs=[cut(x) for x in outs] + [same(x) for x in lines],
        compiler_params=params(),
        name="results",
    )(output, states_grad, up, down, wout, qkv, vec, upb)


def fused_device(
    nf, states, query_weight, key_weight, value_weight, out_weight, query_bias, value_bias,
    out_bias, first_gain, first_shift, up_weight, up_bias, down_weight, down_bias, second_gain,
    second_shift, lengths, cotangent,
):
    tokens, width = states.shape
    rows = width // nf
    hidden = up_weight.shape[1]
    heads = width // 4 // 64
    qb, o, k, v, x_all, vec_all, ctx, wout, up, down = front(
        nf, heads, lengths, states, query_weight, key_weight, value_weight, out_weight, up_weight,
        down_weight,
        (
            query_bias, value_bias, out_bias, first_gain, first_shift, down_bias, second_gain,
            second_shift, up_bias,
        ),
        block=256, key_chunk=512,
    )
    output, first_grad, gctx, up_sum, down_sum, wout_sum, gvec, wq, wk, wv = feed(
        nf, lengths, states, cotangent, ctx, wout.reshape(width, width),
        up.reshape(width, hidden), down.reshape(hidden, width), vec_all,
        (query_weight, key_weight, value_weight),
    )
    states_grad, up_grad, down_grad, out_grad, qkv, vec_grad, upb_grad = back(
        nf, qb, k, v, o, gctx.reshape(4 * tokens, -1), (up_sum, down_sum, wout_sum), x_all,
        (wq, wk, wv), first_grad, gvec, key_block=384,
    )
    done = results(rows, output, states_grad, up_grad, down_grad, out_grad, qkv, vec_grad, upb_grad)
    output, states_grad, q_grad, k_grad, v_grad, out_grad, up_grad, down_grad = done[:8]
    lines = done[8:]
    return (
        output, states_grad, q_grad, k_grad, v_grad, out_grad, *lines[:5], up_grad, lines[8],
        down_grad, *lines[5:8],
    )


def solution(mesh):
    nf, ns = mesh.shape["fsdp"], mesh.shape["seq"]

    def choose(states, query_weight, *rest):
        rows, width = query_weight.shape
        fits = ns == 4 and nf == 8 and rows % 16 == 0 and width == 768 and states.shape[0] % 768 == 0
        device = functools.partial(fused_device, nf) if fits else per_device
        return device(states, query_weight, *rest)

    return jax.shard_map(
        choose,
        mesh=mesh,
        in_specs=(
            P(("fsdp", "seq"), None),
            P("fsdp", None),
            P("fsdp", None),
            P("fsdp", None),
            P("fsdp", None),
            P("fsdp"),
            P("fsdp"),
            P("fsdp"),
            P("fsdp"),
            P("fsdp"),
            P("fsdp", None),
            P("fsdp"),
            P("fsdp", None),
            P("fsdp"),
            P("fsdp"),
            P("fsdp"),
            P("fsdp"),
            P(("fsdp", "seq"), None),
        ),
        out_specs=(
            P(("fsdp", "seq"), None),
            P(("fsdp", "seq"), None),
            P("fsdp", None),
            P("fsdp", None),
            P("fsdp", None),
            P("fsdp", None),
            P("fsdp"),
            P("fsdp"),
            P("fsdp"),
            P("fsdp"),
            P("fsdp"),
            P("fsdp", None),
            P("fsdp"),
            P("fsdp", None),
            P("fsdp"),
            P("fsdp"),
            P("fsdp"),
        ),
        check_vma=False,
    )
```
